32 devices in a mesh: pb: 4 (over y, x), pa: 8 (over z, core).
Axes of the slice: x: 2, y: 2, z: 4, core: 2. Of those that a mesh axis runs over, the one named last changes fastest.
Arguments:
- question_in: bfloat16 [256, 64, 768], P(('pb', 'pa')), may hold values from -6 to 6
- passage_in: bfloat16 [64, 256, 768], P(('pb', 'pa')), may hold values from -6 to 6
- question_len: int32 [256], P(('pb', 'pa')), may hold values from 8 to 64, as said below
- passage_len: int32 [64], P(('pb', 'pa')), may hold values from 40 to 256, as said below
- positive: int32 [256], P('pb'), may hold values from 0 to 63, as said below
- question_cot: bfloat16 [256, 64, 768], P(('pb', 'pa')), may hold values from -6 to 6
- passage_cot: bfloat16 [64, 256, 768], P(('pb', 'pa')), may hold values from -6 to 6
- w_joined: bfloat16 [2, 768, 2304], P(None, ('pb', 'pa')), may hold values from -0.21875 to 0.21875
- w_output: bfloat16 [2, 768, 768], P(None, ('pb', 'pa')), may hold values from -0.875 to 0.875
- w_expand: bfloat16 [2, 768, 3072], P(None, ('pb', 'pa')), may hold values from -0.21875 to 0.21875
- w_reduce: bfloat16 [2, 3072, 768], P(None, ('pb', 'pa')), may hold values from -0.109375 to 0.109375
- vectors: bfloat16 [2, 8, 768], P(None, None, ('pb', 'pa'))
- b_expand: bfloat16 [2, 3072], P(None, ('pb', 'pa')), may hold values from -4 to 4
Outputs:
- question_out: bfloat16 [256, 64, 768], P(('pb', 'pa'))
- passage_out: bfloat16 [64, 256, 768], P(('pb', 'pa'))
- question_loss: float32 [256], P(('pb', 'pa'))
- question_grad: float32 [256, 64, 768], P(('pb', 'pa'))
- passage_grad: float32 [64, 256, 768], P(('pb', 'pa'))
- grad_joined: float32 [2, 768, 2304], P(None, ('pb', 'pa'))
- grad_output: float32 [2, 768, 768], P(None, ('pb', 'pa'))
- grad_expand: float32 [2, 768, 3072], P(None, ('pb', 'pa'))
- grad_reduce: float32 [2, 3072, 768], P(None, ('pb', 'pa'))
- grad_vectors: float32 [2, 8, 768], P(None, None, ('pb', 'pa'))
- grad_b_expand: float32 [2, 3072], P(None, ('pb', 'pa'))
The draws below stay inside these ranges and needn't reach their ends.
Inputs may be any that keep to these rules, and one draw needn't show every extreme that they name: `question_len`: valid tokens of a question; slot 0 is always valid. `passage_len`: valid tokens of a passage; slot 0 is always valid. `positive`: any passage of the batch.
All inputs are finite; a program needn't handle non-finite values.
Results may differ from the reference program's by a relative error of at most 0.014.
Values may be sent and summed in bfloat16 or wider, within the bound.
No kernel may reach another device: no remote copies, remote signals or barrier semaphores. Data moves between devices by JAX's collectives and lax.ppermute only.
A program may use at most 256 MiB of HBM per device.

```python
import jax
import jax.numpy as jnp
from jax import lax

D = 768
HEADS = 12
HDIM = 64
FF = 3072
LQ = 64
LP = 256
QDEV = 8
PDEV = 2
NQ = 256
NP = 64


def draw_ragged(key, count_all, lowest, highest):
    base_key, place_key, other_key = jax.random.split(key, 3)
    values = jax.random.randint(base_key, (count_all,), lowest, highest + 1)
    top_place = jax.random.randint(place_key, (), 0, count_all)
    low_place = (top_place + jax.random.randint(other_key, (), 1, count_all)) % count_all
    positions = jnp.arange(count_all)
    values = jnp.where(positions == top_place, highest, values)
    return jnp.where(positions == low_place, lowest, values).astype(jnp.int32)


def draw_question_len(key, part):
    return draw_ragged(jax.random.fold_in(key, 11), NQ, LQ // 8, LQ)


def draw_passage_len(key, part):
    return draw_ragged(jax.random.fold_in(key, 23), NP, LP // 8 + 8, LP)


def draw_positive(key, part):
    return draw_ragged(jax.random.fold_in(key, 37), NQ, 0, NP - 1)


def draw_vectors(key, part):
    first_key, second_key = jax.random.split(jax.random.fold_in(key, 53))
    shifts = 0.3 * jax.random.normal(first_key, (2, 8, D), jnp.float32)
    scales = 1.0 + 0.25 * jax.random.uniform(second_key, (2, 8, D), jnp.float32, -1.0, 1.0)
    row_ids = jnp.arange(8)
    is_gain = ((row_ids == 3) | (row_ids == 6))[None, :, None]
    return jnp.where(is_gain, scales, shifts).astype(jnp.bfloat16)


def block_levels(rng, extent, cuts, least, top_value):
    factor_of, own = 1.0, jax.random.fold_in(rng, 6)
    for position, shards_of in cuts:
        steps = jnp.exp(jax.random.uniform(jax.random.fold_in(own, position), (shards_of,), jnp.float32, least / len(cuts), top_value / len(cuts)))
        factor_of = factor_of * jnp.repeat(steps, extent[position] // shards_of).reshape([-1 if axis == position else 1 for axis in range(len(extent))])
    return factor_of


def scatter_about(key, extent, width, reach, pieces=(), kind=jnp.bfloat16):
    entries = jax.random.normal(key, extent, jnp.float32) * width
    if len(pieces) > 0:
        entries = block_levels(key, extent, pieces, -0.22, 0.18) * entries
    return jnp.clip(entries, min=-reach, max=reach).astype(kind)


def setup_inputs(seed: int = 0) -> dict:
    arg_keys = jax.random.split(jax.random.key(seed), 14)
    return {
        "question_in": scatter_about(arg_keys[0], (NQ, LQ, D), 1.0, 6.0, ((0, 32),)),
        "passage_in": scatter_about(arg_keys[1], (NP, LP, D), 1.0, 6.0, ((0, 32),)),
        "question_len": draw_question_len(jax.random.fold_in(arg_keys[13], 71), 0),
        "passage_len": draw_passage_len(jax.random.fold_in(arg_keys[13], 71), 0),
        "positive": draw_positive(jax.random.fold_in(arg_keys[13], 71), 0),
        "question_cot": scatter_about(arg_keys[5], (NQ, LQ, D), 1.0, 6.0, ((0, 32),)),
        "passage_cot": scatter_about(arg_keys[6], (NP, LP, D), 1.0, 6.0, ((0, 32),)),
        "w_joined": scatter_about(arg_keys[7], (2, D, 3 * D), D ** -0.5, 0.21875, ((1, 32),)),
        "w_output": scatter_about(arg_keys[8], (2, D, D), (D // 16) ** -0.5, 0.875, ((1, 32),)),
        "w_expand": scatter_about(arg_keys[9], (2, D, FF), D ** -0.5, 0.21875, ((1, 32),)),
        "w_reduce": scatter_about(arg_keys[10], (2, FF, D), FF ** -0.5, 0.109375, ((1, 32),)),
        "vectors": draw_vectors(jax.random.fold_in(arg_keys[13], 71), 0),
        "b_expand": scatter_about(arg_keys[12], (2, FF), 0.3, 4.0, ((1, 32),)),
    }


@jax.custom_vjp
def low(v):
    return lax.optimization_barrier(v.astype(jnp.bfloat16)).astype(jnp.float32)

@jax.custom_vjp
def low_back(v):
    return v

def low_keep(v):
    return (low(v), None)

def low_pass(kept, grad):
    return (grad,)

def back_keep(v):
    return (v, None)

def back_low(kept, grad):
    return (low(grad),)
low.defvjp(low_keep, low_pass)
low_back.defvjp(back_keep, back_low)
norm_eps = 1e-06
masked_score = -1000000000.0
score_scale = 0.0625
loss_weight = 16.0
highest = lax.Precision.HIGHEST

def layer_norm(values, norm_gain, norm_shift):
    centred = values - lax.optimization_barrier(jnp.mean(values, axis=-1, keepdims=True))
    spread = lax.optimization_barrier(jnp.mean(centred * centred, axis=-1, keepdims=True))
    return centred * lax.rsqrt(spread + norm_eps) * norm_gain + norm_shift

def tower_group(inputs, lengths, params):
    w_joined, w_output, w_expand, w_reduce, vectors, b_expand = params
    num_seq, seq_len, model_width = inputs.shape
    token_rows = inputs.reshape(num_seq * seq_len, model_width)
    joined_proj = jnp.dot(token_rows, w_joined, precision=highest)
    head_shape = (num_seq, seq_len, HEADS, HDIM)
    queries = low(low_back(joined_proj[:, :model_width] + vectors[0])).reshape(head_shape)
    key_rows = low(low_back(joined_proj[:, model_width:2 * model_width])).reshape(head_shape)
    value_rows = low(low_back(joined_proj[:, 2 * model_width:] + vectors[1])).reshape(head_shape)
    scores = jnp.einsum('sqhd,skhd->shqk', queries, key_rows, precision=highest) * HDIM ** (-0.5)
    valid_slots = jnp.arange(seq_len, dtype=jnp.int32)[None, :] < lengths[:, None]
    scores = low_back(jnp.where(valid_slots[:, None, None, :], scores, masked_score))
    attn_probs = low(jax.nn.softmax(scores, axis=-1))
    context = jnp.einsum('shqk,skhd->sqhd', attn_probs, value_rows, precision=highest)
    context = low(low_back(context.reshape(num_seq * seq_len, model_width)))
    attended = low_back(jnp.dot(context, w_output, precision=highest) + vectors[2])
    mid_norm = layer_norm(token_rows + attended, vectors[3], vectors[4])
    expanded = low_back(jnp.dot(low(mid_norm), w_expand, precision=highest) + b_expand)
    active = low(jax.nn.gelu(expanded, approximate=False))
    reduced = low_back(jnp.dot(active, w_reduce, precision=highest) + vectors[5])
    row_mask = valid_slots.reshape(-1, 1).astype(jnp.float32)
    outputs = layer_norm(mid_norm + reduced, vectors[6], vectors[7]) * row_mask
    return low(outputs).reshape(num_seq, seq_len, model_width)

def tower(inputs, lengths, params, group_size):
    count_all, seq_len, model_width = inputs.shape
    blocks = (inputs.reshape(count_all // group_size, group_size, seq_len, model_width), lengths.reshape(count_all // group_size, group_size))

    def run_block(block_pair):
        return tower_group(block_pair[0], block_pair[1], params)
    outputs = lax.map(jax.checkpoint(run_block), blocks)
    return outputs.reshape(count_all, seq_len, model_width)

def forward(question_x, passage_x, weights, question_len, passage_len, positive):
    params_q = tuple((weight_piece[0] for weight_piece in weights))
    params_p = tuple((weight_piece[1] for weight_piece in weights))
    question_out = tower(question_x, question_len, params_q, QDEV)
    passage_out = tower(passage_x, passage_len, params_p, PDEV)
    similarity = low_back(jnp.dot(question_out[:, 0, :], passage_out[:, 0, :].T, precision=highest) * score_scale)
    target_hot = (jnp.arange(NP, dtype=jnp.int32)[None, :] == positive[:, None]).astype(jnp.float32)
    question_loss = jax.nn.logsumexp(similarity, axis=1) - lax.optimization_barrier(jnp.sum(similarity * target_hot, axis=1))
    return (question_out, passage_out, question_loss)

def reference(question_in, passage_in, question_len, passage_len, positive, question_cot, passage_cot, w_joined, w_output, w_expand, w_reduce, vectors, b_expand):
    weights = (w_joined.astype(jnp.float32), w_output.astype(jnp.float32), w_expand.astype(jnp.float32), w_reduce.astype(jnp.float32), vectors.astype(jnp.float32), b_expand.astype(jnp.float32))

    def objective(question_x, passage_x, weight_set):
        return forward(question_x, passage_x, weight_set, question_len, passage_len, positive)
    results, pullback = jax.vjp(objective, question_in.astype(jnp.float32), passage_in.astype(jnp.float32), weights)
    question_out, passage_out, question_loss = results
    question_grad, passage_grad, grads = pullback((question_cot.astype(jnp.float32), passage_cot.astype(jnp.float32), jnp.full_like(question_loss, loss_weight)))
    return (question_out.astype(jnp.bfloat16), passage_out.astype(jnp.bfloat16), question_loss, question_grad, passage_grad, grads[0], grads[1], grads[2], grads[3], grads[4], grads[5])
```

```python
import functools

import jax
import jax.numpy as jnp
from jax import lax
from jax.experimental import pallas as pl
from jax.experimental.pallas import tpu as pltpu
from jax.sharding import PartitionSpec as P

D = 768
HEADS = 12
HDIM = 64
FF = 3072
AXES = ("pb", "pa")
BLOCK = 256

norm_eps = 1e-06
masked_score = -1000000000.0
score_scale = 0.0625
loss_weight = 16.0
head_scale = HDIM ** (-0.5)
F32 = jnp.float32
BF16 = jnp.bfloat16
VMEM_LIMIT = 56 * 1024 * 1024


def bits_of(count):
    return [1 << shift for shift in range(count.bit_length() - 1)]


class Places:
    def __init__(self, mesh):
        self.pb_n = mesh.shape["pb"]
        self.pa_n = mesh.shape["pa"]
        self.nz = self.pa_n // 2
        self.half = self.nz // 2
        self.chips = self.pb_n * self.nz
        pb_bits = bits_of(self.pb_n)
        turn = len(pb_bits) // 2
        low_z = [("z", bit) for bit in bits_of(self.half)]
        first = [("pb", bit) for bit in pb_bits]
        second = first[turn:] + first[:turn]
        self.orders = ([("z", self.half)] + low_z + first, [("z", self.half)] + low_z + second)
        self.steps = len(self.orders[0])

    def chip_mask(self, move):
        axis, bit = move
        return bit * self.nz if axis == "pb" else bit

    def stack_masks(self, core):
        masks = [0]
        for move in self.orders[core]:
            masks = masks + [mask ^ self.chip_mask(move) for mask in masks]
        return masks

    def pairs(self, step):
        out = []
        for pb in range(self.pb_n):
            for pa in range(self.pa_n):
                axis, bit = self.orders[pa % 2][step]
                to_pb, to_pa = (pb ^ bit, pa) if axis == "pb" else (pb, pa ^ (2 * bit))
                out.append((pb * self.pa_n + pa, to_pb * self.pa_n + to_pa))
        return out

    def swap(self, values, step):
        return lax.ppermute(values, AXES, self.pairs(step))

    def swap_core(self, values):
        return lax.ppermute(values, "pa", [(i, i ^ 1) for i in range(self.pa_n)])

    def swap_tower(self, values):
        return lax.ppermute(values, "pa", [(i, i ^ (2 * self.half)) for i in range(self.pa_n)])


def dot(left, right, dims=((1,), (0,))):
    return lax.dot_general(left, right, (dims, ((), ())), preferred_element_type=F32)


def assemble_kernel(segments, rows, idx_ref, *refs):
    count = len(segments)
    sources, outs = refs[:4], refs[4 : 4 + count]
    buffer, in_sem, out_sem = refs[4 + count :]
    core = idx_ref[1, 0]
    part = sources[0].shape[0]
    loads = [
        pltpu.make_async_copy(source, buffer.at[pl.ds(k * part, part)], in_sem.at[k])
        for k, source in enumerate(sources)
    ]
    for load in loads:
        load.start()
    stores = []
    for k in range(4):
        loads[k].wait()
        half = core if k < 2 else 1 - core
        for j in range(part):
            slot = k * part + j
            place = idx_ref[0, slot]
            for s, (start, width, both) in enumerate(segments):
                if both and k >= 2:
                    continue
                column = 0 if both else pl.multiple_of(half * width, 128)
                store = pltpu.make_async_copy(
                    buffer.at[slot, :, pl.ds(start, width)],
                    outs[s].at[place, :, pl.ds(column, width)],
                    out_sem.at[s, slot],
                )
                store.start()
                stores.append(store)
    for store in stores:
        store.wait()


def assemble(parts, table, segments):
    part, rows, width = parts[0].shape
    chips = 2 * part
    shapes = [
        jax.ShapeDtypeStruct((chips, rows, w if both else 2 * w), BF16) for _, w, both in segments
    ]
    return pl.pallas_call(
        functools.partial(assemble_kernel, segments, rows),
        out_shape=shapes,
        in_specs=[pl.BlockSpec(memory_space=pltpu.SMEM)] + [pl.BlockSpec(memory_space=pl.ANY)] * 4,
        out_specs=[pl.BlockSpec(memory_space=pl.ANY)] * len(segments),
        scratch_shapes=[
            pltpu.VMEM((2 * chips, rows, width), BF16),
            pltpu.SemaphoreType.DMA((4,)),
            pltpu.SemaphoreType.DMA((len(segments), 2 * chips)),
        ],
        compiler_params=pltpu.CompilerParams(vmem_limit_bytes=VMEM_LIMIT),
        cost_estimate=pl.CostEstimate(
            flops=0, bytes_accessed=4 * 2 * chips * rows * width, transcendentals=0
        ),
        name="assemble",
    )(table, *parts)


def assemble_plain(parts, table, segments, core):
    own = jnp.concatenate(parts[:2], axis=0)
    other = jnp.concatenate(parts[2:], axis=0)
    chips, rows, width = own.shape
    own_order = jnp.argsort(table[0, :chips])
    other_order = jnp.argsort(table[0, chips:])
    own = jnp.take(own, own_order, axis=0)
    other = jnp.take(other, other_order, axis=0)
    left = jnp.where(core == 0, own, other)
    right = jnp.where(core == 0, other, own)
    outs = []
    for start, w, both in segments:
        if both:
            outs.append(left[:, :, start : start + w])
        else:
            outs.append(
                jnp.concatenate(
                    [left[:, :, start : start + w], right[:, :, start : start + w]], axis=2
                )
            )
    return outs


def fold_kernel(widths, idx_ref, core_ref, *refs):
    count = len(widths)
    ins, (keep_ref, send_ref) = refs[: 4 * count], refs[4 * count :]
    column = 0
    for s, width in enumerate(widths):
        mine, got, theirs, also = ins[4 * s : 4 * s + 4]
        keep_ref[:, :, column : column + width] = mine[...] + got[...].astype(F32)
        send_ref[:, :, column : column + width] = (theirs[...] + also[...].astype(F32)).astype(BF16)
        column += width


def fold(fulls, received, idx, core):
    chips, rows = received[0].shape[:2]
    steps = chips // 2
    widths = [r.shape[2] for r in received]
    in_specs, operands = [], []
    for full, got in zip(fulls, received):
        width = got.shape[2]
        wide = full.shape[2] != width
        for offset in (0, steps):
            in_specs.append(
                pl.BlockSpec(
                    (1, rows, width),
                    lambda i, idx, core, o=offset, w=wide: (idx[i + o], 0, core[0] if w else 0),
                )
            )
            in_specs.append(
                pl.BlockSpec((1, rows, width), lambda i, idx, core, o=offset: (idx[i + o], 0, 0))
            )
            operands += [full, got]
    total = sum(widths)
    return pl.pallas_call(
        functools.partial(fold_kernel, widths),
        grid_spec=pltpu.PrefetchScalarGridSpec(
            num_scalar_prefetch=2,
            grid=(steps,),
            in_specs=in_specs,
            out_specs=[
                pl.BlockSpec((1, rows, total), lambda i, idx, core: (i, 0, 0)),
                pl.BlockSpec((1, rows, total), lambda i, idx, core: (i, 0, 0)),
            ],
        ),
        out_shape=[
            jax.ShapeDtypeStruct((steps, rows, total), F32),
            jax.ShapeDtypeStruct((steps, rows, total), BF16),
        ],
        compiler_params=pltpu.CompilerParams(vmem_limit_bytes=VMEM_LIMIT),
        cost_estimate=pl.CostEstimate(
            flops=0, bytes_accessed=chips * rows * total * 9, transcendentals=0
        ),
        name="fold",
    )(idx, core, *operands)


def attention_kernel(qkv_ref, qid_ref, kid_ref, context_ref, probs_ref):
    allowed = qid_ref[...] == kid_ref[0]
    lane = lax.broadcasted_iota(jnp.int32, (BLOCK, 128), 1)
    zero = jnp.zeros((BLOCK, 128), BF16)
    for pair in range(HEADS // 2):
        queries = qkv_ref[:, pair * 128 : pair * 128 + 128]
        keys = qkv_ref[:, D + pair * 128 : D + pair * 128 + 128]
        values = qkv_ref[:, 2 * D + pair * 128 : 2 * D + pair * 128 + 128]
        outs = []
        for side in range(2):
            mine = (lane < HDIM) if side == 0 else (lane >= HDIM)
            scores = dot(queries, jnp.where(mine, keys, zero), ((1,), (1,))) * head_scale
            scores = jnp.where(allowed, scores, masked_score)
            top = jnp.max(scores, axis=1, keepdims=True)
            grown = jnp.exp(scores - top)
            total = jnp.sum(grown, axis=1, keepdims=True)
            probs = (grown * (1.0 / total)).astype(BF16)
            probs_ref[0, 2 * pair + side] = probs
            outs.append(dot(probs, values))
        context_ref[:, pair * 128 : pair * 128 + 128] = jnp.where(
            lane < HDIM, outs[0], outs[1]
        ).astype(BF16)


def attention(qkv, qid, kid):
    rows = qkv.shape[0]
    blocks = rows // BLOCK
    return pl.pallas_call(
        attention_kernel,
        grid=(blocks,),
        in_specs=[
            pl.BlockSpec((BLOCK, 3 * D), lambda i: (i, 0)),
            pl.BlockSpec((BLOCK, 1), lambda i: (i, 0)),
            pl.BlockSpec((1, 1, BLOCK), lambda i: (i, 0, 0)),
        ],
        out_specs=[
            pl.BlockSpec((BLOCK, D), lambda i: (i, 0)),
            pl.BlockSpec((1, HEADS, BLOCK, BLOCK), lambda i: (i, 0, 0, 0)),
        ],
        out_shape=[
            jax.ShapeDtypeStruct((rows, D), BF16),
            jax.ShapeDtypeStruct((blocks, HEADS, BLOCK, BLOCK), BF16),
        ],
        compiler_params=pltpu.CompilerParams(vmem_limit_bytes=VMEM_LIMIT),
        cost_estimate=pl.CostEstimate(
            flops=4 * rows * BLOCK * D * 2,
            bytes_accessed=rows * (4 * D + HEADS * BLOCK) * 2,
            transcendentals=rows * HEADS * BLOCK,
        ),
        name="attention",
    )(qkv, qid, kid)


def attention_back_kernel(qkv_ref, probs_ref, grad_ref, out_ref):
    lane = lax.broadcasted_iota(jnp.int32, (BLOCK, 128), 1)
    zero = jnp.zeros((BLOCK, 128), BF16)
    for pair in range(HEADS // 2):
        cols = slice(pair * 128, pair * 128 + 128)
        queries = qkv_ref[:, pair * 128 : pair * 128 + 128]
        keys = qkv_ref[:, D + pair * 128 : D + pair * 128 + 128]
        values = qkv_ref[:, 2 * D + pair * 128 : 2 * D + pair * 128 + 128]
        grad = grad_ref[:, cols]
        d_q, d_k, d_v = [], [], []
        for side in range(2):
            mine = (lane < HDIM) if side == 0 else (lane >= HDIM)
            low = probs_ref[0, 2 * pair + side]
            d_probs = dot(jnp.where(mine, grad, zero), values, ((1,), (1,)))
            d_v.append(dot(low, grad, ((0,), (0,))))
            probs = low.astype(F32)
            row_dot = jnp.sum(d_probs * probs, axis=1, keepdims=True)
            d_scores = (probs * (d_probs - row_dot)).astype(BF16)
            d_q.append(dot(d_scores, keys))
            d_k.append(dot(d_scores, queries, ((0,), (0,))))
        first = lane < HDIM
        out_ref[:, pair * 128 : pair * 128 + 128] = (
            jnp.where(first, d_q[0], d_q[1]) * head_scale
        ).astype(BF16)
        out_ref[:, D + pair * 128 : D + pair * 128 + 128] = (
            jnp.where(first, d_k[0], d_k[1]) * head_scale
        ).astype(BF16)
        out_ref[:, 2 * D + pair * 128 : 2 * D + pair * 128 + 128] = jnp.where(
            first, d_v[0], d_v[1]
        ).astype(BF16)


def attention_back(qkv, probs, grad_context):
    rows = qkv.shape[0]
    blocks = rows // BLOCK
    return pl.pallas_call(
        attention_back_kernel,
        grid=(blocks,),
        in_specs=[
            pl.BlockSpec((BLOCK, 3 * D), lambda i: (i, 0)),
            pl.BlockSpec((1, HEADS, BLOCK, BLOCK), lambda i: (i, 0, 0, 0)),
            pl.BlockSpec((BLOCK, D), lambda i: (i, 0)),
        ],
        out_specs=pl.BlockSpec((BLOCK, 3 * D), lambda i: (i, 0)),
        out_shape=jax.ShapeDtypeStruct((rows, 3 * D), BF16),
        compiler_params=pltpu.CompilerParams(vmem_limit_bytes=VMEM_LIMIT),
        cost_estimate=pl.CostEstimate(
            flops=8 * rows * BLOCK * D * 2,
            bytes_accessed=rows * (7 * D + HEADS * BLOCK) * 2,
            transcendentals=0,
        ),
        name="attention_back",
    )(qkv, probs, grad_context)


def expand_kernel(mid_ref, w_ref, b_ref, active_ref, slope_ref):
    expanded = dot(mid_ref[...], w_ref[...]) + b_ref[...]
    phi = 0.5 + 0.5 * lax.erf(expanded * 0.7071067811865476)
    density = jnp.exp(expanded * expanded * -0.5) * 0.3989422804014327
    active_ref[...] = (expanded * phi).astype(BF16)
    slope_ref[...] = (phi + expanded * density).astype(BF16)


def expand(mid_low, w_expand, b_expand):
    rows = mid_low.shape[0]
    tile_r, tile_f = 256, 1024
    return pl.pallas_call(
        expand_kernel,
        grid=(FF // tile_f, rows // tile_r),
        in_specs=[
            pl.BlockSpec((tile_r, D), lambda j, i: (i, 0)),
            pl.BlockSpec((D, tile_f), lambda j, i: (0, j)),
            pl.BlockSpec((1, tile_f), lambda j, i: (0, j)),
        ],
        out_specs=[
            pl.BlockSpec((tile_r, tile_f), lambda j, i: (i, j)),
            pl.BlockSpec((tile_r, tile_f), lambda j, i: (i, j)),
        ],
        out_shape=[jax.ShapeDtypeStruct((rows, FF), BF16)] * 2,
        compiler_params=pltpu.CompilerParams(vmem_limit_bytes=VMEM_LIMIT),
        cost_estimate=pl.CostEstimate(
            flops=2 * rows * D * FF,
            bytes_accessed=2 * (rows * D + D * FF + 2 * rows * FF),
            transcendentals=2 * rows * FF,
        ),
        name="expand",
    )(mid_low, w_expand, b_expand)


def normalized(values):
    centred = values - jnp.mean(values, axis=-1, keepdims=True)
    spread = jnp.mean(centred * centred, axis=-1, keepdims=True)
    inverse = lax.rsqrt(spread + norm_eps)
    return centred * inverse, inverse


def norm_back(grad, gain, norm, inverse):
    scaled = grad * gain
    return inverse * (
        scaled
        - jnp.mean(scaled, axis=-1, keepdims=True)
        - norm * jnp.mean(scaled * norm, axis=-1, keepdims=True)
    )


def column_halves(values, core):
    width = values.shape[-1] // 2
    left, right = values[..., :width], values[..., width:]
    return jnp.where(core == 0, left, right), jnp.where(core == 0, right, left)


def per_device(places, *args):
    (
        question_in,
        passage_in,
        question_len,
        passage_len,
        positive,
        question_cot,
        passage_cot,
        w_joined,
        w_output,
        w_expand,
        w_reduce,
        vectors,
        b_expand,
    ) = args
    pb, pa = lax.axis_index("pb"), lax.axis_index("pa")
    z, core = pa // 2, pa % 2
    tower = z // places.half
    is_q = tower == 0
    chip = pb * places.nz + z
    masks = jnp.array([places.stack_masks(0), places.stack_masks(1)], jnp.int32)
    order = lax.dynamic_index_in_dim(masks, core, 0, keepdims=False) ^ chip
    other_order = lax.dynamic_index_in_dim(masks, 1 - core, 0, keepdims=False) ^ chip
    table = jnp.stack(
        [jnp.concatenate([order, other_order]), jnp.full((2 * places.chips,), core, jnp.int32)]
    ).astype(jnp.int32)
    core_arr = jnp.full((1,), core, jnp.int32)
    share = w_joined.shape[1]

    def start(own_half, other_half):
        got = places.swap_core(other_half)
        return jnp.concatenate(
            [jnp.where(core == 0, own_half, got), jnp.where(core == 0, got, own_half)], axis=1
        )

    small = jnp.concatenate(
        [
            vectors.transpose(0, 2, 1),
            b_expand.reshape(2, share, 4),
            jnp.zeros((2, share, 116), BF16),
        ],
        axis=2,
    )
    j_own, j_other = column_halves(w_joined, core)
    o_own, o_other = column_halves(w_output, core)
    e_own, e_other = column_halves(w_expand, core)
    r_own, r_other = column_halves(w_reduce, core)
    first = start(
        jnp.concatenate([j_own, o_own, small], axis=2),
        jnp.concatenate([j_other, o_other, small], axis=2),
    )
    second = start(e_own, e_other)
    third = start(r_own, r_other)

    def gather(piece):
        mine = lax.dynamic_index_in_dim(piece, tower, 0, keepdims=True)
        theirs = lax.dynamic_index_in_dim(piece, 1 - tower, 0, keepdims=True)
        stack = jnp.concatenate([mine, places.swap(theirs, 0)], axis=0)
        for step in range(1, places.steps - 1):
            stack = jnp.concatenate([stack, places.swap(stack, step)], axis=0)
        last = places.swap(stack, places.steps - 1)
        return [stack, last, places.swap_core(stack), places.swap_core(last)]

    def weights(piece, segments):
        parts = gather(piece)
        if parts[0].shape[1] % 8 == 0:
            return assemble(parts, table, segments)
        return assemble_plain(parts, table, segments, core)

    jw, ow = w_joined.shape[2] // 2, D // 2
    full_j, full_o, full_small = weights(
        first, [(0, jw, False), (jw, ow, False), (jw + ow, 128, True)]
    )
    (full_e,) = weights(second, [(0, FF // 2, False)])
    (full_r,) = weights(third, [(0, D // 2, False)])
    wj = full_j.reshape(D, 3 * D)
    wo = full_o.reshape(D, D)
    we = full_e.reshape(D, FF)
    wr = full_r.reshape(FF, D)
    small = full_small.reshape(D, 128).astype(F32)
    vec = small[:, :8].T
    bias_e = small[:, 8:12].reshape(1, FF)

    rows_q = question_in.reshape(-1, D)
    rows_p = passage_in.reshape(-1, D)
    own_rows = rows_q.shape[0]

    def exchange(q_side, p_side):
        mine = jnp.where(is_q, q_side, p_side)
        theirs = jnp.where(is_q, p_side, q_side)
        return jnp.concatenate([mine, places.swap_tower(theirs)], axis=0)

    def give_back(both):
        mine, theirs = both[:own_rows], places.swap_tower(both[own_rows:])
        return jnp.where(is_q, mine, theirs), jnp.where(is_q, theirs, mine)

    lq, lp = question_in.shape[1], passage_in.shape[1]
    valid_q = (jnp.arange(lq, dtype=jnp.int32)[None, :] < question_len[:, None]).astype(jnp.int32)
    valid_p = (jnp.arange(lp, dtype=jnp.int32)[None, :] < passage_len[:, None]).astype(jnp.int32)
    valid = exchange(valid_q.reshape(-1), valid_p.reshape(-1))
    tokens = exchange(rows_q, rows_p)
    cot = exchange(question_cot.reshape(-1, D), passage_cot.reshape(-1, D))
    rows = tokens.shape[0]
    row_ids = jnp.arange(rows, dtype=jnp.int32)
    seq = jnp.where(is_q, row_ids // lq, row_ids // lp)
    qid = seq.reshape(rows, 1)
    kid = jnp.where(valid > 0, seq, -1).reshape(rows // BLOCK, 1, BLOCK)
    row_mask = valid.reshape(rows, 1).astype(F32)

    bias_j = jnp.concatenate([vec[0], jnp.zeros((D,), F32), vec[1]])
    qkv = (dot(tokens, wj) + bias_j).astype(BF16)
    context, probs = attention(qkv, qid, kid)
    attended = dot(context, wo) + vec[2]
    norm_one, inverse_one = normalized(tokens.astype(F32) + attended)
    mid = norm_one * vec[3] + vec[4]
    mid_low = mid.astype(BF16)
    active, slope = expand(mid_low, we, bias_e)
    norm_two, inverse_two = normalized(mid + dot(active, wr) + vec[5])
    out = ((norm_two * vec[6] + vec[7]) * row_mask).astype(BF16)

    per_q = rows // lq
    every = lp // lq
    per_p = rows // lp
    slots = out.reshape(per_q, lq, D)[:, 0, :]
    others = places.swap_tower(slots)
    cls_q = jnp.where(is_q, slots, others)
    cls_p = jnp.where(is_q, others, slots)[::every]
    pad = (-(per_q + per_p)) % 8
    stack = jnp.concatenate([cls_q, cls_p, jnp.zeros((pad, D), BF16)], axis=0)[None]
    pair_masks = [0]
    for bit in bits_of(places.half):
        got = lax.ppermute(stack, "pa", [(i, i ^ (2 * bit)) for i in range(places.pa_n)])
        stack = jnp.concatenate([stack, got], axis=0)
        pair_masks = pair_masks + [m ^ (2 * bit) for m in pair_masks]
    for bit in bits_of(places.pb_n):
        got = lax.ppermute(stack, "pb", [(i, i ^ bit) for i in range(places.pb_n)])
        stack = jnp.concatenate([stack, got], axis=0)
        pair_masks = pair_masks + [m ^ (bit * places.pa_n) for m in pair_masks]
    stack = jnp.concatenate([stack, places.swap_core(stack)], axis=0)
    pair_masks = pair_masks + [m ^ 1 for m in pair_masks]
    groups = len(pair_masks)
    me = pb * places.pa_n + (pa % (2 * places.half))
    place = jnp.array(pair_masks, jnp.int32) ^ me
    shift = 2 * places.half
    dev_q = jnp.stack([place, place + shift], axis=1)
    dev_p = jnp.stack([place + shift, place], axis=1)
    nq, np_ = question_in.shape[0], passage_in.shape[0]
    q_ids = (dev_q[:, :, None] * nq + jnp.arange(nq, dtype=jnp.int32)).reshape(-1)
    p_ids = (dev_p[:, :, None] * np_ + jnp.arange(np_, dtype=jnp.int32)).reshape(-1)
    wanted = positive
    pos_masks = [0]
    for bit in bits_of(places.pb_n):
        got = lax.ppermute(wanted, "pb", [(i, i ^ bit) for i in range(places.pb_n)])
        wanted = jnp.concatenate([wanted, got])
        pos_masks = pos_masks + [m ^ bit for m in pos_masks]
    per_pb = positive.shape[0]
    slot_of_pb = jnp.zeros((places.pb_n,), jnp.int32)
    slot_of_pb = slot_of_pb.at[jnp.array(pos_masks, jnp.int32) ^ pb].set(
        jnp.arange(places.pb_n, dtype=jnp.int32)
    )
    wanted = jnp.take(wanted, slot_of_pb[q_ids // per_pb] * per_pb + q_ids % per_pb)

    all_q = stack[:, :per_q].reshape(groups * per_q, D)
    all_p = stack[:, per_q : per_q + per_p].reshape(groups * per_p, D)
    similarity = dot(all_q, all_p, ((1,), (1,))) * score_scale
    hot = (wanted[:, None] == p_ids[None, :]).astype(F32)
    top = jnp.max(similarity, axis=1, keepdims=True)
    grown = jnp.exp(similarity - top)
    total = jnp.sum(grown, axis=1, keepdims=True)
    own_sim = similarity[:per_q]
    loss = top[:per_q, 0] + jnp.log(total[:per_q, 0]) - jnp.sum(own_sim * hot[:per_q], axis=1)
    question_loss = lax.dynamic_slice_in_dim(loss, tower * nq, nq)
    d_sim = (loss_weight * (grown / total - hot)).astype(BF16)
    d_q = dot(d_sim[:per_q], all_p) * score_scale
    d_p = dot(d_sim[:, :per_p], all_q, ((0,), (0,))) * score_scale
    d_p = jnp.concatenate(
        [d_p.reshape(per_p, 1, D), jnp.zeros((per_p, every - 1, D), F32)], axis=1
    ).reshape(per_q, D)
    d_slot = jnp.where(is_q, d_q, d_p)

    d_out = cot.astype(F32).reshape(per_q, lq, D)
    at_slot = jnp.arange(lq, dtype=jnp.int32)[None, :, None] == 0
    d_out = d_out + jnp.where(at_slot, d_slot[:, None, :], 0.0)
    d_out = d_out.reshape(rows, D) * row_mask
    d_second = norm_back(d_out, vec[6], norm_two, inverse_two)
    g_gain_two = jnp.sum(d_out * norm_two, axis=0)
    g_shift_two = jnp.sum(d_out, axis=0)
    d_reduced = d_second.astype(BF16)
    g_bias_reduce = jnp.sum(d_reduced.astype(F32), axis=0)

    def as_pieces(values):
        return values.reshape(places.chips, values.shape[0] // places.chips, values.shape[1])

    def other_half(full):
        width = full.shape[2] // 2
        return lax.dynamic_slice_in_dim(full, (1 - core) * width, width, axis=2).astype(BF16)

    def scatter(fulls):
        fulls = [as_pieces(full) for full in fulls]
        received = [
            places.swap_core(full.astype(BF16) if full.shape[2] == 128 else other_half(full))
            for full in fulls
        ]
        keep, send = fold(fulls, received, order, core_arr)
        for step in range(places.steps - 1, 0, -1):
            got = places.swap(send, step)
            both = keep.shape[0] // 2
            if step > 1:
                send = (keep[both:] + got[both:].astype(F32)).astype(BF16)
                keep = keep[:both] + got[:both].astype(F32)
            else:
                total = keep + got.astype(F32)
                keep, send = total[0:1], total[1:2].astype(BF16)
        got = places.swap(send, 0)
        mine = keep.astype(BF16)
        towers = jnp.where(
            is_q, jnp.concatenate([mine, got], axis=0), jnp.concatenate([got, mine], axis=0)
        )
        count = towers.shape[1] // 2
        keep_rows = lax.dynamic_slice_in_dim(towers, core * count, count, axis=1)
        send_rows = lax.dynamic_slice_in_dim(towers, (1 - core) * count, count, axis=1)
        got_rows = places.swap_core(send_rows)
        outs, column = [], 0
        for full in fulls:
            if full.shape[2] == 128:
                outs.append(keep_rows[:, :, column : column + 128].astype(F32))
                column += 128
                continue
            width = full.shape[2] // 2
            mine = keep_rows[:, :, column : column + width]
            theirs = got_rows[:, :, column : column + width]
            outs.append(
                jnp.concatenate(
                    [jnp.where(core == 0, mine, theirs), jnp.where(core == 0, theirs, mine)],
                    axis=2,
                ).astype(F32)
            )
            column += width
        return outs

    (grad_reduce,) = scatter([dot(active, d_reduced, ((0,), (0,)))])
    d_active = dot(d_reduced, wr, ((1,), (1,)))
    d_expanded = (d_active * slope.astype(F32)).astype(BF16)
    g_bias_expand = jnp.sum(d_expanded.astype(F32), axis=0)
    (grad_expand,) = scatter([dot(mid_low, d_expanded, ((0,), (0,)))])
    d_mid = d_second + dot(d_expanded, we, ((1,), (1,)))
    d_first = norm_back(d_mid, vec[3], norm_one, inverse_one)
    g_gain_one = jnp.sum(d_mid * norm_one, axis=0)
    g_shift_one = jnp.sum(d_mid, axis=0)
    d_attended = d_first.astype(BF16)
    g_bias_output = jnp.sum(d_attended.astype(F32), axis=0)
    (grad_output,) = scatter([dot(context, d_attended, ((0,), (0,)))])
    d_context = dot(d_attended, wo, ((1,), (1,))).astype(BF16)
    d_joined = attention_back(qkv, probs, d_context)
    d_tokens = d_first + dot(d_joined, wj, ((1,), (1,)))
    g_joined_bias = jnp.sum(d_joined.astype(F32), axis=0)
    g_vec = jnp.stack(
        [
            g_joined_bias[:D],
            g_joined_bias[2 * D :],
            g_bias_output,
            g_gain_one,
            g_shift_one,
            g_bias_reduce,
            g_gain_two,
            g_shift_two,
        ]
    )
    g_small = jnp.concatenate(
        [g_vec.T, g_bias_expand.reshape(D, 4), jnp.zeros((D, 116), F32)], axis=1
    )
    grad_joined, grad_small = scatter([dot(tokens, d_joined, ((0,), (0,))), g_small])
    grad_vectors = grad_small[:, :, :8].transpose(0, 2, 1)
    grad_b_expand = grad_small[:, :, 8:12].reshape(2, 4 * share)

    out_q, out_p = give_back(out)
    grad_q, grad_p = give_back(d_tokens.astype(BF16))
    return (
        out_q.reshape(question_in.shape),
        out_p.reshape(passage_in.shape),
        question_loss,
        grad_q.astype(F32).reshape(question_in.shape),
        grad_p.astype(F32).reshape(passage_in.shape),
        grad_joined,
        grad_output,
        grad_expand,
        grad_reduce,
        grad_vectors,
        grad_b_expand,
    )


def solution(mesh):
    in_specs = (
        P(("pb", "pa"), None, None),
        P(("pb", "pa"), None, None),
        P(("pb", "pa")),
        P(("pb", "pa")),
        P("pb"),
        P(("pb", "pa"), None, None),
        P(("pb", "pa"), None, None),
        P(None, ("pb", "pa"), None),
        P(None, ("pb", "pa"), None),
        P(None, ("pb", "pa"), None),
        P(None, ("pb", "pa"), None),
        P(None, None, ("pb", "pa")),
        P(None, ("pb", "pa")),
    )
    out_specs = (
        P(("pb", "pa"), None, None),
        P(("pb", "pa"), None, None),
        P(("pb", "pa")),
        P(("pb", "pa"), None, None),
        P(("pb", "pa"), None, None),
        P(None, ("pb", "pa"), None),
        P(None, ("pb", "pa"), None),
        P(None, ("pb", "pa"), None),
        P(None, ("pb", "pa"), None),
        P(None, None, ("pb", "pa")),
        P(None, ("pb", "pa")),
    )
    return jax.shard_map(
        functools.partial(per_device, Places(mesh)),
        mesh=mesh,
        in_specs=in_specs,
        out_specs=out_specs,
        check_vma=False,
    )
```

```python
import functools

import jax
import jax.numpy as jnp
from jax import lax
from jax.experimental import pallas as pl
from jax.experimental.pallas import tpu as pltpu
from jax.sharding import PartitionSpec as P

D = 768
HEADS = 12
HDIM = 64
FF = 3072
AXES = ("pb", "pa")
BLOCK = 256

norm_eps = 1e-06
masked_score = -1000000000.0
score_scale = 0.0625
loss_weight = 16.0
head_scale = HDIM ** (-0.5)
F32 = jnp.float32
BF16 = jnp.bfloat16
VMEM_LIMIT = 56 * 1024 * 1024


def bits_of(count):
    return [1 << shift for shift in range(count.bit_length() - 1)]


class Places:
    def __init__(self, mesh):
        self.pb_n = mesh.shape["pb"]
        self.pa_n = mesh.shape["pa"]
        self.nz = self.pa_n // 2
        self.half = self.nz // 2
        self.chips = self.pb_n * self.nz
        pb_bits = bits_of(self.pb_n)
        turn = len(pb_bits) // 2
        low_z = [("z", bit) for bit in bits_of(self.half)]
        first = [("pb", bit) for bit in pb_bits]
        second = first[turn:] + first[:turn]
        self.orders = ([("z", self.half)] + low_z + first, [("z", self.half)] + low_z + second)
        self.steps = len(self.orders[0])

    def chip_mask(self, move):
        axis, bit = move
        return bit * self.nz if axis == "pb" else bit

    def stack_masks(self, core):
        masks = [0]
        for move in self.orders[core]:
            masks = masks + [mask ^ self.chip_mask(move) for mask in masks]
        return masks

    def pairs(self, step):
        out = []
        for pb in range(self.pb_n):
            for pa in range(self.pa_n):
                axis, bit = self.orders[pa % 2][step]
                to_pb, to_pa = (pb ^ bit, pa) if axis == "pb" else (pb, pa ^ (2 * bit))
                out.append((pb * self.pa_n + pa, to_pb * self.pa_n + to_pa))
        return out

    def swap(self, values, step):
        return lax.ppermute(values, AXES, self.pairs(step))

    def swap_core(self, values):
        return lax.ppermute(values, "pa", [(i, i ^ 1) for i in range(self.pa_n)])

    def swap_tower(self, values):
        return lax.ppermute(values, "pa", [(i, i ^ (2 * self.half)) for i in range(self.pa_n)])


def dot(left, right, dims=((1,), (0,))):
    return lax.dot_general(left, right, (dims, ((), ())), preferred_element_type=F32)


def tie(*values):
    return lax.optimization_barrier(values)


def assemble_kernel(segments, idx_ref, *refs):
    count = len(segments)
    sources, outs = refs[:4], refs[4 : 4 + count]
    buffer, in_sem, out_sem = refs[4 + count :]
    core = idx_ref[2, 0]
    part = sources[0].shape[0]
    loads = [
        pltpu.make_async_copy(source, buffer.at[pl.ds(k * part, part)], in_sem.at[k])
        for k, source in enumerate(sources)
    ]
    for load in loads:
        load.start()
    stores = []
    for k in range(4):
        loads[k].wait()
        half = core if k < 2 else 1 - core
        for j in range(part):
            slot = k * part + j
            place = idx_ref[k // 2, (k % 2) * part + j]
            for s, (start, width) in enumerate(segments):
                store = pltpu.make_async_copy(
                    buffer.at[slot, :, pl.ds(start, width)],
                    outs[s].at[place, half],
                    out_sem.at[s, slot],
                )
                store.start()
                stores.append(store)
    for store in stores:
        store.wait()


def assemble(parts, table, segments):
    part, rows, width = parts[0].shape
    chips = 2 * part
    shapes = [jax.ShapeDtypeStruct((chips, 2, rows, w), BF16) for _, w in segments]
    return pl.pallas_call(
        functools.partial(assemble_kernel, segments),
        out_shape=shapes,
        in_specs=[pl.BlockSpec(memory_space=pltpu.SMEM)] + [pl.BlockSpec(memory_space=pl.ANY)] * 4,
        out_specs=[pl.BlockSpec(memory_space=pl.ANY)] * len(segments),
        scratch_shapes=[
            pltpu.VMEM((2 * chips, rows, width), BF16),
            pltpu.SemaphoreType.DMA((4,)),
            pltpu.SemaphoreType.DMA((len(segments), 2 * chips)),
        ],
        compiler_params=pltpu.CompilerParams(vmem_limit_bytes=VMEM_LIMIT),
        cost_estimate=pl.CostEstimate(
            flops=0, bytes_accessed=4 * 2 * chips * rows * width, transcendentals=0
        ),
        name="assemble",
    )(table, *parts)


def assemble_plain(parts, table, segments):
    own = jnp.take(jnp.concatenate(parts[:2], axis=0), jnp.argsort(table[0]), axis=0)
    other = jnp.take(jnp.concatenate(parts[2:], axis=0), jnp.argsort(table[1]), axis=0)
    first = table[2, 0] == 0
    both = jnp.stack([jnp.where(first, own, other), jnp.where(first, other, own)], axis=1)
    return [both[..., start : start + w] for start, w in segments]


def split_slabs(acc, core, chips, mine_ref, theirs_ref, cols, within):
    rows = acc.shape[0] // (2 * chips)
    for s in range(chips):
        low = acc[2 * s * rows : (2 * s + 1) * rows]
        high = acc[(2 * s + 1) * rows : (2 * s + 2) * rows]
        mine, theirs = within(s)
        mine_ref[mine, :, cols] = jnp.where(core == 0, low, high).astype(BF16)
        theirs_ref[theirs, :, cols] = jnp.where(core == 0, high, low).astype(BF16)


def weight_grad_kernel(chips, extra, table_ref, left_ref, right_ref, *refs):
    mine_ref, theirs_ref = refs[-2:]
    core = table_ref[2, 0]
    acc = dot(left_ref[...], right_ref[...], ((0,), (0,)))
    width = acc.shape[1]

    def within(s):
        return table_ref[0, s], table_ref[1, s]

    if not extra:
        split_slabs(acc, core, chips, mine_ref, theirs_ref, slice(None), within)
        return
    step = pl.program_id(0)
    cols = pl.ds(pl.multiple_of(step * width, 128), width)
    split_slabs(acc, core, chips, mine_ref, theirs_ref, cols, within)

    @pl.when(step == 0)
    def _():
        tail = pl.ds(mine_ref.shape[2] - 128, 128)
        split_slabs(refs[0][...], core, chips, mine_ref, theirs_ref, tail, within)


def weight_grad(left, right, slots, tile, extra=None):
    rows, height = left.shape
    width = right.shape[1]
    chips = slots.shape[1]
    slab = height // (2 * chips)
    total = width + (0 if extra is None else extra.shape[1])
    block = (chips, slab, total if extra is not None else tile)
    place = (lambda j, t: (0, 0, 0)) if extra is not None else (lambda j, t: (0, 0, j))
    return pl.pallas_call(
        functools.partial(weight_grad_kernel, chips, extra is not None),
        grid_spec=pltpu.PrefetchScalarGridSpec(
            num_scalar_prefetch=1,
            grid=(width // tile,),
            in_specs=[
                pl.BlockSpec((rows, height), lambda j, t: (0, 0)),
                pl.BlockSpec((rows, tile), lambda j, t: (0, j)),
            ]
            + ([] if extra is None else [pl.BlockSpec((height, 128), lambda j, t: (0, 0))]),
            out_specs=[pl.BlockSpec(block, place)] * 2,
        ),
        out_shape=[jax.ShapeDtypeStruct((chips, slab, total), BF16)] * 2,
        compiler_params=pltpu.CompilerParams(vmem_limit_bytes=VMEM_LIMIT),
        cost_estimate=pl.CostEstimate(
            flops=2 * rows * height * width,
            bytes_accessed=2 * (rows * (height + width) + height * width),
            transcendentals=0,
        ),
        name="weight_grad",
    )(slots, left, right, *([] if extra is None else [extra]))


def tall_grad_kernel(chips, table_ref, left_ref, right_ref, mine_ref, theirs_ref):
    core = table_ref[2, 0]
    acc = dot(left_ref[...], right_ref[...], ((0,), (0,)))
    base = pl.program_id(0) * chips

    def within(s):
        return table_ref[0, base + s] % chips, table_ref[1, base + s] % chips

    split_slabs(acc, core, chips, mine_ref, theirs_ref, slice(None), within)


def tall_grad(left, right, slots, column):
    rows, height = left.shape
    width = right.shape[1]
    chips = slots.shape[1]
    slab = height // (2 * chips)
    tile = height // chips * column
    return pl.pallas_call(
        functools.partial(tall_grad_kernel, column),
        grid_spec=pltpu.PrefetchScalarGridSpec(
            num_scalar_prefetch=1,
            grid=(chips // column,),
            in_specs=[
                pl.BlockSpec((rows, tile), lambda i, t: (0, i)),
                pl.BlockSpec((rows, width), lambda i, t: (0, 0)),
            ],
            out_specs=[
                pl.BlockSpec((column, slab, width), lambda i, t: (t[0, i * column] // column, 0, 0)),
                pl.BlockSpec((column, slab, width), lambda i, t: (t[1, i * column] // column, 0, 0)),
            ],
        ),
        out_shape=[jax.ShapeDtypeStruct((chips, slab, width), BF16)] * 2,
        compiler_params=pltpu.CompilerParams(vmem_limit_bytes=VMEM_LIMIT),
        cost_estimate=pl.CostEstimate(
            flops=2 * rows * height * width,
            bytes_accessed=2 * (rows * (height + width) + height * width),
            transcendentals=0,
        ),
        name="tall_grad",
    )(slots, left, right)


def grad_plain(left, right, table, extra=None):
    full = dot(left, right, ((0,), (0,)))
    if extra is not None:
        full = jnp.concatenate([full, extra], axis=1)
    chips = table.shape[1]
    full = full.astype(BF16).reshape(chips, 2, full.shape[0] // (2 * chips), full.shape[1])
    core = table[2, 0]
    mine = lax.dynamic_index_in_dim(full, core, 1, keepdims=False)
    theirs = lax.dynamic_index_in_dim(full, 1 - core, 1, keepdims=False)
    return jnp.take(mine, table[0], axis=0), jnp.take(theirs, table[1], axis=0)


def hidden_grad_kernel(grad_ref, w_ref, slope_ref, out_ref, sum_ref):
    grad = dot(grad_ref[...], w_ref[...], ((1,), (1,))) * slope_ref[...].astype(F32)
    low = grad.astype(BF16)
    out_ref[...] = low
    sum_ref[...] = jnp.sum(low.astype(F32), axis=0, keepdims=True)


def hidden_grad(grad, w_reduce, slope):
    rows, tile = grad.shape[0], 512
    return pl.pallas_call(
        hidden_grad_kernel,
        grid=(FF // tile,),
        in_specs=[
            pl.BlockSpec((rows, D), lambda j: (0, 0)),
            pl.BlockSpec((tile, D), lambda j: (j, 0)),
            pl.BlockSpec((rows, tile), lambda j: (0, j)),
        ],
        out_specs=[
            pl.BlockSpec((rows, tile), lambda j: (0, j)),
            pl.BlockSpec((1, tile), lambda j: (0, j)),
        ],
        out_shape=[
            jax.ShapeDtypeStruct((rows, FF), BF16),
            jax.ShapeDtypeStruct((1, FF), F32),
        ],
        compiler_params=pltpu.CompilerParams(vmem_limit_bytes=VMEM_LIMIT),
        cost_estimate=pl.CostEstimate(
            flops=2 * rows * D * FF,
            bytes_accessed=2 * (rows * D + D * FF + 2 * rows * FF),
            transcendentals=0,
        ),
        name="hidden_grad",
    )(grad, w_reduce, slope)


def attention_kernel(qkv_ref, qid_ref, kid_ref, context_ref, probs_ref):
    allowed = qid_ref[...] == kid_ref[0]
    lane = lax.broadcasted_iota(jnp.int32, (BLOCK, 128), 1)
    zero = jnp.zeros((BLOCK, 128), BF16)
    for pair in range(HEADS // 2):
        queries = qkv_ref[:, pair * 128 : pair * 128 + 128]
        keys = qkv_ref[:, D + pair * 128 : D + pair * 128 + 128]
        values = qkv_ref[:, 2 * D + pair * 128 : 2 * D + pair * 128 + 128]
        outs = []
        for side in range(2):
            mine = (lane < HDIM) if side == 0 else (lane >= HDIM)
            scores = dot(queries, jnp.where(mine, keys, zero), ((1,), (1,))) * head_scale
            scores = jnp.where(allowed, scores, masked_score)
            top = jnp.max(scores, axis=1, keepdims=True)
            grown = jnp.exp(scores - top)
            total = jnp.sum(grown, axis=1, keepdims=True)
            probs = (grown * (1.0 / total)).astype(BF16)
            probs_ref[0, 2 * pair + side] = probs
            outs.append(dot(probs, values))
        context_ref[:, pair * 128 : pair * 128 + 128] = jnp.where(
            lane < HDIM, outs[0], outs[1]
        ).astype(BF16)


def attention(qkv, qid, kid):
    rows = qkv.shape[0]
    blocks = rows // BLOCK
    return pl.pallas_call(
        attention_kernel,
        grid=(blocks,),
        in_specs=[
            pl.BlockSpec((BLOCK, 3 * D), lambda i: (i, 0)),
            pl.BlockSpec((BLOCK, 1), lambda i: (i, 0)),
            pl.BlockSpec((1, 1, BLOCK), lambda i: (i, 0, 0)),
        ],
        out_specs=[
            pl.BlockSpec((BLOCK, D), lambda i: (i, 0)),
            pl.BlockSpec((1, HEADS, BLOCK, BLOCK), lambda i: (i, 0, 0, 0)),
        ],
        out_shape=[
            jax.ShapeDtypeStruct((rows, D), BF16),
            jax.ShapeDtypeStruct((blocks, HEADS, BLOCK, BLOCK), BF16),
        ],
        compiler_params=pltpu.CompilerParams(vmem_limit_bytes=VMEM_LIMIT),
        cost_estimate=pl.CostEstimate(
            flops=4 * rows * BLOCK * D * 2,
            bytes_accessed=rows * (4 * D + HEADS * BLOCK) * 2,
            transcendentals=rows * HEADS * BLOCK,
        ),
        name="attention",
    )(qkv, qid, kid)


def attention_back_kernel(qkv_ref, probs_ref, grad_ref, out_ref, sum_ref):
    lane = lax.broadcasted_iota(jnp.int32, (BLOCK, 128), 1)
    zero = jnp.zeros((BLOCK, 128), BF16)
    for pair in range(HEADS // 2):
        cols = slice(pair * 128, pair * 128 + 128)
        queries = qkv_ref[:, pair * 128 : pair * 128 + 128]
        keys = qkv_ref[:, D + pair * 128 : D + pair * 128 + 128]
        values = qkv_ref[:, 2 * D + pair * 128 : 2 * D + pair * 128 + 128]
        grad = grad_ref[:, cols]
        d_q, d_k, d_v = [], [], []
        for side in range(2):
            mine = (lane < HDIM) if side == 0 else (lane >= HDIM)
            low = probs_ref[0, 2 * pair + side]
            d_probs = dot(jnp.where(mine, grad, zero), values, ((1,), (1,)))
            d_v.append(dot(low, grad, ((0,), (0,))))
            probs = low.astype(F32)
            row_dot = jnp.sum(d_probs * probs, axis=1, keepdims=True)
            d_scores = (probs * (d_probs - row_dot)).astype(BF16)
            d_q.append(dot(d_scores, keys))
            d_k.append(dot(d_scores, queries, ((0,), (0,))))
        first = lane < HDIM
        out_ref[:, pair * 128 : pair * 128 + 128] = (
            jnp.where(first, d_q[0], d_q[1]) * head_scale
        ).astype(BF16)
        out_ref[:, D + pair * 128 : D + pair * 128 + 128] = (
            jnp.where(first, d_k[0], d_k[1]) * head_scale
        ).astype(BF16)
        out_ref[:, 2 * D + pair * 128 : 2 * D + pair * 128 + 128] = jnp.where(
            first, d_v[0], d_v[1]
        ).astype(BF16)
    sums = jnp.sum(out_ref[...].astype(F32), axis=0, keepdims=True)

    @pl.when(pl.program_id(0) == 0)
    def _():
        sum_ref[...] = sums

    @pl.when(pl.program_id(0) > 0)
    def _():
        sum_ref[...] += sums


def attention_back_more_kernel(qkv_ref, probs_ref, grad_ref, _, out_ref, sum_ref):
    attention_back_kernel(qkv_ref, probs_ref, grad_ref, out_ref, sum_ref)


def attention_back(qkv, probs, grad_context, start, count, into=None):
    rows = qkv.shape[0]
    more = into is not None
    return pl.pallas_call(
        attention_back_more_kernel if more else attention_back_kernel,
        grid=(count,),
        in_specs=[
            pl.BlockSpec((BLOCK, 3 * D), lambda i: (i + start, 0)),
            pl.BlockSpec((1, HEADS, BLOCK, BLOCK), lambda i: (i + start, 0, 0, 0)),
            pl.BlockSpec((BLOCK, D), lambda i: (i + start, 0)),
        ]
        + ([pl.BlockSpec(memory_space=pl.ANY)] if more else []),
        out_specs=[
            pl.BlockSpec((BLOCK, 3 * D), lambda i: (i + start, 0)),
            pl.BlockSpec((1, 3 * D), lambda i: (0, 0)),
        ],
        out_shape=[
            jax.ShapeDtypeStruct((rows, 3 * D), BF16),
            jax.ShapeDtypeStruct((1, 3 * D), F32),
        ],
        input_output_aliases={3: 0} if more else {},
        compiler_params=pltpu.CompilerParams(vmem_limit_bytes=VMEM_LIMIT),
        cost_estimate=pl.CostEstimate(
            flops=8 * count * BLOCK * BLOCK * D * 2,
            bytes_accessed=count * BLOCK * (7 * D + HEADS * BLOCK) * 2,
            transcendentals=0,
        ),
        name="attention_back",
    )(qkv, probs, grad_context, *([into] if more else []))


def expand_kernel(mid_ref, w_ref, b_ref, active_ref, slope_ref):
    expanded = dot(mid_ref[...], w_ref[...]) + b_ref[...]
    phi = 0.5 + 0.5 * lax.erf(expanded * 0.7071067811865476)
    density = jnp.exp(expanded * expanded * -0.5) * 0.3989422804014327
    active_ref[...] = (expanded * phi).astype(BF16)
    slope_ref[...] = (phi + expanded * density).astype(BF16)


def expand(mid_low, w_expand, b_expand):
    rows = mid_low.shape[0]
    tile_r, tile_f = 256, 1024
    return pl.pallas_call(
        expand_kernel,
        grid=(FF // tile_f, rows // tile_r),
        in_specs=[
            pl.BlockSpec((tile_r, D), lambda j, i: (i, 0)),
            pl.BlockSpec((D, tile_f), lambda j, i: (0, j)),
            pl.BlockSpec((1, tile_f), lambda j, i: (0, j)),
        ],
        out_specs=[
            pl.BlockSpec((tile_r, tile_f), lambda j, i: (i, j)),
            pl.BlockSpec((tile_r, tile_f), lambda j, i: (i, j)),
        ],
        out_shape=[jax.ShapeDtypeStruct((rows, FF), BF16)] * 2,
        compiler_params=pltpu.CompilerParams(vmem_limit_bytes=VMEM_LIMIT),
        cost_estimate=pl.CostEstimate(
            flops=2 * rows * D * FF,
            bytes_accessed=2 * (rows * D + D * FF + 2 * rows * FF),
            transcendentals=2 * rows * FF,
        ),
        name="expand",
    )(mid_low, w_expand, b_expand)


def normalized(values):
    centred = values - jnp.mean(values, axis=-1, keepdims=True)
    spread = jnp.mean(centred * centred, axis=-1, keepdims=True)
    inverse = lax.rsqrt(spread + norm_eps)
    return centred * inverse, inverse


def norm_back(grad, gain, norm, inverse):
    scaled = grad * gain
    return inverse * (
        scaled
        - jnp.mean(scaled, axis=-1, keepdims=True)
        - norm * jnp.mean(scaled * norm, axis=-1, keepdims=True)
    )


def per_device(places, *args):
    (
        question_in,
        passage_in,
        question_len,
        passage_len,
        positive,
        question_cot,
        passage_cot,
        w_joined,
        w_output,
        w_expand,
        w_reduce,
        vectors,
        b_expand,
    ) = args
    pb, pa = lax.axis_index("pb"), lax.axis_index("pa")
    z, core = pa // 2, pa % 2
    tower = z // places.half
    is_q = tower == 0
    chip = pb * places.nz + z
    masks = [places.stack_masks(side) for side in range(2)]
    slots_of = [sorted(range(places.chips), key=side.__getitem__) for side in masks]

    def of_core(rows_of):
        both = jnp.array(rows_of, jnp.int32)
        return (
            lax.dynamic_index_in_dim(both, core, 0, keepdims=False),
            lax.dynamic_index_in_dim(both, 1 - core, 0, keepdims=False),
        )

    side = jnp.full((places.chips,), core, jnp.int32)
    table = jnp.stack([x ^ chip for x in of_core(masks)] + [side]).astype(jnp.int32)
    away = jnp.arange(places.chips, dtype=jnp.int32) ^ chip
    slots = jnp.stack([jnp.take(x, away) for x in of_core(slots_of)] + [side]).astype(jnp.int32)
    share = w_joined.shape[1]

    small = jnp.concatenate(
        [
            vectors.transpose(0, 2, 1),
            b_expand.reshape(2, share, 4),
            jnp.zeros((2, share, 116), BF16),
        ],
        axis=2,
    )
    first = jnp.concatenate([w_joined, w_output, small], axis=2)
    second, third = w_expand, w_reduce

    class Gather:
        def __init__(self, piece):
            self.stack = lax.dynamic_index_in_dim(piece, tower, 0, keepdims=True)
            self.send = lax.dynamic_index_in_dim(piece, 1 - tower, 0, keepdims=True)
            self.held = None

        def join(self, got):
            self.stack = jnp.concatenate([self.stack, got], axis=0)
            self.send = self.stack

        def move(self, first, last):
            for step in range(first, last):
                self.join(places.swap(self.send, step))

        def mid(self):
            self.move(0, 1)

        def along_z(self):
            self.move(1, z_steps)

        def pb_first(self):
            self.move(z_steps, places.steps - 1)

        def pb_last(self):
            self.held = places.swap(self.send, places.steps - 1)

        def core_stack(self):
            self.other = places.swap_core(self.stack)

        def core_held(self):
            self.parts = [self.stack, self.held, self.other, places.swap_core(self.held)]

        def whole(self, segments):
            if self.stack.shape[1] % 8 == 0:
                return assemble(self.parts, table, segments)
            return assemble_plain(self.parts, table, segments)

    z_steps = 1 + len(bits_of(places.half))

    rows_q = question_in.reshape(-1, D)
    rows_p = passage_in.reshape(-1, D)
    own_rows = rows_q.shape[0]

    def sides(q_side, p_side):
        return jnp.where(is_q, q_side, p_side), jnp.where(is_q, p_side, q_side)

    lq, lp = question_in.shape[1], passage_in.shape[1]
    valid_q = (jnp.arange(lq, dtype=jnp.int32)[None, :] < question_len[:, None]).astype(jnp.int32)
    valid_p = (jnp.arange(lp, dtype=jnp.int32)[None, :] < passage_len[:, None]).astype(jnp.int32)
    my_valid, send_valid = sides(valid_q.reshape(-1), valid_p.reshape(-1))
    valid = jnp.concatenate([my_valid, places.swap_tower(send_valid)])
    my_tokens, send_tokens = sides(rows_q, rows_p)
    my_cot, send_cot = sides(question_cot.reshape(-1, D), passage_cot.reshape(-1, D))
    rows = 2 * own_rows
    row_ids = jnp.arange(rows, dtype=jnp.int32)
    seq = jnp.where(is_q, row_ids // lq, row_ids // lp)
    qid = seq.reshape(rows, 1)
    kid = jnp.where(valid > 0, seq, -1).reshape(rows // BLOCK, 1, BLOCK)
    row_mask = valid.reshape(rows, 1).astype(F32)

    def chunked(values):
        step = values.shape[0] // 4
        return [values[i * step : (i + 1) * step] for i in range(4)]

    def hand(values):
        return [places.swap_tower(x) for x in values]

    g1, g2, g3 = Gather(first), Gather(second), Gather(third)
    tokens_out, cot_out = chunked(send_tokens), chunked(send_cot)
    g1.mid()
    g1.send, g2.send = tie(g1.send, g2.send)
    g1.along_z()
    g2.mid()
    g1.send, g2.send, g3.send = tie(g1.send, g2.send, g3.send)
    g1.pb_first()
    g2.along_z()
    g3.mid()
    g1.stack, g2.send, g3.send, tokens_out = tie(g1.stack, g2.send, g3.send, tokens_out)
    g1.send = g1.stack
    g1.pb_last()
    g1.core_stack()
    g3.along_z()
    tokens_in = hand(tokens_out[:2])
    g1.held, g1.other, g2.send, g3.send, tokens_in, tokens_out = tie(
        g1.held, g1.other, g2.send, g3.send, tokens_in, tokens_out
    )
    g1.core_held()
    g2.pb_first()
    tokens_in = tokens_in + hand(tokens_out[2:3])
    g1.parts, g2.stack, g3.send, tokens_in, tokens_out = tie(
        g1.parts, g2.stack, g3.send, tokens_in, tokens_out
    )
    g2.send = g2.stack
    g2.pb_last()
    g2.core_stack()
    tokens_in = tokens_in + hand(tokens_out[3:])
    full_j, full_o, full_small = g1.whole([(0, 3 * D), (3 * D, D), (4 * D, 128)])
    wj = full_j.reshape(D, 3 * D)
    wo = full_o.reshape(D, D)
    small = full_small.reshape(D, 128).astype(F32)
    vec = small[:, :8].T
    bias_e = small[:, 8:12].reshape(1, FF)
    bias_j = jnp.concatenate([vec[0], jnp.zeros((D,), F32), vec[1]])
    tokens = jnp.concatenate([my_tokens] + tokens_in, axis=0)
    wj, tokens, cot_out = tie(wj, tokens, cot_out)
    cot_in = hand(cot_out[:1])
    qkv = (dot(tokens, wj) + bias_j).astype(BF16)
    qkv, g2.held, g2.other, g2.stack, g3.send, cot_in, cot_out = tie(
        qkv, g2.held, g2.other, g2.stack, g3.send, cot_in, cot_out
    )
    g3.pb_first()
    g2.core_held()
    cot_in = cot_in + hand(cot_out[1:2])
    context, probs = attention(qkv, qid, kid)
    context, g2.parts, g3.stack, cot_in, cot_out = tie(context, g2.parts, g3.stack, cot_in, cot_out)
    g3.send = g3.stack
    g3.pb_last()
    g3.core_stack()
    cot_in = cot_in + hand(cot_out[2:3])
    (full_e,) = g2.whole([(0, FF)])
    we = full_e.reshape(D, FF)
    attended = dot(context, wo) + vec[2]
    norm_one, inverse_one = normalized(tokens.astype(F32) + attended)
    mid = norm_one * vec[3] + vec[4]
    mid_low = mid.astype(BF16)
    mid_low, we, g3.held, g3.other, g3.stack, cot_in, cot_out = tie(
        mid_low, we, g3.held, g3.other, g3.stack, cot_in, cot_out
    )
    g3.core_held()
    cot_in = cot_in + hand(cot_out[3:])
    active, slope = expand(mid_low, we, bias_e)
    active, g3.parts, cot_in = tie(active, g3.parts, cot_in)
    (full_r,) = g3.whole([(0, D)])
    wr = full_r.reshape(FF, D)
    norm_two, inverse_two = normalized(mid + dot(active, wr) + vec[5])
    out = ((norm_two * vec[6] + vec[7]) * row_mask).astype(BF16)

    per_q = rows // lq
    every = lp // lq
    per_p = rows // lp
    firsts = out.reshape(per_q, lq, D)[:, 0, :]
    others = places.swap_tower(firsts)
    cls_q = jnp.where(is_q, firsts, others)
    cls_p = jnp.where(is_q, others, firsts)[::every]
    pad = (-(per_q + per_p)) % 8
    stack = jnp.concatenate([cls_q, cls_p, jnp.zeros((pad, D), BF16)], axis=0)[None]
    pair_masks = [0]
    for bit in bits_of(places.half):
        got = lax.ppermute(stack, "pa", [(i, i ^ (2 * bit)) for i in range(places.pa_n)])
        stack = jnp.concatenate([stack, got], axis=0)
        pair_masks = pair_masks + [m ^ (2 * bit) for m in pair_masks]
    for bit in bits_of(places.pb_n):
        got = lax.ppermute(stack, "pb", [(i, i ^ bit) for i in range(places.pb_n)])
        stack = jnp.concatenate([stack, got], axis=0)
        pair_masks = pair_masks + [m ^ (bit * places.pa_n) for m in pair_masks]
    stack = jnp.concatenate([stack, places.swap_core(stack)], axis=0)
    pair_masks = pair_masks + [m ^ 1 for m in pair_masks]
    groups = len(pair_masks)
    me = pb * places.pa_n + (pa % (2 * places.half))
    place = jnp.array(pair_masks, jnp.int32) ^ me
    shift = 2 * places.half
    dev_q = jnp.stack([place, place + shift], axis=1)
    dev_p = jnp.stack([place + shift, place], axis=1)
    nq, np_ = question_in.shape[0], passage_in.shape[0]
    q_ids = (dev_q[:, :, None] * nq + jnp.arange(nq, dtype=jnp.int32)).reshape(-1)
    p_ids = (dev_p[:, :, None] * np_ + jnp.arange(np_, dtype=jnp.int32)).reshape(-1)
    wanted = positive
    pos_masks = [0]
    for bit in bits_of(places.pb_n):
        got = lax.ppermute(wanted, "pb", [(i, i ^ bit) for i in range(places.pb_n)])
        wanted = jnp.concatenate([wanted, got])
        pos_masks = pos_masks + [m ^ bit for m in pos_masks]
    per_pb = positive.shape[0]
    slot_of_pb = jnp.zeros((places.pb_n,), jnp.int32)
    slot_of_pb = slot_of_pb.at[jnp.array(pos_masks, jnp.int32) ^ pb].set(
        jnp.arange(places.pb_n, dtype=jnp.int32)
    )
    wanted = jnp.take(wanted, slot_of_pb[q_ids // per_pb] * per_pb + q_ids % per_pb)

    all_q = stack[:, :per_q].reshape(groups * per_q, D)
    all_p = stack[:, per_q : per_q + per_p].reshape(groups * per_p, D)
    similarity = dot(all_q, all_p, ((1,), (1,))) * score_scale
    hot = (wanted[:, None] == p_ids[None, :]).astype(F32)
    top = jnp.max(similarity, axis=1, keepdims=True)
    grown = jnp.exp(similarity - top)
    total = jnp.sum(grown, axis=1, keepdims=True)
    own_sim = similarity[:per_q]
    loss = top[:per_q, 0] + jnp.log(total[:per_q, 0]) - jnp.sum(own_sim * hot[:per_q], axis=1)
    question_loss = lax.dynamic_slice_in_dim(loss, tower * nq, nq)
    d_sim = (loss_weight * (grown / total - hot)).astype(BF16)
    d_q = dot(d_sim[:per_q], all_p) * score_scale
    d_p = dot(d_sim[:, :per_p], all_q, ((0,), (0,))) * score_scale
    d_p = jnp.concatenate(
        [d_p.reshape(per_p, 1, D), jnp.zeros((per_p, every - 1, D), F32)], axis=1
    ).reshape(per_q, D)
    d_slot = jnp.where(is_q, d_q, d_p)

    cot = jnp.concatenate([my_cot] + cot_in, axis=0)
    d_out = cot.astype(F32).reshape(per_q, lq, D)
    at_slot = jnp.arange(lq, dtype=jnp.int32)[None, :, None] == 0
    d_out = d_out + jnp.where(at_slot, d_slot[:, None, :], 0.0)
    d_out = d_out.reshape(rows, D) * row_mask
    d_second = norm_back(d_out, vec[6], norm_two, inverse_two)
    g_gain_two = jnp.sum(d_out * norm_two, axis=0)
    g_shift_two = jnp.sum(d_out, axis=0)
    d_reduced = d_second.astype(BF16)
    g_bias_reduce = jnp.sum(d_reduced.astype(F32), axis=0)

    even = share % 8 == 0

    def gradient(left, right, tile, extra=None):
        if not even:
            return grad_plain(left, right, table, extra)
        if left.shape[1] > D:
            return tall_grad(left, right, slots, places.nz)
        return weight_grad(left, right, slots, tile, extra)

    class Scatter:
        def __init__(self, mine, theirs):
            self.parts, self.theirs = [mine], theirs
            self.count = mine.shape[0]

        def cores(self):
            self.parts = self.parts + [places.swap_core(self.theirs)]

        def total(self, start, stop):
            out = self.parts[0][start:stop].astype(F32)
            for part in self.parts[1:]:
                out = out + part[start:stop].astype(F32)
            return out

        def move(self, step):
            half = self.count // 2
            send = self.total(half, self.count).astype(BF16)
            self.parts = self.parts + [places.swap(send, step)]
            self.count = half

        def pb_first(self):
            self.move(places.steps - 1)

        def pb_rest(self):
            for step in range(places.steps - 2, z_steps - 1, -1):
                self.move(step)

        def along_z(self):
            for step in range(z_steps - 1, 0, -1):
                self.move(step)

        def mid(self):
            got = places.swap(self.total(1, 2).astype(BF16), 0).astype(F32)
            keep = self.total(0, 1)
            self.out = jnp.concatenate(
                [jnp.where(is_q, keep, got), jnp.where(is_q, got, keep)], axis=0
            )

    send_out = chunked(out[own_rows:])
    sr = Scatter(*gradient(active, d_reduced, D))
    sr.parts, sr.theirs, d_reduced, send_out = tie(sr.parts, sr.theirs, d_reduced, send_out)
    sr.cores()
    got_out = hand(send_out[:1])
    d_expanded, g_bias_expand = hidden_grad(d_reduced, wr, slope)
    sr.parts, d_expanded, got_out, send_out = tie(sr.parts, d_expanded, got_out, send_out)
    sr.pb_first()
    got_out = got_out + hand(send_out[1:2])
    se = Scatter(*gradient(mid_low, d_expanded, 1024))
    se.parts, se.theirs, d_expanded, got_out, send_out = tie(
        se.parts, se.theirs, d_expanded, got_out, send_out
    )
    se.cores()
    got_out = got_out + hand(send_out[2:3])
    d_mid = d_second + dot(d_expanded, we, ((1,), (1,)))
    sr.parts, se.parts, d_mid, got_out, send_out = tie(
        sr.parts, se.parts, d_mid, got_out, send_out
    )
    sr.pb_rest()
    got_out = got_out + hand(send_out[3:])
    d_first = norm_back(d_mid, vec[3], norm_one, inverse_one)
    g_gain_one = jnp.sum(d_mid * norm_one, axis=0)
    g_shift_one = jnp.sum(d_mid, axis=0)
    d_attended = d_first.astype(BF16)
    g_bias_output = jnp.sum(d_attended.astype(F32), axis=0)
    so = Scatter(*gradient(context, d_attended, D))
    d_context = dot(d_attended, wo, ((1,), (1,))).astype(BF16)
    sr.parts, se.parts, so.parts, so.theirs, d_context, got_out = tie(
        sr.parts, se.parts, so.parts, so.theirs, d_context, got_out
    )
    se.pb_first()
    sr.along_z()
    so.cores()
    blocks = rows // BLOCK
    d_joined, sums_one = attention_back(qkv, probs, d_context, 0, blocks // 2)
    sr.parts, so.parts, d_joined = tie(sr.parts, so.parts, d_joined)
    sr.mid()
    d_joined, sums_two = attention_back(
        qkv, probs, d_context, blocks // 2, blocks - blocks // 2, d_joined
    )
    sr.out, se.parts, so.parts, d_joined = tie(sr.out, se.parts, so.parts, d_joined)
    se.pb_rest()
    so.pb_first()
    send_grad = (d_first[own_rows:] + dot(d_joined[own_rows:], wj, ((1,), (1,)))).astype(BF16)
    send_grad = chunked(send_grad)
    se.parts, so.parts, d_joined, send_grad = tie(se.parts, so.parts, d_joined, send_grad)
    se.along_z()
    so.pb_rest()
    got_grad = hand(send_grad[:1])
    g_joined_bias = (sums_one + sums_two)[0]
    g_vec = jnp.stack(
        [
            g_joined_bias[:D],
            g_joined_bias[2 * D :],
            g_bias_output,
            g_gain_one,
            g_shift_one,
            g_bias_reduce,
            g_gain_two,
            g_shift_two,
        ]
    )
    g_small = jnp.concatenate(
        [g_vec.T, g_bias_expand.reshape(D, 4), jnp.zeros((D, 116), F32)], axis=1
    )
    sj = Scatter(*gradient(tokens, d_joined, D, g_small))
    se.parts, so.parts, sj.parts, sj.theirs, d_joined, got_grad, send_grad = tie(
        se.parts, so.parts, sj.parts, sj.theirs, d_joined, got_grad, send_grad
    )
    sj.cores()
    so.along_z()
    se.mid()
    got_grad = got_grad + hand(send_grad[1:2])
    own_grad = d_first[:own_rows] + dot(d_joined[:own_rows], wj, ((1,), (1,)))
    sj.parts, so.parts, own_grad, got_grad, send_grad = tie(
        sj.parts, so.parts, own_grad, got_grad, send_grad
    )
    sj.pb_first()
    so.mid()
    got_grad = got_grad + hand(send_grad[2:3])
    sj.parts, got_grad, send_grad = tie(sj.parts, got_grad, send_grad)
    sj.pb_rest()
    got_grad = got_grad + hand(send_grad[3:])
    sj.along_z()
    sj.mid()
    grad_joined = sj.out[:, :, : 3 * D]
    grad_output, grad_expand, grad_reduce = so.out, se.out, sr.out
    extra = sj.out[:, :, 3 * D :]
    grad_vectors = extra[:, :, :8].transpose(0, 2, 1)
    grad_b_expand = extra[:, :, 8:12].reshape(2, 4 * share)

    out_q, out_p = sides(out[:own_rows], jnp.concatenate(got_out, axis=0))
    grad_q, grad_p = sides(own_grad, jnp.concatenate(got_grad, axis=0).astype(F32))
    return (
        out_q.reshape(question_in.shape),
        out_p.reshape(passage_in.shape),
        question_loss,
        grad_q.reshape(question_in.shape),
        grad_p.reshape(passage_in.shape),
        grad_joined,
        grad_output,
        grad_expand,
        grad_reduce,
        grad_vectors,
        grad_b_expand,
    )


def solution(mesh):
    in_specs = (
        P(("pb", "pa"), None, None),
        P(("pb", "pa"), None, None),
        P(("pb", "pa")),
        P(("pb", "pa")),
        P("pb"),
        P(("pb", "pa"), None, None),
        P(("pb", "pa"), None, None),
        P(None, ("pb", "pa"), None),
        P(None, ("pb", "pa"), None),
        P(None, ("pb", "pa"), None),
        P(None, ("pb", "pa"), None),
        P(None, None, ("pb", "pa")),
        P(None, ("pb", "pa")),
    )
    out_specs = (
        P(("pb", "pa"), None, None),
        P(("pb", "pa"), None, None),
        P(("pb", "pa")),
        P(("pb", "pa"), None, None),
        P(("pb", "pa"), None, None),
        P(None, ("pb", "pa"), None),
        P(None, ("pb", "pa"), None),
        P(None, ("pb", "pa"), None),
        P(None, ("pb", "pa"), None),
        P(None, None, ("pb", "pa")),
        P(None, ("pb", "pa")),
    )
    return jax.shard_map(
        functools.partial(per_device, Places(mesh)),
        mesh=mesh,
        in_specs=in_specs,
        out_specs=out_specs,
        check_vma=False,
    )
```

```python
import functools

import jax
import jax.numpy as jnp
from jax import lax
from jax.experimental import pallas as pl
from jax.experimental.pallas import tpu as pltpu
from jax.sharding import PartitionSpec as P

D = 768
HEADS = 12
HDIM = 64
FF = 3072
AXES = ("pb", "pa")
BLOCK = 256

norm_eps = 1e-06
masked_score = -1000000000.0
score_scale = 0.0625
loss_weight = 16.0
head_scale = HDIM ** (-0.5)
F32 = jnp.float32
BF16 = jnp.bfloat16
VMEM_LIMIT = 56 * 1024 * 1024


def bits_of(count):
    return [1 << shift for shift in range(count.bit_length() - 1)]


class Places:
    def __init__(self, mesh):
        self.pb_n = mesh.shape["pb"]
        self.pa_n = mesh.shape["pa"]
        self.nz = self.pa_n // 2
        self.half = self.nz // 2
        self.chips = self.pb_n * self.nz
        pb_bits = bits_of(self.pb_n)
        turn = len(pb_bits) // 2
        low_z = [("z", bit) for bit in bits_of(self.half)]
        first = [("pb", bit) for bit in pb_bits]
        second = first[turn:] + first[:turn]
        self.orders = ([("z", self.half)] + low_z + first, [("z", self.half)] + low_z + second)
        self.steps = len(self.orders[0])

    def chip_mask(self, move):
        axis, bit = move
        return bit * self.nz if axis == "pb" else bit

    def stack_masks(self, core):
        masks = [0]
        for move in self.orders[core]:
            masks = masks + [mask ^ self.chip_mask(move) for mask in masks]
        return masks

    def pairs(self, step):
        out = []
        for pb in range(self.pb_n):
            for pa in range(self.pa_n):
                axis, bit = self.orders[pa % 2][step]
                to_pb, to_pa = (pb ^ bit, pa) if axis == "pb" else (pb, pa ^ (2 * bit))
                out.append((pb * self.pa_n + pa, to_pb * self.pa_n + to_pa))
        return out

    def swap(self, values, step):
        return lax.ppermute(values, AXES, self.pairs(step))

    def swap_core(self, values):
        return lax.ppermute(values, "pa", [(i, i ^ 1) for i in range(self.pa_n)])

    def swap_tower(self, values):
        return lax.ppermute(values, "pa", [(i, i ^ (2 * self.half)) for i in range(self.pa_n)])


def dot(left, right, dims=((1,), (0,))):
    return lax.dot_general(left, right, (dims, ((), ())), preferred_element_type=F32)


def tie(*values):
    return lax.optimization_barrier(values)


def assemble_kernel(segments, idx_ref, *refs):
    count = len(segments)
    sources, outs = refs[:4], refs[4 : 4 + count]
    buffer, in_sem, out_sem = refs[4 + count :]
    core = idx_ref[2, 0]
    part = sources[0].shape[0]
    loads = [
        pltpu.make_async_copy(source, buffer.at[pl.ds(k * part, part)], in_sem.at[k])
        for k, source in enumerate(sources)
    ]
    for load in loads:
        load.start()
    stores = []
    for k in range(4):
        loads[k].wait()
        half = core if k < 2 else 1 - core
        for j in range(part):
            slot = k * part + j
            place = idx_ref[k // 2, (k % 2) * part + j]
            for s, (start, width) in enumerate(segments):
                store = pltpu.make_async_copy(
                    buffer.at[slot, :, pl.ds(start, width)],
                    outs[s].at[place, half],
                    out_sem.at[s, slot],
                )
                store.start()
                stores.append(store)
    for store in stores:
        store.wait()


def assemble(parts, table, segments):
    part, rows, width = parts[0].shape
    chips = 2 * part
    shapes = [jax.ShapeDtypeStruct((chips, 2, rows, w), BF16) for _, w in segments]
    return pl.pallas_call(
        functools.partial(assemble_kernel, segments),
        out_shape=shapes,
        in_specs=[pl.BlockSpec(memory_space=pltpu.SMEM)] + [pl.BlockSpec(memory_space=pl.ANY)] * 4,
        out_specs=[pl.BlockSpec(memory_space=pl.ANY)] * len(segments),
        scratch_shapes=[
            pltpu.VMEM((2 * chips, rows, width), BF16),
            pltpu.SemaphoreType.DMA((4,)),
            pltpu.SemaphoreType.DMA((len(segments), 2 * chips)),
        ],
        compiler_params=pltpu.CompilerParams(vmem_limit_bytes=VMEM_LIMIT),
        cost_estimate=pl.CostEstimate(
            flops=0, bytes_accessed=4 * 2 * chips * rows * width, transcendentals=0
        ),
        name="assemble",
    )(table, *parts)


def assemble_plain(parts, table, segments):
    own = jnp.take(jnp.concatenate(parts[:2], axis=0), jnp.argsort(table[0]), axis=0)
    other = jnp.take(jnp.concatenate(parts[2:], axis=0), jnp.argsort(table[1]), axis=0)
    first = table[2, 0] == 0
    both = jnp.stack([jnp.where(first, own, other), jnp.where(first, other, own)], axis=1)
    return [both[..., start : start + w] for start, w in segments]


def split_slabs(acc, core, chips, mine_ref, theirs_ref, cols, within):
    rows = acc.shape[0] // (2 * chips)
    for s in range(chips):
        low = acc[2 * s * rows : (2 * s + 1) * rows]
        high = acc[(2 * s + 1) * rows : (2 * s + 2) * rows]
        mine, theirs = within(s)
        mine_ref[mine, :, cols] = jnp.where(core == 0, low, high).astype(BF16)
        theirs_ref[theirs, :, cols] = jnp.where(core == 0, high, low).astype(BF16)


def weight_grad_kernel(chips, extra, table_ref, left_ref, right_ref, *refs):
    mine_ref, theirs_ref = refs[-2:]
    core = table_ref[2, 0]
    acc = dot(left_ref[...], right_ref[...], ((0,), (0,)))
    width = acc.shape[1]

    def within(s):
        return table_ref[0, s], table_ref[1, s]

    if not extra:
        split_slabs(acc, core, chips, mine_ref, theirs_ref, slice(None), within)
        return
    step = pl.program_id(0)
    cols = pl.ds(pl.multiple_of(step * width, 128), width)
    split_slabs(acc, core, chips, mine_ref, theirs_ref, cols, within)

    @pl.when(step == 0)
    def _():
        tail = pl.ds(mine_ref.shape[2] - 128, 128)
        split_slabs(refs[0][...], core, chips, mine_ref, theirs_ref, tail, within)


def weight_grad(left, right, slots, tile, extra=None):
    rows, height = left.shape
    width = right.shape[1]
    chips = slots.shape[1]
    slab = height // (2 * chips)
    total = width + (0 if extra is None else extra.shape[1])
    block = (chips, slab, total if extra is not None else tile)
    place = (lambda j, t: (0, 0, 0)) if extra is not None else (lambda j, t: (0, 0, j))
    return pl.pallas_call(
        functools.partial(weight_grad_kernel, chips, extra is not None),
        grid_spec=pltpu.PrefetchScalarGridSpec(
            num_scalar_prefetch=1,
            grid=(width // tile,),
            in_specs=[
                pl.BlockSpec((rows, height), lambda j, t: (0, 0)),
                pl.BlockSpec((rows, tile), lambda j, t: (0, j)),
            ]
            + ([] if extra is None else [pl.BlockSpec((height, 128), lambda j, t: (0, 0))]),
            out_specs=[pl.BlockSpec(block, place)] * 2,
        ),
        out_shape=[jax.ShapeDtypeStruct((chips, slab, total), BF16)] * 2,
        compiler_params=pltpu.CompilerParams(vmem_limit_bytes=VMEM_LIMIT),
        cost_estimate=pl.CostEstimate(
            flops=2 * rows * height * width,
            bytes_accessed=2 * (rows * (height + width) + height * width),
            transcendentals=0,
        ),
        name="weight_grad",
    )(slots, left, right, *([] if extra is None else [extra]))


def tall_grad_kernel(chips, table_ref, left_ref, right_ref, mine_ref, theirs_ref):
    core = table_ref[2, 0]
    acc = dot(left_ref[...], right_ref[...], ((0,), (0,)))
    base = pl.program_id(0) * chips

    def within(s):
        return table_ref[0, base + s] % chips, table_ref[1, base + s] % chips

    split_slabs(acc, core, chips, mine_ref, theirs_ref, slice(None), within)


def tall_grad(left, right, slots, column):
    rows, height = left.shape
    width = right.shape[1]
    chips = slots.shape[1]
    slab = height // (2 * chips)
    tile = height // chips * column
    return pl.pallas_call(
        functools.partial(tall_grad_kernel, column),
        grid_spec=pltpu.PrefetchScalarGridSpec(
            num_scalar_prefetch=1,
            grid=(chips // column,),
            in_specs=[
                pl.BlockSpec((rows, tile), lambda i, t: (0, i)),
                pl.BlockSpec((rows, width), lambda i, t: (0, 0)),
            ],
            out_specs=[
                pl.BlockSpec((column, slab, width), lambda i, t: (t[0, i * column] // column, 0, 0)),
                pl.BlockSpec((column, slab, width), lambda i, t: (t[1, i * column] // column, 0, 0)),
            ],
        ),
        out_shape=[jax.ShapeDtypeStruct((chips, slab, width), BF16)] * 2,
        compiler_params=pltpu.CompilerParams(vmem_limit_bytes=VMEM_LIMIT),
        cost_estimate=pl.CostEstimate(
            flops=2 * rows * height * width,
            bytes_accessed=2 * (rows * (height + width) + height * width),
            transcendentals=0,
        ),
        name="tall_grad",
    )(slots, left, right)


def grad_plain(left, right, table, extra=None):
    full = dot(left, right, ((0,), (0,)))
    if extra is not None:
        full = jnp.concatenate([full, extra], axis=1)
    chips = table.shape[1]
    full = full.astype(BF16).reshape(chips, 2, full.shape[0] // (2 * chips), full.shape[1])
    core = table[2, 0]
    mine = lax.dynamic_index_in_dim(full, core, 1, keepdims=False)
    theirs = lax.dynamic_index_in_dim(full, 1 - core, 1, keepdims=False)
    return jnp.take(mine, table[0], axis=0), jnp.take(theirs, table[1], axis=0)


def hidden_grad_kernel(grad_ref, w_ref, slope_ref, out_ref, sum_ref):
    grad = dot(grad_ref[...], w_ref[...], ((1,), (1,))) * slope_ref[...].astype(F32)
    low = grad.astype(BF16)
    out_ref[...] = low
    sum_ref[...] = jnp.sum(low.astype(F32), axis=0, keepdims=True)


def hidden_grad(grad, w_reduce, slope):
    rows, tile = grad.shape[0], 512
    return pl.pallas_call(
        hidden_grad_kernel,
        grid=(FF // tile,),
        in_specs=[
            pl.BlockSpec((rows, D), lambda j: (0, 0)),
            pl.BlockSpec((tile, D), lambda j: (j, 0)),
            pl.BlockSpec((rows, tile), lambda j: (0, j)),
        ],
        out_specs=[
            pl.BlockSpec((rows, tile), lambda j: (0, j)),
            pl.BlockSpec((1, tile), lambda j: (0, j)),
        ],
        out_shape=[
            jax.ShapeDtypeStruct((rows, FF), BF16),
            jax.ShapeDtypeStruct((1, FF), F32),
        ],
        compiler_params=pltpu.CompilerParams(vmem_limit_bytes=VMEM_LIMIT),
        cost_estimate=pl.CostEstimate(
            flops=2 * rows * D * FF,
            bytes_accessed=2 * (rows * D + D * FF + 2 * rows * FF),
            transcendentals=0,
        ),
        name="hidden_grad",
    )(grad, w_reduce, slope)


def attention_kernel(qkv_ref, qid_ref, kid_ref, context_ref, probs_ref):
    allowed = qid_ref[...] == kid_ref[0]
    lane = lax.broadcasted_iota(jnp.int32, (BLOCK, 128), 1)
    zero = jnp.zeros((BLOCK, 128), BF16)
    for pair in range(HEADS // 2):
        queries = qkv_ref[:, pair * 128 : pair * 128 + 128]
        keys = qkv_ref[:, D + pair * 128 : D + pair * 128 + 128]
        values = qkv_ref[:, 2 * D + pair * 128 : 2 * D + pair * 128 + 128]
        outs = []
        for side in range(2):
            mine = (lane < HDIM) if side == 0 else (lane >= HDIM)
            scores = dot(queries, jnp.where(mine, keys, zero), ((1,), (1,))) * head_scale
            scores = jnp.where(allowed, scores, masked_score)
            top = jnp.max(scores, axis=1, keepdims=True)
            grown = jnp.exp(scores - top)
            total = jnp.sum(grown, axis=1, keepdims=True)
            probs = (grown * (1.0 / total)).astype(BF16)
            probs_ref[0, 2 * pair + side] = probs
            outs.append(dot(probs, values))
        context_ref[:, pair * 128 : pair * 128 + 128] = jnp.where(
            lane < HDIM, outs[0], outs[1]
        ).astype(BF16)


def attention(qkv, qid, kid):
    rows = qkv.shape[0]
    blocks = rows // BLOCK
    return pl.pallas_call(
        attention_kernel,
        grid=(blocks,),
        in_specs=[
            pl.BlockSpec((BLOCK, 3 * D), lambda i: (i, 0)),
            pl.BlockSpec((BLOCK, 1), lambda i: (i, 0)),
            pl.BlockSpec((1, 1, BLOCK), lambda i: (i, 0, 0)),
        ],
        out_specs=[
            pl.BlockSpec((BLOCK, D), lambda i: (i, 0)),
            pl.BlockSpec((1, HEADS, BLOCK, BLOCK), lambda i: (i, 0, 0, 0)),
        ],
        out_shape=[
            jax.ShapeDtypeStruct((rows, D), BF16),
            jax.ShapeDtypeStruct((blocks, HEADS, BLOCK, BLOCK), BF16),
        ],
        compiler_params=pltpu.CompilerParams(vmem_limit_bytes=VMEM_LIMIT),
        cost_estimate=pl.CostEstimate(
            flops=4 * rows * BLOCK * D * 2,
            bytes_accessed=rows * (4 * D + HEADS * BLOCK) * 2,
            transcendentals=rows * HEADS * BLOCK,
        ),
        name="attention",
    )(qkv, qid, kid)


def attention_back_kernel(qkv_ref, probs_ref, grad_ref, out_ref, sum_ref):
    lane = lax.broadcasted_iota(jnp.int32, (BLOCK, 128), 1)
    zero = jnp.zeros((BLOCK, 128), BF16)
    for pair in range(HEADS // 2):
        cols = slice(pair * 128, pair * 128 + 128)
        queries = qkv_ref[:, pair * 128 : pair * 128 + 128]
        keys = qkv_ref[:, D + pair * 128 : D + pair * 128 + 128]
        values = qkv_ref[:, 2 * D + pair * 128 : 2 * D + pair * 128 + 128]
        grad = grad_ref[:, cols]
        d_q, d_k, d_v = [], [], []
        for side in range(2):
            mine = (lane < HDIM) if side == 0 else (lane >= HDIM)
            low = probs_ref[0, 2 * pair + side]
            d_probs = dot(jnp.where(mine, grad, zero), values, ((1,), (1,)))
            d_v.append(dot(low, grad, ((0,), (0,))))
            probs = low.astype(F32)
            row_dot = jnp.sum(d_probs * probs, axis=1, keepdims=True)
            d_scores = (probs * (d_probs - row_dot)).astype(BF16)
            d_q.append(dot(d_scores, keys))
            d_k.append(dot(d_scores, queries, ((0,), (0,))))
        first = lane < HDIM
        out_ref[:, pair * 128 : pair * 128 + 128] = (
            jnp.where(first, d_q[0], d_q[1]) * head_scale
        ).astype(BF16)
        out_ref[:, D + pair * 128 : D + pair * 128 + 128] = (
            jnp.where(first, d_k[0], d_k[1]) * head_scale
        ).astype(BF16)
        out_ref[:, 2 * D + pair * 128 : 2 * D + pair * 128 + 128] = jnp.where(
            first, d_v[0], d_v[1]
        ).astype(BF16)
    sums = jnp.sum(out_ref[...].astype(F32), axis=0, keepdims=True)

    @pl.when(pl.program_id(0) == 0)
    def _():
        sum_ref[...] = sums

    @pl.when(pl.program_id(0) > 0)
    def _():
        sum_ref[...] += sums


def attention_back_more_kernel(qkv_ref, probs_ref, grad_ref, _, out_ref, sum_ref):
    attention_back_kernel(qkv_ref, probs_ref, grad_ref, out_ref, sum_ref)


def attention_back(qkv, probs, grad_context, start, count, into=None):
    rows = qkv.shape[0]
    more = into is not None
    return pl.pallas_call(
        attention_back_more_kernel if more else attention_back_kernel,
        grid=(count,),
        in_specs=[
            pl.BlockSpec((BLOCK, 3 * D), lambda i: (i + start, 0)),
            pl.BlockSpec((1, HEADS, BLOCK, BLOCK), lambda i: (i + start, 0, 0, 0)),
            pl.BlockSpec((BLOCK, D), lambda i: (i + start, 0)),
        ]
        + ([pl.BlockSpec(memory_space=pl.ANY)] if more else []),
        out_specs=[
            pl.BlockSpec((BLOCK, 3 * D), lambda i: (i + start, 0)),
            pl.BlockSpec((1, 3 * D), lambda i: (0, 0)),
        ],
        out_shape=[
            jax.ShapeDtypeStruct((rows, 3 * D), BF16),
            jax.ShapeDtypeStruct((1, 3 * D), F32),
        ],
        input_output_aliases={3: 0} if more else {},
        compiler_params=pltpu.CompilerParams(vmem_limit_bytes=VMEM_LIMIT),
        cost_estimate=pl.CostEstimate(
            flops=8 * count * BLOCK * BLOCK * D * 2,
            bytes_accessed=count * BLOCK * (7 * D + HEADS * BLOCK) * 2,
            transcendentals=0,
        ),
        name="attention_back",
    )(qkv, probs, grad_context, *([into] if more else []))


def join_kernel(*refs):
    count = len(refs) - 2
    sources, out, sem = refs[:count], refs[count], refs[count + 1]
    copies, row = [], 0
    for k, source in enumerate(sources):
        rows = source.shape[0]
        copies.append(
            pltpu.make_async_copy(source, out.at[pl.ds(row, rows)], sem.at[k])
        )
        copies[-1].start()
        row += rows
    for copy in copies:
        copy.wait()


def join(pieces):
    rows, width = sum(x.shape[0] for x in pieces), pieces[0].shape[1]
    return pl.pallas_call(
        join_kernel,
        in_specs=[pl.BlockSpec(memory_space=pl.ANY)] * len(pieces),
        out_specs=pl.BlockSpec(memory_space=pl.ANY),
        out_shape=jax.ShapeDtypeStruct((rows, width), pieces[0].dtype),
        scratch_shapes=[pltpu.SemaphoreType.DMA((len(pieces),))],
        cost_estimate=pl.CostEstimate(
            flops=0, bytes_accessed=4 * rows * width, transcendentals=0
        ),
        name="join",
    )(*pieces)


def deal_kernel(tower_ref, own_ref, *refs):
    pieces, (q_ref, p_ref) = refs[:-2], refs[-2:]

    def give(own_out, other_out):
        own_out[...] = own_ref[...]
        row = 0
        for piece in pieces:
            rows = piece.shape[0]
            other_out[row : row + rows, :] = piece[...].astype(other_out.dtype)
            row += rows

    @pl.when(tower_ref[0] == 0)
    def _():
        give(q_ref, p_ref)

    @pl.when(tower_ref[0] != 0)
    def _():
        give(p_ref, q_ref)


def deal(tower, own, pieces):
    rows, width = sum(x.shape[0] for x in pieces), own.shape[1]
    shape = jax.ShapeDtypeStruct((rows, width), own.dtype)
    return pl.pallas_call(
        deal_kernel,
        grid=(1,),
        in_specs=[
            pl.BlockSpec(memory_space=pltpu.SMEM),
            pl.BlockSpec((rows, width), lambda i: (0, 0)),
        ]
        + [pl.BlockSpec(x.shape, lambda i: (0, 0)) for x in pieces],
        out_specs=[pl.BlockSpec((rows, width), lambda i: (0, 0))] * 2,
        out_shape=[shape] * 2,
        compiler_params=pltpu.CompilerParams(vmem_limit_bytes=VMEM_LIMIT),
        cost_estimate=pl.CostEstimate(
            flops=0, bytes_accessed=12 * rows * width, transcendentals=0
        ),
        name="deal",
    )(tower, own, *pieces)


def add_sums(sum_ref, values):
    total = jnp.concatenate(
        [jnp.sum(x, axis=0, keepdims=True) for x in values]
        + [jnp.zeros((8 - len(values), values[0].shape[1]), F32)],
        axis=0,
    )

    @pl.when(pl.program_id(0) == 0)
    def _():
        sum_ref[...] = total

    @pl.when(pl.program_id(0) > 0)
    def _():
        sum_ref[...] += total


def second_back_kernel(
    cot_ref, slot_ref, mask_ref, norm_ref, inverse_ref, gain_ref, grad_ref, low_ref, sum_ref
):
    group = slot_ref.shape[1]
    cot = cot_ref[...].astype(F32).reshape(group, BLOCK // group, D)
    first = lax.broadcasted_iota(jnp.int32, cot.shape, 1) == 0
    grad = cot + jnp.where(first, slot_ref[0][:, None, :], 0.0)
    grad = grad.reshape(BLOCK, D) * mask_ref[...]
    norm = norm_ref[...]
    second = norm_back(grad, gain_ref[...], norm, inverse_ref[...])
    low = second.astype(BF16)
    grad_ref[...] = second
    low_ref[...] = low
    add_sums(sum_ref, [grad * norm, grad, low.astype(F32)])


def second_back(cot, d_slot, mask, norm, inverse, gain):
    rows = cot.shape[0]
    blocks = rows // BLOCK
    wide = pl.BlockSpec((BLOCK, D), lambda i: (i, 0))
    thin = pl.BlockSpec((BLOCK, 1), lambda i: (i, 0))
    group = d_slot.shape[0] // blocks
    return pl.pallas_call(
        second_back_kernel,
        grid=(blocks,),
        in_specs=[
            wide,
            pl.BlockSpec((1, group, D), lambda i: (i, 0, 0)),
            thin,
            wide,
            thin,
            pl.BlockSpec((1, D), lambda i: (0, 0)),
        ],
        out_specs=[wide, wide, pl.BlockSpec((8, D), lambda i: (0, 0))],
        out_shape=[
            jax.ShapeDtypeStruct((rows, D), F32),
            jax.ShapeDtypeStruct((rows, D), BF16),
            jax.ShapeDtypeStruct((8, D), F32),
        ],
        compiler_params=pltpu.CompilerParams(vmem_limit_bytes=VMEM_LIMIT),
        cost_estimate=pl.CostEstimate(
            flops=20 * rows * D, bytes_accessed=12 * rows * D, transcendentals=0
        ),
        name="second_back",
    )(cot, d_slot.reshape(blocks, group, D), mask, norm, inverse, gain)


def first_back_kernel(
    hidden_ref, w_ref, second_ref, norm_ref, inverse_ref, gain_ref, grad_ref, low_ref, sum_ref
):
    grad = second_ref[...] + dot(hidden_ref[...], w_ref[...], ((1,), (1,)))
    norm = norm_ref[...]
    first = norm_back(grad, gain_ref[...], norm, inverse_ref[...])
    low = first.astype(BF16)
    grad_ref[...] = first
    low_ref[...] = low
    add_sums(sum_ref, [grad * norm, grad, low.astype(F32)])


def first_back(d_expanded, w_expand, d_second, norm, inverse, gain):
    rows = d_expanded.shape[0]
    wide = pl.BlockSpec((BLOCK, D), lambda i: (i, 0))
    return pl.pallas_call(
        first_back_kernel,
        grid=(rows // BLOCK,),
        in_specs=[
            pl.BlockSpec((BLOCK, FF), lambda i: (i, 0)),
            pl.BlockSpec((D, FF), lambda i: (0, 0)),
            wide,
            wide,
            pl.BlockSpec((BLOCK, 1), lambda i: (i, 0)),
            pl.BlockSpec((1, D), lambda i: (0, 0)),
        ],
        out_specs=[wide, wide, pl.BlockSpec((8, D), lambda i: (0, 0))],
        out_shape=[
            jax.ShapeDtypeStruct((rows, D), F32),
            jax.ShapeDtypeStruct((rows, D), BF16),
            jax.ShapeDtypeStruct((8, D), F32),
        ],
        compiler_params=pltpu.CompilerParams(vmem_limit_bytes=VMEM_LIMIT),
        cost_estimate=pl.CostEstimate(
            flops=2 * rows * D * FF,
            bytes_accessed=2 * (rows * FF + D * FF) + 14 * rows * D,
            transcendentals=0,
        ),
        name="first_back",
    )(d_expanded, w_expand, d_second, norm, inverse, gain)


def expand_kernel(mid_ref, w_ref, b_ref, active_ref, slope_ref):
    expanded = dot(mid_ref[...], w_ref[...]) + b_ref[...]
    phi = 0.5 + 0.5 * lax.erf(expanded * 0.7071067811865476)
    density = jnp.exp(expanded * expanded * -0.5) * 0.3989422804014327
    active_ref[...] = (expanded * phi).astype(BF16)
    slope_ref[...] = (phi + expanded * density).astype(BF16)


def expand(mid_low, w_expand, b_expand):
    rows = mid_low.shape[0]
    tile_r, tile_f = 256, 1024
    return pl.pallas_call(
        expand_kernel,
        grid=(FF // tile_f, rows // tile_r),
        in_specs=[
            pl.BlockSpec((tile_r, D), lambda j, i: (i, 0)),
            pl.BlockSpec((D, tile_f), lambda j, i: (0, j)),
            pl.BlockSpec((1, tile_f), lambda j, i: (0, j)),
        ],
        out_specs=[
            pl.BlockSpec((tile_r, tile_f), lambda j, i: (i, j)),
            pl.BlockSpec((tile_r, tile_f), lambda j, i: (i, j)),
        ],
        out_shape=[jax.ShapeDtypeStruct((rows, FF), BF16)] * 2,
        compiler_params=pltpu.CompilerParams(vmem_limit_bytes=VMEM_LIMIT),
        cost_estimate=pl.CostEstimate(
            flops=2 * rows * D * FF,
            bytes_accessed=2 * (rows * D + D * FF + 2 * rows * FF),
            transcendentals=2 * rows * FF,
        ),
        name="expand",
    )(mid_low, w_expand, b_expand)


def normalized(values):
    centred = values - jnp.mean(values, axis=-1, keepdims=True)
    spread = jnp.mean(centred * centred, axis=-1, keepdims=True)
    inverse = lax.rsqrt(spread + norm_eps)
    return centred * inverse, inverse


def norm_back(grad, gain, norm, inverse):
    scaled = grad * gain
    return inverse * (
        scaled
        - jnp.mean(scaled, axis=-1, keepdims=True)
        - norm * jnp.mean(scaled * norm, axis=-1, keepdims=True)
    )


def per_device(places, *args):
    (
        question_in,
        passage_in,
        question_len,
        passage_len,
        positive,
        question_cot,
        passage_cot,
        w_joined,
        w_output,
        w_expand,
        w_reduce,
        vectors,
        b_expand,
    ) = args
    pb, pa = lax.axis_index("pb"), lax.axis_index("pa")
    z, core = pa // 2, pa % 2
    tower = z // places.half
    is_q = tower == 0
    chip = pb * places.nz + z
    masks = [places.stack_masks(side) for side in range(2)]
    slots_of = [sorted(range(places.chips), key=side.__getitem__) for side in masks]

    def of_core(rows_of):
        both = jnp.array(rows_of, jnp.int32)
        return (
            lax.dynamic_index_in_dim(both, core, 0, keepdims=False),
            lax.dynamic_index_in_dim(both, 1 - core, 0, keepdims=False),
        )

    side = jnp.full((places.chips,), core, jnp.int32)
    table = jnp.stack([x ^ chip for x in of_core(masks)] + [side]).astype(jnp.int32)
    slots = [x ^ lax.dynamic_index_in_dim(x, chip, 0, keepdims=False) for x in of_core(slots_of)]
    slots = jnp.stack(slots + [side]).astype(jnp.int32)
    share = w_joined.shape[1]

    small = jnp.concatenate(
        [
            vectors.transpose(0, 2, 1),
            b_expand.reshape(2, share, 4),
            jnp.zeros((2, share, 116), BF16),
        ],
        axis=2,
    )
    first = jnp.concatenate([w_joined, w_output, small], axis=2)
    second, third = w_expand, w_reduce

    class Gather:
        def __init__(self, piece):
            self.stack = lax.dynamic_index_in_dim(piece, tower, 0, keepdims=True)
            self.send = lax.dynamic_index_in_dim(piece, 1 - tower, 0, keepdims=True)
            self.held = None

        def join(self, got):
            self.stack = jnp.concatenate([self.stack, got], axis=0)
            self.send = self.stack

        def move(self, first, last):
            for step in range(first, last):
                self.join(places.swap(self.send, step))

        def mid(self):
            self.move(0, 1)

        def along_z(self):
            self.move(1, z_steps)

        def pb_first(self):
            self.move(z_steps, places.steps - 1)

        def pb_last(self):
            self.held = places.swap(self.send, places.steps - 1)

        def core_stack(self):
            self.other = places.swap_core(self.stack)

        def core_held(self):
            self.parts = [self.stack, self.held, self.other, places.swap_core(self.held)]

        def whole(self, segments):
            if self.stack.shape[1] % 8 == 0:
                return assemble(self.parts, table, segments)
            return assemble_plain(self.parts, table, segments)

    z_steps = 1 + len(bits_of(places.half))

    rows_q = question_in.reshape(-1, D)
    rows_p = passage_in.reshape(-1, D)
    own_rows = rows_q.shape[0]

    def sides(q_side, p_side):
        return jnp.where(is_q, q_side, p_side), jnp.where(is_q, p_side, q_side)

    lq, lp = question_in.shape[1], passage_in.shape[1]
    rows = 2 * own_rows

    def chunked(values, sixteenths):
        out, row = [], 0
        for part in sixteenths:
            step = values.shape[0] * part // 16
            out.append(values[row : row + step])
            row += step
        return out

    def hand(values):
        return [places.swap_tower(x) for x in values]

    g1, g2, g3 = Gather(first), Gather(second), Gather(third)
    my_tokens, send_tokens = sides(rows_q, rows_p)
    tokens_out = chunked(send_tokens, (4, 6, 4, 2))
    g1.mid()
    g1.send, tokens_out = tie(g1.send, tokens_out)
    g1.along_z()
    tokens_in = hand(tokens_out[:1])
    g1.send, g2.send, tokens_in = tie(g1.send, g2.send, tokens_in)
    g1.pb_first()
    g2.mid()
    g1.stack, g2.send, tokens_out = tie(g1.stack, g2.send, tokens_out)
    g1.send = g1.stack
    g1.pb_last()
    g1.core_stack()
    g2.along_z()
    tokens_in = tokens_in + hand(tokens_out[1:2])
    (
        g1.held,
        g2.send,
        tokens_in,
        tokens_out,
        question_len,
        passage_len,
        positive,
        question_cot,
        passage_cot,
    ) = tie(
        g1.held,
        g2.send,
        tokens_in,
        tokens_out,
        question_len,
        passage_len,
        positive,
        question_cot,
        passage_cot,
    )
    g1.core_held()
    g2.pb_first()
    tokens_in = tokens_in + hand(tokens_out[2:3])
    g1.parts, g2.stack, g3.send, tokens_in, tokens_out = tie(
        g1.parts, g2.stack, g3.send, tokens_in, tokens_out
    )
    g2.send = g2.stack
    g2.pb_last()
    g2.core_stack()
    tokens_in = tokens_in + hand(tokens_out[3:])
    full_j, full_o, full_small = g1.whole([(0, 3 * D), (3 * D, D), (4 * D, 128)])
    wj = full_j.reshape(D, 3 * D)
    wo = full_o.reshape(D, D)
    small = full_small.reshape(D, 128).astype(F32)
    vec = small[:, :8].T
    bias_e = small[:, 8:12].reshape(1, FF)
    bias_j = jnp.concatenate([vec[0], jnp.zeros((D,), F32), vec[1]])
    wj, tokens_in, g3.send = tie(wj, tokens_in, g3.send)
    g3.mid()
    tokens = join([my_tokens] + tokens_in)
    qkv = (dot(tokens, wj) + bias_j).astype(BF16)

    my_cot, send_cot = sides(question_cot.reshape(-1, D), passage_cot.reshape(-1, D))
    cot_out = chunked(send_cot, (4, 6, 6))
    valid_q = (jnp.arange(lq, dtype=jnp.int32)[None, :] < question_len[:, None]).astype(jnp.int32)
    valid_p = (jnp.arange(lp, dtype=jnp.int32)[None, :] < passage_len[:, None]).astype(jnp.int32)
    my_valid, send_valid = sides(valid_q.reshape(-1), valid_p.reshape(-1))
    valid = jnp.concatenate([my_valid, places.swap_tower(send_valid)])
    row_ids = jnp.arange(rows, dtype=jnp.int32)
    seq = jnp.where(is_q, row_ids // lq, row_ids // lp)
    qid = seq.reshape(rows, 1)
    kid = jnp.where(valid > 0, seq, -1).reshape(rows // BLOCK, 1, BLOCK)
    row_mask = valid.reshape(rows, 1).astype(F32)

    qkv, g2.held, g3.send, cot_out = tie(qkv, g2.held, g3.send, cot_out)
    g2.core_held()
    g3.along_z()
    cot_in = hand(cot_out[:1])
    context, probs = attention(qkv, qid, kid)
    context, g2.parts, g3.send, cot_in, cot_out = tie(context, g2.parts, g3.send, cot_in, cot_out)
    g3.pb_first()
    (full_e,) = g2.whole([(0, FF)])
    we = full_e.reshape(D, FF)
    attended = dot(context, wo) + vec[2]
    norm_one, inverse_one = normalized(tokens.astype(F32) + attended)
    mid = norm_one * vec[3] + vec[4]
    mid_low = mid.astype(BF16)
    mid_low, we, g3.stack, cot_in, cot_out = tie(mid_low, we, g3.stack, cot_in, cot_out)
    g3.send = g3.stack
    g3.pb_last()
    g3.core_stack()
    cot_in = cot_in + hand(cot_out[1:2])
    active, slope = expand(mid_low, we, bias_e)
    active, g3.held, g3.other, cot_in, cot_out = tie(active, g3.held, g3.other, cot_in, cot_out)
    g3.core_held()
    cot_in = cot_in + hand(cot_out[2:])
    (full_r,) = g3.whole([(0, D)])
    wr = full_r.reshape(FF, D)
    norm_two, inverse_two = normalized(mid + dot(active, wr) + vec[5])
    out = ((norm_two * vec[6] + vec[7]) * row_mask).astype(BF16)

    per_q = rows // lq
    every = lp // lq
    per_p = rows // lp
    firsts = out.reshape(per_q, lq, D)[:, 0, :]
    others = places.swap_tower(firsts)
    cls_q = jnp.where(is_q, firsts, others)
    cls_p = jnp.where(is_q, others, firsts)[::every]
    pad = (-(per_q + per_p)) % 8
    stack = jnp.concatenate([cls_q, cls_p, jnp.zeros((pad, D), BF16)], axis=0)[None]
    pair_masks = [0]
    for bit in bits_of(places.half):
        got = lax.ppermute(stack, "pa", [(i, i ^ (2 * bit)) for i in range(places.pa_n)])
        stack = jnp.concatenate([stack, got], axis=0)
        pair_masks = pair_masks + [m ^ (2 * bit) for m in pair_masks]
    for bit in bits_of(places.pb_n):
        got = lax.ppermute(stack, "pb", [(i, i ^ bit) for i in range(places.pb_n)])
        stack = jnp.concatenate([stack, got], axis=0)
        pair_masks = pair_masks + [m ^ (bit * places.pa_n) for m in pair_masks]
    stack = jnp.concatenate([stack, places.swap_core(stack)], axis=0)
    pair_masks = pair_masks + [m ^ 1 for m in pair_masks]
    groups = len(pair_masks)
    me = pb * places.pa_n + (pa % (2 * places.half))
    place = jnp.array(pair_masks, jnp.int32) ^ me
    shift = 2 * places.half
    dev_q = jnp.stack([place, place + shift], axis=1)
    dev_p = jnp.stack([place + shift, place], axis=1)
    nq, np_ = question_in.shape[0], passage_in.shape[0]
    q_ids = (dev_q[:, :, None] * nq + jnp.arange(nq, dtype=jnp.int32)).reshape(-1)
    p_ids = (dev_p[:, :, None] * np_ + jnp.arange(np_, dtype=jnp.int32)).reshape(-1)
    wanted = positive
    pos_masks = [0]
    for bit in bits_of(places.pb_n):
        got = lax.ppermute(wanted, "pb", [(i, i ^ bit) for i in range(places.pb_n)])
        wanted = jnp.concatenate([wanted, got])
        pos_masks = pos_masks + [m ^ bit for m in pos_masks]
    per_pb = positive.shape[0]
    slot_of_pb = jnp.zeros((places.pb_n,), jnp.int32)
    slot_of_pb = slot_of_pb.at[jnp.array(pos_masks, jnp.int32) ^ pb].set(
        jnp.arange(places.pb_n, dtype=jnp.int32)
    )
    wanted = jnp.take(wanted, slot_of_pb[q_ids // per_pb] * per_pb + q_ids % per_pb)

    all_q = stack[:, :per_q].reshape(groups * per_q, D)
    all_p = stack[:, per_q : per_q + per_p].reshape(groups * per_p, D)
    similarity = dot(all_q, all_p, ((1,), (1,))) * score_scale
    hot = (wanted[:, None] == p_ids[None, :]).astype(F32)
    top = jnp.max(similarity, axis=1, keepdims=True)
    grown = jnp.exp(similarity - top)
    total = jnp.sum(grown, axis=1, keepdims=True)
    own_sim = similarity[:per_q]
    loss = top[:per_q, 0] + jnp.log(total[:per_q, 0]) - jnp.sum(own_sim * hot[:per_q], axis=1)
    question_loss = lax.dynamic_slice_in_dim(loss, tower * nq, nq)
    d_sim = (loss_weight * (grown / total - hot)).astype(BF16)
    d_q = dot(d_sim[:per_q], all_p) * score_scale
    d_p = dot(d_sim[:, :per_p], all_q, ((0,), (0,))) * score_scale
    d_p = jnp.concatenate(
        [d_p.reshape(per_p, 1, D), jnp.zeros((per_p, every - 1, D), F32)], axis=1
    ).reshape(per_q, D)
    d_slot = jnp.where(is_q, d_q, d_p)

    d_second, d_reduced, sums_second = second_back(
        join([my_cot] + cot_in), d_slot, row_mask, norm_two, inverse_two, vec[6][None, :]
    )
    even = share % 8 == 0

    def gradient(left, right, tile, extra=None):
        if not even:
            return grad_plain(left, right, table, extra)
        if left.shape[1] > D:
            return tall_grad(left, right, slots, places.nz)
        return weight_grad(left, right, slots, tile, extra)

    class Scatter:
        def __init__(self, mine, theirs):
            self.parts, self.theirs = [mine], theirs
            self.count = mine.shape[0]

        def cores(self):
            self.parts = self.parts + [places.swap_core(self.theirs)]

        def total(self, start, stop):
            out = self.parts[0][start:stop].astype(F32)
            for part in self.parts[1:]:
                out = out + part[start:stop].astype(F32)
            return out

        def move(self, step):
            half = self.count // 2
            send = self.total(half, self.count).astype(BF16)
            self.parts = self.parts + [places.swap(send, step)]
            self.count = half

        def pb_first(self):
            self.move(places.steps - 1)

        def pb_rest(self):
            for step in range(places.steps - 2, z_steps - 1, -1):
                self.move(step)

        def along_z(self):
            for step in range(z_steps - 1, 0, -1):
                self.move(step)

        def mid(self):
            got = places.swap(self.total(1, 2).astype(BF16), 0).astype(F32)
            keep = self.total(0, 1)
            self.out = jnp.concatenate(
                [jnp.where(is_q, keep, got), jnp.where(is_q, got, keep)], axis=0
            )

    send_out = chunked(out[own_rows:], (5, 6, 5))
    sr = Scatter(*gradient(active, d_reduced, D))
    sr.parts, sr.theirs, d_reduced, send_out = tie(sr.parts, sr.theirs, d_reduced, send_out)
    sr.cores()
    got_out = hand(send_out[:1])
    d_expanded, g_bias_expand = hidden_grad(d_reduced, wr, slope)
    sr.parts, d_expanded, got_out, send_out = tie(sr.parts, d_expanded, got_out, send_out)
    sr.pb_first()
    got_out = got_out + hand(send_out[1:2])
    se = Scatter(*gradient(mid_low, d_expanded, 1024))
    se.parts, se.theirs, d_expanded = tie(se.parts, se.theirs, d_expanded)
    se.cores()
    d_first, d_attended, sums_first = first_back(
        d_expanded, we, d_second, norm_one, inverse_one, vec[3][None, :]
    )
    sr.parts, se.parts, d_attended, got_out, send_out = tie(
        sr.parts, se.parts, d_attended, got_out, send_out
    )
    sr.pb_rest()
    got_out = got_out + hand(send_out[2:])
    so = Scatter(*gradient(context, d_attended, D))
    d_context = dot(d_attended, wo, ((1,), (1,))).astype(BF16)
    sr.parts, se.parts, so.parts, so.theirs, d_context, got_out = tie(
        sr.parts, se.parts, so.parts, so.theirs, d_context, got_out
    )
    se.pb_first()
    sr.along_z()
    so.cores()
    blocks = rows // BLOCK
    later = blocks // 2
    d_joined, sums_one = attention_back(qkv, probs, d_context, later, blocks - later)
    sr.parts, so.parts, d_joined = tie(sr.parts, so.parts, d_joined)
    sr.mid()
    send_grad = (d_first[own_rows:] + dot(d_joined[own_rows:], wj, ((1,), (1,)))).astype(BF16)
    se.parts, sr.out, d_joined, send_grad = tie(
        se.parts, sr.out, d_joined, chunked(send_grad, (5, 5, 6))
    )
    se.pb_rest()
    so.pb_first()
    got_grad = hand(send_grad[:1])
    d_joined, sums_two = attention_back(qkv, probs, d_context, 0, later, d_joined)
    se.parts, so.parts, d_joined, got_grad, send_grad = tie(
        se.parts, so.parts, d_joined, got_grad, send_grad
    )
    se.along_z()
    so.pb_rest()
    got_grad = got_grad + hand(send_grad[1:2])
    g_joined_bias = (sums_one + sums_two)[0]
    g_vec = jnp.concatenate(
        [
            g_joined_bias[None, :D],
            g_joined_bias[None, 2 * D :],
            sums_first[2:3],
            sums_first[:2],
            sums_second[2:3],
            sums_second[:2],
        ]
    )
    g_small = jnp.concatenate(
        [g_vec.T, g_bias_expand.reshape(D, 4), jnp.zeros((D, 116), F32)], axis=1
    )
    sj = Scatter(*gradient(tokens, d_joined, D, g_small))
    se.parts, so.parts, sj.parts, sj.theirs, d_joined = tie(
        se.parts, so.parts, sj.parts, sj.theirs, d_joined
    )
    sj.cores()
    so.along_z()
    own_grad = d_first[:own_rows] + dot(d_joined[:own_rows], wj, ((1,), (1,)))
    sj.parts, so.parts, own_grad, got_grad, send_grad = tie(
        sj.parts, so.parts, own_grad, got_grad, send_grad
    )
    sj.pb_first()
    got_grad = got_grad + hand(send_grad[2:])
    out_q, out_p = deal(tower.reshape(1), out, got_out)
    sj.parts, se.parts, so.parts = tie(sj.parts, se.parts, so.parts)
    sj.pb_rest()
    se.mid()
    so.mid()
    sj.parts, se.out, so.out, got_grad = tie(sj.parts, se.out, so.out, got_grad)
    sj.along_z()
    grad_q, grad_p = deal(tower.reshape(1), own_grad, got_grad)
    sj.mid()
    grad_joined = sj.out[:, :, : 3 * D]
    grad_output, grad_expand, grad_reduce = so.out, se.out, sr.out
    extra = sj.out[:, :, 3 * D :]
    grad_vectors = extra[:, :, :8].transpose(0, 2, 1)
    grad_b_expand = extra[:, :, 8:12].reshape(2, 4 * share)

    return (
        out_q.reshape(question_in.shape),
        out_p.reshape(passage_in.shape),
        question_loss,
        grad_q.reshape(question_in.shape),
        grad_p.reshape(passage_in.shape),
        grad_joined,
        grad_output,
        grad_expand,
        grad_reduce,
        grad_vectors,
        grad_b_expand,
    )


def solution(mesh):
    in_specs = (
        P(("pb", "pa"), None, None),
        P(("pb", "pa"), None, None),
        P(("pb", "pa")),
        P(("pb", "pa")),
        P("pb"),
        P(("pb", "pa"), None, None),
        P(("pb", "pa"), None, None),
        P(None, ("pb", "pa"), None),
        P(None, ("pb", "pa"), None),
        P(None, ("pb", "pa"), None),
        P(None, ("pb", "pa"), None),
        P(None, None, ("pb", "pa")),
        P(None, ("pb", "pa")),
    )
    out_specs = (
        P(("pb", "pa"), None, None),
        P(("pb", "pa"), None, None),
        P(("pb", "pa")),
        P(("pb", "pa"), None, None),
        P(("pb", "pa"), None, None),
        P(None, ("pb", "pa"), None),
        P(None, ("pb", "pa"), None),
        P(None, ("pb", "pa"), None),
        P(None, ("pb", "pa"), None),
        P(None, None, ("pb", "pa")),
        P(None, ("pb", "pa")),
    )
    return jax.shard_map(
        functools.partial(per_device, Places(mesh)),
        mesh=mesh,
        in_specs=in_specs,
        out_specs=out_specs,
        check_vma=False,
    )
```

```python
import functools

import jax
import jax.numpy as jnp
from jax import lax
from jax.experimental import pallas as pl
from jax.experimental.pallas import tpu as pltpu
from jax.sharding import PartitionSpec as P

D = 768
HEADS = 12
HDIM = 64
FF = 3072
AXES = ("pb", "pa")
BLOCK = 256

norm_eps = 1e-06
masked_score = -1000000000.0
score_scale = 0.0625
loss_weight = 16.0
head_scale = HDIM ** (-0.5)
F32 = jnp.float32
BF16 = jnp.bfloat16
VMEM_LIMIT = 56 * 1024 * 1024


def bits_of(count):
    return [1 << shift for shift in range(count.bit_length() - 1)]


class Places:
    def __init__(self, mesh):
        self.pb_n = mesh.shape["pb"]
        self.pa_n = mesh.shape["pa"]
        self.nz = self.pa_n // 2
        self.half = self.nz // 2
        self.chips = self.pb_n * self.nz
        pb_bits = bits_of(self.pb_n)
        turn = len(pb_bits) // 2
        low_z = [("z", bit) for bit in bits_of(self.half)]
        first = [("pb", bit) for bit in pb_bits]
        second = first[turn:] + first[:turn]
        self.orders = ([("z", self.half)] + low_z + first, [("z", self.half)] + low_z + second)
        self.steps = len(self.orders[0])

    def chip_mask(self, move):
        axis, bit = move
        return bit * self.nz if axis == "pb" else bit

    def stack_masks(self, core):
        masks = [0]
        for move in self.orders[core]:
            masks = masks + [mask ^ self.chip_mask(move) for mask in masks]
        return masks

    def pairs(self, step):
        out = []
        for pb in range(self.pb_n):
            for pa in range(self.pa_n):
                axis, bit = self.orders[pa % 2][step]
                to_pb, to_pa = (pb ^ bit, pa) if axis == "pb" else (pb, pa ^ (2 * bit))
                out.append((pb * self.pa_n + pa, to_pb * self.pa_n + to_pa))
        return out

    def swap(self, values, step):
        return lax.ppermute(values, AXES, self.pairs(step))

    def swap_core(self, values):
        return lax.ppermute(values, "pa", [(i, i ^ 1) for i in range(self.pa_n)])

    def swap_tower(self, values):
        return lax.ppermute(values, "pa", [(i, i ^ (2 * self.half)) for i in range(self.pa_n)])


def dot(left, right, dims=((1,), (0,))):
    return lax.dot_general(left, right, (dims, ((), ())), preferred_element_type=F32)


def tie(*values):
    return lax.optimization_barrier(values)


def assemble_kernel(segments, idx_ref, *refs):
    count = len(segments)
    sources, outs = refs[:4], refs[4 : 4 + count]
    buffer, in_sem, out_sem = refs[4 + count :]
    core = idx_ref[2, 0]
    part = sources[0].shape[0]
    loads = [
        pltpu.make_async_copy(source, buffer.at[pl.ds(k * part, part)], in_sem.at[k])
        for k, source in enumerate(sources)
    ]
    for load in loads:
        load.start()
    stores = []
    for k in range(4):
        loads[k].wait()
        half = core if k < 2 else 1 - core
        for j in range(part):
            slot = k * part + j
            place = idx_ref[k // 2, (k % 2) * part + j]
            for s, (start, width) in enumerate(segments):
                store = pltpu.make_async_copy(
                    buffer.at[slot, :, pl.ds(start, width)],
                    outs[s].at[place, half],
                    out_sem.at[s, slot],
                )
                store.start()
                stores.append(store)
    for store in stores:
        store.wait()


def assemble(parts, table, segments):
    part, rows, width = parts[0].shape
    chips = 2 * part
    shapes = [jax.ShapeDtypeStruct((chips, 2, rows, w), BF16) for _, w in segments]
    return pl.pallas_call(
        functools.partial(assemble_kernel, segments),
        out_shape=shapes,
        in_specs=[pl.BlockSpec(memory_space=pltpu.SMEM)] + [pl.BlockSpec(memory_space=pl.ANY)] * 4,
        out_specs=[pl.BlockSpec(memory_space=pl.ANY)] * len(segments),
        scratch_shapes=[
            pltpu.VMEM((2 * chips, rows, width), BF16),
            pltpu.SemaphoreType.DMA((4,)),
            pltpu.SemaphoreType.DMA((len(segments), 2 * chips)),
        ],
        compiler_params=pltpu.CompilerParams(vmem_limit_bytes=VMEM_LIMIT),
        cost_estimate=pl.CostEstimate(
            flops=0, bytes_accessed=4 * 2 * chips * rows * width, transcendentals=0
        ),
        name="assemble",
    )(table, *parts)


def assemble_plain(parts, table, segments):
    own = jnp.take(jnp.concatenate(parts[:2], axis=0), jnp.argsort(table[0]), axis=0)
    other = jnp.take(jnp.concatenate(parts[2:], axis=0), jnp.argsort(table[1]), axis=0)
    first = table[2, 0] == 0
    both = jnp.stack([jnp.where(first, own, other), jnp.where(first, other, own)], axis=1)
    return [both[..., start : start + w] for start, w in segments]


def split_slabs(acc, core, chips, mine_ref, theirs_ref, cols, within):
    rows = acc.shape[0] // (2 * chips)
    for s in range(chips):
        low = acc[2 * s * rows : (2 * s + 1) * rows]
        high = acc[(2 * s + 1) * rows : (2 * s + 2) * rows]
        mine, theirs = within(s)
        mine_ref[mine, :, cols] = jnp.where(core == 0, low, high).astype(BF16)
        theirs_ref[theirs, :, cols] = jnp.where(core == 0, high, low).astype(BF16)


def weight_grad_kernel(chips, extra, table_ref, left_ref, right_ref, *refs):
    mine_ref, theirs_ref = refs[-2:]
    core = table_ref[2, 0]
    acc = dot(left_ref[...], right_ref[...], ((0,), (0,)))
    width = acc.shape[1]

    def within(s):
        return table_ref[0, s], table_ref[1, s]

    if not extra:
        split_slabs(acc, core, chips, mine_ref, theirs_ref, slice(None), within)
        return
    step = pl.program_id(0)
    cols = pl.ds(pl.multiple_of(step * width, 128), width)
    split_slabs(acc, core, chips, mine_ref, theirs_ref, cols, within)

    @pl.when(step == 0)
    def _():
        tail = pl.ds(mine_ref.shape[2] - 128, 128)
        split_slabs(refs[0][...], core, chips, mine_ref, theirs_ref, tail, within)


def weight_grad(left, right, slots, tile, extra=None, room=0, into=()):
    rows, height = left.shape
    width = right.shape[1]
    chips = slots.shape[1]
    slab = height // (2 * chips)
    total = width + (room if extra is None else extra.shape[1])
    first = 0
    if into:
        total = into[0].shape[2]
        first = (total - width) // tile
    block = (chips, slab, total if extra is not None else tile)
    place = (lambda j, t: (0, 0, 0)) if extra is not None else (lambda j, t: (0, 0, j + first))
    return pl.pallas_call(
        functools.partial(weight_grad_kernel, chips, extra is not None),
        grid_spec=pltpu.PrefetchScalarGridSpec(
            num_scalar_prefetch=1,
            grid=(width // tile,),
            in_specs=[
                pl.BlockSpec((rows, height), lambda j, t: (0, 0)),
                pl.BlockSpec((rows, tile), lambda j, t: (0, j)),
            ]
            + ([] if extra is None else [pl.BlockSpec((height, 128), lambda j, t: (0, 0))])
            + [pl.BlockSpec(memory_space=pl.ANY)] * len(into),
            out_specs=[pl.BlockSpec(block, place)] * 2,
        ),
        out_shape=[jax.ShapeDtypeStruct((chips, slab, total), BF16)] * 2,
        input_output_aliases={3: 0, 4: 1} if into else {},
        compiler_params=pltpu.CompilerParams(vmem_limit_bytes=VMEM_LIMIT),
        cost_estimate=pl.CostEstimate(
            flops=2 * rows * height * width,
            bytes_accessed=2 * (rows * (height + width) + height * width),
            transcendentals=0,
        ),
        name="weight_grad",
    )(slots, left, right, *([] if extra is None else [extra]), *into)


def tall_grad_kernel(chips, table_ref, left_ref, right_ref, mine_ref, theirs_ref):
    core = table_ref[2, 0]
    acc = dot(left_ref[...], right_ref[...], ((0,), (0,)))
    base = pl.program_id(0) * chips

    def within(s):
        return table_ref[0, base + s] % chips, table_ref[1, base + s] % chips

    split_slabs(acc, core, chips, mine_ref, theirs_ref, slice(None), within)


def tall_grad(left, right, slots, column):
    rows, height = left.shape
    width = right.shape[1]
    chips = slots.shape[1]
    slab = height // (2 * chips)
    tile = height // chips * column
    return pl.pallas_call(
        functools.partial(tall_grad_kernel, column),
        grid_spec=pltpu.PrefetchScalarGridSpec(
            num_scalar_prefetch=1,
            grid=(chips // column,),
            in_specs=[
                pl.BlockSpec((rows, tile), lambda i, t: (0, i)),
                pl.BlockSpec((rows, width), lambda i, t: (0, 0)),
            ],
            out_specs=[
                pl.BlockSpec((column, slab, width), lambda i, t: (t[0, i * column] // column, 0, 0)),
                pl.BlockSpec((column, slab, width), lambda i, t: (t[1, i * column] // column, 0, 0)),
            ],
        ),
        out_shape=[jax.ShapeDtypeStruct((chips, slab, width), BF16)] * 2,
        compiler_params=pltpu.CompilerParams(vmem_limit_bytes=VMEM_LIMIT),
        cost_estimate=pl.CostEstimate(
            flops=2 * rows * height * width,
            bytes_accessed=2 * (rows * (height + width) + height * width),
            transcendentals=0,
        ),
        name="tall_grad",
    )(slots, left, right)


def grad_plain(left, right, table, extra=None):
    full = dot(left, right, ((0,), (0,)))
    if extra is not None:
        full = jnp.concatenate([full, extra], axis=1)
    chips = table.shape[1]
    full = full.astype(BF16).reshape(chips, 2, full.shape[0] // (2 * chips), full.shape[1])
    core = table[2, 0]
    mine = lax.dynamic_index_in_dim(full, core, 1, keepdims=False)
    theirs = lax.dynamic_index_in_dim(full, 1 - core, 1, keepdims=False)
    return jnp.take(mine, table[0], axis=0), jnp.take(theirs, table[1], axis=0)


def hidden_grad_kernel(grad_ref, w_ref, slope_ref, out_ref, sum_ref):
    grad = dot(grad_ref[...], w_ref[...], ((1,), (1,))) * slope_ref[...].astype(F32)
    low = grad.astype(BF16)
    out_ref[...] = low
    sum_ref[...] = jnp.sum(low.astype(F32), axis=0, keepdims=True)


def hidden_grad(grad, w_reduce, slope):
    rows, tile = grad.shape[0], 512
    return pl.pallas_call(
        hidden_grad_kernel,
        grid=(FF // tile,),
        in_specs=[
            pl.BlockSpec((rows, D), lambda j: (0, 0)),
            pl.BlockSpec((tile, D), lambda j: (j, 0)),
            pl.BlockSpec((rows, tile), lambda j: (0, j)),
        ],
        out_specs=[
            pl.BlockSpec((rows, tile), lambda j: (0, j)),
            pl.BlockSpec((1, tile), lambda j: (0, j)),
        ],
        out_shape=[
            jax.ShapeDtypeStruct((rows, FF), BF16),
            jax.ShapeDtypeStruct((1, FF), F32),
        ],
        compiler_params=pltpu.CompilerParams(vmem_limit_bytes=VMEM_LIMIT),
        cost_estimate=pl.CostEstimate(
            flops=2 * rows * D * FF,
            bytes_accessed=2 * (rows * D + D * FF + 2 * rows * FF),
            transcendentals=0,
        ),
        name="hidden_grad",
    )(grad, w_reduce, slope)


def attention_kernel(qkv_ref, qid_ref, kid_ref, context_ref, probs_ref):
    allowed = qid_ref[...] == kid_ref[0]
    lane = lax.broadcasted_iota(jnp.int32, (BLOCK, 128), 1)
    zero = jnp.zeros((BLOCK, 128), BF16)
    for pair in range(HEADS // 2):
        queries = qkv_ref[:, pair * 128 : pair * 128 + 128]
        keys = qkv_ref[:, D + pair * 128 : D + pair * 128 + 128]
        values = qkv_ref[:, 2 * D + pair * 128 : 2 * D + pair * 128 + 128]
        outs = []
        for side in range(2):
            mine = (lane < HDIM) if side == 0 else (lane >= HDIM)
            scores = dot(queries, jnp.where(mine, keys, zero), ((1,), (1,))) * head_scale
            scores = jnp.where(allowed, scores, masked_score)
            top = jnp.max(scores, axis=1, keepdims=True)
            grown = jnp.exp(scores - top)
            total = jnp.sum(grown, axis=1, keepdims=True)
            probs = (grown * (1.0 / total)).astype(BF16)
            probs_ref[0, 2 * pair + side] = probs
            outs.append(dot(probs, values))
        context_ref[:, pair * 128 : pair * 128 + 128] = jnp.where(
            lane < HDIM, outs[0], outs[1]
        ).astype(BF16)


def attention_more_kernel(qkv_ref, qid_ref, kid_ref, _, __, context_ref, probs_ref):
    attention_kernel(qkv_ref, qid_ref, kid_ref, context_ref, probs_ref)


def attention(qkv, qid, kid, start, count, into=()):
    rows = qkv.shape[0]
    blocks = rows // BLOCK
    return pl.pallas_call(
        attention_more_kernel if into else attention_kernel,
        grid=(count,),
        in_specs=[
            pl.BlockSpec((BLOCK, 3 * D), lambda i: (i + start, 0)),
            pl.BlockSpec((BLOCK, 1), lambda i: (i + start, 0)),
            pl.BlockSpec((1, 1, BLOCK), lambda i: (i + start, 0, 0)),
        ]
        + [pl.BlockSpec(memory_space=pl.ANY)] * len(into),
        out_specs=[
            pl.BlockSpec((BLOCK, D), lambda i: (i + start, 0)),
            pl.BlockSpec((1, HEADS, BLOCK, BLOCK), lambda i: (i + start, 0, 0, 0)),
        ],
        input_output_aliases={3: 0, 4: 1} if into else {},
        out_shape=[
            jax.ShapeDtypeStruct((rows, D), BF16),
            jax.ShapeDtypeStruct((blocks, HEADS, BLOCK, BLOCK), BF16),
        ],
        compiler_params=pltpu.CompilerParams(vmem_limit_bytes=VMEM_LIMIT),
        cost_estimate=pl.CostEstimate(
            flops=4 * count * BLOCK * BLOCK * D * 2,
            bytes_accessed=count * BLOCK * (4 * D + HEADS * BLOCK) * 2,
            transcendentals=count * BLOCK * HEADS * BLOCK,
        ),
        name="attention",
    )(qkv, qid, kid, *into)


def attention_back_kernel(qkv_ref, probs_ref, grad_ref, out_ref, sum_ref):
    lane = lax.broadcasted_iota(jnp.int32, (BLOCK, 128), 1)
    zero = jnp.zeros((BLOCK, 128), BF16)
    for pair in range(HEADS // 2):
        cols = slice(pair * 128, pair * 128 + 128)
        queries = qkv_ref[:, pair * 128 : pair * 128 + 128]
        keys = qkv_ref[:, D + pair * 128 : D + pair * 128 + 128]
        values = qkv_ref[:, 2 * D + pair * 128 : 2 * D + pair * 128 + 128]
        grad = grad_ref[:, cols]
        d_q, d_k, d_v = [], [], []
        for side in range(2):
            mine = (lane < HDIM) if side == 0 else (lane >= HDIM)
            low = probs_ref[0, 2 * pair + side]
            d_probs = dot(jnp.where(mine, grad, zero), values, ((1,), (1,)))
            d_v.append(dot(low, grad, ((0,), (0,))))
            probs = low.astype(F32)
            row_dot = jnp.sum(d_probs * probs, axis=1, keepdims=True)
            d_scores = (probs * (d_probs - row_dot)).astype(BF16)
            d_q.append(dot(d_scores, keys))
            d_k.append(dot(d_scores, queries, ((0,), (0,))))
        first = lane < HDIM
        out_ref[:, pair * 128 : pair * 128 + 128] = (
            jnp.where(first, d_q[0], d_q[1]) * head_scale
        ).astype(BF16)
        out_ref[:, D + pair * 128 : D + pair * 128 + 128] = (
            jnp.where(first, d_k[0], d_k[1]) * head_scale
        ).astype(BF16)
        out_ref[:, 2 * D + pair * 128 : 2 * D + pair * 128 + 128] = jnp.where(
            first, d_v[0], d_v[1]
        ).astype(BF16)
    sums = jnp.sum(out_ref[...].astype(F32), axis=0, keepdims=True)

    @pl.when(pl.program_id(0) == 0)
    def _():
        sum_ref[...] = sums

    @pl.when(pl.program_id(0) > 0)
    def _():
        sum_ref[...] += sums


def attention_back_more_kernel(qkv_ref, probs_ref, grad_ref, _, out_ref, sum_ref):
    attention_back_kernel(qkv_ref, probs_ref, grad_ref, out_ref, sum_ref)


def attention_back(qkv, probs, grad_context, start, count, into=None):
    rows = qkv.shape[0]
    more = into is not None
    return pl.pallas_call(
        attention_back_more_kernel if more else attention_back_kernel,
        grid=(count,),
        in_specs=[
            pl.BlockSpec((BLOCK, 3 * D), lambda i: (i + start, 0)),
            pl.BlockSpec((1, HEADS, BLOCK, BLOCK), lambda i: (i + start, 0, 0, 0)),
            pl.BlockSpec((BLOCK, D), lambda i: (i + start, 0)),
        ]
        + ([pl.BlockSpec(memory_space=pl.ANY)] if more else []),
        out_specs=[
            pl.BlockSpec((BLOCK, 3 * D), lambda i: (i + start, 0)),
            pl.BlockSpec((1, 3 * D), lambda i: (0, 0)),
        ],
        out_shape=[
            jax.ShapeDtypeStruct((rows, 3 * D), BF16),
            jax.ShapeDtypeStruct((1, 3 * D), F32),
        ],
        input_output_aliases={3: 0} if more else {},
        compiler_params=pltpu.CompilerParams(vmem_limit_bytes=VMEM_LIMIT),
        cost_estimate=pl.CostEstimate(
            flops=8 * count * BLOCK * BLOCK * D * 2,
            bytes_accessed=count * BLOCK * (7 * D + HEADS * BLOCK) * 2,
            transcendentals=0,
        ),
        name="attention_back",
    )(qkv, probs, grad_context, *([into] if more else []))


def join_kernel(*refs):
    row = 0
    for piece in refs[:-1]:
        rows = piece.shape[0]
        refs[-1][row : row + rows, :] = piece[...]
        row += rows


def join(pieces):
    rows, width = sum(x.shape[0] for x in pieces), pieces[0].shape[1]
    return pl.pallas_call(
        join_kernel,
        grid=(1,),
        in_specs=[pl.BlockSpec(x.shape, lambda i: (0, 0)) for x in pieces],
        out_specs=pl.BlockSpec((rows, width), lambda i: (0, 0)),
        out_shape=jax.ShapeDtypeStruct((rows, width), pieces[0].dtype),
        compiler_params=pltpu.CompilerParams(vmem_limit_bytes=VMEM_LIMIT),
        cost_estimate=pl.CostEstimate(
            flops=0, bytes_accessed=4 * rows * width, transcendentals=0
        ),
        name="join",
    )(*pieces)


def deal_kernel(tower_ref, own_ref, *refs):
    pieces, (q_ref, p_ref) = refs[:-2], refs[-2:]

    def give(own_out, other_out):
        own_out[...] = own_ref[...]
        row = 0
        for piece in pieces:
            rows = piece.shape[0]
            other_out[row : row + rows, :] = piece[...].astype(other_out.dtype)
            row += rows

    @pl.when(tower_ref[0] == 0)
    def _():
        give(q_ref, p_ref)

    @pl.when(tower_ref[0] != 0)
    def _():
        give(p_ref, q_ref)


def deal(tower, own, pieces):
    rows, width = sum(x.shape[0] for x in pieces), own.shape[1]
    shape = jax.ShapeDtypeStruct((rows, width), own.dtype)
    return pl.pallas_call(
        deal_kernel,
        grid=(1,),
        in_specs=[
            pl.BlockSpec(memory_space=pltpu.SMEM),
            pl.BlockSpec((rows, width), lambda i: (0, 0)),
        ]
        + [pl.BlockSpec(x.shape, lambda i: (0, 0)) for x in pieces],
        out_specs=[pl.BlockSpec((rows, width), lambda i: (0, 0))] * 2,
        out_shape=[shape] * 2,
        compiler_params=pltpu.CompilerParams(vmem_limit_bytes=VMEM_LIMIT),
        cost_estimate=pl.CostEstimate(
            flops=0, bytes_accessed=12 * rows * width, transcendentals=0
        ),
        name="deal",
    )(tower, own, *pieces)


def add_sums(sum_ref, values):
    total = jnp.concatenate(
        [jnp.sum(x, axis=0, keepdims=True) for x in values]
        + [jnp.zeros((8 - len(values), values[0].shape[1]), F32)],
        axis=0,
    )

    @pl.when(pl.program_id(0) == 0)
    def _():
        sum_ref[...] = total

    @pl.when(pl.program_id(0) > 0)
    def _():
        sum_ref[...] += total


def second_back_kernel(
    cot_ref, slot_ref, mask_ref, norm_ref, inverse_ref, gain_ref, grad_ref, low_ref, sum_ref
):
    group = slot_ref.shape[1]
    cot = cot_ref[...].astype(F32).reshape(group, BLOCK // group, D)
    first = lax.broadcasted_iota(jnp.int32, cot.shape, 1) == 0
    grad = cot + jnp.where(first, slot_ref[0][:, None, :], 0.0)
    grad = grad.reshape(BLOCK, D) * mask_ref[...]
    norm = norm_ref[...]
    second = norm_back(grad, gain_ref[...], norm, inverse_ref[...])
    low = second.astype(BF16)
    grad_ref[...] = second
    low_ref[...] = low
    add_sums(sum_ref, [grad * norm, grad, low.astype(F32)])


def second_back(cot, d_slot, mask, norm, inverse, gain):
    rows = cot.shape[0]
    blocks = rows // BLOCK
    wide = pl.BlockSpec((BLOCK, D), lambda i: (i, 0))
    thin = pl.BlockSpec((BLOCK, 1), lambda i: (i, 0))
    group = d_slot.shape[0] // blocks
    return pl.pallas_call(
        second_back_kernel,
        grid=(blocks,),
        in_specs=[
            wide,
            pl.BlockSpec((1, group, D), lambda i: (i, 0, 0)),
            thin,
            wide,
            thin,
            pl.BlockSpec((1, D), lambda i: (0, 0)),
        ],
        out_specs=[wide, wide, pl.BlockSpec((8, D), lambda i: (0, 0))],
        out_shape=[
            jax.ShapeDtypeStruct((rows, D), F32),
            jax.ShapeDtypeStruct((rows, D), BF16),
            jax.ShapeDtypeStruct((8, D), F32),
        ],
        compiler_params=pltpu.CompilerParams(vmem_limit_bytes=VMEM_LIMIT),
        cost_estimate=pl.CostEstimate(
            flops=20 * rows * D, bytes_accessed=12 * rows * D, transcendentals=0
        ),
        name="second_back",
    )(cot, d_slot.reshape(blocks, group, D), mask, norm, inverse, gain)


def first_back_kernel(
    hidden_ref, w_ref, second_ref, norm_ref, inverse_ref, gain_ref, grad_ref, low_ref, sum_ref
):
    grad = second_ref[...] + dot(hidden_ref[...], w_ref[...], ((1,), (1,)))
    norm = norm_ref[...]
    first = norm_back(grad, gain_ref[...], norm, inverse_ref[...])
    low = first.astype(BF16)
    grad_ref[...] = first
    low_ref[...] = low
    add_sums(sum_ref, [grad * norm, grad, low.astype(F32)])


def first_back(d_expanded, w_expand, d_second, norm, inverse, gain):
    rows = d_expanded.shape[0]
    wide = pl.BlockSpec((BLOCK, D), lambda i: (i, 0))
    return pl.pallas_call(
        first_back_kernel,
        grid=(rows // BLOCK,),
        in_specs=[
            pl.BlockSpec((BLOCK, FF), lambda i: (i, 0)),
            pl.BlockSpec((D, FF), lambda i: (0, 0)),
            wide,
            wide,
            pl.BlockSpec((BLOCK, 1), lambda i: (i, 0)),
            pl.BlockSpec((1, D), lambda i: (0, 0)),
        ],
        out_specs=[wide, wide, pl.BlockSpec((8, D), lambda i: (0, 0))],
        out_shape=[
            jax.ShapeDtypeStruct((rows, D), F32),
            jax.ShapeDtypeStruct((rows, D), BF16),
            jax.ShapeDtypeStruct((8, D), F32),
        ],
        compiler_params=pltpu.CompilerParams(vmem_limit_bytes=VMEM_LIMIT),
        cost_estimate=pl.CostEstimate(
            flops=2 * rows * D * FF,
            bytes_accessed=2 * (rows * FF + D * FF) + 14 * rows * D,
            transcendentals=0,
        ),
        name="first_back",
    )(d_expanded, w_expand, d_second, norm, inverse, gain)


def expand_kernel(mid_ref, w_ref, b_ref, active_ref, slope_ref):
    expanded = dot(mid_ref[...], w_ref[...]) + b_ref[...]
    phi = 0.5 + 0.5 * lax.erf(expanded * 0.7071067811865476)
    density = jnp.exp(expanded * expanded * -0.5) * 0.3989422804014327
    active_ref[...] = (expanded * phi).astype(BF16)
    slope_ref[...] = (phi + expanded * density).astype(BF16)


def expand_more_kernel(mid_ref, w_ref, b_ref, _, __, active_ref, slope_ref):
    expand_kernel(mid_ref, w_ref, b_ref, active_ref, slope_ref)


def expand(mid_low, w_expand, b_expand, start, count, into=()):
    rows = mid_low.shape[0]
    tile_r, tile_f = 256, FF // 4
    return pl.pallas_call(
        expand_more_kernel if into else expand_kernel,
        grid=(count, rows // tile_r),
        in_specs=[
            pl.BlockSpec((tile_r, D), lambda j, i: (i, 0)),
            pl.BlockSpec((D, tile_f), lambda j, i: (0, j + start)),
            pl.BlockSpec((1, tile_f), lambda j, i: (0, j + start)),
        ]
        + [pl.BlockSpec(memory_space=pl.ANY)] * len(into),
        out_specs=[
            pl.BlockSpec((tile_r, tile_f), lambda j, i: (i, j + start)),
            pl.BlockSpec((tile_r, tile_f), lambda j, i: (i, j + start)),
        ],
        out_shape=[jax.ShapeDtypeStruct((rows, FF), BF16)] * 2,
        input_output_aliases={3: 0, 4: 1} if into else {},
        compiler_params=pltpu.CompilerParams(vmem_limit_bytes=VMEM_LIMIT),
        cost_estimate=pl.CostEstimate(
            flops=2 * rows * D * count * tile_f,
            bytes_accessed=2 * (rows * D + D * count * tile_f + 2 * rows * count * tile_f),
            transcendentals=2 * rows * count * tile_f,
        ),
        name="expand",
    )(mid_low, w_expand, b_expand, *into)


def normalized(values):
    centred = values - jnp.mean(values, axis=-1, keepdims=True)
    spread = jnp.mean(centred * centred, axis=-1, keepdims=True)
    inverse = lax.rsqrt(spread + norm_eps)
    return centred * inverse, inverse


def norm_back(grad, gain, norm, inverse):
    scaled = grad * gain
    return inverse * (
        scaled
        - jnp.mean(scaled, axis=-1, keepdims=True)
        - norm * jnp.mean(scaled * norm, axis=-1, keepdims=True)
    )


def per_device(places, *args):
    (
        question_in,
        passage_in,
        question_len,
        passage_len,
        positive,
        question_cot,
        passage_cot,
        w_joined,
        w_output,
        w_expand,
        w_reduce,
        vectors,
        b_expand,
    ) = args
    pb, pa = lax.axis_index("pb"), lax.axis_index("pa")
    z, core = pa // 2, pa % 2
    tower = z // places.half
    is_q = tower == 0
    chip = pb * places.nz + z
    masks = [places.stack_masks(side) for side in range(2)]
    slots_of = [sorted(range(places.chips), key=side.__getitem__) for side in masks]

    def of_core(rows_of):
        both = jnp.array(rows_of, jnp.int32)
        return (
            lax.dynamic_index_in_dim(both, core, 0, keepdims=False),
            lax.dynamic_index_in_dim(both, 1 - core, 0, keepdims=False),
        )

    side = jnp.full((places.chips,), core, jnp.int32)
    table = jnp.stack([x ^ chip for x in of_core(masks)] + [side]).astype(jnp.int32)
    slots = [x ^ lax.dynamic_index_in_dim(x, chip, 0, keepdims=False) for x in of_core(slots_of)]
    slots = jnp.stack(slots + [side]).astype(jnp.int32)
    share = w_joined.shape[1]

    small = jnp.concatenate(
        [
            vectors.transpose(0, 2, 1),
            b_expand.reshape(2, share, 4),
            jnp.zeros((2, share, 116), BF16),
        ],
        axis=2,
    )
    first = jnp.concatenate([w_joined, w_output, small], axis=2)
    second, third = w_expand, w_reduce

    class Gather:
        def __init__(self, piece):
            self.stack = lax.dynamic_index_in_dim(piece, tower, 0, keepdims=True)
            self.send = lax.dynamic_index_in_dim(piece, 1 - tower, 0, keepdims=True)
            self.held = None

        def join(self, got):
            self.stack = jnp.concatenate([self.stack, got], axis=0)
            self.send = self.stack

        def move(self, first, last):
            for step in range(first, last):
                self.join(places.swap(self.send, step))

        def mid(self):
            self.move(0, 1)

        def along_z(self):
            self.move(1, z_steps)

        def pb_first(self):
            self.move(z_steps, places.steps - 1)

        def pb_last(self):
            self.held = places.swap(self.send, places.steps - 1)

        def core_stack(self):
            self.other = places.swap_core(self.stack)

        def core_held(self):
            self.parts = [self.stack, self.held, self.other, places.swap_core(self.held)]

        def whole(self, segments):
            if self.stack.shape[1] % 8 == 0:
                return assemble(self.parts, table, segments)
            return assemble_plain(self.parts, table, segments)

    z_steps = 1 + len(bits_of(places.half))

    rows_q = question_in.reshape(-1, D)
    rows_p = passage_in.reshape(-1, D)
    own_rows = rows_q.shape[0]

    def sides(q_side, p_side):
        return jnp.where(is_q, q_side, p_side), jnp.where(is_q, p_side, q_side)

    lq, lp = question_in.shape[1], passage_in.shape[1]
    rows = 2 * own_rows

    def chunked(values, sixteenths):
        out, row = [], 0
        for part in sixteenths:
            step = values.shape[0] * part // 16
            out.append(values[row : row + step])
            row += step
        return out

    def hand(values):
        return [places.swap_tower(x) for x in values]

    g1, g2, g3 = Gather(first), Gather(second), Gather(third)
    my_tokens, send_tokens = sides(rows_q, rows_p)
    tokens_out = chunked(send_tokens, (5, 6, 5))
    g1.mid()
    g1.send, tokens_out = tie(g1.send, tokens_out)
    g1.along_z()
    tokens_in = hand(tokens_out[:1])
    g1.send, g2.send, tokens_in = tie(g1.send, g2.send, tokens_in)
    g1.pb_first()
    g2.mid()
    g1.stack, g2.send, tokens_out = tie(g1.stack, g2.send, tokens_out)
    g1.send = g1.stack
    g1.pb_last()
    g1.core_stack()
    g2.along_z()
    tokens_in = tokens_in + hand(tokens_out[1:2])
    (
        g1.held,
        g2.send,
        tokens_in,
        tokens_out,
        question_len,
        passage_len,
        positive,
        question_cot,
        passage_cot,
    ) = tie(
        g1.held,
        g2.send,
        tokens_in,
        tokens_out,
        question_len,
        passage_len,
        positive,
        question_cot,
        passage_cot,
    )
    g1.core_held()
    g2.pb_first()
    tokens_in = tokens_in + hand(tokens_out[2:])
    full_j, full_o, full_small = g1.whole([(0, 3 * D), (3 * D, D), (4 * D, 128)])
    full_j, full_o, full_small, g2.stack, g3.send, tokens_in = tie(
        full_j, full_o, full_small, g2.stack, g3.send, tokens_in
    )
    g2.send = g2.stack
    g2.pb_last()
    g2.core_stack()
    g3.mid()
    wj = full_j.reshape(D, 3 * D)
    wo = full_o.reshape(D, D)
    small = full_small.reshape(D, 128).astype(F32)
    vec = small[:, :8].T
    bias_e = small[:, 8:12].reshape(1, FF)
    bias_j = jnp.concatenate([vec[0], jnp.zeros((D,), F32), vec[1]])
    tokens = join([my_tokens] + tokens_in)
    qkv = (dot(tokens, wj) + bias_j).astype(BF16)

    my_cot, send_cot = sides(question_cot.reshape(-1, D), passage_cot.reshape(-1, D))
    cot_out = chunked(send_cot, (4, 5, 7))
    valid_q = (jnp.arange(lq, dtype=jnp.int32)[None, :] < question_len[:, None]).astype(jnp.int32)
    valid_p = (jnp.arange(lp, dtype=jnp.int32)[None, :] < passage_len[:, None]).astype(jnp.int32)
    my_valid, send_valid = sides(valid_q.reshape(-1), valid_p.reshape(-1))
    valid = jnp.concatenate([my_valid, places.swap_tower(send_valid)])
    row_ids = jnp.arange(rows, dtype=jnp.int32)
    seq = jnp.where(is_q, row_ids // lq, row_ids // lp)
    qid = seq.reshape(rows, 1)
    kid = jnp.where(valid > 0, seq, -1).reshape(rows // BLOCK, 1, BLOCK)
    row_mask = valid.reshape(rows, 1).astype(F32)

    blocks = rows // BLOCK
    later = blocks // 2
    qkv, g3.send, cot_out = tie(qkv, g3.send, cot_out)
    g3.along_z()
    cot_in = hand(cot_out[:1])
    spread = attention(qkv, qid, kid, 0, later)
    spread, g2.held, g3.send = tie(spread, g2.held, g3.send)
    g2.core_held()
    g3.pb_first()
    context, probs = attention(qkv, qid, kid, later, blocks - later, tuple(spread))
    context, g2.parts, cot_in, cot_out = tie(context, g2.parts, cot_in, cot_out)
    cot_in = cot_in + hand(cot_out[1:2])
    (full_e,) = g2.whole([(0, FF)])
    we = full_e.reshape(D, FF)
    context, we, g3.stack = tie(context, we, g3.stack)
    g3.send = g3.stack
    g3.pb_last()
    g3.core_stack()
    attended = dot(context, wo) + vec[2]
    norm_one, inverse_one = normalized(tokens.astype(F32) + attended)
    mid = norm_one * vec[3] + vec[4]
    mid_low = mid.astype(BF16)
    mid_low, cot_in, cot_out = tie(mid_low, cot_in, cot_out)
    cot_in = cot_in + hand(cot_out[2:])
    gelu = expand(mid_low, we, bias_e, 0, 2)
    gelu, g3.held, g3.other, g3.stack = tie(gelu, g3.held, g3.other, g3.stack)
    g3.core_held()
    active, slope = expand(mid_low, we, bias_e, 2, 2, tuple(gelu))
    active, g3.parts, cot_in = tie(active, g3.parts, cot_in)
    (full_r,) = g3.whole([(0, D)])
    wr = full_r.reshape(FF, D)
    norm_two, inverse_two = normalized(mid + dot(active, wr) + vec[5])
    out = ((norm_two * vec[6] + vec[7]) * row_mask).astype(BF16)

    per_q = rows // lq
    every = lp // lq
    per_p = rows // lp
    firsts = out.reshape(per_q, lq, D)[:, 0, :]
    others = places.swap_tower(firsts)
    cls_q = jnp.where(is_q, firsts, others)
    cls_p = jnp.where(is_q, others, firsts)[::every]
    pad = (-(per_q + per_p)) % 8
    stack = jnp.concatenate([cls_q, cls_p, jnp.zeros((pad, D), BF16)], axis=0)[None]
    pair_masks = [0]
    for bit in bits_of(places.half):
        got = lax.ppermute(stack, "pa", [(i, i ^ (2 * bit)) for i in range(places.pa_n)])
        stack = jnp.concatenate([stack, got], axis=0)
        pair_masks = pair_masks + [m ^ (2 * bit) for m in pair_masks]
    for bit in bits_of(places.pb_n):
        got = lax.ppermute(stack, "pb", [(i, i ^ bit) for i in range(places.pb_n)])
        stack = jnp.concatenate([stack, got], axis=0)
        pair_masks = pair_masks + [m ^ (bit * places.pa_n) for m in pair_masks]
    stack = jnp.concatenate([stack, places.swap_core(stack)], axis=0)
    pair_masks = pair_masks + [m ^ 1 for m in pair_masks]
    groups = len(pair_masks)
    me = pb * places.pa_n + (pa % (2 * places.half))
    place = jnp.array(pair_masks, jnp.int32) ^ me
    shift = 2 * places.half
    dev_q = jnp.stack([place, place + shift], axis=1)
    dev_p = jnp.stack([place + shift, place], axis=1)
    nq, np_ = question_in.shape[0], passage_in.shape[0]
    q_ids = (dev_q[:, :, None] * nq + jnp.arange(nq, dtype=jnp.int32)).reshape(-1)
    p_ids = (dev_p[:, :, None] * np_ + jnp.arange(np_, dtype=jnp.int32)).reshape(-1)
    wanted = positive
    pos_masks = [0]
    for bit in bits_of(places.pb_n):
        got = lax.ppermute(wanted, "pb", [(i, i ^ bit) for i in range(places.pb_n)])
        wanted = jnp.concatenate([wanted, got])
        pos_masks = pos_masks + [m ^ bit for m in pos_masks]
    per_pb = positive.shape[0]
    slot_of_pb = jnp.zeros((places.pb_n,), jnp.int32)
    slot_of_pb = slot_of_pb.at[jnp.array(pos_masks, jnp.int32) ^ pb].set(
        jnp.arange(places.pb_n, dtype=jnp.int32)
    )
    wanted = jnp.take(wanted, slot_of_pb[q_ids // per_pb] * per_pb + q_ids % per_pb)

    all_q = stack[:, :per_q].reshape(groups * per_q, D)
    all_p = stack[:, per_q : per_q + per_p].reshape(groups * per_p, D)
    similarity = dot(all_q, all_p, ((1,), (1,))) * score_scale
    hot = (wanted[:, None] == p_ids[None, :]).astype(F32)
    top = jnp.max(similarity, axis=1, keepdims=True)
    grown = jnp.exp(similarity - top)
    total = jnp.sum(grown, axis=1, keepdims=True)
    own_sim = similarity[:per_q]
    loss = top[:per_q, 0] + jnp.log(total[:per_q, 0]) - jnp.sum(own_sim * hot[:per_q], axis=1)
    question_loss = lax.dynamic_slice_in_dim(loss, tower * nq, nq)
    d_sim = (loss_weight * (grown / total - hot)).astype(BF16)
    d_q = dot(d_sim[:per_q], all_p) * score_scale
    d_p = dot(d_sim[:, :per_p], all_q, ((0,), (0,))) * score_scale
    d_p = jnp.concatenate(
        [d_p.reshape(per_p, 1, D), jnp.zeros((per_p, every - 1, D), F32)], axis=1
    ).reshape(per_q, D)
    d_slot = jnp.where(is_q, d_q, d_p)

    d_second, d_reduced, sums_second = second_back(
        join([my_cot] + cot_in), d_slot, row_mask, norm_two, inverse_two, vec[6][None, :]
    )
    even = share % 8 == 0

    def gradient(left, right, **more):
        if left.shape[1] > D:
            return tall_grad(left, right, slots, places.nz)
        return weight_grad(left, right, slots, D, **more)

    def plain(left, right, extra=None):
        return grad_plain(left, right, table, extra)

    class Scatter:
        def __init__(self, mine, theirs):
            self.parts, self.theirs = [mine], theirs
            self.count = mine.shape[0]

        def cores(self):
            self.parts = self.parts + [places.swap_core(self.theirs)]

        def total(self, start, stop):
            out = self.parts[0][start:stop].astype(F32)
            for part in self.parts[1:]:
                out = out + part[start:stop].astype(F32)
            return out

        def move(self, step):
            half = self.count // 2
            send = self.total(half, self.count).astype(BF16)
            self.parts = self.parts + [places.swap(send, step)]
            self.count = half

        def pb_first(self):
            self.move(places.steps - 1)

        def pb_rest(self):
            for step in range(places.steps - 2, z_steps - 1, -1):
                self.move(step)

        def along_z(self):
            for step in range(z_steps - 1, 0, -1):
                self.move(step)

        def mid(self):
            got = places.swap(self.total(1, 2).astype(BF16), 0).astype(F32)
            keep = self.total(0, 1)
            self.out = jnp.concatenate(
                [jnp.where(is_q, keep, got), jnp.where(is_q, got, keep)], axis=0
            )

    send_out = chunked(out[own_rows:], (5, 6, 5))
    sr = Scatter(*(gradient if even else plain)(active, d_reduced))
    sr.parts, sr.theirs, d_reduced, send_out = tie(sr.parts, sr.theirs, d_reduced, send_out)
    sr.cores()
    got_out = hand(send_out[:1])
    d_expanded, g_bias_expand = hidden_grad(d_reduced, wr, slope)
    sr.parts, d_expanded, got_out, send_out = tie(sr.parts, d_expanded, got_out, send_out)
    sr.pb_first()
    got_out = got_out + hand(send_out[1:2])
    if even:
        partial = gradient(mid_low, d_expanded, room=D)
    else:
        partial = plain(mid_low, d_expanded)
    partial, d_expanded = tie(partial, d_expanded)
    d_first, d_attended, sums_first = first_back(
        d_expanded, we, d_second, norm_one, inverse_one, vec[3][None, :]
    )
    sr.parts, partial, d_attended, got_out, send_out = tie(
        sr.parts, partial, d_attended, got_out, send_out
    )
    sr.pb_rest()
    got_out = got_out + hand(send_out[2:])
    if even:
        partial = gradient(context, d_attended, into=tuple(partial))
    else:
        also = plain(context, d_attended)
        partial = [jnp.concatenate(x, axis=2) for x in zip(partial, also)]
    se = Scatter(*partial)
    se.parts, se.theirs, d_attended = tie(se.parts, se.theirs, d_attended)
    se.cores()
    d_context = dot(d_attended, wo, ((1,), (1,))).astype(BF16)
    sr.parts, se.parts, d_context, got_out = tie(sr.parts, se.parts, d_context, got_out)
    se.pb_first()
    sr.along_z()
    d_joined, sums_one = attention_back(qkv, probs, d_context, later, blocks - later)
    sr.parts, d_joined = tie(sr.parts, d_joined)
    sr.mid()
    send_grad = (d_first[own_rows:] + dot(d_joined[own_rows:], wj, ((1,), (1,)))).astype(BF16)
    se.parts, sr.out, d_joined, send_grad = tie(
        se.parts, sr.out, d_joined, chunked(send_grad, (5, 5, 6))
    )
    se.pb_rest()
    got_grad = hand(send_grad[:1])
    d_joined, sums_two = attention_back(qkv, probs, d_context, 0, later, d_joined)
    se.parts, d_joined, got_grad, send_grad = tie(se.parts, d_joined, got_grad, send_grad)
    se.along_z()
    got_grad = got_grad + hand(send_grad[1:2])
    g_joined_bias = (sums_one + sums_two)[0]
    g_vec = jnp.concatenate(
        [
            g_joined_bias[None, :D],
            g_joined_bias[None, 2 * D :],
            sums_first[2:3],
            sums_first[:2],
            sums_second[2:3],
            sums_second[:2],
        ]
    )
    g_small = jnp.concatenate(
        [g_vec.T, g_bias_expand.reshape(D, 4), jnp.zeros((D, 116), F32)], axis=1
    )
    sj = Scatter(*(gradient if even else plain)(tokens, d_joined, extra=g_small))
    se.parts, sj.parts, sj.theirs, d_joined, got_grad, send_grad = tie(
        se.parts, sj.parts, sj.theirs, d_joined, got_grad, send_grad
    )
    sj.cores()
    got_grad = got_grad + hand(send_grad[2:])
    own_grad = d_first[:own_rows] + dot(d_joined[:own_rows], wj, ((1,), (1,)))
    sj.parts, own_grad = tie(sj.parts, own_grad)
    sj.pb_first()
    se.mid()
    out_q, out_p = deal(tower.reshape(1), out, got_out)
    sj.parts, se.out, got_grad = tie(sj.parts, se.out, got_grad)
    sj.pb_rest()
    grad_q, grad_p = deal(tower.reshape(1), own_grad, got_grad)
    sj.parts, grad_q, grad_p = tie(sj.parts, grad_q, grad_p)
    sj.along_z()
    sj.mid()
    grad_joined = sj.out[:, :, : 3 * D]
    grad_expand, grad_output, grad_reduce = se.out[:, :, :FF], se.out[:, :, FF:], sr.out
    extra = sj.out[:, :, 3 * D :]
    grad_vectors = extra[:, :, :8].transpose(0, 2, 1)
    grad_b_expand = extra[:, :, 8:12].reshape(2, 4 * share)

    return (
        out_q.reshape(question_in.shape),
        out_p.reshape(passage_in.shape),
        question_loss,
        grad_q.reshape(question_in.shape),
        grad_p.reshape(passage_in.shape),
        grad_joined,
        grad_output,
        grad_expand,
        grad_reduce,
        grad_vectors,
        grad_b_expand,
    )


def solution(mesh):
    in_specs = (
        P(("pb", "pa"), None, None),
        P(("pb", "pa"), None, None),
        P(("pb", "pa")),
        P(("pb", "pa")),
        P("pb"),
        P(("pb", "pa"), None, None),
        P(("pb", "pa"), None, None),
        P(None, ("pb", "pa"), None),
        P(None, ("pb", "pa"), None),
        P(None, ("pb", "pa"), None),
        P(None, ("pb", "pa"), None),
        P(None, None, ("pb", "pa")),
        P(None, ("pb", "pa")),
    )
    out_specs = (
        P(("pb", "pa"), None, None),
        P(("pb", "pa"), None, None),
        P(("pb", "pa")),
        P(("pb", "pa"), None, None),
        P(("pb", "pa"), None, None),
        P(None, ("pb", "pa"), None),
        P(None, ("pb", "pa"), None),
        P(None, ("pb", "pa"), None),
        P(None, ("pb", "pa"), None),
        P(None, None, ("pb", "pa")),
        P(None, ("pb", "pa")),
    )
    return jax.shard_map(
        functools.partial(per_device, Places(mesh)),
        mesh=mesh,
        in_specs=in_specs,
        out_specs=out_specs,
        check_vma=False,
    )
```

```python
import functools

import jax
import jax.numpy as jnp
from jax import lax
from jax.experimental import pallas as pl
from jax.experimental.pallas import tpu as pltpu
from jax.sharding import PartitionSpec as P

D = 768
HEADS = 12
HDIM = 64
FF = 3072
AXES = ("pb", "pa")
BLOCK = 256

norm_eps = 1e-06
masked_score = -1000000000.0
score_scale = 0.0625
loss_weight = 16.0
head_scale = HDIM ** (-0.5)
F32 = jnp.float32
BF16 = jnp.bfloat16
VMEM_LIMIT = 56 * 1024 * 1024


def bits_of(count):
    return [1 << shift for shift in range(count.bit_length() - 1)]


class Places:
    def __init__(self, mesh):
        self.pb_n = mesh.shape["pb"]
        self.pa_n = mesh.shape["pa"]
        self.nz = self.pa_n // 2
        self.half = self.nz // 2
        self.chips = self.pb_n * self.nz
        pb_bits = bits_of(self.pb_n)
        turn = len(pb_bits) // 2
        low_z = [("z", bit) for bit in bits_of(self.half)]
        first = [("pb", bit) for bit in pb_bits]
        second = first[turn:] + first[:turn]
        self.orders = ([("z", self.half)] + low_z + first, [("z", self.half)] + low_z + second)
        self.steps = len(self.orders[0])

    def chip_mask(self, move):
        axis, bit = move
        return bit * self.nz if axis == "pb" else bit

    def stack_masks(self, core):
        masks = [0]
        for move in self.orders[core]:
            masks = masks + [mask ^ self.chip_mask(move) for mask in masks]
        return masks

    def pairs(self, step):
        out = []
        for pb in range(self.pb_n):
            for pa in range(self.pa_n):
                axis, bit = self.orders[pa % 2][step]
                to_pb, to_pa = (pb ^ bit, pa) if axis == "pb" else (pb, pa ^ (2 * bit))
                out.append((pb * self.pa_n + pa, to_pb * self.pa_n + to_pa))
        return out

    def swap(self, values, step):
        return lax.ppermute(values, AXES, self.pairs(step))

    def swap_core(self, values):
        return lax.ppermute(values, "pa", [(i, i ^ 1) for i in range(self.pa_n)])

    def swap_tower(self, values):
        return lax.ppermute(values, "pa", [(i, i ^ (2 * self.half)) for i in range(self.pa_n)])


def dot(left, right, dims=((1,), (0,))):
    return lax.dot_general(left, right, (dims, ((), ())), preferred_element_type=F32)


def tie(*values):
    return lax.optimization_barrier(values)


def assemble_kernel(segments, idx_ref, *refs):
    count = len(segments)
    sources, outs = refs[:4], refs[4 : 4 + count]
    buffer, in_sem, out_sem = refs[4 + count :]
    core = idx_ref[2, 0]
    part = sources[0].shape[0]
    loads = [
        pltpu.make_async_copy(source, buffer.at[pl.ds(k * part, part)], in_sem.at[k])
        for k, source in enumerate(sources)
    ]
    for load in loads:
        load.start()
    stores = []
    for k in range(4):
        loads[k].wait()
        half = core if k < 2 else 1 - core
        for j in range(part):
            slot = k * part + j
            place = idx_ref[k // 2, (k % 2) * part + j]
            for s, (start, width) in enumerate(segments):
                store = pltpu.make_async_copy(
                    buffer.at[slot, :, pl.ds(start, width)],
                    outs[s].at[place, half],
                    out_sem.at[s, slot],
                )
                store.start()
                stores.append(store)
    for store in stores:
        store.wait()


def assemble(parts, table, segments):
    part, rows, width = parts[0].shape
    chips = 2 * part
    shapes = [jax.ShapeDtypeStruct((chips, 2, rows, w), BF16) for _, w in segments]
    return pl.pallas_call(
        functools.partial(assemble_kernel, segments),
        out_shape=shapes,
        in_specs=[pl.BlockSpec(memory_space=pltpu.SMEM)] + [pl.BlockSpec(memory_space=pl.ANY)] * 4,
        out_specs=[pl.BlockSpec(memory_space=pl.ANY)] * len(segments),
        scratch_shapes=[
            pltpu.VMEM((2 * chips, rows, width), BF16),
            pltpu.SemaphoreType.DMA((4,)),
            pltpu.SemaphoreType.DMA((len(segments), 2 * chips)),
        ],
        compiler_params=pltpu.CompilerParams(vmem_limit_bytes=VMEM_LIMIT),
        cost_estimate=pl.CostEstimate(
            flops=0, bytes_accessed=4 * 2 * chips * rows * width, transcendentals=0
        ),
        name="assemble",
    )(table, *parts)


def assemble_plain(parts, table, segments):
    own = jnp.take(jnp.concatenate(parts[:2], axis=0), jnp.argsort(table[0]), axis=0)
    other = jnp.take(jnp.concatenate(parts[2:], axis=0), jnp.argsort(table[1]), axis=0)
    first = table[2, 0] == 0
    both = jnp.stack([jnp.where(first, own, other), jnp.where(first, other, own)], axis=1)
    return [both[..., start : start + w] for start, w in segments]


def split_slabs(acc, core, chips, mine_ref, theirs_ref, cols, within):
    rows = acc.shape[0] // (2 * chips)
    for s in range(chips):
        low = acc[2 * s * rows : (2 * s + 1) * rows]
        high = acc[(2 * s + 1) * rows : (2 * s + 2) * rows]
        mine, theirs = within(s)
        mine_ref[mine, :, cols] = jnp.where(core == 0, low, high).astype(BF16)
        theirs_ref[theirs, :, cols] = jnp.where(core == 0, high, low).astype(BF16)


def weight_grad_kernel(chips, extra, table_ref, left_ref, right_ref, *refs):
    mine_ref, theirs_ref = refs[-2:]
    core = table_ref[2, 0]
    acc = dot(left_ref[...], right_ref[...], ((0,), (0,)))
    width = acc.shape[1]

    def within(s):
        return table_ref[0, s], table_ref[1, s]

    if not extra:
        split_slabs(acc, core, chips, mine_ref, theirs_ref, slice(None), within)
        return
    step = pl.program_id(0)
    cols = pl.ds(pl.multiple_of(step * width, 128), width)
    split_slabs(acc, core, chips, mine_ref, theirs_ref, cols, within)

    @pl.when(step == 0)
    def _():
        tail = pl.ds(mine_ref.shape[2] - 128, 128)
        split_slabs(refs[0][...], core, chips, mine_ref, theirs_ref, tail, within)


def weight_grad(left, right, slots, tile, extra=None, room=0, into=()):
    rows, height = left.shape
    width = right.shape[1]
    chips = slots.shape[1]
    slab = height // (2 * chips)
    total = width + (room if extra is None else extra.shape[1])
    first = 0
    if into:
        total = into[0].shape[2]
        first = (total - width) // tile
    block = (chips, slab, total if extra is not None else tile)
    place = (lambda j, t: (0, 0, 0)) if extra is not None else (lambda j, t: (0, 0, j + first))
    return pl.pallas_call(
        functools.partial(weight_grad_kernel, chips, extra is not None),
        grid_spec=pltpu.PrefetchScalarGridSpec(
            num_scalar_prefetch=1,
            grid=(width // tile,),
            in_specs=[
                pl.BlockSpec((rows, height), lambda j, t: (0, 0)),
                pl.BlockSpec((rows, tile), lambda j, t: (0, j)),
            ]
            + ([] if extra is None else [pl.BlockSpec((height, 128), lambda j, t: (0, 0))])
            + [pl.BlockSpec(memory_space=pl.ANY)] * len(into),
            out_specs=[pl.BlockSpec(block, place)] * 2,
        ),
        out_shape=[jax.ShapeDtypeStruct((chips, slab, total), BF16)] * 2,
        input_output_aliases={3: 0, 4: 1} if into else {},
        compiler_params=pltpu.CompilerParams(vmem_limit_bytes=VMEM_LIMIT),
        cost_estimate=pl.CostEstimate(
            flops=2 * rows * height * width,
            bytes_accessed=2 * (rows * (height + width) + height * width),
            transcendentals=0,
        ),
        name="weight_grad",
    )(slots, left, right, *([] if extra is None else [extra]), *into)


def tall_grad_kernel(chips, table_ref, left_ref, right_ref, mine_ref, theirs_ref):
    core = table_ref[2, 0]
    acc = dot(left_ref[...], right_ref[...], ((0,), (0,)))
    base = pl.program_id(0) * chips

    def within(s):
        return table_ref[0, base + s] % chips, table_ref[1, base + s] % chips

    split_slabs(acc, core, chips, mine_ref, theirs_ref, slice(None), within)


def tall_grad(left, right, slots, column):
    rows, height = left.shape
    width = right.shape[1]
    chips = slots.shape[1]
    slab = height // (2 * chips)
    tile = height // chips * column
    return pl.pallas_call(
        functools.partial(tall_grad_kernel, column),
        grid_spec=pltpu.PrefetchScalarGridSpec(
            num_scalar_prefetch=1,
            grid=(chips // column,),
            in_specs=[
                pl.BlockSpec((rows, tile), lambda i, t: (0, i)),
                pl.BlockSpec((rows, width), lambda i, t: (0, 0)),
            ],
            out_specs=[
                pl.BlockSpec((column, slab, width), lambda i, t: (t[0, i * column] // column, 0, 0)),
                pl.BlockSpec((column, slab, width), lambda i, t: (t[1, i * column] // column, 0, 0)),
            ],
        ),
        out_shape=[jax.ShapeDtypeStruct((chips, slab, width), BF16)] * 2,
        compiler_params=pltpu.CompilerParams(vmem_limit_bytes=VMEM_LIMIT),
        cost_estimate=pl.CostEstimate(
            flops=2 * rows * height * width,
            bytes_accessed=2 * (rows * (height + width) + height * width),
            transcendentals=0,
        ),
        name="tall_grad",
    )(slots, left, right)


def grad_plain(left, right, table, extra=None):
    full = dot(left, right, ((0,), (0,)))
    if extra is not None:
        full = jnp.concatenate([full, extra], axis=1)
    chips = table.shape[1]
    full = full.astype(BF16).reshape(chips, 2, full.shape[0] // (2 * chips), full.shape[1])
    core = table[2, 0]
    mine = lax.dynamic_index_in_dim(full, core, 1, keepdims=False)
    theirs = lax.dynamic_index_in_dim(full, 1 - core, 1, keepdims=False)
    return jnp.take(mine, table[0], axis=0), jnp.take(theirs, table[1], axis=0)


def hidden_grad_kernel(grad_ref, w_ref, slope_ref, out_ref, sum_ref):
    grad = dot(grad_ref[...], w_ref[...], ((1,), (1,))) * slope_ref[...].astype(F32)
    low = grad.astype(BF16)
    out_ref[...] = low
    sum_ref[...] = jnp.sum(low.astype(F32), axis=0, keepdims=True)


def hidden_grad(grad, w_reduce, slope):
    rows, tile = grad.shape[0], 512
    return pl.pallas_call(
        hidden_grad_kernel,
        grid=(FF // tile,),
        in_specs=[
            pl.BlockSpec((rows, D), lambda j: (0, 0)),
            pl.BlockSpec((tile, D), lambda j: (j, 0)),
            pl.BlockSpec((rows, tile), lambda j: (0, j)),
        ],
        out_specs=[
            pl.BlockSpec((rows, tile), lambda j: (0, j)),
            pl.BlockSpec((1, tile), lambda j: (0, j)),
        ],
        out_shape=[
            jax.ShapeDtypeStruct((rows, FF), BF16),
            jax.ShapeDtypeStruct((1, FF), F32),
        ],
        compiler_params=pltpu.CompilerParams(vmem_limit_bytes=VMEM_LIMIT),
        cost_estimate=pl.CostEstimate(
            flops=2 * rows * D * FF,
            bytes_accessed=2 * (rows * D + D * FF + 2 * rows * FF),
            transcendentals=0,
        ),
        name="hidden_grad",
    )(grad, w_reduce, slope)


def attention_kernel(qkv_ref, qid_ref, kid_ref, context_ref, probs_ref):
    allowed = qid_ref[...] == kid_ref[0]
    lane = lax.broadcasted_iota(jnp.int32, (BLOCK, 128), 1)
    zero = jnp.zeros((BLOCK, 128), BF16)
    for pair in range(HEADS // 2):
        queries = qkv_ref[:, pair * 128 : pair * 128 + 128]
        keys = qkv_ref[:, D + pair * 128 : D + pair * 128 + 128]
        values = qkv_ref[:, 2 * D + pair * 128 : 2 * D + pair * 128 + 128]
        outs = []
        for side in range(2):
            mine = (lane < HDIM) if side == 0 else (lane >= HDIM)
            scores = dot(queries, jnp.where(mine, keys, zero), ((1,), (1,))) * head_scale
            scores = jnp.where(allowed, scores, masked_score)
            top = jnp.max(scores, axis=1, keepdims=True)
            grown = jnp.exp(scores - top)
            total = jnp.sum(grown, axis=1, keepdims=True)
            probs = (grown * (1.0 / total)).astype(BF16)
            probs_ref[0, 2 * pair + side] = probs
            outs.append(dot(probs, values))
        context_ref[:, pair * 128 : pair * 128 + 128] = jnp.where(
            lane < HDIM, outs[0], outs[1]
        ).astype(BF16)


def attention_more_kernel(qkv_ref, qid_ref, kid_ref, _, __, context_ref, probs_ref):
    attention_kernel(qkv_ref, qid_ref, kid_ref, context_ref, probs_ref)


def attention(qkv, qid, kid, start, count, into=()):
    rows = qkv.shape[0]
    blocks = rows // BLOCK
    return pl.pallas_call(
        attention_more_kernel if into else attention_kernel,
        grid=(count,),
        in_specs=[
            pl.BlockSpec((BLOCK, 3 * D), lambda i: (i + start, 0)),
            pl.BlockSpec((BLOCK, 1), lambda i: (i + start, 0)),
            pl.BlockSpec((1, 1, BLOCK), lambda i: (i + start, 0, 0)),
        ]
        + [pl.BlockSpec(memory_space=pl.ANY)] * len(into),
        out_specs=[
            pl.BlockSpec((BLOCK, D), lambda i: (i + start, 0)),
            pl.BlockSpec((1, HEADS, BLOCK, BLOCK), lambda i: (i + start, 0, 0, 0)),
        ],
        input_output_aliases={3: 0, 4: 1} if into else {},
        out_shape=[
            jax.ShapeDtypeStruct((rows, D), BF16),
            jax.ShapeDtypeStruct((blocks, HEADS, BLOCK, BLOCK), BF16),
        ],
        compiler_params=pltpu.CompilerParams(vmem_limit_bytes=VMEM_LIMIT),
        cost_estimate=pl.CostEstimate(
            flops=4 * count * BLOCK * BLOCK * D * 2,
            bytes_accessed=count * BLOCK * (4 * D + HEADS * BLOCK) * 2,
            transcendentals=count * BLOCK * HEADS * BLOCK,
        ),
        name="attention",
    )(qkv, qid, kid, *into)


def attention_back_kernel(qkv_ref, probs_ref, grad_ref, out_ref, sum_ref):
    lane = lax.broadcasted_iota(jnp.int32, (BLOCK, 128), 1)
    zero = jnp.zeros((BLOCK, 128), BF16)
    for pair in range(HEADS // 2):
        cols = slice(pair * 128, pair * 128 + 128)
        queries = qkv_ref[:, pair * 128 : pair * 128 + 128]
        keys = qkv_ref[:, D + pair * 128 : D + pair * 128 + 128]
        values = qkv_ref[:, 2 * D + pair * 128 : 2 * D + pair * 128 + 128]
        grad = grad_ref[:, cols]
        d_q, d_k, d_v = [], [], []
        for side in range(2):
            mine = (lane < HDIM) if side == 0 else (lane >= HDIM)
            low = probs_ref[0, 2 * pair + side]
            d_probs = dot(jnp.where(mine, grad, zero), values, ((1,), (1,)))
            d_v.append(dot(low, grad, ((0,), (0,))))
            probs = low.astype(F32)
            row_dot = jnp.sum(d_probs * probs, axis=1, keepdims=True)
            d_scores = (probs * (d_probs - row_dot)).astype(BF16)
            d_q.append(dot(d_scores, keys))
            d_k.append(dot(d_scores, queries, ((0,), (0,))))
        first = lane < HDIM
        out_ref[:, pair * 128 : pair * 128 + 128] = (
            jnp.where(first, d_q[0], d_q[1]) * head_scale
        ).astype(BF16)
        out_ref[:, D + pair * 128 : D + pair * 128 + 128] = (
            jnp.where(first, d_k[0], d_k[1]) * head_scale
        ).astype(BF16)
        out_ref[:, 2 * D + pair * 128 : 2 * D + pair * 128 + 128] = jnp.where(
            first, d_v[0], d_v[1]
        ).astype(BF16)
    sums = jnp.sum(out_ref[...].astype(F32), axis=0, keepdims=True)

    @pl.when(pl.program_id(0) == 0)
    def _():
        sum_ref[...] = sums

    @pl.when(pl.program_id(0) > 0)
    def _():
        sum_ref[...] += sums


def attention_back_more_kernel(qkv_ref, probs_ref, grad_ref, _, out_ref, sum_ref):
    attention_back_kernel(qkv_ref, probs_ref, grad_ref, out_ref, sum_ref)


def attention_back(qkv, probs, grad_context, start, count, into=None):
    rows = qkv.shape[0]
    more = into is not None
    return pl.pallas_call(
        attention_back_more_kernel if more else attention_back_kernel,
        grid=(count,),
        in_specs=[
            pl.BlockSpec((BLOCK, 3 * D), lambda i: (i + start, 0)),
            pl.BlockSpec((1, HEADS, BLOCK, BLOCK), lambda i: (i + start, 0, 0, 0)),
            pl.BlockSpec((BLOCK, D), lambda i: (i + start, 0)),
        ]
        + ([pl.BlockSpec(memory_space=pl.ANY)] if more else []),
        out_specs=[
            pl.BlockSpec((BLOCK, 3 * D), lambda i: (i + start, 0)),
            pl.BlockSpec((1, 3 * D), lambda i: (0, 0)),
        ],
        out_shape=[
            jax.ShapeDtypeStruct((rows, 3 * D), BF16),
            jax.ShapeDtypeStruct((1, 3 * D), F32),
        ],
        input_output_aliases={3: 0} if more else {},
        compiler_params=pltpu.CompilerParams(vmem_limit_bytes=VMEM_LIMIT),
        cost_estimate=pl.CostEstimate(
            flops=8 * count * BLOCK * BLOCK * D * 2,
            bytes_accessed=count * BLOCK * (7 * D + HEADS * BLOCK) * 2,
            transcendentals=0,
        ),
        name="attention_back",
    )(qkv, probs, grad_context, *([into] if more else []))


def join_kernel(*refs):
    row = 0
    for piece in refs[:-1]:
        rows = piece.shape[0]
        refs[-1][row : row + rows, :] = piece[...]
        row += rows


def join(pieces):
    rows, width = sum(x.shape[0] for x in pieces), pieces[0].shape[1]
    return pl.pallas_call(
        join_kernel,
        grid=(1,),
        in_specs=[pl.BlockSpec(x.shape, lambda i: (0, 0)) for x in pieces],
        out_specs=pl.BlockSpec((rows, width), lambda i: (0, 0)),
        out_shape=jax.ShapeDtypeStruct((rows, width), pieces[0].dtype),
        compiler_params=pltpu.CompilerParams(vmem_limit_bytes=VMEM_LIMIT),
        cost_estimate=pl.CostEstimate(
            flops=0, bytes_accessed=4 * rows * width, transcendentals=0
        ),
        name="join",
    )(*pieces)


def deal_kernel(tower_ref, own_ref, *refs):
    pieces, (q_ref, p_ref) = refs[:-2], refs[-2:]

    def give(own_out, other_out):
        own_out[...] = own_ref[...]
        row = 0
        for piece in pieces:
            rows = piece.shape[0]
            other_out[row : row + rows, :] = piece[...].astype(other_out.dtype)
            row += rows

    @pl.when(tower_ref[0] == 0)
    def _():
        give(q_ref, p_ref)

    @pl.when(tower_ref[0] != 0)
    def _():
        give(p_ref, q_ref)


def deal(tower, own, pieces):
    rows, width = sum(x.shape[0] for x in pieces), own.shape[1]
    shape = jax.ShapeDtypeStruct((rows, width), own.dtype)
    return pl.pallas_call(
        deal_kernel,
        grid=(1,),
        in_specs=[
            pl.BlockSpec(memory_space=pltpu.SMEM),
            pl.BlockSpec((rows, width), lambda i: (0, 0)),
        ]
        + [pl.BlockSpec(x.shape, lambda i: (0, 0)) for x in pieces],
        out_specs=[pl.BlockSpec((rows, width), lambda i: (0, 0))] * 2,
        out_shape=[shape] * 2,
        compiler_params=pltpu.CompilerParams(vmem_limit_bytes=VMEM_LIMIT),
        cost_estimate=pl.CostEstimate(
            flops=0, bytes_accessed=12 * rows * width, transcendentals=0
        ),
        name="deal",
    )(tower, own, *pieces)


def add_sums(sum_ref, values):
    total = jnp.concatenate(
        [jnp.sum(x, axis=0, keepdims=True) for x in values]
        + [jnp.zeros((8 - len(values), values[0].shape[1]), F32)],
        axis=0,
    )

    @pl.when(pl.program_id(0) == 0)
    def _():
        sum_ref[...] = total

    @pl.when(pl.program_id(0) > 0)
    def _():
        sum_ref[...] += total


def second_back_kernel(
    cot_ref, slot_ref, mask_ref, norm_ref, inverse_ref, gain_ref, grad_ref, low_ref, sum_ref
):
    group = slot_ref.shape[1]
    cot = cot_ref[...].astype(F32).reshape(group, BLOCK // group, D)
    first = lax.broadcasted_iota(jnp.int32, cot.shape, 1) == 0
    grad = cot + jnp.where(first, slot_ref[0][:, None, :], 0.0)
    grad = grad.reshape(BLOCK, D) * mask_ref[...]
    norm = norm_ref[...]
    second = norm_back(grad, gain_ref[...], norm, inverse_ref[...])
    low = second.astype(BF16)
    grad_ref[...] = second
    low_ref[...] = low
    add_sums(sum_ref, [grad * norm, grad, low.astype(F32)])


def second_back(cot, d_slot, mask, norm, inverse, gain):
    rows = cot.shape[0]
    blocks = rows // BLOCK
    wide = pl.BlockSpec((BLOCK, D), lambda i: (i, 0))
    thin = pl.BlockSpec((BLOCK, 1), lambda i: (i, 0))
    group = d_slot.shape[0] // blocks
    return pl.pallas_call(
        second_back_kernel,
        grid=(blocks,),
        in_specs=[
            wide,
            pl.BlockSpec((1, group, D), lambda i: (i, 0, 0)),
            thin,
            wide,
            thin,
            pl.BlockSpec((1, D), lambda i: (0, 0)),
        ],
        out_specs=[wide, wide, pl.BlockSpec((8, D), lambda i: (0, 0))],
        out_shape=[
            jax.ShapeDtypeStruct((rows, D), F32),
            jax.ShapeDtypeStruct((rows, D), BF16),
            jax.ShapeDtypeStruct((8, D), F32),
        ],
        compiler_params=pltpu.CompilerParams(vmem_limit_bytes=VMEM_LIMIT),
        cost_estimate=pl.CostEstimate(
            flops=20 * rows * D, bytes_accessed=12 * rows * D, transcendentals=0
        ),
        name="second_back",
    )(cot, d_slot.reshape(blocks, group, D), mask, norm, inverse, gain)


def first_back_kernel(
    hidden_ref, w_ref, second_ref, norm_ref, inverse_ref, gain_ref, grad_ref, low_ref, sum_ref
):
    grad = second_ref[...] + dot(hidden_ref[...], w_ref[...], ((1,), (1,)))
    norm = norm_ref[...]
    first = norm_back(grad, gain_ref[...], norm, inverse_ref[...])
    low = first.astype(BF16)
    grad_ref[...] = first
    low_ref[...] = low
    add_sums(sum_ref, [grad * norm, grad, low.astype(F32)])


def first_back(d_expanded, w_expand, d_second, norm, inverse, gain):
    rows = d_expanded.shape[0]
    wide = pl.BlockSpec((BLOCK, D), lambda i: (i, 0))
    return pl.pallas_call(
        first_back_kernel,
        grid=(rows // BLOCK,),
        in_specs=[
            pl.BlockSpec((BLOCK, FF), lambda i: (i, 0)),
            pl.BlockSpec((D, FF), lambda i: (0, 0)),
            wide,
            wide,
            pl.BlockSpec((BLOCK, 1), lambda i: (i, 0)),
            pl.BlockSpec((1, D), lambda i: (0, 0)),
        ],
        out_specs=[wide, wide, pl.BlockSpec((8, D), lambda i: (0, 0))],
        out_shape=[
            jax.ShapeDtypeStruct((rows, D), F32),
            jax.ShapeDtypeStruct((rows, D), BF16),
            jax.ShapeDtypeStruct((8, D), F32),
        ],
        compiler_params=pltpu.CompilerParams(vmem_limit_bytes=VMEM_LIMIT),
        cost_estimate=pl.CostEstimate(
            flops=2 * rows * D * FF,
            bytes_accessed=2 * (rows * FF + D * FF) + 14 * rows * D,
            transcendentals=0,
        ),
        name="first_back",
    )(d_expanded, w_expand, d_second, norm, inverse, gain)


def expand_kernel(mid_ref, w_ref, b_ref, active_ref, slope_ref):
    expanded = dot(mid_ref[...], w_ref[...]) + b_ref[...]
    phi = 0.5 + 0.5 * lax.erf(expanded * 0.7071067811865476)
    density = jnp.exp(expanded * expanded * -0.5) * 0.3989422804014327
    active_ref[...] = (expanded * phi).astype(BF16)
    slope_ref[...] = (phi + expanded * density).astype(BF16)


def expand_more_kernel(mid_ref, w_ref, b_ref, _, __, active_ref, slope_ref):
    expand_kernel(mid_ref, w_ref, b_ref, active_ref, slope_ref)


def expand(mid_low, w_expand, b_expand, start, count, into=()):
    rows = mid_low.shape[0]
    tile_r, tile_f = 256, FF // 2
    return pl.pallas_call(
        expand_more_kernel if into else expand_kernel,
        grid=(count, rows // tile_r),
        in_specs=[
            pl.BlockSpec((tile_r, D), lambda j, i: (i, 0)),
            pl.BlockSpec((D, tile_f), lambda j, i: (0, j + start)),
            pl.BlockSpec((1, tile_f), lambda j, i: (0, j + start)),
        ]
        + [pl.BlockSpec(memory_space=pl.ANY)] * len(into),
        out_specs=[
            pl.BlockSpec((tile_r, tile_f), lambda j, i: (i, j + start)),
            pl.BlockSpec((tile_r, tile_f), lambda j, i: (i, j + start)),
        ],
        out_shape=[jax.ShapeDtypeStruct((rows, FF), BF16)] * 2,
        input_output_aliases={3: 0, 4: 1} if into else {},
        compiler_params=pltpu.CompilerParams(vmem_limit_bytes=VMEM_LIMIT),
        cost_estimate=pl.CostEstimate(
            flops=2 * rows * D * count * tile_f,
            bytes_accessed=2 * (rows * D + D * count * tile_f + 2 * rows * count * tile_f),
            transcendentals=2 * rows * count * tile_f,
        ),
        name="expand",
    )(mid_low, w_expand, b_expand, *into)


def normalized(values):
    centred = values - jnp.mean(values, axis=-1, keepdims=True)
    spread = jnp.mean(centred * centred, axis=-1, keepdims=True)
    inverse = lax.rsqrt(spread + norm_eps)
    return centred * inverse, inverse


def norm_back(grad, gain, norm, inverse):
    scaled = grad * gain
    return inverse * (
        scaled
        - jnp.mean(scaled, axis=-1, keepdims=True)
        - norm * jnp.mean(scaled * norm, axis=-1, keepdims=True)
    )


def per_device(places, *args):
    (
        question_in,
        passage_in,
        question_len,
        passage_len,
        positive,
        question_cot,
        passage_cot,
        w_joined,
        w_output,
        w_expand,
        w_reduce,
        vectors,
        b_expand,
    ) = args
    pb, pa = lax.axis_index("pb"), lax.axis_index("pa")
    z, core = pa // 2, pa % 2
    tower = z // places.half
    is_q = tower == 0
    chip = pb * places.nz + z
    masks = [places.stack_masks(side) for side in range(2)]
    slots_of = [sorted(range(places.chips), key=side.__getitem__) for side in masks]

    def of_core(rows_of):
        both = jnp.array(rows_of, jnp.int32)
        return (
            lax.dynamic_index_in_dim(both, core, 0, keepdims=False),
            lax.dynamic_index_in_dim(both, 1 - core, 0, keepdims=False),
        )

    side = jnp.full((places.chips,), core, jnp.int32)
    table = jnp.stack([x ^ chip for x in of_core(masks)] + [side]).astype(jnp.int32)
    slots = [x ^ lax.dynamic_index_in_dim(x, chip, 0, keepdims=False) for x in of_core(slots_of)]
    slots = jnp.stack(slots + [side]).astype(jnp.int32)
    share = w_joined.shape[1]

    small = jnp.concatenate(
        [
            vectors.transpose(0, 2, 1),
            b_expand.reshape(2, share, 4),
            jnp.zeros((2, share, 116), BF16),
        ],
        axis=2,
    )
    first = jnp.concatenate([w_joined, w_output, small], axis=2)
    second, third = w_expand, w_reduce

    class Gather:
        def __init__(self, piece):
            self.stack = lax.dynamic_index_in_dim(piece, tower, 0, keepdims=True)
            self.send = lax.dynamic_index_in_dim(piece, 1 - tower, 0, keepdims=True)
            self.held = None

        def join(self, got):
            self.stack = jnp.concatenate([self.stack, got], axis=0)
            self.send = self.stack

        def move(self, first, last):
            for step in range(first, last):
                self.join(places.swap(self.send, step))

        def mid(self):
            self.move(0, 1)

        def along_z(self):
            self.move(1, z_steps)

        def pb_first(self):
            self.move(z_steps, places.steps - 1)

        def pb_last(self):
            self.held = places.swap(self.send, places.steps - 1)

        def core_stack(self):
            self.other = places.swap_core(self.stack)

        def core_held(self):
            self.parts = [self.stack, self.held, self.other, places.swap_core(self.held)]

        def whole(self, segments):
            if self.stack.shape[1] % 8 == 0:
                return assemble(self.parts, table, segments)
            return assemble_plain(self.parts, table, segments)

    z_steps = 1 + len(bits_of(places.half))

    rows_q = question_in.reshape(-1, D)
    rows_p = passage_in.reshape(-1, D)
    own_rows = rows_q.shape[0]

    def sides(q_side, p_side):
        return jnp.where(is_q, q_side, p_side), jnp.where(is_q, p_side, q_side)

    lq, lp = question_in.shape[1], passage_in.shape[1]
    rows = 2 * own_rows

    def chunked(values, sixteenths):
        out, row = [], 0
        for part in sixteenths:
            step = values.shape[0] * part // 16
            out.append(values[row : row + step])
            row += step
        return out

    def hand(values):
        return [places.swap_tower(x) for x in values]

    per_q = rows // lq
    every = lp // lq
    per_p = rows // lp
    nq, np_ = question_in.shape[0], passage_in.shape[0]
    shift = 2 * places.half
    low_pa = pa % shift
    g1, g2, g3 = Gather(first), Gather(second), Gather(third)
    my_tokens, send_tokens = sides(rows_q, rows_p)
    tokens_out = chunked(send_tokens, (5, 6, 5))
    g1.mid()
    g1.send, tokens_out, question_cot, passage_cot = tie(
        g1.send, tokens_out, question_cot, passage_cot
    )
    g1.along_z()
    tokens_in = hand(tokens_out[:1])
    my_cot, send_cot = sides(question_cot.reshape(-1, D), passage_cot.reshape(-1, D))
    g1.send, g2.send, tokens_in, my_cot, send_cot = tie(
        g1.send, g2.send, tokens_in, my_cot, send_cot
    )
    g1.pb_first()
    g2.mid()
    g1.stack, g2.send, tokens_out = tie(g1.stack, g2.send, tokens_out)
    g1.send = g1.stack
    g1.pb_last()
    g1.core_stack()
    g2.along_z()
    tokens_in = tokens_in + hand(tokens_out[1:2])
    g1.held, g2.send, tokens_in, tokens_out, question_len, passage_len, positive = tie(
        g1.held, g2.send, tokens_in, tokens_out, question_len, passage_len, positive
    )
    g1.core_held()
    g2.pb_first()
    tokens_in = tokens_in + hand(tokens_out[2:])
    full_j, full_o, full_small = g1.whole([(0, 3 * D), (3 * D, D), (4 * D, 128)])
    full_j, full_o, full_small, g2.stack, g3.send, tokens_in = tie(
        full_j, full_o, full_small, g2.stack, g3.send, tokens_in
    )
    g2.send = g2.stack
    g2.pb_last()
    g2.core_stack()
    g3.mid()
    wj = full_j.reshape(D, 3 * D)
    wo = full_o.reshape(D, D)
    small = full_small.reshape(D, 128).astype(F32)
    vec = small[:, :8].T
    bias_e = small[:, 8:12].reshape(1, FF)
    bias_j = jnp.concatenate([vec[0], jnp.zeros((D,), F32), vec[1]])
    tokens = join([my_tokens] + tokens_in)
    qkv = (dot(tokens, wj) + bias_j).astype(BF16)

    cot_out = chunked(send_cot, (3, 3, 3, 4, 3))
    by_pa = positive.reshape(places.pa_n, nq)
    pair = [lax.dynamic_index_in_dim(by_pa, low_pa + k, 0, keepdims=False) for k in (0, shift)]
    pair = jnp.concatenate(pair)[None]
    wanted_rows = jnp.concatenate([pair // 16, pair % 16], axis=0).astype(BF16)
    wanted_rows = jnp.pad(wanted_rows, ((0, 0), (0, D - per_q)))
    valid_q = (jnp.arange(lq, dtype=jnp.int32)[None, :] < question_len[:, None]).astype(jnp.int32)
    valid_p = (jnp.arange(lp, dtype=jnp.int32)[None, :] < passage_len[:, None]).astype(jnp.int32)
    my_valid, send_valid = sides(valid_q.reshape(-1), valid_p.reshape(-1))
    valid = jnp.concatenate([my_valid, places.swap_tower(send_valid)])
    row_ids = jnp.arange(rows, dtype=jnp.int32)
    seq = jnp.where(is_q, row_ids // lq, row_ids // lp)
    qid = seq.reshape(rows, 1)
    kid = jnp.where(valid > 0, seq, -1).reshape(rows // BLOCK, 1, BLOCK)
    row_mask = valid.reshape(rows, 1).astype(F32)

    blocks = rows // BLOCK
    later = blocks // 2
    qkv, g3.send, cot_out = tie(qkv, g3.send, cot_out)
    g3.along_z()
    cot_in = hand(cot_out[:1])
    spread = attention(qkv, qid, kid, 0, later)
    spread, g2.held, g3.send, cot_in, cot_out = tie(spread, g2.held, g3.send, cot_in, cot_out)
    g2.core_held()
    g3.pb_first()
    cot_in = cot_in + hand(cot_out[1:2])
    context, probs = attention(qkv, qid, kid, later, blocks - later, tuple(spread))
    context, g2.parts, g3.stack, cot_in, cot_out = tie(context, g2.parts, g3.stack, cot_in, cot_out)
    g3.send = g3.stack
    g3.pb_last()
    g3.core_stack()
    cot_in = cot_in + hand(cot_out[2:3])
    (full_e,) = g2.whole([(0, FF)])
    we = full_e.reshape(D, FF)
    attended = dot(context, wo) + vec[2]
    norm_one, inverse_one = normalized(tokens.astype(F32) + attended)
    mid = norm_one * vec[3] + vec[4]
    mid_low = mid.astype(BF16)
    mid_low, we, cot_in, cot_out = tie(mid_low, we, cot_in, cot_out)
    cot_in = cot_in + hand(cot_out[3:4])
    gelu = expand(mid_low, we, bias_e, 0, 1)
    gelu, g3.held, g3.other, g3.stack, cot_in, cot_out = tie(
        gelu, g3.held, g3.other, g3.stack, cot_in, cot_out
    )
    g3.core_held()
    cot_in = cot_in + hand(cot_out[4:])
    active, slope = expand(mid_low, we, bias_e, 1, 1, tuple(gelu))
    active, g3.parts, cot_in = tie(active, g3.parts, cot_in)
    (full_r,) = g3.whole([(0, D)])
    wr = full_r.reshape(FF, D)
    norm_two, inverse_two = normalized(mid + dot(active, wr) + vec[5])
    out = ((norm_two * vec[6] + vec[7]) * row_mask).astype(BF16)

    firsts = out.reshape(per_q, lq, D)[:, 0, :]
    others = places.swap_tower(firsts)
    cls_q = jnp.where(is_q, firsts, others)
    cls_p = jnp.where(is_q, others, firsts)[::every]
    pad = (-(per_q + per_p + 2)) % 8
    stack = jnp.concatenate([cls_q, cls_p, wanted_rows, jnp.zeros((pad, D), BF16)], axis=0)[None]
    pair_masks = [0]
    for bit in bits_of(places.half):
        got = lax.ppermute(stack, "pa", [(i, i ^ (2 * bit)) for i in range(places.pa_n)])
        stack = jnp.concatenate([stack, got], axis=0)
        pair_masks = pair_masks + [m ^ (2 * bit) for m in pair_masks]
    for bit in bits_of(places.pb_n):
        got = lax.ppermute(stack, "pb", [(i, i ^ bit) for i in range(places.pb_n)])
        stack = jnp.concatenate([stack, got], axis=0)
        pair_masks = pair_masks + [m ^ (bit * places.pa_n) for m in pair_masks]
    stack = jnp.concatenate([stack, places.swap_core(stack)], axis=0)
    pair_masks = pair_masks + [m ^ 1 for m in pair_masks]
    groups = len(pair_masks)
    me = pb * places.pa_n + low_pa
    place = jnp.array(pair_masks, jnp.int32) ^ me
    dev_p = jnp.stack([place + shift, place], axis=1)
    p_ids = (dev_p[:, :, None] * np_ + jnp.arange(np_, dtype=jnp.int32)).reshape(-1)
    digits = stack[:, per_q + per_p : per_q + per_p + 2, :per_q].astype(jnp.int32)
    wanted = (digits[:, 0] * 16 + digits[:, 1]).reshape(-1)

    all_q = stack[:, :per_q].reshape(groups * per_q, D)
    all_p = stack[:, per_q : per_q + per_p].reshape(groups * per_p, D)
    similarity = dot(all_q, all_p, ((1,), (1,))) * score_scale
    hot = (wanted[:, None] == p_ids[None, :]).astype(F32)
    top = jnp.max(similarity, axis=1, keepdims=True)
    grown = jnp.exp(similarity - top)
    total = jnp.sum(grown, axis=1, keepdims=True)
    own_sim = similarity[:per_q]
    loss = top[:per_q, 0] + jnp.log(total[:per_q, 0]) - jnp.sum(own_sim * hot[:per_q], axis=1)
    question_loss = lax.dynamic_slice_in_dim(loss, tower * nq, nq)
    d_sim = (loss_weight * (grown / total - hot)).astype(BF16)
    d_q = dot(d_sim[:per_q], all_p) * score_scale
    d_p = dot(d_sim[:, :per_p], all_q, ((0,), (0,))) * score_scale
    d_p = jnp.concatenate(
        [d_p.reshape(per_p, 1, D), jnp.zeros((per_p, every - 1, D), F32)], axis=1
    ).reshape(per_q, D)
    d_slot = jnp.where(is_q, d_q, d_p)

    d_second, d_reduced, sums_second = second_back(
        join([my_cot] + cot_in), d_slot, row_mask, norm_two, inverse_two, vec[6][None, :]
    )
    even = share % 8 == 0

    def gradient(left, right, **more):
        if left.shape[1] > D:
            return tall_grad(left, right, slots, places.nz)
        return weight_grad(left, right, slots, D, **more)

    def plain(left, right, extra=None):
        return grad_plain(left, right, table, extra)

    class Scatter:
        def __init__(self, mine, theirs):
            self.parts, self.theirs = [mine], theirs
            self.count = mine.shape[0]

        def cores(self):
            self.parts = self.parts + [places.swap_core(self.theirs)]

        def total(self, start, stop):
            out = self.parts[0][start:stop].astype(F32)
            for part in self.parts[1:]:
                out = out + part[start:stop].astype(F32)
            return out

        def move(self, step):
            half = self.count // 2
            send = self.total(half, self.count).astype(BF16)
            self.parts = self.parts + [places.swap(send, step)]
            self.count = half

        def pb_first(self):
            self.move(places.steps - 1)

        def pb_rest(self):
            for step in range(places.steps - 2, z_steps - 1, -1):
                self.move(step)

        def along_z(self):
            for step in range(z_steps - 1, 0, -1):
                self.move(step)

        def mid(self):
            got = places.swap(self.total(1, 2).astype(BF16), 0).astype(F32)
            keep = self.total(0, 1)
            self.out = jnp.concatenate(
                [jnp.where(is_q, keep, got), jnp.where(is_q, got, keep)], axis=0
            )

    send_out = chunked(out[own_rows:], (4, 4, 4, 4))
    d_reduced, send_out = tie(d_reduced, send_out)
    got_out = hand(send_out[:1])
    sr = Scatter(*(gradient if even else plain)(active, d_reduced))
    sr.parts, sr.theirs, d_reduced, got_out, send_out = tie(
        sr.parts, sr.theirs, d_reduced, got_out, send_out
    )
    sr.cores()
    got_out = got_out + hand(send_out[1:2])
    d_expanded, g_bias_expand = hidden_grad(d_reduced, wr, slope)
    sr.parts, d_expanded, got_out, send_out = tie(sr.parts, d_expanded, got_out, send_out)
    sr.pb_first()
    got_out = got_out + hand(send_out[2:3])
    if even:
        partial = gradient(mid_low, d_expanded, room=D)
    else:
        partial = plain(mid_low, d_expanded)
    partial, d_expanded, got_out, send_out = tie(partial, d_expanded, got_out, send_out)
    got_out = got_out + hand(send_out[3:])
    d_first, d_attended, sums_first = first_back(
        d_expanded, we, d_second, norm_one, inverse_one, vec[3][None, :]
    )
    sr.parts, partial, d_attended, got_out = tie(sr.parts, partial, d_attended, got_out)
    sr.pb_rest()
    if even:
        partial = gradient(context, d_attended, into=tuple(partial))
    else:
        also = plain(context, d_attended)
        partial = [jnp.concatenate(x, axis=2) for x in zip(partial, also)]
    se = Scatter(*partial)
    se.parts, se.theirs, d_attended = tie(se.parts, se.theirs, d_attended)
    se.cores()
    d_context = dot(d_attended, wo, ((1,), (1,))).astype(BF16)
    d_joined, sums_one = attention_back(qkv, probs, d_context, later, blocks - later)
    sr.parts, se.parts, d_joined = tie(sr.parts, se.parts, d_joined)
    se.pb_first()
    sr.along_z()
    send_grad = (d_first[own_rows:] + dot(d_joined[own_rows:], wj, ((1,), (1,)))).astype(BF16)
    d_joined, send_grad = tie(d_joined, chunked(send_grad, (4, 4, 2, 6)))
    got_grad = hand(send_grad[:1])
    d_joined, sums_two = attention_back(qkv, probs, d_context, 0, later, d_joined)
    sr.parts, d_joined, got_grad, send_grad = tie(sr.parts, d_joined, got_grad, send_grad)
    sr.mid()
    got_grad = got_grad + hand(send_grad[1:2])
    g_joined_bias = (sums_one + sums_two)[0]
    g_vec = jnp.concatenate(
        [
            g_joined_bias[None, :D],
            g_joined_bias[None, 2 * D :],
            sums_first[2:3],
            sums_first[:2],
            sums_second[2:3],
            sums_second[:2],
        ]
    )
    g_small = jnp.concatenate(
        [g_vec.T, g_bias_expand.reshape(D, 4), jnp.zeros((D, 116), F32)], axis=1
    )
    sj = Scatter(*(gradient if even else plain)(tokens, d_joined, extra=g_small))
    se.parts, sj.parts, sj.theirs, d_joined, sr.out, got_grad, send_grad = tie(
        se.parts, sj.parts, sj.theirs, d_joined, sr.out, got_grad, send_grad
    )
    sj.cores()
    se.pb_rest()
    got_grad = got_grad + hand(send_grad[2:3])
    own_grad = d_first[:own_rows] + dot(d_joined[:own_rows], wj, ((1,), (1,)))
    sj.parts, own_grad, got_grad, send_grad = tie(sj.parts, own_grad, got_grad, send_grad)
    sj.pb_first()
    got_grad = got_grad + hand(send_grad[3:])
    out_q, out_p = deal(tower.reshape(1), out, got_out)
    sj.parts, se.parts, got_grad = tie(sj.parts, se.parts, got_grad)
    se.along_z()
    sj.pb_rest()
    grad_q, grad_p = deal(tower.reshape(1), own_grad, got_grad)
    sj.parts, se.parts, grad_q, grad_p = tie(sj.parts, se.parts, grad_q, grad_p)
    sj.along_z()
    se.mid()
    sj.parts, se.out = tie(sj.parts, se.out)
    sj.mid()
    grad_joined = sj.out[:, :, : 3 * D]
    grad_expand, grad_output, grad_reduce = se.out[:, :, :FF], se.out[:, :, FF:], sr.out
    extra = sj.out[:, :, 3 * D :]
    grad_vectors = extra[:, :, :8].transpose(0, 2, 1)
    grad_b_expand = extra[:, :, 8:12].reshape(2, 4 * share)

    return (
        out_q.reshape(question_in.shape),
        out_p.reshape(passage_in.shape),
        question_loss,
        grad_q.reshape(question_in.shape),
        grad_p.reshape(passage_in.shape),
        grad_joined,
        grad_output,
        grad_expand,
        grad_reduce,
        grad_vectors,
        grad_b_expand,
    )


def solution(mesh):
    in_specs = (
        P(("pb", "pa"), None, None),
        P(("pb", "pa"), None, None),
        P(("pb", "pa")),
        P(("pb", "pa")),
        P("pb"),
        P(("pb", "pa"), None, None),
        P(("pb", "pa"), None, None),
        P(None, ("pb", "pa"), None),
        P(None, ("pb", "pa"), None),
        P(None, ("pb", "pa"), None),
        P(None, ("pb", "pa"), None),
        P(None, None, ("pb", "pa")),
        P(None, ("pb", "pa")),
    )
    out_specs = (
        P(("pb", "pa"), None, None),
        P(("pb", "pa"), None, None),
        P(("pb", "pa")),
        P(("pb", "pa"), None, None),
        P(("pb", "pa"), None, None),
        P(None, ("pb", "pa"), None),
        P(None, ("pb", "pa"), None),
        P(None, ("pb", "pa"), None),
        P(None, ("pb", "pa"), None),
        P(None, None, ("pb", "pa")),
        P(None, ("pb", "pa")),
    )
    return jax.shard_map(
        functools.partial(per_device, Places(mesh)),
        mesh=mesh,
        in_specs=in_specs,
        out_specs=out_specs,
        check_vma=False,
    )
```

```python
import functools

import jax
import jax.numpy as jnp
from jax import lax
from jax.experimental import pallas as pl
from jax.experimental.pallas import tpu as pltpu
from jax.sharding import PartitionSpec as P

D = 768
HEADS = 12
HDIM = 64
FF = 3072
AXES = ("pb", "pa")
BLOCK = 256

norm_eps = 1e-06
masked_score = -1000000000.0
score_scale = 0.0625
loss_weight = 16.0
head_scale = HDIM ** (-0.5)
F32 = jnp.float32
BF16 = jnp.bfloat16
VMEM_LIMIT = 56 * 1024 * 1024


def bits_of(count):
    return [1 << shift for shift in range(count.bit_length() - 1)]


class Places:
    def __init__(self, mesh):
        self.pb_n = mesh.shape["pb"]
        self.pa_n = mesh.shape["pa"]
        self.nz = self.pa_n // 2
        self.half = self.nz // 2
        self.chips = self.pb_n * self.nz
        pb_bits = bits_of(self.pb_n)
        turn = len(pb_bits) // 2
        low_z = [("z", bit) for bit in bits_of(self.half)]
        first = [("pb", bit) for bit in pb_bits]
        second = first[turn:] + first[:turn]
        self.orders = ([("z", self.half)] + low_z + first, [("z", self.half)] + low_z + second)
        self.steps = len(self.orders[0])

    def chip_mask(self, move):
        axis, bit = move
        return bit * self.nz if axis == "pb" else bit

    def stack_masks(self, core):
        masks = [0]
        for move in self.orders[core]:
            masks = masks + [mask ^ self.chip_mask(move) for mask in masks]
        return masks

    def pairs(self, step):
        out = []
        for pb in range(self.pb_n):
            for pa in range(self.pa_n):
                axis, bit = self.orders[pa % 2][step]
                to_pb, to_pa = (pb ^ bit, pa) if axis == "pb" else (pb, pa ^ (2 * bit))
                out.append((pb * self.pa_n + pa, to_pb * self.pa_n + to_pa))
        return out

    def swap(self, values, step):
        return lax.ppermute(values, AXES, self.pairs(step))

    def swap_core(self, values):
        return lax.ppermute(values, "pa", [(i, i ^ 1) for i in range(self.pa_n)])

    def swap_tower(self, values):
        return lax.ppermute(values, "pa", [(i, i ^ (2 * self.half)) for i in range(self.pa_n)])


def dot(left, right, dims=((1,), (0,))):
    return lax.dot_general(left, right, (dims, ((), ())), preferred_element_type=F32)


def tie(*values):
    return lax.optimization_barrier(values)


def assemble_kernel(segments, idx_ref, *refs):
    count = len(segments)
    sources, outs = refs[:4], refs[4 : 4 + count]
    buffer, in_sem, out_sem = refs[4 + count :]
    core = idx_ref[2, 0]
    part = sources[0].shape[0]
    loads = [
        pltpu.make_async_copy(source, buffer.at[pl.ds(k * part, part)], in_sem.at[k])
        for k, source in enumerate(sources)
    ]
    for load in loads:
        load.start()
    stores = []
    for k in range(4):
        loads[k].wait()
        half = core if k < 2 else 1 - core
        for j in range(part):
            slot = k * part + j
            place = idx_ref[k // 2, (k % 2) * part + j]
            for s, (start, width) in enumerate(segments):
                store = pltpu.make_async_copy(
                    buffer.at[slot, :, pl.ds(start, width)],
                    outs[s].at[place, half],
                    out_sem.at[s, slot],
                )
                store.start()
                stores.append(store)
    for store in stores:
        store.wait()


def assemble(parts, table, segments):
    part, rows, width = parts[0].shape
    chips = 2 * part
    shapes = [jax.ShapeDtypeStruct((chips, 2, rows, w), BF16) for _, w in segments]
    return pl.pallas_call(
        functools.partial(assemble_kernel, segments),
        out_shape=shapes,
        in_specs=[pl.BlockSpec(memory_space=pltpu.SMEM)] + [pl.BlockSpec(memory_space=pl.ANY)] * 4,
        out_specs=[pl.BlockSpec(memory_space=pl.ANY)] * len(segments),
        scratch_shapes=[
            pltpu.VMEM((2 * chips, rows, width), BF16),
            pltpu.SemaphoreType.DMA((4,)),
            pltpu.SemaphoreType.DMA((len(segments), 2 * chips)),
        ],
        compiler_params=pltpu.CompilerParams(vmem_limit_bytes=VMEM_LIMIT),
        cost_estimate=pl.CostEstimate(
            flops=0, bytes_accessed=4 * 2 * chips * rows * width, transcendentals=0
        ),
        name="assemble",
    )(table, *parts)


def assemble_plain(parts, table, segments):
    own = jnp.take(jnp.concatenate(parts[:2], axis=0), jnp.argsort(table[0]), axis=0)
    other = jnp.take(jnp.concatenate(parts[2:], axis=0), jnp.argsort(table[1]), axis=0)
    first = table[2, 0] == 0
    both = jnp.stack([jnp.where(first, own, other), jnp.where(first, other, own)], axis=1)
    return [both[..., start : start + w] for start, w in segments]


def split_slabs(acc, core, chips, mine_ref, theirs_ref, cols, within):
    rows = acc.shape[0] // (2 * chips)
    for s in range(chips):
        low = acc[2 * s * rows : (2 * s + 1) * rows]
        high = acc[(2 * s + 1) * rows : (2 * s + 2) * rows]
        mine, theirs = within(s)
        mine_ref[mine, :, cols] = jnp.where(core == 0, low, high).astype(BF16)
        theirs_ref[theirs, :, cols] = jnp.where(core == 0, high, low).astype(BF16)


def weight_grad_kernel(chips, extra, table_ref, left_ref, right_ref, *refs):
    mine_ref, theirs_ref = refs[-2:]
    core = table_ref[2, 0]
    acc = dot(left_ref[...], right_ref[...], ((0,), (0,)))
    width = acc.shape[1]

    def within(s):
        return table_ref[0, s], table_ref[1, s]

    if not extra:
        split_slabs(acc, core, chips, mine_ref, theirs_ref, slice(None), within)
        return
    step = pl.program_id(0)
    cols = pl.ds(pl.multiple_of(step * width, 128), width)
    split_slabs(acc, core, chips, mine_ref, theirs_ref, cols, within)

    @pl.when(step == 0)
    def _():
        tail = pl.ds(mine_ref.shape[2] - 128, 128)
        split_slabs(refs[0][...], core, chips, mine_ref, theirs_ref, tail, within)


def weight_grad(left, right, slots, tile, extra=None, room=0, into=()):
    rows, height = left.shape
    width = right.shape[1]
    chips = slots.shape[1]
    slab = height // (2 * chips)
    total = width + (room if extra is None else extra.shape[1])
    first = 0
    if into:
        total = into[0].shape[2]
        first = (total - width) // tile
    block = (chips, slab, total if extra is not None else tile)
    place = (lambda j, t: (0, 0, 0)) if extra is not None else (lambda j, t: (0, 0, j + first))
    return pl.pallas_call(
        functools.partial(weight_grad_kernel, chips, extra is not None),
        grid_spec=pltpu.PrefetchScalarGridSpec(
            num_scalar_prefetch=1,
            grid=(width // tile,),
            in_specs=[
                pl.BlockSpec((rows, height), lambda j, t: (0, 0)),
                pl.BlockSpec((rows, tile), lambda j, t: (0, j)),
            ]
            + ([] if extra is None else [pl.BlockSpec((height, 128), lambda j, t: (0, 0))])
            + [pl.BlockSpec(memory_space=pl.ANY)] * len(into),
            out_specs=[pl.BlockSpec(block, place)] * 2,
        ),
        out_shape=[jax.ShapeDtypeStruct((chips, slab, total), BF16)] * 2,
        input_output_aliases={3: 0, 4: 1} if into else {},
        compiler_params=pltpu.CompilerParams(vmem_limit_bytes=VMEM_LIMIT),
        cost_estimate=pl.CostEstimate(
            flops=2 * rows * height * width,
            bytes_accessed=2 * (rows * (height + width) + height * width),
            transcendentals=0,
        ),
        name="weight_grad",
    )(slots, left, right, *([] if extra is None else [extra]), *into)


def tall_grad_kernel(chips, table_ref, left_ref, right_ref, mine_ref, theirs_ref):
    core = table_ref[2, 0]
    acc = dot(left_ref[...], right_ref[...], ((0,), (0,)))
    base = pl.program_id(0) * chips

    def within(s):
        return table_ref[0, base + s] % chips, table_ref[1, base + s] % chips

    split_slabs(acc, core, chips, mine_ref, theirs_ref, slice(None), within)


def tall_grad(left, right, slots, column):
    rows, height = left.shape
    width = right.shape[1]
    chips = slots.shape[1]
    slab = height // (2 * chips)
    tile = height // chips * column
    return pl.pallas_call(
        functools.partial(tall_grad_kernel, column),
        grid_spec=pltpu.PrefetchScalarGridSpec(
            num_scalar_prefetch=1,
            grid=(chips // column,),
            in_specs=[
                pl.BlockSpec((rows, tile), lambda i, t: (0, i)),
                pl.BlockSpec((rows, width), lambda i, t: (0, 0)),
            ],
            out_specs=[
                pl.BlockSpec((column, slab, width), lambda i, t: (t[0, i * column] // column, 0, 0)),
                pl.BlockSpec((column, slab, width), lambda i, t: (t[1, i * column] // column, 0, 0)),
            ],
        ),
        out_shape=[jax.ShapeDtypeStruct((chips, slab, width), BF16)] * 2,
        compiler_params=pltpu.CompilerParams(vmem_limit_bytes=VMEM_LIMIT),
        cost_estimate=pl.CostEstimate(
            flops=2 * rows * height * width,
            bytes_accessed=2 * (rows * (height + width) + height * width),
            transcendentals=0,
        ),
        name="tall_grad",
    )(slots, left, right)


def grad_plain(left, right, table, extra=None):
    full = dot(left, right, ((0,), (0,)))
    if extra is not None:
        full = jnp.concatenate([full, extra], axis=1)
    chips = table.shape[1]
    full = full.astype(BF16).reshape(chips, 2, full.shape[0] // (2 * chips), full.shape[1])
    core = table[2, 0]
    mine = lax.dynamic_index_in_dim(full, core, 1, keepdims=False)
    theirs = lax.dynamic_index_in_dim(full, 1 - core, 1, keepdims=False)
    return jnp.take(mine, table[0], axis=0), jnp.take(theirs, table[1], axis=0)


def hidden_grad_kernel(grad_ref, w_ref, slope_ref, out_ref, sum_ref):
    grad = dot(grad_ref[...], w_ref[...], ((1,), (1,))) * slope_ref[...].astype(F32)
    low = grad.astype(BF16)
    out_ref[...] = low
    sum_ref[...] = jnp.sum(low.astype(F32), axis=0, keepdims=True)


def hidden_grad(grad, w_reduce, slope):
    rows, tile = grad.shape[0], 512
    return pl.pallas_call(
        hidden_grad_kernel,
        grid=(FF // tile,),
        in_specs=[
            pl.BlockSpec((rows, D), lambda j: (0, 0)),
            pl.BlockSpec((tile, D), lambda j: (j, 0)),
            pl.BlockSpec((rows, tile), lambda j: (0, j)),
        ],
        out_specs=[
            pl.BlockSpec((rows, tile), lambda j: (0, j)),
            pl.BlockSpec((1, tile), lambda j: (0, j)),
        ],
        out_shape=[
            jax.ShapeDtypeStruct((rows, FF), BF16),
            jax.ShapeDtypeStruct((1, FF), F32),
        ],
        compiler_params=pltpu.CompilerParams(vmem_limit_bytes=VMEM_LIMIT),
        cost_estimate=pl.CostEstimate(
            flops=2 * rows * D * FF,
            bytes_accessed=2 * (rows * D + D * FF + 2 * rows * FF),
            transcendentals=0,
        ),
        name="hidden_grad",
    )(grad, w_reduce, slope)


def project_kernel(tokens_ref, w_ref, b_ref, *refs):
    refs[-1][...] = (dot(tokens_ref[...], w_ref[...]) + b_ref[...]).astype(BF16)


def project(tokens, weight, bias, rows, start, into=()):
    width = weight.shape[1]
    count = tokens.shape[0] // BLOCK - (start if into else 0)
    first = start if into else 0
    return pl.pallas_call(
        project_kernel,
        grid=(count,),
        in_specs=[
            pl.BlockSpec((BLOCK, D), lambda i: (i + first, 0)),
            pl.BlockSpec((D, width), lambda i: (0, 0)),
            pl.BlockSpec((1, width), lambda i: (0, 0)),
        ]
        + [pl.BlockSpec(memory_space=pl.ANY)] * len(into),
        out_specs=pl.BlockSpec((BLOCK, width), lambda i: (i + start, 0)),
        out_shape=jax.ShapeDtypeStruct((rows, width), BF16),
        input_output_aliases={3: 0} if into else {},
        compiler_params=pltpu.CompilerParams(vmem_limit_bytes=VMEM_LIMIT),
        cost_estimate=pl.CostEstimate(
            flops=2 * count * BLOCK * D * width,
            bytes_accessed=2 * (count * BLOCK * (D + width) + D * width),
            transcendentals=0,
        ),
        name="project",
    )(tokens, weight, bias, *into)


def attention_kernel(qkv_ref, qid_ref, kid_ref, context_ref, probs_ref):
    allowed = qid_ref[...] == kid_ref[0]
    lane = lax.broadcasted_iota(jnp.int32, (BLOCK, 128), 1)
    zero = jnp.zeros((BLOCK, 128), BF16)
    for pair in range(HEADS // 2):
        queries = qkv_ref[:, pair * 128 : pair * 128 + 128]
        keys = qkv_ref[:, D + pair * 128 : D + pair * 128 + 128]
        values = qkv_ref[:, 2 * D + pair * 128 : 2 * D + pair * 128 + 128]
        outs = []
        for side in range(2):
            mine = (lane < HDIM) if side == 0 else (lane >= HDIM)
            scores = dot(queries, jnp.where(mine, keys, zero), ((1,), (1,))) * head_scale
            scores = jnp.where(allowed, scores, masked_score)
            top = jnp.max(scores, axis=1, keepdims=True)
            grown = jnp.exp(scores - top)
            total = jnp.sum(grown, axis=1, keepdims=True)
            probs = (grown * (1.0 / total)).astype(BF16)
            probs_ref[0, 2 * pair + side] = probs
            outs.append(dot(probs, values))
        context_ref[:, pair * 128 : pair * 128 + 128] = jnp.where(
            lane < HDIM, outs[0], outs[1]
        ).astype(BF16)


def attention_more_kernel(qkv_ref, qid_ref, kid_ref, _, __, context_ref, probs_ref):
    attention_kernel(qkv_ref, qid_ref, kid_ref, context_ref, probs_ref)


def attention(qkv, qid, kid, start, count, into=()):
    rows = qkv.shape[0]
    blocks = rows // BLOCK
    return pl.pallas_call(
        attention_more_kernel if into else attention_kernel,
        grid=(count,),
        in_specs=[
            pl.BlockSpec((BLOCK, 3 * D), lambda i: (i + start, 0)),
            pl.BlockSpec((BLOCK, 1), lambda i: (i + start, 0)),
            pl.BlockSpec((1, 1, BLOCK), lambda i: (i + start, 0, 0)),
        ]
        + [pl.BlockSpec(memory_space=pl.ANY)] * len(into),
        out_specs=[
            pl.BlockSpec((BLOCK, D), lambda i: (i + start, 0)),
            pl.BlockSpec((1, HEADS, BLOCK, BLOCK), lambda i: (i + start, 0, 0, 0)),
        ],
        input_output_aliases={3: 0, 4: 1} if into else {},
        out_shape=[
            jax.ShapeDtypeStruct((rows, D), BF16),
            jax.ShapeDtypeStruct((blocks, HEADS, BLOCK, BLOCK), BF16),
        ],
        compiler_params=pltpu.CompilerParams(vmem_limit_bytes=VMEM_LIMIT),
        cost_estimate=pl.CostEstimate(
            flops=4 * count * BLOCK * BLOCK * D * 2,
            bytes_accessed=count * BLOCK * (4 * D + HEADS * BLOCK) * 2,
            transcendentals=count * BLOCK * HEADS * BLOCK,
        ),
        name="attention",
    )(qkv, qid, kid, *into)


def attention_back_kernel(qkv_ref, probs_ref, grad_ref, out_ref, sum_ref):
    lane = lax.broadcasted_iota(jnp.int32, (BLOCK, 128), 1)
    zero = jnp.zeros((BLOCK, 128), BF16)
    for pair in range(HEADS // 2):
        cols = slice(pair * 128, pair * 128 + 128)
        queries = qkv_ref[:, pair * 128 : pair * 128 + 128]
        keys = qkv_ref[:, D + pair * 128 : D + pair * 128 + 128]
        values = qkv_ref[:, 2 * D + pair * 128 : 2 * D + pair * 128 + 128]
        grad = grad_ref[:, cols]
        d_q, d_k, d_v = [], [], []
        for side in range(2):
            mine = (lane < HDIM) if side == 0 else (lane >= HDIM)
            low = probs_ref[0, 2 * pair + side]
            d_probs = dot(jnp.where(mine, grad, zero), values, ((1,), (1,)))
            d_v.append(dot(low, grad, ((0,), (0,))))
            probs = low.astype(F32)
            row_dot = jnp.sum(d_probs * probs, axis=1, keepdims=True)
            d_scores = (probs * (d_probs - row_dot)).astype(BF16)
            d_q.append(dot(d_scores, keys))
            d_k.append(dot(d_scores, queries, ((0,), (0,))))
        first = lane < HDIM
        out_ref[:, pair * 128 : pair * 128 + 128] = (
            jnp.where(first, d_q[0], d_q[1]) * head_scale
        ).astype(BF16)
        out_ref[:, D + pair * 128 : D + pair * 128 + 128] = (
            jnp.where(first, d_k[0], d_k[1]) * head_scale
        ).astype(BF16)
        out_ref[:, 2 * D + pair * 128 : 2 * D + pair * 128 + 128] = jnp.where(
            first, d_v[0], d_v[1]
        ).astype(BF16)
    sums = jnp.sum(out_ref[...].astype(F32), axis=0, keepdims=True)

    @pl.when(pl.program_id(0) == 0)
    def _():
        sum_ref[...] = sums

    @pl.when(pl.program_id(0) > 0)
    def _():
        sum_ref[...] += sums


def attention_back_more_kernel(qkv_ref, probs_ref, grad_ref, _, out_ref, sum_ref):
    attention_back_kernel(qkv_ref, probs_ref, grad_ref, out_ref, sum_ref)


def attention_back(qkv, probs, grad_context, start, count, into=None):
    rows = qkv.shape[0]
    more = into is not None
    return pl.pallas_call(
        attention_back_more_kernel if more else attention_back_kernel,
        grid=(count,),
        in_specs=[
            pl.BlockSpec((BLOCK, 3 * D), lambda i: (i + start, 0)),
            pl.BlockSpec((1, HEADS, BLOCK, BLOCK), lambda i: (i + start, 0, 0, 0)),
            pl.BlockSpec((BLOCK, D), lambda i: (i + start, 0)),
        ]
        + ([pl.BlockSpec(memory_space=pl.ANY)] if more else []),
        out_specs=[
            pl.BlockSpec((BLOCK, 3 * D), lambda i: (i + start, 0)),
            pl.BlockSpec((1, 3 * D), lambda i: (0, 0)),
        ],
        out_shape=[
            jax.ShapeDtypeStruct((rows, 3 * D), BF16),
            jax.ShapeDtypeStruct((1, 3 * D), F32),
        ],
        input_output_aliases={3: 0} if more else {},
        compiler_params=pltpu.CompilerParams(vmem_limit_bytes=VMEM_LIMIT),
        cost_estimate=pl.CostEstimate(
            flops=8 * count * BLOCK * BLOCK * D * 2,
            bytes_accessed=count * BLOCK * (7 * D + HEADS * BLOCK) * 2,
            transcendentals=0,
        ),
        name="attention_back",
    )(qkv, probs, grad_context, *([into] if more else []))


def join_kernel(*refs):
    row = 0
    for piece in refs[:-1]:
        rows = piece.shape[0]
        refs[-1][row : row + rows, :] = piece[...]
        row += rows


def join(pieces):
    rows, width = sum(x.shape[0] for x in pieces), pieces[0].shape[1]
    return pl.pallas_call(
        join_kernel,
        grid=(1,),
        in_specs=[pl.BlockSpec(x.shape, lambda i: (0, 0)) for x in pieces],
        out_specs=pl.BlockSpec((rows, width), lambda i: (0, 0)),
        out_shape=jax.ShapeDtypeStruct((rows, width), pieces[0].dtype),
        compiler_params=pltpu.CompilerParams(vmem_limit_bytes=VMEM_LIMIT),
        cost_estimate=pl.CostEstimate(
            flops=0, bytes_accessed=4 * rows * width, transcendentals=0
        ),
        name="join",
    )(*pieces)


def deal_kernel(tower_ref, own_ref, *refs):
    pieces, (q_ref, p_ref) = refs[:-2], refs[-2:]

    def give(own_out, other_out):
        own_out[...] = own_ref[...]
        row = 0
        for piece in pieces:
            rows = piece.shape[0]
            other_out[row : row + rows, :] = piece[...].astype(other_out.dtype)
            row += rows

    @pl.when(tower_ref[0] == 0)
    def _():
        give(q_ref, p_ref)

    @pl.when(tower_ref[0] != 0)
    def _():
        give(p_ref, q_ref)


def deal(tower, own, pieces):
    rows, width = sum(x.shape[0] for x in pieces), own.shape[1]
    shape = jax.ShapeDtypeStruct((rows, width), own.dtype)
    return pl.pallas_call(
        deal_kernel,
        grid=(1,),
        in_specs=[
            pl.BlockSpec(memory_space=pltpu.SMEM),
            pl.BlockSpec((rows, width), lambda i: (0, 0)),
        ]
        + [pl.BlockSpec(x.shape, lambda i: (0, 0)) for x in pieces],
        out_specs=[pl.BlockSpec((rows, width), lambda i: (0, 0))] * 2,
        out_shape=[shape] * 2,
        compiler_params=pltpu.CompilerParams(vmem_limit_bytes=VMEM_LIMIT),
        cost_estimate=pl.CostEstimate(
            flops=0, bytes_accessed=12 * rows * width, transcendentals=0
        ),
        name="deal",
    )(tower, own, *pieces)


def add_sums(sum_ref, values):
    total = jnp.concatenate(
        [jnp.sum(x, axis=0, keepdims=True) for x in values]
        + [jnp.zeros((8 - len(values), values[0].shape[1]), F32)],
        axis=0,
    )

    @pl.when(pl.program_id(0) == 0)
    def _():
        sum_ref[...] = total

    @pl.when(pl.program_id(0) > 0)
    def _():
        sum_ref[...] += total


def second_back_kernel(
    cot_ref, slot_ref, mask_ref, norm_ref, inverse_ref, gain_ref, grad_ref, low_ref, sum_ref
):
    group = slot_ref.shape[1]
    cot = cot_ref[...].astype(F32).reshape(group, BLOCK // group, D)
    first = lax.broadcasted_iota(jnp.int32, cot.shape, 1) == 0
    grad = cot + jnp.where(first, slot_ref[0][:, None, :], 0.0)
    grad = grad.reshape(BLOCK, D) * mask_ref[...]
    norm = norm_ref[...]
    second = norm_back(grad, gain_ref[...], norm, inverse_ref[...])
    low = second.astype(BF16)
    grad_ref[...] = second
    low_ref[...] = low
    add_sums(sum_ref, [grad * norm, grad, low.astype(F32)])


def second_back(cot, d_slot, mask, norm, inverse, gain):
    rows = cot.shape[0]
    blocks = rows // BLOCK
    wide = pl.BlockSpec((BLOCK, D), lambda i: (i, 0))
    thin = pl.BlockSpec((BLOCK, 1), lambda i: (i, 0))
    group = d_slot.shape[0] // blocks
    return pl.pallas_call(
        second_back_kernel,
        grid=(blocks,),
        in_specs=[
            wide,
            pl.BlockSpec((1, group, D), lambda i: (i, 0, 0)),
            thin,
            wide,
            thin,
            pl.BlockSpec((1, D), lambda i: (0, 0)),
        ],
        out_specs=[wide, wide, pl.BlockSpec((8, D), lambda i: (0, 0))],
        out_shape=[
            jax.ShapeDtypeStruct((rows, D), F32),
            jax.ShapeDtypeStruct((rows, D), BF16),
            jax.ShapeDtypeStruct((8, D), F32),
        ],
        compiler_params=pltpu.CompilerParams(vmem_limit_bytes=VMEM_LIMIT),
        cost_estimate=pl.CostEstimate(
            flops=20 * rows * D, bytes_accessed=12 * rows * D, transcendentals=0
        ),
        name="second_back",
    )(cot, d_slot.reshape(blocks, group, D), mask, norm, inverse, gain)


def first_back_kernel(
    hidden_ref, w_ref, second_ref, norm_ref, inverse_ref, gain_ref, grad_ref, low_ref, sum_ref
):
    grad = second_ref[...] + dot(hidden_ref[...], w_ref[...], ((1,), (1,)))
    norm = norm_ref[...]
    first = norm_back(grad, gain_ref[...], norm, inverse_ref[...])
    low = first.astype(BF16)
    grad_ref[...] = first
    low_ref[...] = low
    add_sums(sum_ref, [grad * norm, grad, low.astype(F32)])


def first_back(d_expanded, w_expand, d_second, norm, inverse, gain):
    rows = d_expanded.shape[0]
    wide = pl.BlockSpec((BLOCK, D), lambda i: (i, 0))
    return pl.pallas_call(
        first_back_kernel,
        grid=(rows // BLOCK,),
        in_specs=[
            pl.BlockSpec((BLOCK, FF), lambda i: (i, 0)),
            pl.BlockSpec((D, FF), lambda i: (0, 0)),
            wide,
            wide,
            pl.BlockSpec((BLOCK, 1), lambda i: (i, 0)),
            pl.BlockSpec((1, D), lambda i: (0, 0)),
        ],
        out_specs=[wide, wide, pl.BlockSpec((8, D), lambda i: (0, 0))],
        out_shape=[
            jax.ShapeDtypeStruct((rows, D), F32),
            jax.ShapeDtypeStruct((rows, D), BF16),
            jax.ShapeDtypeStruct((8, D), F32),
        ],
        compiler_params=pltpu.CompilerParams(vmem_limit_bytes=VMEM_LIMIT),
        cost_estimate=pl.CostEstimate(
            flops=2 * rows * D * FF,
            bytes_accessed=2 * (rows * FF + D * FF) + 14 * rows * D,
            transcendentals=0,
        ),
        name="first_back",
    )(d_expanded, w_expand, d_second, norm, inverse, gain)


def expand_kernel(mid_ref, w_ref, b_ref, active_ref, slope_ref):
    expanded = dot(mid_ref[...], w_ref[...]) + b_ref[...]
    phi = 0.5 + 0.5 * lax.erf(expanded * 0.7071067811865476)
    density = jnp.exp(expanded * expanded * -0.5) * 0.3989422804014327
    active_ref[...] = (expanded * phi).astype(BF16)
    slope_ref[...] = (phi + expanded * density).astype(BF16)


def expand_more_kernel(mid_ref, w_ref, b_ref, _, __, active_ref, slope_ref):
    expand_kernel(mid_ref, w_ref, b_ref, active_ref, slope_ref)


def expand(mid_low, w_expand, b_expand, start, count, into=()):
    rows = mid_low.shape[0]
    tile_r, tile_f = 256, FF // 2
    return pl.pallas_call(
        expand_more_kernel if into else expand_kernel,
        grid=(count, rows // tile_r),
        in_specs=[
            pl.BlockSpec((tile_r, D), lambda j, i: (i, 0)),
            pl.BlockSpec((D, tile_f), lambda j, i: (0, j + start)),
            pl.BlockSpec((1, tile_f), lambda j, i: (0, j + start)),
        ]
        + [pl.BlockSpec(memory_space=pl.ANY)] * len(into),
        out_specs=[
            pl.BlockSpec((tile_r, tile_f), lambda j, i: (i, j + start)),
            pl.BlockSpec((tile_r, tile_f), lambda j, i: (i, j + start)),
        ],
        out_shape=[jax.ShapeDtypeStruct((rows, FF), BF16)] * 2,
        input_output_aliases={3: 0, 4: 1} if into else {},
        compiler_params=pltpu.CompilerParams(vmem_limit_bytes=VMEM_LIMIT),
        cost_estimate=pl.CostEstimate(
            flops=2 * rows * D * count * tile_f,
            bytes_accessed=2 * (rows * D + D * count * tile_f + 2 * rows * count * tile_f),
            transcendentals=2 * rows * count * tile_f,
        ),
        name="expand",
    )(mid_low, w_expand, b_expand, *into)


def normalized(values):
    centred = values - jnp.mean(values, axis=-1, keepdims=True)
    spread = jnp.mean(centred * centred, axis=-1, keepdims=True)
    inverse = lax.rsqrt(spread + norm_eps)
    return centred * inverse, inverse


def norm_back(grad, gain, norm, inverse):
    scaled = grad * gain
    return inverse * (
        scaled
        - jnp.mean(scaled, axis=-1, keepdims=True)
        - norm * jnp.mean(scaled * norm, axis=-1, keepdims=True)
    )


def per_device(places, *args):
    (
        question_in,
        passage_in,
        question_len,
        passage_len,
        positive,
        question_cot,
        passage_cot,
        w_joined,
        w_output,
        w_expand,
        w_reduce,
        vectors,
        b_expand,
    ) = args
    pb, pa = lax.axis_index("pb"), lax.axis_index("pa")
    z, core = pa // 2, pa % 2
    tower = z // places.half
    is_q = tower == 0
    chip = pb * places.nz + z
    masks = [places.stack_masks(side) for side in range(2)]
    slots_of = [sorted(range(places.chips), key=side.__getitem__) for side in masks]

    def of_core(rows_of):
        both = jnp.array(rows_of, jnp.int32)
        return (
            lax.dynamic_index_in_dim(both, core, 0, keepdims=False),
            lax.dynamic_index_in_dim(both, 1 - core, 0, keepdims=False),
        )

    side = jnp.full((places.chips,), core, jnp.int32)
    table = jnp.stack([x ^ chip for x in of_core(masks)] + [side]).astype(jnp.int32)
    slots = [x ^ lax.dynamic_index_in_dim(x, chip, 0, keepdims=False) for x in of_core(slots_of)]
    slots = jnp.stack(slots + [side]).astype(jnp.int32)
    share = w_joined.shape[1]

    small = jnp.concatenate(
        [
            vectors.transpose(0, 2, 1),
            b_expand.reshape(2, share, 4),
            jnp.zeros((2, share, 116), BF16),
        ],
        axis=2,
    )
    first = jnp.concatenate([w_joined, w_output, small], axis=2)
    second, third = w_expand, w_reduce

    class Gather:
        def __init__(self, piece):
            self.stack = lax.dynamic_index_in_dim(piece, tower, 0, keepdims=True)
            self.send = lax.dynamic_index_in_dim(piece, 1 - tower, 0, keepdims=True)
            self.held = None

        def join(self, got):
            self.stack = jnp.concatenate([self.stack, got], axis=0)
            self.send = self.stack

        def move(self, first, last):
            for step in range(first, last):
                self.join(places.swap(self.send, step))

        def mid(self):
            self.move(0, 1)

        def along_z(self):
            self.move(1, z_steps)

        def pb_first(self):
            self.move(z_steps, places.steps - 1)

        def pb_last(self):
            self.held = places.swap(self.send, places.steps - 1)

        def core_stack(self):
            self.other = places.swap_core(self.stack)

        def core_held(self):
            self.parts = [self.stack, self.held, self.other, places.swap_core(self.held)]

        def whole(self, segments):
            if self.stack.shape[1] % 8 == 0:
                return assemble(self.parts, table, segments)
            return assemble_plain(self.parts, table, segments)

    z_steps = 1 + len(bits_of(places.half))

    rows_q = question_in.reshape(-1, D)
    rows_p = passage_in.reshape(-1, D)
    own_rows = rows_q.shape[0]

    def sides(q_side, p_side):
        return jnp.where(is_q, q_side, p_side), jnp.where(is_q, p_side, q_side)

    lq, lp = question_in.shape[1], passage_in.shape[1]
    rows = 2 * own_rows

    def chunked(values, sixteenths):
        out, row = [], 0
        for part in sixteenths:
            step = values.shape[0] * part // 16
            out.append(values[row : row + step])
            row += step
        return out

    def hand(values):
        return [places.swap_tower(x) for x in values]

    per_q = rows // lq
    every = lp // lq
    per_p = rows // lp
    nq, np_ = question_in.shape[0], passage_in.shape[0]
    shift = 2 * places.half
    low_pa = pa % shift
    g1, g2, g3 = Gather(first), Gather(second), Gather(third)
    my_tokens, send_tokens = sides(rows_q, rows_p)
    tokens_out = chunked(send_tokens, (5, 6, 5))
    g1.mid()
    g1.send, tokens_out, question_cot, passage_cot = tie(
        g1.send, tokens_out, question_cot, passage_cot
    )
    g1.along_z()
    tokens_in = hand(tokens_out[:1])
    my_cot, send_cot = sides(question_cot.reshape(-1, D), passage_cot.reshape(-1, D))
    g1.send, g2.send, tokens_in, my_cot, send_cot = tie(
        g1.send, g2.send, tokens_in, my_cot, send_cot
    )
    g1.pb_first()
    g2.mid()
    g1.stack, g2.send, tokens_out = tie(g1.stack, g2.send, tokens_out)
    g1.send = g1.stack
    g1.pb_last()
    g1.core_stack()
    g2.along_z()
    tokens_in = tokens_in + hand(tokens_out[1:2])
    g1.held, g2.send, tokens_in, tokens_out, question_len, passage_len, positive = tie(
        g1.held, g2.send, tokens_in, tokens_out, question_len, passage_len, positive
    )
    g1.core_held()
    g2.pb_first()
    tokens_in = tokens_in + hand(tokens_out[2:])
    full_j, full_o, full_small = g1.whole([(0, 3 * D), (3 * D, D), (4 * D, 128)])
    wj = full_j.reshape(D, 3 * D)
    wo = full_o.reshape(D, D)
    small = full_small.reshape(D, 128).astype(F32)
    vec = small[:, :8].T
    bias_e = small[:, 8:12].reshape(1, FF)
    bias_j = jnp.concatenate([vec[0], jnp.zeros((D,), F32), vec[1]])[None]
    wj, wo, vec, bias_e, bias_j, g2.stack, g3.send = tie(
        wj, wo, vec, bias_e, bias_j, g2.stack, g3.send
    )
    g2.send = g2.stack
    g2.pb_last()
    g2.core_stack()
    qkv = project(my_tokens, wj, bias_j, rows, 0)
    qkv, tokens_in, g3.send = tie(qkv, tokens_in, g3.send)
    g3.mid()
    tokens = join([my_tokens] + tokens_in)
    qkv = project(tokens, wj, bias_j, rows, own_rows // BLOCK, (qkv,))
    cot_out = chunked(send_cot, (3, 3, 3, 4, 3))
    by_pa = positive.reshape(places.pa_n, nq)
    pair = [lax.dynamic_index_in_dim(by_pa, low_pa + k, 0, keepdims=False) for k in (0, shift)]
    pair = jnp.concatenate(pair)[None]
    wanted_rows = jnp.concatenate([pair // 16, pair % 16], axis=0).astype(BF16)
    wanted_rows = jnp.pad(wanted_rows, ((0, 0), (0, D - per_q)))
    valid_q = (jnp.arange(lq, dtype=jnp.int32)[None, :] < question_len[:, None]).astype(jnp.int32)
    valid_p = (jnp.arange(lp, dtype=jnp.int32)[None, :] < passage_len[:, None]).astype(jnp.int32)
    my_valid, send_valid = sides(valid_q.reshape(-1), valid_p.reshape(-1))
    valid = jnp.concatenate([my_valid, places.swap_tower(send_valid)])
    row_ids = jnp.arange(rows, dtype=jnp.int32)
    seq = jnp.where(is_q, row_ids // lq, row_ids // lp)
    qid = seq.reshape(rows, 1)
    kid = jnp.where(valid > 0, seq, -1).reshape(rows // BLOCK, 1, BLOCK)
    row_mask = valid.reshape(rows, 1).astype(F32)

    blocks = rows // BLOCK
    later = blocks // 2
    qkv, g3.send, cot_out = tie(qkv, g3.send, cot_out)
    g3.along_z()
    cot_in = hand(cot_out[:1])
    spread = attention(qkv, qid, kid, 0, later)
    spread, g2.held, g3.send, cot_in, cot_out = tie(spread, g2.held, g3.send, cot_in, cot_out)
    g2.core_held()
    g3.pb_first()
    cot_in = cot_in + hand(cot_out[1:2])
    context, probs = attention(qkv, qid, kid, later, blocks - later, tuple(spread))
    context, g2.parts, g3.stack, cot_in, cot_out = tie(context, g2.parts, g3.stack, cot_in, cot_out)
    g3.send = g3.stack
    g3.pb_last()
    g3.core_stack()
    cot_in = cot_in + hand(cot_out[2:3])
    (full_e,) = g2.whole([(0, FF)])
    we = full_e.reshape(D, FF)
    attended = dot(context, wo) + vec[2]
    norm_one, inverse_one = normalized(tokens.astype(F32) + attended)
    mid = norm_one * vec[3] + vec[4]
    mid_low = mid.astype(BF16)
    mid_low, we, cot_in, cot_out = tie(mid_low, we, cot_in, cot_out)
    cot_in = cot_in + hand(cot_out[3:4])
    gelu = expand(mid_low, we, bias_e, 0, 1)
    gelu, g3.held, g3.other, g3.stack, cot_in, cot_out = tie(
        gelu, g3.held, g3.other, g3.stack, cot_in, cot_out
    )
    g3.core_held()
    cot_in = cot_in + hand(cot_out[4:])
    active, slope = expand(mid_low, we, bias_e, 1, 1, tuple(gelu))
    active, g3.parts, cot_in = tie(active, g3.parts, cot_in)
    (full_r,) = g3.whole([(0, D)])
    wr = full_r.reshape(FF, D)
    norm_two, inverse_two = normalized(mid + dot(active, wr) + vec[5])
    out = ((norm_two * vec[6] + vec[7]) * row_mask).astype(BF16)

    firsts = out.reshape(per_q, lq, D)[:, 0, :]
    others = places.swap_tower(firsts)
    cls_q = jnp.where(is_q, firsts, others)
    cls_p = jnp.where(is_q, others, firsts)[::every]
    pad = (-(per_q + per_p + 2)) % 8
    stack = jnp.concatenate([cls_q, cls_p, wanted_rows, jnp.zeros((pad, D), BF16)], axis=0)[None]
    pair_masks = [0]
    for bit in bits_of(places.half):
        got = lax.ppermute(stack, "pa", [(i, i ^ (2 * bit)) for i in range(places.pa_n)])
        stack = jnp.concatenate([stack, got], axis=0)
        pair_masks = pair_masks + [m ^ (2 * bit) for m in pair_masks]
    for bit in bits_of(places.pb_n):
        got = lax.ppermute(stack, "pb", [(i, i ^ bit) for i in range(places.pb_n)])
        stack = jnp.concatenate([stack, got], axis=0)
        pair_masks = pair_masks + [m ^ (bit * places.pa_n) for m in pair_masks]
    stack = jnp.concatenate([stack, places.swap_core(stack)], axis=0)
    pair_masks = pair_masks + [m ^ 1 for m in pair_masks]
    groups = len(pair_masks)
    me = pb * places.pa_n + low_pa
    place = jnp.array(pair_masks, jnp.int32) ^ me
    dev_p = jnp.stack([place + shift, place], axis=1)
    p_ids = (dev_p[:, :, None] * np_ + jnp.arange(np_, dtype=jnp.int32)).reshape(-1)
    digits = stack[:, per_q + per_p : per_q + per_p + 2, :per_q].astype(jnp.int32)
    wanted = (digits[:, 0] * 16 + digits[:, 1]).reshape(-1)

    all_q = stack[:, :per_q].reshape(groups * per_q, D)
    all_p = stack[:, per_q : per_q + per_p].reshape(groups * per_p, D)
    similarity = dot(all_q, all_p, ((1,), (1,))) * score_scale
    hot = (wanted[:, None] == p_ids[None, :]).astype(F32)
    top = jnp.max(similarity, axis=1, keepdims=True)
    grown = jnp.exp(similarity - top)
    total = jnp.sum(grown, axis=1, keepdims=True)
    own_sim = similarity[:per_q]
    loss = top[:per_q, 0] + jnp.log(total[:per_q, 0]) - jnp.sum(own_sim * hot[:per_q], axis=1)
    question_loss = lax.dynamic_slice_in_dim(loss, tower * nq, nq)
    d_sim = (loss_weight * (grown / total - hot)).astype(BF16)
    d_q = dot(d_sim[:per_q], all_p) * score_scale
    d_p = dot(d_sim[:, :per_p], all_q, ((0,), (0,))) * score_scale
    d_p = jnp.concatenate(
        [d_p.reshape(per_p, 1, D), jnp.zeros((per_p, every - 1, D), F32)], axis=1
    ).reshape(per_q, D)
    d_slot = jnp.where(is_q, d_q, d_p)

    d_second, d_reduced, sums_second = second_back(
        join([my_cot] + cot_in), d_slot, row_mask, norm_two, inverse_two, vec[6][None, :]
    )
    even = share % 8 == 0

    def gradient(left, right, **more):
        if left.shape[1] > D:
            return tall_grad(left, right, slots, places.nz)
        return weight_grad(left, right, slots, D, **more)

    def plain(left, right, extra=None):
        return grad_plain(left, right, table, extra)

    class Scatter:
        def __init__(self, mine, theirs):
            self.groups, self.theirs, self.parts = [], [], []
            self.send = self.keep = self.out = None
            self.count = places.chips
            self.add(mine, theirs)

        def add(self, mine, theirs):
            self.groups = self.groups + [[mine]]
            self.theirs = self.theirs + [theirs]

        def cores(self, k=0):
            got = places.swap_core(self.theirs[k])
            self.groups = [g + [got] if i == k else g for i, g in enumerate(self.groups)]

        def total(self, start, stop):
            sums = [sum(x[start:stop].astype(F32) for x in group) for group in self.groups]
            out = sums[0] if len(sums) == 1 else jnp.concatenate(sums, axis=2)
            for part in self.parts:
                out = out + part[start:stop].astype(F32)
            return out

        def prepare(self):
            self.send = self.total(self.count // 2, self.count).astype(BF16)

        def move(self, step):
            if self.send is None:
                self.prepare()
            self.parts = self.parts + [places.swap(self.send, step)]
            self.send = None
            self.count = self.count // 2

        def pb_first(self):
            self.move(places.steps - 1)

        def pb_rest(self):
            for step in range(places.steps - 2, z_steps - 1, -1):
                self.move(step)

        def along_z(self):
            for step in range(z_steps - 1, 0, -1):
                self.move(step)

        def prepare_mid(self):
            self.keep = self.total(0, 1)
            self.send = self.total(1, 2).astype(BF16)

        def mid(self):
            got = places.swap(self.send, 0).astype(F32)
            self.out = jnp.concatenate(
                [jnp.where(is_q, self.keep, got), jnp.where(is_q, got, self.keep)], axis=0
            )
            self.groups = self.theirs = self.parts = []
            self.send = self.keep = None

    def hold(chains, *values):
        names = ("groups", "theirs", "parts", "send", "keep", "out")
        states, values = tie([[getattr(c, n) for n in names] for c in chains], values)
        for chain, state in zip(chains, states):
            for name, value in zip(names, state):
                setattr(chain, name, value)
        return values

    make = gradient if even else plain
    send_out = chunked(out[own_rows:], (4, 4, 4, 4))
    d_reduced, send_out = tie(d_reduced, send_out)
    got_out = hand(send_out[:1])
    sr = Scatter(*make(active, d_reduced))
    d_reduced, got_out, send_out = hold([sr], d_reduced, got_out, send_out)
    sr.cores()
    got_out = got_out + hand(send_out[1:2])
    d_expanded, g_bias_expand = hidden_grad(d_reduced, wr, slope)
    d_expanded, got_out, send_out = hold([sr], d_expanded, got_out, send_out)
    sr.prepare()
    d_expanded, send_out = hold([sr], d_expanded, send_out)
    sr.pb_first()
    got_out = got_out + hand(send_out[2:3])
    se = Scatter(*make(mid_low, d_expanded))
    d_expanded, got_out, send_out = hold([se], d_expanded, got_out, send_out)
    se.cores()
    got_out = got_out + hand(send_out[3:])
    d_first, d_attended, sums_first = first_back(
        d_expanded, we, d_second, norm_one, inverse_one, vec[3][None, :]
    )
    d_attended, got_out = hold([sr, se], d_attended, got_out)
    sr.prepare()
    (d_attended,) = hold([sr], d_attended)
    sr.pb_rest()
    se.add(*make(context, d_attended))
    (d_attended,) = hold([se], d_attended)
    se.cores(1)
    d_context = dot(d_attended, wo, ((1,), (1,))).astype(BF16)
    (d_context,) = hold([sr, se], d_context)
    se.prepare()
    sr.prepare()
    (d_context,) = hold([sr, se], d_context)
    se.pb_first()
    sr.along_z()
    d_joined, sums_one = attention_back(qkv, probs, d_context, later, blocks - later)
    (d_joined,) = hold([sr], d_joined)
    sr.prepare_mid()
    (d_joined,) = hold([sr], d_joined)
    sr.mid()
    send_grad = (d_first[own_rows:] + dot(d_joined[own_rows:], wj, ((1,), (1,)))).astype(BF16)
    d_joined, send_grad = hold([sr, se], d_joined, chunked(send_grad, (4, 3, 6, 3)))
    se.prepare()
    d_joined, send_grad = hold([se], d_joined, send_grad)
    se.pb_rest()
    got_grad = hand(send_grad[:1])
    d_joined, sums_two = attention_back(qkv, probs, d_context, 0, later, d_joined)
    d_joined, sums_two, got_grad, send_grad = hold([se], d_joined, sums_two, got_grad, send_grad)
    se.prepare()
    g_joined_bias = sums_one + sums_two
    g_vec = jnp.concatenate(
        [
            g_joined_bias[:, :D],
            g_joined_bias[:, 2 * D :],
            sums_first[2:3],
            sums_first[:2],
            sums_second[2:3],
            sums_second[:2],
        ]
    )
    g_small = jnp.concatenate(
        [g_vec.T, g_bias_expand.reshape(D, 4), jnp.zeros((D, 116), F32)], axis=1
    )
    d_joined, g_small, send_grad = hold([se], d_joined, g_small, send_grad)
    se.along_z()
    got_grad = got_grad + hand(send_grad[1:2])
    sj = Scatter(*make(tokens, d_joined, extra=g_small))
    d_joined, got_grad, send_grad = hold([se, sj], d_joined, got_grad, send_grad)
    sj.cores()
    se.prepare_mid()
    (d_joined,) = hold([se], d_joined)
    se.mid()
    own_grad = d_first[:own_rows] + dot(d_joined[:own_rows], wj, ((1,), (1,)))
    own_grad, send_grad = hold([sj], own_grad, send_grad)
    sj.prepare()
    send_grad = hold([sj], send_grad)[0]
    sj.pb_first()
    got_grad = got_grad + hand(send_grad[2:3])
    out_q, out_p = deal(tower.reshape(1), out, got_out)
    got_grad, send_grad, out_q, out_p = hold([sj, se], got_grad, send_grad, out_q, out_p)
    sj.prepare()
    send_grad = hold([sj], send_grad)[0]
    sj.pb_rest()
    got_grad = got_grad + hand(send_grad[3:])
    got_grad = hold([sj], got_grad)[0]
    sj.prepare()
    got_grad = hold([sj], got_grad)[0]
    sj.along_z()
    grad_q, grad_p = deal(tower.reshape(1), own_grad, got_grad)
    grad_q, grad_p = hold([sj], grad_q, grad_p)
    sj.prepare_mid()
    sj.mid()
    grad_joined = sj.out[:, :, : 3 * D]
    grad_expand, grad_output, grad_reduce = se.out[:, :, :FF], se.out[:, :, FF:], sr.out
    extra = sj.out[:, :, 3 * D :]
    grad_vectors = extra[:, :, :8].transpose(0, 2, 1)
    grad_b_expand = extra[:, :, 8:12].reshape(2, 4 * share)

    return (
        out_q.reshape(question_in.shape),
        out_p.reshape(passage_in.shape),
        question_loss,
        grad_q.reshape(question_in.shape),
        grad_p.reshape(passage_in.shape),
        grad_joined,
        grad_output,
        grad_expand,
        grad_reduce,
        grad_vectors,
        grad_b_expand,
    )


def solution(mesh):
    in_specs = (
        P(("pb", "pa"), None, None),
        P(("pb", "pa"), None, None),
        P(("pb", "pa")),
        P(("pb", "pa")),
        P("pb"),
        P(("pb", "pa"), None, None),
        P(("pb", "pa"), None, None),
        P(None, ("pb", "pa"), None),
        P(None, ("pb", "pa"), None),
        P(None, ("pb", "pa"), None),
        P(None, ("pb", "pa"), None),
        P(None, None, ("pb", "pa")),
        P(None, ("pb", "pa")),
    )
    out_specs = (
        P(("pb", "pa"), None, None),
        P(("pb", "pa"), None, None),
        P(("pb", "pa")),
        P(("pb", "pa"), None, None),
        P(("pb", "pa"), None, None),
        P(None, ("pb", "pa"), None),
        P(None, ("pb", "pa"), None),
        P(None, ("pb", "pa"), None),
        P(None, ("pb", "pa"), None),
        P(None, None, ("pb", "pa")),
        P(None, ("pb", "pa")),
    )
    return jax.shard_map(
        functools.partial(per_device, Places(mesh)),
        mesh=mesh,
        in_specs=in_specs,
        out_specs=out_specs,
        check_vma=False,
    )
```

```python
import functools

import jax
import jax.numpy as jnp
from jax import lax
from jax.experimental import pallas as pl
from jax.experimental.pallas import tpu as pltpu
from jax.sharding import PartitionSpec as P

D = 768
HEADS = 12
HDIM = 64
FF = 3072
AXES = ("pb", "pa")
BLOCK = 256

norm_eps = 1e-06
masked_score = -1000000000.0
score_scale = 0.0625
loss_weight = 16.0
head_scale = HDIM ** (-0.5)
F32 = jnp.float32
BF16 = jnp.bfloat16
VMEM_LIMIT = 56 * 1024 * 1024


def bits_of(count):
    return [1 << shift for shift in range(count.bit_length() - 1)]


class Places:
    def __init__(self, mesh):
        self.pb_n = mesh.shape["pb"]
        self.pa_n = mesh.shape["pa"]
        self.nz = self.pa_n // 2
        self.half = self.nz // 2
        self.chips = self.pb_n * self.nz
        pb_bits = bits_of(self.pb_n)
        turn = len(pb_bits) // 2
        low_z = [("z", bit) for bit in bits_of(self.half)]
        first = [("pb", bit) for bit in pb_bits]
        second = first[turn:] + first[:turn]
        self.orders = ([("z", self.half)] + low_z + first, [("z", self.half)] + low_z + second)
        self.steps = len(self.orders[0])

    def chip_mask(self, move):
        axis, bit = move
        return bit * self.nz if axis == "pb" else bit

    def stack_masks(self, core):
        masks = [0]
        for move in self.orders[core]:
            masks = masks + [mask ^ self.chip_mask(move) for mask in masks]
        return masks

    def pairs(self, step):
        out = []
        for pb in range(self.pb_n):
            for pa in range(self.pa_n):
                axis, bit = self.orders[pa % 2][step]
                to_pb, to_pa = (pb ^ bit, pa) if axis == "pb" else (pb, pa ^ (2 * bit))
                out.append((pb * self.pa_n + pa, to_pb * self.pa_n + to_pa))
        return out

    def swap(self, values, step):
        return lax.ppermute(values, AXES, self.pairs(step))

    def swap_core(self, values):
        return lax.ppermute(values, "pa", [(i, i ^ 1) for i in range(self.pa_n)])

    def swap_tower(self, values):
        return lax.ppermute(values, "pa", [(i, i ^ (2 * self.half)) for i in range(self.pa_n)])


def dot(left, right, dims=((1,), (0,))):
    return lax.dot_general(left, right, (dims, ((), ())), preferred_element_type=F32)


def tie(*values):
    return lax.optimization_barrier(values)


def assemble_kernel(segments, idx_ref, *refs):
    count = len(segments)
    sources, outs = refs[:4], refs[4 : 4 + count]
    buffer, in_sem, out_sem = refs[4 + count :]
    core = idx_ref[2, 0]
    part = sources[0].shape[0]
    loads = [
        pltpu.make_async_copy(source, buffer.at[pl.ds(k * part, part)], in_sem.at[k])
        for k, source in enumerate(sources)
    ]
    for load in loads:
        load.start()
    stores = []
    for k in range(4):
        loads[k].wait()
        half = core if k < 2 else 1 - core
        for j in range(part):
            slot = k * part + j
            place = idx_ref[k // 2, (k % 2) * part + j]
            for s, (start, width) in enumerate(segments):
                store = pltpu.make_async_copy(
                    buffer.at[slot, :, pl.ds(start, width)],
                    outs[s].at[place, half],
                    out_sem.at[s, slot],
                )
                store.start()
                stores.append(store)
    for store in stores:
        store.wait()


def assemble(parts, table, segments):
    part, rows, width = parts[0].shape
    chips = 2 * part
    shapes = [jax.ShapeDtypeStruct((chips, 2, rows, w), BF16) for _, w in segments]
    return pl.pallas_call(
        functools.partial(assemble_kernel, segments),
        out_shape=shapes,
        in_specs=[pl.BlockSpec(memory_space=pltpu.SMEM)] + [pl.BlockSpec(memory_space=pl.ANY)] * 4,
        out_specs=[pl.BlockSpec(memory_space=pl.ANY)] * len(segments),
        scratch_shapes=[
            pltpu.VMEM((2 * chips, rows, width), BF16),
            pltpu.SemaphoreType.DMA((4,)),
            pltpu.SemaphoreType.DMA((len(segments), 2 * chips)),
        ],
        compiler_params=pltpu.CompilerParams(vmem_limit_bytes=VMEM_LIMIT),
        cost_estimate=pl.CostEstimate(
            flops=0, bytes_accessed=4 * 2 * chips * rows * width, transcendentals=0
        ),
        name="assemble",
    )(table, *parts)


def assemble_plain(parts, table, segments):
    own = jnp.take(jnp.concatenate(parts[:2], axis=0), jnp.argsort(table[0]), axis=0)
    other = jnp.take(jnp.concatenate(parts[2:], axis=0), jnp.argsort(table[1]), axis=0)
    first = table[2, 0] == 0
    both = jnp.stack([jnp.where(first, own, other), jnp.where(first, other, own)], axis=1)
    return [both[..., start : start + w] for start, w in segments]


def split_slabs(acc, core, chips, mine_ref, theirs_ref, cols, within):
    rows = acc.shape[0] // (2 * chips)
    for s in range(chips):
        low = acc[2 * s * rows : (2 * s + 1) * rows]
        high = acc[(2 * s + 1) * rows : (2 * s + 2) * rows]
        mine, theirs = within(s)
        mine_ref[mine, :, cols] = jnp.where(core == 0, low, high).astype(BF16)
        theirs_ref[theirs, :, cols] = jnp.where(core == 0, high, low).astype(BF16)


def weight_grad_kernel(chips, extra, table_ref, left_ref, right_ref, *refs):
    mine_ref, theirs_ref = refs[-2:]
    core = table_ref[2, 0]
    acc = dot(left_ref[...], right_ref[...], ((0,), (0,)))
    width = acc.shape[1]

    def within(s):
        return table_ref[0, s], table_ref[1, s]

    if not extra:
        split_slabs(acc, core, chips, mine_ref, theirs_ref, slice(None), within)
        return
    step = pl.program_id(0)
    cols = pl.ds(pl.multiple_of(step * width, 128), width)
    split_slabs(acc, core, chips, mine_ref, theirs_ref, cols, within)

    @pl.when(step == 0)
    def _():
        tail = pl.ds(mine_ref.shape[2] - 128, 128)
        split_slabs(refs[0][...], core, chips, mine_ref, theirs_ref, tail, within)


def weight_grad(left, right, slots, tile, extra=None, room=0, into=()):
    rows, height = left.shape
    width = right.shape[1]
    chips = slots.shape[1]
    slab = height // (2 * chips)
    total = width + (room if extra is None else extra.shape[1])
    first = 0
    if into:
        total = into[0].shape[2]
        first = (total - width) // tile
    block = (chips, slab, total if extra is not None else tile)
    place = (lambda j, t: (0, 0, 0)) if extra is not None else (lambda j, t: (0, 0, j + first))
    return pl.pallas_call(
        functools.partial(weight_grad_kernel, chips, extra is not None),
        grid_spec=pltpu.PrefetchScalarGridSpec(
            num_scalar_prefetch=1,
            grid=(width // tile,),
            in_specs=[
                pl.BlockSpec((rows, height), lambda j, t: (0, 0)),
                pl.BlockSpec((rows, tile), lambda j, t: (0, j)),
            ]
            + ([] if extra is None else [pl.BlockSpec((height, 128), lambda j, t: (0, 0))])
            + [pl.BlockSpec(memory_space=pl.ANY)] * len(into),
            out_specs=[pl.BlockSpec(block, place)] * 2,
        ),
        out_shape=[jax.ShapeDtypeStruct((chips, slab, total), BF16)] * 2,
        input_output_aliases={3: 0, 4: 1} if into else {},
        compiler_params=pltpu.CompilerParams(vmem_limit_bytes=VMEM_LIMIT),
        cost_estimate=pl.CostEstimate(
            flops=2 * rows * height * width,
            bytes_accessed=2 * (rows * (height + width) + height * width),
            transcendentals=0,
        ),
        name="weight_grad",
    )(slots, left, right, *([] if extra is None else [extra]), *into)


def tall_grad_kernel(chips, table_ref, left_ref, right_ref, mine_ref, theirs_ref):
    core = table_ref[2, 0]
    acc = dot(left_ref[...], right_ref[...], ((0,), (0,)))
    base = pl.program_id(0) * chips

    def within(s):
        return table_ref[0, base + s] % chips, table_ref[1, base + s] % chips

    split_slabs(acc, core, chips, mine_ref, theirs_ref, slice(None), within)


def tall_grad(left, right, slots, column):
    rows, height = left.shape
    width = right.shape[1]
    chips = slots.shape[1]
    slab = height // (2 * chips)
    tile = height // chips * column
    return pl.pallas_call(
        functools.partial(tall_grad_kernel, column),
        grid_spec=pltpu.PrefetchScalarGridSpec(
            num_scalar_prefetch=1,
            grid=(chips // column,),
            in_specs=[
                pl.BlockSpec((rows, tile), lambda i, t: (0, i)),
                pl.BlockSpec((rows, width), lambda i, t: (0, 0)),
            ],
            out_specs=[
                pl.BlockSpec((column, slab, width), lambda i, t: (t[0, i * column] // column, 0, 0)),
                pl.BlockSpec((column, slab, width), lambda i, t: (t[1, i * column] // column, 0, 0)),
            ],
        ),
        out_shape=[jax.ShapeDtypeStruct((chips, slab, width), BF16)] * 2,
        compiler_params=pltpu.CompilerParams(vmem_limit_bytes=VMEM_LIMIT),
        cost_estimate=pl.CostEstimate(
            flops=2 * rows * height * width,
            bytes_accessed=2 * (rows * (height + width) + height * width),
            transcendentals=0,
        ),
        name="tall_grad",
    )(slots, left, right)


def grad_plain(left, right, table, extra=None):
    full = dot(left, right, ((0,), (0,)))
    if extra is not None:
        full = jnp.concatenate([full, extra], axis=1)
    chips = table.shape[1]
    full = full.astype(BF16).reshape(chips, 2, full.shape[0] // (2 * chips), full.shape[1])
    core = table[2, 0]
    mine = lax.dynamic_index_in_dim(full, core, 1, keepdims=False)
    theirs = lax.dynamic_index_in_dim(full, 1 - core, 1, keepdims=False)
    return jnp.take(mine, table[0], axis=0), jnp.take(theirs, table[1], axis=0)


def hidden_grad_kernel(grad_ref, w_ref, slope_ref, out_ref, sum_ref):
    grad = dot(grad_ref[...], w_ref[...], ((1,), (1,))) * slope_ref[...].astype(F32)
    low = grad.astype(BF16)
    out_ref[...] = low
    sum_ref[...] = jnp.sum(low.astype(F32), axis=0, keepdims=True)


def hidden_grad(grad, w_reduce, slope):
    rows, tile = grad.shape[0], 512
    return pl.pallas_call(
        hidden_grad_kernel,
        grid=(FF // tile,),
        in_specs=[
            pl.BlockSpec((rows, D), lambda j: (0, 0)),
            pl.BlockSpec((tile, D), lambda j: (j, 0)),
            pl.BlockSpec((rows, tile), lambda j: (0, j)),
        ],
        out_specs=[
            pl.BlockSpec((rows, tile), lambda j: (0, j)),
            pl.BlockSpec((1, tile), lambda j: (0, j)),
        ],
        out_shape=[
            jax.ShapeDtypeStruct((rows, FF), BF16),
            jax.ShapeDtypeStruct((1, FF), F32),
        ],
        compiler_params=pltpu.CompilerParams(vmem_limit_bytes=VMEM_LIMIT),
        cost_estimate=pl.CostEstimate(
            flops=2 * rows * D * FF,
            bytes_accessed=2 * (rows * D + D * FF + 2 * rows * FF),
            transcendentals=0,
        ),
        name="hidden_grad",
    )(grad, w_reduce, slope)


def attention_kernel(qkv_ref, qid_ref, kid_ref, context_ref, probs_ref):
    allowed = qid_ref[...] == kid_ref[0]
    lane = lax.broadcasted_iota(jnp.int32, (BLOCK, 128), 1)
    zero = jnp.zeros((BLOCK, 128), BF16)

    def at(pair, start=0):
        return pl.ds(pl.multiple_of(start + pair * 128, 128), 128)

    def some(step, carry):
        for k in range(1):
            pair = step * 1 + k
            queries = qkv_ref[:, at(pair)]
            keys = qkv_ref[:, at(pair, D)]
            values = qkv_ref[:, at(pair, 2 * D)]
            outs = []
            for side in range(2):
                mine = (lane < HDIM) if side == 0 else (lane >= HDIM)
                scores = dot(queries, jnp.where(mine, keys, zero), ((1,), (1,))) * head_scale
                scores = jnp.where(allowed, scores, masked_score)
                top = jnp.max(scores, axis=1, keepdims=True)
                grown = jnp.exp(scores - top)
                total = jnp.sum(grown, axis=1, keepdims=True)
                probs = (grown * (1.0 / total)).astype(BF16)
                probs_ref[0, 2 * pair + side] = probs
                outs.append(dot(probs, values))
            context_ref[:, at(pair)] = jnp.where(
                lane < HDIM, outs[0], outs[1]
            ).astype(BF16)
        return carry

    lax.fori_loop(0, HEADS // 2 // 1, some, 0)


def attention_more_kernel(qkv_ref, qid_ref, kid_ref, _, __, context_ref, probs_ref):
    attention_kernel(qkv_ref, qid_ref, kid_ref, context_ref, probs_ref)


def attention(qkv, qid, kid, start, count, into=()):
    rows = qkv.shape[0]
    blocks = rows // BLOCK
    return pl.pallas_call(
        attention_more_kernel if into else attention_kernel,
        grid=(count,),
        in_specs=[
            pl.BlockSpec((BLOCK, 3 * D), lambda i: (i + start, 0)),
            pl.BlockSpec((BLOCK, 1), lambda i: (i + start, 0)),
            pl.BlockSpec((1, 1, BLOCK), lambda i: (i + start, 0, 0)),
        ]
        + [pl.BlockSpec(memory_space=pl.ANY)] * len(into),
        out_specs=[
            pl.BlockSpec((BLOCK, D), lambda i: (i + start, 0)),
            pl.BlockSpec((1, HEADS, BLOCK, BLOCK), lambda i: (i + start, 0, 0, 0)),
        ],
        input_output_aliases={3: 0, 4: 1} if into else {},
        out_shape=[
            jax.ShapeDtypeStruct((rows, D), BF16),
            jax.ShapeDtypeStruct((blocks, HEADS, BLOCK, BLOCK), BF16),
        ],
        compiler_params=pltpu.CompilerParams(vmem_limit_bytes=VMEM_LIMIT),
        cost_estimate=pl.CostEstimate(
            flops=4 * count * BLOCK * BLOCK * D * 2,
            bytes_accessed=count * BLOCK * (4 * D + HEADS * BLOCK) * 2,
            transcendentals=count * BLOCK * HEADS * BLOCK,
        ),
        name="attention",
    )(qkv, qid, kid, *into)


def attention_back_kernel(qkv_ref, probs_ref, grad_ref, out_ref, sum_ref):
    lane = lax.broadcasted_iota(jnp.int32, (BLOCK, 128), 1)
    zero = jnp.zeros((BLOCK, 128), BF16)

    def at(pair, start=0):
        return pl.ds(pl.multiple_of(start + pair * 128, 128), 128)

    def some(step, carry):
        for k in range(1):
            pair = step * 1 + k
            cols = at(pair)
            queries = qkv_ref[:, at(pair)]
            keys = qkv_ref[:, at(pair, D)]
            values = qkv_ref[:, at(pair, 2 * D)]
            grad = grad_ref[:, cols]
            d_q, d_k, d_v = [], [], []
            for side in range(2):
                mine = (lane < HDIM) if side == 0 else (lane >= HDIM)
                low = probs_ref[0, 2 * pair + side]
                d_probs = dot(jnp.where(mine, grad, zero), values, ((1,), (1,)))
                d_v.append(dot(low, grad, ((0,), (0,))))
                probs = low.astype(F32)
                row_dot = jnp.sum(d_probs * probs, axis=1, keepdims=True)
                d_scores = (probs * (d_probs - row_dot)).astype(BF16)
                d_q.append(dot(d_scores, keys))
                d_k.append(dot(d_scores, queries, ((0,), (0,))))
            first = lane < HDIM
            out_ref[:, at(pair)] = (
                jnp.where(first, d_q[0], d_q[1]) * head_scale
            ).astype(BF16)
            out_ref[:, at(pair, D)] = (
                jnp.where(first, d_k[0], d_k[1]) * head_scale
            ).astype(BF16)
            out_ref[:, at(pair, 2 * D)] = jnp.where(
                first, d_v[0], d_v[1]
            ).astype(BF16)
        return carry

    lax.fori_loop(0, HEADS // 2 // 1, some, 0)
    sums = jnp.sum(out_ref[...].astype(F32), axis=0, keepdims=True)

    @pl.when(pl.program_id(0) == 0)
    def _():
        sum_ref[...] = sums

    @pl.when(pl.program_id(0) > 0)
    def _():
        sum_ref[...] += sums


def attention_back_more_kernel(qkv_ref, probs_ref, grad_ref, _, out_ref, sum_ref):
    attention_back_kernel(qkv_ref, probs_ref, grad_ref, out_ref, sum_ref)


def attention_back(qkv, probs, grad_context, start, count, into=None):
    rows = qkv.shape[0]
    more = into is not None
    return pl.pallas_call(
        attention_back_more_kernel if more else attention_back_kernel,
        grid=(count,),
        in_specs=[
            pl.BlockSpec((BLOCK, 3 * D), lambda i: (i + start, 0)),
            pl.BlockSpec((1, HEADS, BLOCK, BLOCK), lambda i: (i + start, 0, 0, 0)),
            pl.BlockSpec((BLOCK, D), lambda i: (i + start, 0)),
        ]
        + ([pl.BlockSpec(memory_space=pl.ANY)] if more else []),
        out_specs=[
            pl.BlockSpec((BLOCK, 3 * D), lambda i: (i + start, 0)),
            pl.BlockSpec((1, 3 * D), lambda i: (0, 0)),
        ],
        out_shape=[
            jax.ShapeDtypeStruct((rows, 3 * D), BF16),
            jax.ShapeDtypeStruct((1, 3 * D), F32),
        ],
        input_output_aliases={3: 0} if more else {},
        compiler_params=pltpu.CompilerParams(vmem_limit_bytes=VMEM_LIMIT),
        cost_estimate=pl.CostEstimate(
            flops=8 * count * BLOCK * BLOCK * D * 2,
            bytes_accessed=count * BLOCK * (7 * D + HEADS * BLOCK) * 2,
            transcendentals=0,
        ),
        name="attention_back",
    )(qkv, probs, grad_context, *([into] if more else []))


def join_kernel(*refs):
    row = 0
    for piece in refs[:-1]:
        rows = piece.shape[0]
        refs[-1][row : row + rows, :] = piece[...]
        row += rows


def join(pieces):
    rows, width = sum(x.shape[0] for x in pieces), pieces[0].shape[1]
    return pl.pallas_call(
        join_kernel,
        grid=(1,),
        in_specs=[pl.BlockSpec(x.shape, lambda i: (0, 0)) for x in pieces],
        out_specs=pl.BlockSpec((rows, width), lambda i: (0, 0)),
        out_shape=jax.ShapeDtypeStruct((rows, width), pieces[0].dtype),
        compiler_params=pltpu.CompilerParams(vmem_limit_bytes=VMEM_LIMIT),
        cost_estimate=pl.CostEstimate(
            flops=0, bytes_accessed=4 * rows * width, transcendentals=0
        ),
        name="join",
    )(*pieces)


def deal_kernel(tower_ref, own_ref, *refs):
    pieces, (q_ref, p_ref) = refs[:-2], refs[-2:]

    def give(own_out, other_out):
        own_out[...] = own_ref[...]
        row = 0
        for piece in pieces:
            rows = piece.shape[0]
            other_out[row : row + rows, :] = piece[...].astype(other_out.dtype)
            row += rows

    @pl.when(tower_ref[0] == 0)
    def _():
        give(q_ref, p_ref)

    @pl.when(tower_ref[0] != 0)
    def _():
        give(p_ref, q_ref)


def deal(tower, own, pieces):
    rows, width = sum(x.shape[0] for x in pieces), own.shape[1]
    shape = jax.ShapeDtypeStruct((rows, width), own.dtype)
    return pl.pallas_call(
        deal_kernel,
        grid=(1,),
        in_specs=[
            pl.BlockSpec(memory_space=pltpu.SMEM),
            pl.BlockSpec((rows, width), lambda i: (0, 0)),
        ]
        + [pl.BlockSpec(x.shape, lambda i: (0, 0)) for x in pieces],
        out_specs=[pl.BlockSpec((rows, width), lambda i: (0, 0))] * 2,
        out_shape=[shape] * 2,
        compiler_params=pltpu.CompilerParams(vmem_limit_bytes=VMEM_LIMIT),
        cost_estimate=pl.CostEstimate(
            flops=0, bytes_accessed=12 * rows * width, transcendentals=0
        ),
        name="deal",
    )(tower, own, *pieces)


def add_sums(sum_ref, values):
    total = jnp.concatenate(
        [jnp.sum(x, axis=0, keepdims=True) for x in values]
        + [jnp.zeros((8 - len(values), values[0].shape[1]), F32)],
        axis=0,
    )

    @pl.when(pl.program_id(0) == 0)
    def _():
        sum_ref[...] = total

    @pl.when(pl.program_id(0) > 0)
    def _():
        sum_ref[...] += total


def second_back_kernel(
    cot_ref, slot_ref, mask_ref, norm_ref, inverse_ref, gain_ref, grad_ref, low_ref, sum_ref
):
    group = slot_ref.shape[1]
    cot = cot_ref[...].astype(F32).reshape(group, BLOCK // group, D)
    first = lax.broadcasted_iota(jnp.int32, cot.shape, 1) == 0
    grad = cot + jnp.where(first, slot_ref[0][:, None, :], 0.0)
    grad = grad.reshape(BLOCK, D) * mask_ref[...]
    norm = norm_ref[...]
    second = norm_back(grad, gain_ref[...], norm, inverse_ref[...])
    low = second.astype(BF16)
    grad_ref[...] = second
    low_ref[...] = low
    add_sums(sum_ref, [grad * norm, grad, low.astype(F32)])


def second_back(cot, d_slot, mask, norm, inverse, gain):
    rows = cot.shape[0]
    blocks = rows // BLOCK
    wide = pl.BlockSpec((BLOCK, D), lambda i: (i, 0))
    thin = pl.BlockSpec((BLOCK, 1), lambda i: (i, 0))
    group = d_slot.shape[0] // blocks
    return pl.pallas_call(
        second_back_kernel,
        grid=(blocks,),
        in_specs=[
            wide,
            pl.BlockSpec((1, group, D), lambda i: (i, 0, 0)),
            thin,
            wide,
            thin,
            pl.BlockSpec((1, D), lambda i: (0, 0)),
        ],
        out_specs=[wide, wide, pl.BlockSpec((8, D), lambda i: (0, 0))],
        out_shape=[
            jax.ShapeDtypeStruct((rows, D), F32),
            jax.ShapeDtypeStruct((rows, D), BF16),
            jax.ShapeDtypeStruct((8, D), F32),
        ],
        compiler_params=pltpu.CompilerParams(vmem_limit_bytes=VMEM_LIMIT),
        cost_estimate=pl.CostEstimate(
            flops=20 * rows * D, bytes_accessed=12 * rows * D, transcendentals=0
        ),
        name="second_back",
    )(cot, d_slot.reshape(blocks, group, D), mask, norm, inverse, gain)


def first_back_kernel(
    hidden_ref, w_ref, second_ref, norm_ref, inverse_ref, gain_ref, grad_ref, low_ref, sum_ref
):
    grad = second_ref[...] + dot(hidden_ref[...], w_ref[...], ((1,), (1,)))
    norm = norm_ref[...]
    first = norm_back(grad, gain_ref[...], norm, inverse_ref[...])
    low = first.astype(BF16)
    grad_ref[...] = first
    low_ref[...] = low
    add_sums(sum_ref, [grad * norm, grad, low.astype(F32)])


def first_back(d_expanded, w_expand, d_second, norm, inverse, gain):
    rows = d_expanded.shape[0]
    wide = pl.BlockSpec((BLOCK, D), lambda i: (i, 0))
    return pl.pallas_call(
        first_back_kernel,
        grid=(rows // BLOCK,),
        in_specs=[
            pl.BlockSpec((BLOCK, FF), lambda i: (i, 0)),
            pl.BlockSpec((D, FF), lambda i: (0, 0)),
            wide,
            wide,
            pl.BlockSpec((BLOCK, 1), lambda i: (i, 0)),
            pl.BlockSpec((1, D), lambda i: (0, 0)),
        ],
        out_specs=[wide, wide, pl.BlockSpec((8, D), lambda i: (0, 0))],
        out_shape=[
            jax.ShapeDtypeStruct((rows, D), F32),
            jax.ShapeDtypeStruct((rows, D), BF16),
            jax.ShapeDtypeStruct((8, D), F32),
        ],
        compiler_params=pltpu.CompilerParams(vmem_limit_bytes=VMEM_LIMIT),
        cost_estimate=pl.CostEstimate(
            flops=2 * rows * D * FF,
            bytes_accessed=2 * (rows * FF + D * FF) + 14 * rows * D,
            transcendentals=0,
        ),
        name="first_back",
    )(d_expanded, w_expand, d_second, norm, inverse, gain)


def expand_kernel(mid_ref, w_ref, b_ref, active_ref, slope_ref):
    expanded = dot(mid_ref[...], w_ref[...]) + b_ref[...]
    phi = 0.5 + 0.5 * lax.erf(expanded * 0.7071067811865476)
    density = jnp.exp(expanded * expanded * -0.5) * 0.3989422804014327
    active_ref[...] = (expanded * phi).astype(BF16)
    slope_ref[...] = (phi + expanded * density).astype(BF16)


def expand_more_kernel(mid_ref, w_ref, b_ref, _, __, active_ref, slope_ref):
    expand_kernel(mid_ref, w_ref, b_ref, active_ref, slope_ref)


def expand(mid_low, w_expand, b_expand, start, count, into=()):
    rows = mid_low.shape[0]
    tile_r, tile_f = 256, FF // 2
    return pl.pallas_call(
        expand_more_kernel if into else expand_kernel,
        grid=(count, rows // tile_r),
        in_specs=[
            pl.BlockSpec((tile_r, D), lambda j, i: (i, 0)),
            pl.BlockSpec((D, tile_f), lambda j, i: (0, j + start)),
            pl.BlockSpec((1, tile_f), lambda j, i: (0, j + start)),
        ]
        + [pl.BlockSpec(memory_space=pl.ANY)] * len(into),
        out_specs=[
            pl.BlockSpec((tile_r, tile_f), lambda j, i: (i, j + start)),
            pl.BlockSpec((tile_r, tile_f), lambda j, i: (i, j + start)),
        ],
        out_shape=[jax.ShapeDtypeStruct((rows, FF), BF16)] * 2,
        input_output_aliases={3: 0, 4: 1} if into else {},
        compiler_params=pltpu.CompilerParams(vmem_limit_bytes=VMEM_LIMIT),
        cost_estimate=pl.CostEstimate(
            flops=2 * rows * D * count * tile_f,
            bytes_accessed=2 * (rows * D + D * count * tile_f + 2 * rows * count * tile_f),
            transcendentals=2 * rows * count * tile_f,
        ),
        name="expand",
    )(mid_low, w_expand, b_expand, *into)


def project_kernel(tokens_ref, w_ref, b_ref, out_ref):
    out_ref[...] = (dot(tokens_ref[...], w_ref[...]) + b_ref[...]).astype(BF16)


def project(tokens, weight, bias):
    rows, width = tokens.shape[0], weight.shape[1]
    return pl.pallas_call(
        project_kernel,
        grid=(rows // BLOCK,),
        in_specs=[
            pl.BlockSpec((BLOCK, D), lambda i: (i, 0)),
            pl.BlockSpec((D, width), lambda i: (0, 0)),
            pl.BlockSpec((1, width), lambda i: (0, 0)),
        ],
        out_specs=pl.BlockSpec((BLOCK, width), lambda i: (i, 0)),
        out_shape=jax.ShapeDtypeStruct((rows, width), BF16),
        compiler_params=pltpu.CompilerParams(vmem_limit_bytes=VMEM_LIMIT),
        cost_estimate=pl.CostEstimate(
            flops=2 * rows * D * width,
            bytes_accessed=2 * (rows * (D + width) + D * width),
            transcendentals=0,
        ),
        name="project",
    )(tokens, weight, bias)


def add_norm_kernel(
    rows_of, left_ref, w_ref, base_ref, mask_ref, vec_ref, norm_ref, inverse_ref, low_ref, *more
):
    bias, gain, shift = (vec_ref[k : k + 1, :] for k in rows_of)
    norm, inverse = normalized(base_ref[...].astype(F32) + dot(left_ref[...], w_ref[...]) + bias)
    value = norm * gain + shift
    norm_ref[...] = norm
    inverse_ref[...] = inverse
    if more:
        more[0][...] = value
        low_ref[...] = value.astype(BF16)
    else:
        low_ref[...] = (value * mask_ref[...]).astype(BF16)


def add_norm(left, weight, base, mask, vec, rows_of, keep):
    rows, depth = left.shape
    wide = pl.BlockSpec((BLOCK, D), lambda i: (i, 0))
    thin = pl.BlockSpec((BLOCK, 1), lambda i: (i, 0))
    shape = jax.ShapeDtypeStruct((rows, D), F32)
    return pl.pallas_call(
        functools.partial(add_norm_kernel, rows_of),
        grid=(rows // BLOCK,),
        in_specs=[
            pl.BlockSpec((BLOCK, depth), lambda i: (i, 0)),
            pl.BlockSpec((depth, D), lambda i: (0, 0)),
            wide,
            thin,
            pl.BlockSpec((8, D), lambda i: (0, 0)),
        ],
        out_specs=[wide, thin, wide] + [wide] * keep,
        out_shape=[
            shape,
            jax.ShapeDtypeStruct((rows, 1), F32),
            jax.ShapeDtypeStruct((rows, D), BF16),
        ]
        + [shape] * keep,
        compiler_params=pltpu.CompilerParams(vmem_limit_bytes=VMEM_LIMIT),
        cost_estimate=pl.CostEstimate(
            flops=2 * rows * D * depth,
            bytes_accessed=2 * (rows + D) * depth + 12 * rows * D,
            transcendentals=0,
        ),
        name="add_norm",
    )(left, weight, base, mask, vec)


def normalized(values):
    centred = values - jnp.mean(values, axis=-1, keepdims=True)
    spread = jnp.mean(centred * centred, axis=-1, keepdims=True)
    inverse = lax.rsqrt(spread + norm_eps)
    return centred * inverse, inverse


def norm_back(grad, gain, norm, inverse):
    scaled = grad * gain
    return inverse * (
        scaled
        - jnp.mean(scaled, axis=-1, keepdims=True)
        - norm * jnp.mean(scaled * norm, axis=-1, keepdims=True)
    )


def per_device(places, *args):
    (
        question_in,
        passage_in,
        question_len,
        passage_len,
        positive,
        question_cot,
        passage_cot,
        w_joined,
        w_output,
        w_expand,
        w_reduce,
        vectors,
        b_expand,
    ) = args
    pb, pa = lax.axis_index("pb"), lax.axis_index("pa")
    z, core = pa // 2, pa % 2
    tower = z // places.half
    is_q = tower == 0
    chip = pb * places.nz + z
    masks = [places.stack_masks(side) for side in range(2)]
    slots_of = [sorted(range(places.chips), key=side.__getitem__) for side in masks]

    def of_core(rows_of):
        both = jnp.array(rows_of, jnp.int32)
        return (
            lax.dynamic_index_in_dim(both, core, 0, keepdims=False),
            lax.dynamic_index_in_dim(both, 1 - core, 0, keepdims=False),
        )

    side = jnp.full((places.chips,), core, jnp.int32)
    table = jnp.stack([x ^ chip for x in of_core(masks)] + [side]).astype(jnp.int32)
    slots = [x ^ lax.dynamic_index_in_dim(x, chip, 0, keepdims=False) for x in of_core(slots_of)]
    slots = jnp.stack(slots + [side]).astype(jnp.int32)
    share = w_joined.shape[1]

    small = jnp.concatenate(
        [
            vectors.transpose(0, 2, 1),
            b_expand.reshape(2, share, 4),
            jnp.zeros((2, share, 116), BF16),
        ],
        axis=2,
    )
    first = jnp.concatenate([w_joined, w_output, small], axis=2)
    second, third = w_expand, w_reduce

    class Gather:
        def __init__(self, piece):
            self.stack = lax.dynamic_index_in_dim(piece, tower, 0, keepdims=True)
            self.send = lax.dynamic_index_in_dim(piece, 1 - tower, 0, keepdims=True)
            self.held = None

        def join(self, got):
            self.stack = jnp.concatenate([self.stack, got], axis=0)
            self.send = self.stack

        def move(self, first, last):
            for step in range(first, last):
                self.join(places.swap(self.send, step))

        def mid(self):
            self.move(0, 1)

        def along_z(self):
            self.move(1, z_steps)

        def pb_first(self):
            self.move(z_steps, places.steps - 1)

        def pb_last(self):
            self.held = places.swap(self.send, places.steps - 1)

        def core_stack(self):
            self.other = places.swap_core(self.stack)

        def core_held(self):
            self.parts = [self.stack, self.held, self.other, places.swap_core(self.held)]

        def whole(self, segments):
            if self.stack.shape[1] % 8 == 0:
                return assemble(self.parts, table, segments)
            return assemble_plain(self.parts, table, segments)

    z_steps = 1 + len(bits_of(places.half))

    rows_q = question_in.reshape(-1, D)
    rows_p = passage_in.reshape(-1, D)
    own_rows = rows_q.shape[0]

    def sides(q_side, p_side):
        return jnp.where(is_q, q_side, p_side), jnp.where(is_q, p_side, q_side)

    lq, lp = question_in.shape[1], passage_in.shape[1]
    rows = 2 * own_rows

    def chunked(values, sixteenths):
        out, row = [], 0
        for part in sixteenths:
            step = values.shape[0] * part // 16
            out.append(values[row : row + step])
            row += step
        return out

    def hand(values):
        return [places.swap_tower(x) for x in values]

    per_q = rows // lq
    every = lp // lq
    per_p = rows // lp
    nq, np_ = question_in.shape[0], passage_in.shape[0]
    shift = 2 * places.half
    low_pa = pa % shift
    g1, g2, g3 = Gather(first), Gather(second), Gather(third)
    my_tokens, send_tokens = sides(rows_q, rows_p)
    tokens_out = chunked(send_tokens, (5, 6, 5))
    g1.mid()
    g1.send, tokens_out, question_cot, passage_cot = tie(
        g1.send, tokens_out, question_cot, passage_cot
    )
    g1.along_z()
    tokens_in = hand(tokens_out[:1])
    my_cot, send_cot = sides(question_cot.reshape(-1, D), passage_cot.reshape(-1, D))
    g1.send, g2.send, tokens_in, my_cot, send_cot = tie(
        g1.send, g2.send, tokens_in, my_cot, send_cot
    )
    g1.pb_first()
    g2.mid()
    g1.stack, g2.send, tokens_out = tie(g1.stack, g2.send, tokens_out)
    g1.send = g1.stack
    g1.pb_last()
    g1.core_stack()
    g2.along_z()
    tokens_in = tokens_in + hand(tokens_out[1:2])
    g1.held, g2.send, tokens_in, tokens_out, question_len, passage_len, positive = tie(
        g1.held, g2.send, tokens_in, tokens_out, question_len, passage_len, positive
    )
    g1.core_held()
    g2.pb_first()
    tokens_in = tokens_in + hand(tokens_out[2:])
    full_j, full_o, full_small = g1.whole([(0, 3 * D), (3 * D, D), (4 * D, 128)])
    full_j, full_o, full_small, g2.stack, g3.send, tokens_in = tie(
        full_j, full_o, full_small, g2.stack, g3.send, tokens_in
    )
    g2.send = g2.stack
    g2.pb_last()
    g2.core_stack()
    g3.mid()
    wj = full_j.reshape(D, 3 * D)
    wo = full_o.reshape(D, D)
    small = full_small.reshape(D, 128).astype(F32)
    vec = small[:, :8].T
    bias_e = small[:, 8:12].reshape(1, FF)
    bias_j = jnp.concatenate([vec[0], jnp.zeros((D,), F32), vec[1]])
    tokens = join([my_tokens] + tokens_in)
    qkv = project(tokens, wj, bias_j[None])

    cot_out = chunked(send_cot, (3, 3, 3, 4, 3))
    by_pa = positive.reshape(places.pa_n, nq)
    pair = [lax.dynamic_index_in_dim(by_pa, low_pa + k, 0, keepdims=False) for k in (0, shift)]
    pair = jnp.concatenate(pair)[None]
    wanted_rows = jnp.concatenate([pair // 16, pair % 16], axis=0).astype(BF16)
    wanted_rows = jnp.pad(wanted_rows, ((0, 0), (0, D - per_q)))
    valid_q = (jnp.arange(lq, dtype=jnp.int32)[None, :] < question_len[:, None]).astype(jnp.int32)
    valid_p = (jnp.arange(lp, dtype=jnp.int32)[None, :] < passage_len[:, None]).astype(jnp.int32)
    my_valid, send_valid = sides(valid_q.reshape(-1), valid_p.reshape(-1))
    valid = jnp.concatenate([my_valid, places.swap_tower(send_valid)])
    row_ids = jnp.arange(rows, dtype=jnp.int32)
    seq = jnp.where(is_q, row_ids // lq, row_ids // lp)
    qid = seq.reshape(rows, 1)
    kid = jnp.where(valid > 0, seq, -1).reshape(rows // BLOCK, 1, BLOCK)
    row_mask = valid.reshape(rows, 1).astype(F32)

    blocks = rows // BLOCK
    later = blocks // 2
    qkv, g3.send, cot_out = tie(qkv, g3.send, cot_out)
    g3.along_z()
    cot_in = hand(cot_out[:1])
    spread = attention(qkv, qid, kid, 0, later)
    spread, g2.held, g3.send, cot_in, cot_out = tie(spread, g2.held, g3.send, cot_in, cot_out)
    g2.core_held()
    g3.pb_first()
    cot_in = cot_in + hand(cot_out[1:2])
    context, probs = attention(qkv, qid, kid, later, blocks - later, tuple(spread))
    context, g2.parts, g3.stack, cot_in, cot_out = tie(context, g2.parts, g3.stack, cot_in, cot_out)
    g3.send = g3.stack
    g3.pb_last()
    g3.core_stack()
    cot_in = cot_in + hand(cot_out[2:3])
    (full_e,) = g2.whole([(0, FF)])
    we = full_e.reshape(D, FF)
    norm_one, inverse_one, mid_low, mid = add_norm(
        context, wo, tokens, row_mask, vec, (2, 3, 4), True
    )
    mid_low, we, cot_in, cot_out = tie(mid_low, we, cot_in, cot_out)
    cot_in = cot_in + hand(cot_out[3:4])
    gelu = expand(mid_low, we, bias_e, 0, 1)
    gelu, g3.held, g3.other, g3.stack, cot_in, cot_out = tie(
        gelu, g3.held, g3.other, g3.stack, cot_in, cot_out
    )
    g3.core_held()
    cot_in = cot_in + hand(cot_out[4:])
    active, slope = expand(mid_low, we, bias_e, 1, 1, tuple(gelu))
    active, g3.parts, cot_in = tie(active, g3.parts, cot_in)
    (full_r,) = g3.whole([(0, D)])
    wr = full_r.reshape(FF, D)
    norm_two, inverse_two, out = add_norm(active, wr, mid, row_mask, vec, (5, 6, 7), False)

    firsts = out.reshape(per_q, lq, D)[:, 0, :]
    others = places.swap_tower(firsts)
    cls_q = jnp.where(is_q, firsts, others)
    cls_p = jnp.where(is_q, others, firsts)[::every]
    pad = (-(per_q + per_p + 2)) % 8
    stack = jnp.concatenate([cls_q, cls_p, wanted_rows, jnp.zeros((pad, D), BF16)], axis=0)[None]
    pair_masks = [0]
    for bit in bits_of(places.half):
        got = lax.ppermute(stack, "pa", [(i, i ^ (2 * bit)) for i in range(places.pa_n)])
        stack = jnp.concatenate([stack, got], axis=0)
        pair_masks = pair_masks + [m ^ (2 * bit) for m in pair_masks]
    for bit in bits_of(places.pb_n):
        got = lax.ppermute(stack, "pb", [(i, i ^ bit) for i in range(places.pb_n)])
        stack = jnp.concatenate([stack, got], axis=0)
        pair_masks = pair_masks + [m ^ (bit * places.pa_n) for m in pair_masks]
    stack = jnp.concatenate([stack, places.swap_core(stack)], axis=0)
    pair_masks = pair_masks + [m ^ 1 for m in pair_masks]
    groups = len(pair_masks)
    me = pb * places.pa_n + low_pa
    place = jnp.array(pair_masks, jnp.int32) ^ me
    dev_p = jnp.stack([place + shift, place], axis=1)
    p_ids = (dev_p[:, :, None] * np_ + jnp.arange(np_, dtype=jnp.int32)).reshape(-1)
    digits = stack[:, per_q + per_p : per_q + per_p + 2, :per_q].astype(jnp.int32)
    wanted = (digits[:, 0] * 16 + digits[:, 1]).reshape(-1)

    all_q = stack[:, :per_q].reshape(groups * per_q, D)
    all_p = stack[:, per_q : per_q + per_p].reshape(groups * per_p, D)
    similarity = dot(all_q, all_p, ((1,), (1,))) * score_scale
    hot = (wanted[:, None] == p_ids[None, :]).astype(F32)
    top = jnp.max(similarity, axis=1, keepdims=True)
    grown = jnp.exp(similarity - top)
    total = jnp.sum(grown, axis=1, keepdims=True)
    own_sim = similarity[:per_q]
    loss = top[:per_q, 0] + jnp.log(total[:per_q, 0]) - jnp.sum(own_sim * hot[:per_q], axis=1)
    question_loss = lax.dynamic_slice_in_dim(loss, tower * nq, nq)
    d_sim = (loss_weight * (grown / total - hot)).astype(BF16)
    d_q = dot(d_sim[:per_q], all_p) * score_scale
    d_p = dot(d_sim[:, :per_p], all_q, ((0,), (0,))) * score_scale
    d_p = jnp.concatenate(
        [d_p.reshape(per_p, 1, D), jnp.zeros((per_p, every - 1, D), F32)], axis=1
    ).reshape(per_q, D)
    d_slot = jnp.where(is_q, d_q, d_p)

    d_second, d_reduced, sums_second = second_back(
        join([my_cot] + cot_in), d_slot, row_mask, norm_two, inverse_two, vec[6][None, :]
    )
    even = share % 8 == 0

    def gradient(left, right, **more):
        if left.shape[1] > D:
            return tall_grad(left, right, slots, places.nz)
        return weight_grad(left, right, slots, D, **more)

    def plain(left, right, extra=None):
        return grad_plain(left, right, table, extra)

    class Scatter:
        def __init__(self, mine, theirs):
            self.parts, self.theirs, self.send = [mine], theirs, None
            self.count = mine.shape[0]

        def cores(self):
            self.parts = self.parts + [places.swap_core(self.theirs)]

        def total(self, start, stop):
            out = self.parts[0][start:stop].astype(F32)
            for part in self.parts[1:]:
                out = out + part[start:stop].astype(F32)
            return out

        def prepare(self):
            self.send = self.total(self.count // 2, self.count).astype(BF16)

        def move(self, step):
            if self.send is None:
                self.prepare()
            self.parts = self.parts + [places.swap(self.send, step)]
            self.send = None
            self.count = self.count // 2

        def pb_first(self):
            self.move(places.steps - 1)

        def pb_rest(self):
            for step in range(places.steps - 2, z_steps - 1, -1):
                self.move(step)

        def along_z(self):
            for step in range(z_steps - 1, 0, -1):
                self.move(step)

        def mid(self):
            got = places.swap(self.total(1, 2).astype(BF16), 0).astype(F32)
            keep = self.total(0, 1)
            self.out = jnp.concatenate(
                [jnp.where(is_q, keep, got), jnp.where(is_q, got, keep)], axis=0
            )

    send_out = chunked(out[own_rows:], (4, 4, 4, 4))
    d_reduced, send_out = tie(d_reduced, send_out)
    got_out = hand(send_out[:1])
    sr = Scatter(*(gradient if even else plain)(active, d_reduced))
    sr.parts, sr.theirs, d_reduced, got_out, send_out = tie(
        sr.parts, sr.theirs, d_reduced, got_out, send_out
    )
    sr.cores()
    got_out = got_out + hand(send_out[1:2])
    d_expanded, g_bias_expand = hidden_grad(d_reduced, wr, slope)
    sr.parts, d_expanded, got_out, send_out = tie(sr.parts, d_expanded, got_out, send_out)
    sr.pb_first()
    got_out = got_out + hand(send_out[2:3])
    if even:
        partial = gradient(mid_low, d_expanded, room=D)
    else:
        partial = plain(mid_low, d_expanded)
    partial, d_expanded, got_out, send_out = tie(partial, d_expanded, got_out, send_out)
    got_out = got_out + hand(send_out[3:])
    d_first, d_attended, sums_first = first_back(
        d_expanded, we, d_second, norm_one, inverse_one, vec[3][None, :]
    )
    sr.parts, partial, d_attended, got_out = tie(sr.parts, partial, d_attended, got_out)
    sr.pb_rest()
    if even:
        partial = gradient(context, d_attended, into=tuple(partial))
    else:
        also = plain(context, d_attended)
        partial = [jnp.concatenate(x, axis=2) for x in zip(partial, also)]
    se = Scatter(*partial)
    se.parts, se.theirs, d_attended = tie(se.parts, se.theirs, d_attended)
    se.cores()
    d_context = dot(d_attended, wo, ((1,), (1,))).astype(BF16)
    d_joined, sums_one = attention_back(qkv, probs, d_context, later, blocks - later)
    sr.parts, se.parts, d_joined = tie(sr.parts, se.parts, d_joined)
    se.prepare()
    sr.prepare()
    sr.send, sr.parts, se.send, se.parts, d_joined = tie(
        sr.send, sr.parts, se.send, se.parts, d_joined
    )
    se.pb_first()
    sr.along_z()
    send_grad = (d_first[own_rows:] + dot(d_joined[own_rows:], wj, ((1,), (1,)))).astype(BF16)
    d_joined, send_grad = tie(d_joined, chunked(send_grad, (4, 3, 2, 7)))
    got_grad = hand(send_grad[:1])
    d_joined, sums_two = attention_back(qkv, probs, d_context, 0, later, d_joined)
    sr.parts, se.parts, d_joined, sums_two, got_grad, send_grad = tie(
        sr.parts, se.parts, d_joined, sums_two, got_grad, send_grad
    )
    se.prepare()
    se.send, se.parts, d_joined, send_grad = tie(se.send, se.parts, d_joined, send_grad)
    se.pb_rest()
    sr.mid()
    got_grad = got_grad + hand(send_grad[1:2])
    g_joined_bias = (sums_one + sums_two)[0]
    g_vec = jnp.concatenate(
        [
            g_joined_bias[None, :D],
            g_joined_bias[None, 2 * D :],
            sums_first[2:3],
            sums_first[:2],
            sums_second[2:3],
            sums_second[:2],
        ]
    )
    g_small = jnp.concatenate(
        [g_vec.T, g_bias_expand.reshape(D, 4), jnp.zeros((D, 116), F32)], axis=1
    )
    sj = Scatter(*(gradient if even else plain)(tokens, d_joined, extra=g_small))
    se.parts, sj.parts, sj.theirs, d_joined, got_grad, send_grad = tie(
        se.parts, sj.parts, sj.theirs, d_joined, got_grad, send_grad
    )
    sj.cores()
    se.along_z()
    got_grad = got_grad + hand(send_grad[2:3])
    own_grad = d_first[:own_rows] + dot(d_joined[:own_rows], wj, ((1,), (1,)))
    sj.parts, own_grad, got_grad, send_grad = tie(sj.parts, own_grad, got_grad, send_grad)
    sj.pb_first()
    got_grad = got_grad + hand(send_grad[3:])
    out_q, out_p = deal(tower.reshape(1), out, got_out)
    sj.parts, se.parts, out_q, out_p = tie(sj.parts, se.parts, out_q, out_p)
    sj.pb_rest()
    se.mid()
    sj.parts, se.out, sr.out, got_grad = tie(sj.parts, se.out, sr.out, got_grad)
    sj.along_z()
    grad_q, grad_p = deal(tower.reshape(1), own_grad, got_grad)
    sj.parts, grad_q, grad_p = tie(sj.parts, grad_q, grad_p)
    sj.mid()
    grad_joined = sj.out[:, :, : 3 * D]
    grad_expand, grad_output, grad_reduce = se.out[:, :, :FF], se.out[:, :, FF:], sr.out
    extra = sj.out[:, :, 3 * D :]
    grad_vectors = extra[:, :, :8].transpose(0, 2, 1)
    grad_b_expand = extra[:, :, 8:12].reshape(2, 4 * share)

    return (
        out_q.reshape(question_in.shape),
        out_p.reshape(passage_in.shape),
        question_loss,
        grad_q.reshape(question_in.shape),
        grad_p.reshape(passage_in.shape),
        grad_joined,
        grad_output,
        grad_expand,
        grad_reduce,
        grad_vectors,
        grad_b_expand,
    )


def solution(mesh):
    in_specs = (
        P(("pb", "pa"), None, None),
        P(("pb", "pa"), None, None),
        P(("pb", "pa")),
        P(("pb", "pa")),
        P("pb"),
        P(("pb", "pa"), None, None),
        P(("pb", "pa"), None, None),
        P(None, ("pb", "pa"), None),
        P(None, ("pb", "pa"), None),
        P(None, ("pb", "pa"), None),
        P(None, ("pb", "pa"), None),
        P(None, None, ("pb", "pa")),
        P(None, ("pb", "pa")),
    )
    out_specs = (
        P(("pb", "pa"), None, None),
        P(("pb", "pa"), None, None),
        P(("pb", "pa")),
        P(("pb", "pa"), None, None),
        P(("pb", "pa"), None, None),
        P(None, ("pb", "pa"), None),
        P(None, ("pb", "pa"), None),
        P(None, ("pb", "pa"), None),
        P(None, ("pb", "pa"), None),
        P(None, None, ("pb", "pa")),
        P(None, ("pb", "pa")),
    )
    return jax.shard_map(
        functools.partial(per_device, Places(mesh)),
        mesh=mesh,
        in_specs=in_specs,
        out_specs=out_specs,
        check_vma=False,
    )
```

```python
import functools

import jax
import jax.numpy as jnp
from jax import lax
from jax.experimental import pallas as pl
from jax.experimental.pallas import tpu as pltpu
from jax.sharding import PartitionSpec as P

D = 768
HEADS = 12
HDIM = 64
FF = 3072
AXES = ("pb", "pa")
BLOCK = 256

norm_eps = 1e-06
masked_score = -1000000000.0
score_scale = 0.0625
loss_weight = 16.0
head_scale = HDIM ** (-0.5)
F32 = jnp.float32
BF16 = jnp.bfloat16
VMEM_LIMIT = 56 * 1024 * 1024


def bits_of(count):
    return [1 << shift for shift in range(count.bit_length() - 1)]


class Places:
    def __init__(self, mesh):
        self.pb_n = mesh.shape["pb"]
        self.pa_n = mesh.shape["pa"]
        self.nz = self.pa_n // 2
        self.half = self.nz // 2
        self.chips = self.pb_n * self.nz
        pb_bits = bits_of(self.pb_n)
        turn = len(pb_bits) // 2
        low_z = [("z", bit) for bit in bits_of(self.half)]
        first = [("pb", bit) for bit in pb_bits]
        second = first[turn:] + first[:turn]
        self.orders = ([("z", self.half)] + low_z + first, [("z", self.half)] + low_z + second)
        self.steps = len(self.orders[0])

    def chip_mask(self, move):
        axis, bit = move
        return bit * self.nz if axis == "pb" else bit

    def stack_masks(self, core):
        masks = [0]
        for move in self.orders[core]:
            masks = masks + [mask ^ self.chip_mask(move) for mask in masks]
        return masks

    def pairs(self, step):
        out = []
        for pb in range(self.pb_n):
            for pa in range(self.pa_n):
                axis, bit = self.orders[pa % 2][step]
                to_pb, to_pa = (pb ^ bit, pa) if axis == "pb" else (pb, pa ^ (2 * bit))
                out.append((pb * self.pa_n + pa, to_pb * self.pa_n + to_pa))
        return out

    def swap(self, values, step):
        return lax.ppermute(values, AXES, self.pairs(step))

    def swap_core(self, values):
        return lax.ppermute(values, "pa", [(i, i ^ 1) for i in range(self.pa_n)])

    def swap_tower(self, values):
        return lax.ppermute(values, "pa", [(i, i ^ (2 * self.half)) for i in range(self.pa_n)])


def dot(left, right, dims=((1,), (0,))):
    return lax.dot_general(left, right, (dims, ((), ())), preferred_element_type=F32)


def tie(*values):
    return lax.optimization_barrier(values)


def assemble_kernel(segments, idx_ref, *refs):
    count = len(segments)
    sources, outs = refs[:4], refs[4 : 4 + count]
    buffer, in_sem, out_sem = refs[4 + count :]
    core = idx_ref[2, 0]
    part = sources[0].shape[0]
    loads = [
        pltpu.make_async_copy(source, buffer.at[pl.ds(k * part, part)], in_sem.at[k])
        for k, source in enumerate(sources)
    ]
    for load in loads:
        load.start()
    stores = []
    for k in range(4):
        loads[k].wait()
        half = core if k < 2 else 1 - core
        for j in range(part):
            slot = k * part + j
            place = idx_ref[k // 2, (k % 2) * part + j]
            for s, (start, width) in enumerate(segments):
                store = pltpu.make_async_copy(
                    buffer.at[slot, :, pl.ds(start, width)],
                    outs[s].at[place, half],
                    out_sem.at[s, slot],
                )
                store.start()
                stores.append(store)
    for store in stores:
        store.wait()


def assemble(parts, table, segments):
    part, rows, width = parts[0].shape
    chips = 2 * part
    shapes = [jax.ShapeDtypeStruct((chips, 2, rows, w), BF16) for _, w in segments]
    return pl.pallas_call(
        functools.partial(assemble_kernel, segments),
        out_shape=shapes,
        in_specs=[pl.BlockSpec(memory_space=pltpu.SMEM)] + [pl.BlockSpec(memory_space=pl.ANY)] * 4,
        out_specs=[pl.BlockSpec(memory_space=pl.ANY)] * len(segments),
        scratch_shapes=[
            pltpu.VMEM((2 * chips, rows, width), BF16),
            pltpu.SemaphoreType.DMA((4,)),
            pltpu.SemaphoreType.DMA((len(segments), 2 * chips)),
        ],
        compiler_params=pltpu.CompilerParams(vmem_limit_bytes=VMEM_LIMIT),
        cost_estimate=pl.CostEstimate(
            flops=0, bytes_accessed=4 * 2 * chips * rows * width, transcendentals=0
        ),
        name="assemble",
    )(table, *parts)


def assemble_plain(parts, table, segments):
    own = jnp.take(jnp.concatenate(parts[:2], axis=0), jnp.argsort(table[0]), axis=0)
    other = jnp.take(jnp.concatenate(parts[2:], axis=0), jnp.argsort(table[1]), axis=0)
    first = table[2, 0] == 0
    both = jnp.stack([jnp.where(first, own, other), jnp.where(first, other, own)], axis=1)
    return [both[..., start : start + w] for start, w in segments]


def split_slabs(acc, core, chips, mine_ref, theirs_ref, cols, within):
    rows = acc.shape[0] // (2 * chips)
    for s in range(chips):
        low = acc[2 * s * rows : (2 * s + 1) * rows]
        high = acc[(2 * s + 1) * rows : (2 * s + 2) * rows]
        mine, theirs = within(s)
        mine_ref[mine, :, cols] = jnp.where(core == 0, low, high).astype(BF16)
        theirs_ref[theirs, :, cols] = jnp.where(core == 0, high, low).astype(BF16)


def weight_grad_kernel(chips, extra, table_ref, left_ref, right_ref, *refs):
    mine_ref, theirs_ref = refs[-2:]
    core = table_ref[2, 0]
    acc = dot(left_ref[...], right_ref[...], ((0,), (0,)))
    width = acc.shape[1]

    def within(s):
        return table_ref[0, s], table_ref[1, s]

    if not extra:
        split_slabs(acc, core, chips, mine_ref, theirs_ref, slice(None), within)
        return
    step = pl.program_id(0)
    cols = pl.ds(pl.multiple_of(step * width, 128), width)
    split_slabs(acc, core, chips, mine_ref, theirs_ref, cols, within)

    @pl.when(step == 0)
    def _():
        tail = pl.ds(mine_ref.shape[2] - 128, 128)
        split_slabs(refs[0][...], core, chips, mine_ref, theirs_ref, tail, within)


def weight_grad(left, right, slots, tile, extra=None, room=0, into=()):
    rows, height = left.shape
    width = right.shape[1]
    chips = slots.shape[1]
    slab = height // (2 * chips)
    total = width + (room if extra is None else extra.shape[1])
    first = 0
    if into:
        total = into[0].shape[2]
        first = (total - width) // tile
    block = (chips, slab, total if extra is not None else tile)
    place = (lambda j, t: (0, 0, 0)) if extra is not None else (lambda j, t: (0, 0, j + first))
    return pl.pallas_call(
        functools.partial(weight_grad_kernel, chips, extra is not None),
        grid_spec=pltpu.PrefetchScalarGridSpec(
            num_scalar_prefetch=1,
            grid=(width // tile,),
            in_specs=[
                pl.BlockSpec((rows, height), lambda j, t: (0, 0)),
                pl.BlockSpec((rows, tile), lambda j, t: (0, j)),
            ]
            + ([] if extra is None else [pl.BlockSpec((height, 128), lambda j, t: (0, 0))])
            + [pl.BlockSpec(memory_space=pl.ANY)] * len(into),
            out_specs=[pl.BlockSpec(block, place)] * 2,
        ),
        out_shape=[jax.ShapeDtypeStruct((chips, slab, total), BF16)] * 2,
        input_output_aliases={3: 0, 4: 1} if into else {},
        compiler_params=pltpu.CompilerParams(vmem_limit_bytes=VMEM_LIMIT),
        cost_estimate=pl.CostEstimate(
            flops=2 * rows * height * width,
            bytes_accessed=2 * (rows * (height + width) + height * width),
            transcendentals=0,
        ),
        name="weight_grad",
    )(slots, left, right, *([] if extra is None else [extra]), *into)


def tall_grad_kernel(chips, table_ref, left_ref, right_ref, mine_ref, theirs_ref):
    core = table_ref[2, 0]
    acc = dot(left_ref[...], right_ref[...], ((0,), (0,)))
    base = pl.program_id(0) * chips

    def within(s):
        return table_ref[0, base + s] % chips, table_ref[1, base + s] % chips

    split_slabs(acc, core, chips, mine_ref, theirs_ref, slice(None), within)


def tall_grad(left, right, slots, column):
    rows, height = left.shape
    width = right.shape[1]
    chips = slots.shape[1]
    slab = height // (2 * chips)
    tile = height // chips * column
    return pl.pallas_call(
        functools.partial(tall_grad_kernel, column),
        grid_spec=pltpu.PrefetchScalarGridSpec(
            num_scalar_prefetch=1,
            grid=(chips // column,),
            in_specs=[
                pl.BlockSpec((rows, tile), lambda i, t: (0, i)),
                pl.BlockSpec((rows, width), lambda i, t: (0, 0)),
            ],
            out_specs=[
                pl.BlockSpec((column, slab, width), lambda i, t: (t[0, i * column] // column, 0, 0)),
                pl.BlockSpec((column, slab, width), lambda i, t: (t[1, i * column] // column, 0, 0)),
            ],
        ),
        out_shape=[jax.ShapeDtypeStruct((chips, slab, width), BF16)] * 2,
        compiler_params=pltpu.CompilerParams(vmem_limit_bytes=VMEM_LIMIT),
        cost_estimate=pl.CostEstimate(
            flops=2 * rows * height * width,
            bytes_accessed=2 * (rows * (height + width) + height * width),
            transcendentals=0,
        ),
        name="tall_grad",
    )(slots, left, right)


def grad_plain(left, right, table, extra=None):
    full = dot(left, right, ((0,), (0,)))
    if extra is not None:
        full = jnp.concatenate([full, extra], axis=1)
    chips = table.shape[1]
    full = full.astype(BF16).reshape(chips, 2, full.shape[0] // (2 * chips), full.shape[1])
    core = table[2, 0]
    mine = lax.dynamic_index_in_dim(full, core, 1, keepdims=False)
    theirs = lax.dynamic_index_in_dim(full, 1 - core, 1, keepdims=False)
    return jnp.take(mine, table[0], axis=0), jnp.take(theirs, table[1], axis=0)


def hidden_grad_kernel(grad_ref, w_ref, slope_ref, out_ref, sum_ref):
    grad = dot(grad_ref[...], w_ref[...], ((1,), (1,))) * slope_ref[...].astype(F32)
    low = grad.astype(BF16)
    out_ref[...] = low
    sum_ref[...] = jnp.sum(low.astype(F32), axis=0, keepdims=True)


def hidden_grad(grad, w_reduce, slope):
    rows, tile = grad.shape[0], 512
    return pl.pallas_call(
        hidden_grad_kernel,
        grid=(FF // tile,),
        in_specs=[
            pl.BlockSpec((rows, D), lambda j: (0, 0)),
            pl.BlockSpec((tile, D), lambda j: (j, 0)),
            pl.BlockSpec((rows, tile), lambda j: (0, j)),
        ],
        out_specs=[
            pl.BlockSpec((rows, tile), lambda j: (0, j)),
            pl.BlockSpec((1, tile), lambda j: (0, j)),
        ],
        out_shape=[
            jax.ShapeDtypeStruct((rows, FF), BF16),
            jax.ShapeDtypeStruct((1, FF), F32),
        ],
        compiler_params=pltpu.CompilerParams(vmem_limit_bytes=VMEM_LIMIT),
        cost_estimate=pl.CostEstimate(
            flops=2 * rows * D * FF,
            bytes_accessed=2 * (rows * D + D * FF + 2 * rows * FF),
            transcendentals=0,
        ),
        name="hidden_grad",
    )(grad, w_reduce, slope)


def attention_kernel(qkv_ref, qid_ref, kid_ref, context_ref, probs_ref):
    allowed = qid_ref[...] == kid_ref[0]
    lane = lax.broadcasted_iota(jnp.int32, (BLOCK, 128), 1)
    zero = jnp.zeros((BLOCK, 128), BF16)
    for pair in range(HEADS // 2):
        queries = qkv_ref[:, pair * 128 : pair * 128 + 128]
        keys = qkv_ref[:, D + pair * 128 : D + pair * 128 + 128]
        values = qkv_ref[:, 2 * D + pair * 128 : 2 * D + pair * 128 + 128]
        outs = []
        for side in range(2):
            mine = (lane < HDIM) if side == 0 else (lane >= HDIM)
            scores = dot(queries, jnp.where(mine, keys, zero), ((1,), (1,))) * head_scale
            scores = jnp.where(allowed, scores, masked_score)
            top = jnp.max(scores, axis=1, keepdims=True)
            grown = jnp.exp(scores - top)
            total = jnp.sum(grown, axis=1, keepdims=True)
            probs = (grown * (1.0 / total)).astype(BF16)
            probs_ref[0, 2 * pair + side] = probs
            outs.append(dot(probs, values))
        context_ref[:, pair * 128 : pair * 128 + 128] = jnp.where(
            lane < HDIM, outs[0], outs[1]
        ).astype(BF16)


def attention(qkv, qid, kid):
    rows = qkv.shape[0]
    blocks = rows // BLOCK
    return pl.pallas_call(
        attention_kernel,
        grid=(blocks,),
        in_specs=[
            pl.BlockSpec((BLOCK, 3 * D), lambda i: (i, 0)),
            pl.BlockSpec((BLOCK, 1), lambda i: (i, 0)),
            pl.BlockSpec((1, 1, BLOCK), lambda i: (i, 0, 0)),
        ],
        out_specs=[
            pl.BlockSpec((BLOCK, D), lambda i: (i, 0)),
            pl.BlockSpec((1, HEADS, BLOCK, BLOCK), lambda i: (i, 0, 0, 0)),
        ],
        out_shape=[
            jax.ShapeDtypeStruct((rows, D), BF16),
            jax.ShapeDtypeStruct((blocks, HEADS, BLOCK, BLOCK), BF16),
        ],
        compiler_params=pltpu.CompilerParams(vmem_limit_bytes=VMEM_LIMIT),
        cost_estimate=pl.CostEstimate(
            flops=4 * rows * BLOCK * D * 2,
            bytes_accessed=rows * (4 * D + HEADS * BLOCK) * 2,
            transcendentals=rows * HEADS * BLOCK,
        ),
        name="attention",
    )(qkv, qid, kid)


def attention_back_kernel(qkv_ref, probs_ref, grad_ref, out_ref, sum_ref):
    lane = lax.broadcasted_iota(jnp.int32, (BLOCK, 128), 1)
    zero = jnp.zeros((BLOCK, 128), BF16)

    def at(pair, start=0):
        return pl.ds(pl.multiple_of(start + pair * 128, 128), 128)

    def some(step, carry):
        for k in range(2):
            pair = step * 2 + k
            cols = at(pair)
            queries = qkv_ref[:, at(pair)]
            keys = qkv_ref[:, at(pair, D)]
            values = qkv_ref[:, at(pair, 2 * D)]
            grad = grad_ref[:, cols]
            d_q, d_k, d_v = [], [], []
            for side in range(2):
                mine = (lane < HDIM) if side == 0 else (lane >= HDIM)
                low = probs_ref[0, 2 * pair + side]
                d_probs = dot(jnp.where(mine, grad, zero), values, ((1,), (1,)))
                d_v.append(dot(low, grad, ((0,), (0,))))
                probs = low.astype(F32)
                row_dot = jnp.sum(d_probs * probs, axis=1, keepdims=True)
                d_scores = (probs * (d_probs - row_dot)).astype(BF16)
                d_q.append(dot(d_scores, keys))
                d_k.append(dot(d_scores, queries, ((0,), (0,))))
            first = lane < HDIM
            out_ref[:, at(pair)] = (
                jnp.where(first, d_q[0], d_q[1]) * head_scale
            ).astype(BF16)
            out_ref[:, at(pair, D)] = (
                jnp.where(first, d_k[0], d_k[1]) * head_scale
            ).astype(BF16)
            out_ref[:, at(pair, 2 * D)] = jnp.where(
                first, d_v[0], d_v[1]
            ).astype(BF16)
        return carry

    lax.fori_loop(0, HEADS // 2 // 2, some, 0)
    sums = jnp.sum(out_ref[...].astype(F32), axis=0, keepdims=True)

    @pl.when(pl.program_id(0) == 0)
    def _():
        sum_ref[...] = sums

    @pl.when(pl.program_id(0) > 0)
    def _():
        sum_ref[...] += sums


def attention_back_more_kernel(qkv_ref, probs_ref, grad_ref, _, out_ref, sum_ref):
    attention_back_kernel(qkv_ref, probs_ref, grad_ref, out_ref, sum_ref)


def attention_back(qkv, probs, grad_context, start, count, into=None):
    rows = qkv.shape[0]
    more = into is not None
    return pl.pallas_call(
        attention_back_more_kernel if more else attention_back_kernel,
        grid=(count,),
        in_specs=[
            pl.BlockSpec((BLOCK, 3 * D), lambda i: (i + start, 0)),
            pl.BlockSpec((1, HEADS, BLOCK, BLOCK), lambda i: (i + start, 0, 0, 0)),
            pl.BlockSpec((BLOCK, D), lambda i: (i + start, 0)),
        ]
        + ([pl.BlockSpec(memory_space=pl.ANY)] if more else []),
        out_specs=[
            pl.BlockSpec((BLOCK, 3 * D), lambda i: (i + start, 0)),
            pl.BlockSpec((1, 3 * D), lambda i: (0, 0)),
        ],
        out_shape=[
            jax.ShapeDtypeStruct((rows, 3 * D), BF16),
            jax.ShapeDtypeStruct((1, 3 * D), F32),
        ],
        input_output_aliases={3: 0} if more else {},
        compiler_params=pltpu.CompilerParams(vmem_limit_bytes=VMEM_LIMIT),
        cost_estimate=pl.CostEstimate(
            flops=8 * count * BLOCK * BLOCK * D * 2,
            bytes_accessed=count * BLOCK * (7 * D + HEADS * BLOCK) * 2,
            transcendentals=0,
        ),
        name="attention_back",
    )(qkv, probs, grad_context, *([into] if more else []))


def join_kernel(*refs):
    row = 0
    for piece in refs[:-1]:
        rows = piece.shape[0]
        refs[-1][row : row + rows, :] = piece[...]
        row += rows


def join(pieces):
    rows, width = sum(x.shape[0] for x in pieces), pieces[0].shape[1]
    return pl.pallas_call(
        join_kernel,
        grid=(1,),
        in_specs=[pl.BlockSpec(x.shape, lambda i: (0, 0)) for x in pieces],
        out_specs=pl.BlockSpec((rows, width), lambda i: (0, 0)),
        out_shape=jax.ShapeDtypeStruct((rows, width), pieces[0].dtype),
        compiler_params=pltpu.CompilerParams(vmem_limit_bytes=VMEM_LIMIT),
        cost_estimate=pl.CostEstimate(
            flops=0, bytes_accessed=4 * rows * width, transcendentals=0
        ),
        name="join",
    )(*pieces)


def deal_kernel(tower_ref, own_ref, *refs):
    pieces, (q_ref, p_ref) = refs[:-2], refs[-2:]

    def give(own_out, other_out):
        own_out[...] = own_ref[...]
        row = 0
        for piece in pieces:
            rows = piece.shape[0]
            other_out[row : row + rows, :] = piece[...].astype(other_out.dtype)
            row += rows

    @pl.when(tower_ref[0] == 0)
    def _():
        give(q_ref, p_ref)

    @pl.when(tower_ref[0] != 0)
    def _():
        give(p_ref, q_ref)


def deal(tower, own, pieces):
    rows, width = sum(x.shape[0] for x in pieces), own.shape[1]
    shape = jax.ShapeDtypeStruct((rows, width), own.dtype)
    return pl.pallas_call(
        deal_kernel,
        grid=(1,),
        in_specs=[
            pl.BlockSpec(memory_space=pltpu.SMEM),
            pl.BlockSpec((rows, width), lambda i: (0, 0)),
        ]
        + [pl.BlockSpec(x.shape, lambda i: (0, 0)) for x in pieces],
        out_specs=[pl.BlockSpec((rows, width), lambda i: (0, 0))] * 2,
        out_shape=[shape] * 2,
        compiler_params=pltpu.CompilerParams(vmem_limit_bytes=VMEM_LIMIT),
        cost_estimate=pl.CostEstimate(
            flops=0, bytes_accessed=12 * rows * width, transcendentals=0
        ),
        name="deal",
    )(tower, own, *pieces)


def add_sums(sum_ref, values):
    total = jnp.concatenate(
        [jnp.sum(x, axis=0, keepdims=True) for x in values]
        + [jnp.zeros((8 - len(values), values[0].shape[1]), F32)],
        axis=0,
    )

    @pl.when(pl.program_id(0) == 0)
    def _():
        sum_ref[...] = total

    @pl.when(pl.program_id(0) > 0)
    def _():
        sum_ref[...] += total


def second_back_kernel(
    cot_ref, slot_ref, mask_ref, norm_ref, inverse_ref, gain_ref, grad_ref, low_ref, sum_ref
):
    group = slot_ref.shape[1]
    cot = cot_ref[...].astype(F32).reshape(group, BLOCK // group, D)
    first = lax.broadcasted_iota(jnp.int32, cot.shape, 1) == 0
    grad = cot + jnp.where(first, slot_ref[0][:, None, :], 0.0)
    grad = grad.reshape(BLOCK, D) * mask_ref[...]
    norm = norm_ref[...]
    second = norm_back(grad, gain_ref[...], norm, inverse_ref[...])
    low = second.astype(BF16)
    grad_ref[...] = second
    low_ref[...] = low
    add_sums(sum_ref, [grad * norm, grad, low.astype(F32)])


def second_back(cot, d_slot, mask, norm, inverse, gain):
    rows = cot.shape[0]
    blocks = rows // BLOCK
    wide = pl.BlockSpec((BLOCK, D), lambda i: (i, 0))
    thin = pl.BlockSpec((BLOCK, 1), lambda i: (i, 0))
    group = d_slot.shape[0] // blocks
    return pl.pallas_call(
        second_back_kernel,
        grid=(blocks,),
        in_specs=[
            wide,
            pl.BlockSpec((1, group, D), lambda i: (i, 0, 0)),
            thin,
            wide,
            thin,
            pl.BlockSpec((1, D), lambda i: (0, 0)),
        ],
        out_specs=[wide, wide, pl.BlockSpec((8, D), lambda i: (0, 0))],
        out_shape=[
            jax.ShapeDtypeStruct((rows, D), F32),
            jax.ShapeDtypeStruct((rows, D), BF16),
            jax.ShapeDtypeStruct((8, D), F32),
        ],
        compiler_params=pltpu.CompilerParams(vmem_limit_bytes=VMEM_LIMIT),
        cost_estimate=pl.CostEstimate(
            flops=20 * rows * D, bytes_accessed=12 * rows * D, transcendentals=0
        ),
        name="second_back",
    )(cot, d_slot.reshape(blocks, group, D), mask, norm, inverse, gain)


def first_back_kernel(
    hidden_ref, w_ref, second_ref, norm_ref, inverse_ref, gain_ref, grad_ref, low_ref, sum_ref
):
    grad = second_ref[...] + dot(hidden_ref[...], w_ref[...], ((1,), (1,)))
    norm = norm_ref[...]
    first = norm_back(grad, gain_ref[...], norm, inverse_ref[...])
    low = first.astype(BF16)
    grad_ref[...] = first
    low_ref[...] = low
    add_sums(sum_ref, [grad * norm, grad, low.astype(F32)])


def first_back(d_expanded, w_expand, d_second, norm, inverse, gain):
    rows = d_expanded.shape[0]
    wide = pl.BlockSpec((BLOCK, D), lambda i: (i, 0))
    return pl.pallas_call(
        first_back_kernel,
        grid=(rows // BLOCK,),
        in_specs=[
            pl.BlockSpec((BLOCK, FF), lambda i: (i, 0)),
            pl.BlockSpec((D, FF), lambda i: (0, 0)),
            wide,
            wide,
            pl.BlockSpec((BLOCK, 1), lambda i: (i, 0)),
            pl.BlockSpec((1, D), lambda i: (0, 0)),
        ],
        out_specs=[wide, wide, pl.BlockSpec((8, D), lambda i: (0, 0))],
        out_shape=[
            jax.ShapeDtypeStruct((rows, D), F32),
            jax.ShapeDtypeStruct((rows, D), BF16),
            jax.ShapeDtypeStruct((8, D), F32),
        ],
        compiler_params=pltpu.CompilerParams(vmem_limit_bytes=VMEM_LIMIT),
        cost_estimate=pl.CostEstimate(
            flops=2 * rows * D * FF,
            bytes_accessed=2 * (rows * FF + D * FF) + 14 * rows * D,
            transcendentals=0,
        ),
        name="first_back",
    )(d_expanded, w_expand, d_second, norm, inverse, gain)


def expand_kernel(mid_ref, w_ref, b_ref, active_ref, slope_ref):
    expanded = dot(mid_ref[...], w_ref[...]) + b_ref[...]
    phi = 0.5 + 0.5 * lax.erf(expanded * 0.7071067811865476)
    density = jnp.exp(expanded * expanded * -0.5) * 0.3989422804014327
    active_ref[...] = (expanded * phi).astype(BF16)
    slope_ref[...] = (phi + expanded * density).astype(BF16)


def expand_more_kernel(mid_ref, w_ref, b_ref, _, __, active_ref, slope_ref):
    expand_kernel(mid_ref, w_ref, b_ref, active_ref, slope_ref)


def expand(mid_low, w_expand, b_expand, start, count, into=()):
    rows = mid_low.shape[0]
    tile_r, tile_f = 256, FF // 2
    return pl.pallas_call(
        expand_more_kernel if into else expand_kernel,
        grid=(count, rows // tile_r),
        in_specs=[
            pl.BlockSpec((tile_r, D), lambda j, i: (i, 0)),
            pl.BlockSpec((D, tile_f), lambda j, i: (0, j + start)),
            pl.BlockSpec((1, tile_f), lambda j, i: (0, j + start)),
        ]
        + [pl.BlockSpec(memory_space=pl.ANY)] * len(into),
        out_specs=[
            pl.BlockSpec((tile_r, tile_f), lambda j, i: (i, j + start)),
            pl.BlockSpec((tile_r, tile_f), lambda j, i: (i, j + start)),
        ],
        out_shape=[jax.ShapeDtypeStruct((rows, FF), BF16)] * 2,
        input_output_aliases={3: 0, 4: 1} if into else {},
        compiler_params=pltpu.CompilerParams(vmem_limit_bytes=VMEM_LIMIT),
        cost_estimate=pl.CostEstimate(
            flops=2 * rows * D * count * tile_f,
            bytes_accessed=2 * (rows * D + D * count * tile_f + 2 * rows * count * tile_f),
            transcendentals=2 * rows * count * tile_f,
        ),
        name="expand",
    )(mid_low, w_expand, b_expand, *into)


def token_grad_kernel(grad_ref, w_ref, first_ref, *outs):
    block = first_ref[...] + dot(grad_ref[...], w_ref[...], ((1,), (1,)))
    block = block.astype(outs[0].dtype)
    step, start = pl.program_id(0), 0
    for out in outs:
        stop = start + out.shape[0]
        for k in range(start // BLOCK, (stop - 1) // BLOCK + 1):
            low, high = max(start, k * BLOCK), min(stop, (k + 1) * BLOCK)

            @pl.when(step == k)
            def _(out=out, k=k, low=low, high=high, start=start):
                out[low - start : high - start, :] = block[low - k * BLOCK : high - k * BLOCK]

        start = stop


def token_grad(d_joined, weight, d_first, start, pieces, dtype):
    width = weight.shape[1]
    first, count = start // BLOCK, sum(pieces) // BLOCK
    return pl.pallas_call(
        token_grad_kernel,
        grid=(count,),
        in_specs=[
            pl.BlockSpec((BLOCK, width), lambda i: (i + first, 0)),
            pl.BlockSpec((D, width), lambda i: (0, 0)),
            pl.BlockSpec((BLOCK, D), lambda i: (i + first, 0)),
        ],
        out_specs=[pl.BlockSpec((n, D), lambda i: (0, 0)) for n in pieces],
        out_shape=[jax.ShapeDtypeStruct((n, D), dtype) for n in pieces],
        compiler_params=pltpu.CompilerParams(vmem_limit_bytes=VMEM_LIMIT),
        cost_estimate=pl.CostEstimate(
            flops=2 * count * BLOCK * D * width,
            bytes_accessed=2 * D * width + count * BLOCK * (2 * width + 6 * D),
            transcendentals=0,
        ),
        name="token_grad",
    )(d_joined, weight, d_first)


def project_kernel(tokens_ref, w_ref, b_ref, out_ref):
    out_ref[...] = (dot(tokens_ref[...], w_ref[...]) + b_ref[...]).astype(BF16)


def project(tokens, weight, bias):
    rows, width = tokens.shape[0], weight.shape[1]
    return pl.pallas_call(
        project_kernel,
        grid=(rows // BLOCK,),
        in_specs=[
            pl.BlockSpec((BLOCK, D), lambda i: (i, 0)),
            pl.BlockSpec((D, width), lambda i: (0, 0)),
            pl.BlockSpec((1, width), lambda i: (0, 0)),
        ],
        out_specs=pl.BlockSpec((BLOCK, width), lambda i: (i, 0)),
        out_shape=jax.ShapeDtypeStruct((rows, width), BF16),
        compiler_params=pltpu.CompilerParams(vmem_limit_bytes=VMEM_LIMIT),
        cost_estimate=pl.CostEstimate(
            flops=2 * rows * D * width,
            bytes_accessed=2 * (rows * (D + width) + D * width),
            transcendentals=0,
        ),
        name="project",
    )(tokens, weight, bias)


def add_norm_kernel(
    rows_of, left_ref, w_ref, base_ref, mask_ref, vec_ref, norm_ref, inverse_ref, low_ref, *more
):
    bias, gain, shift = (vec_ref[k : k + 1, :] for k in rows_of)
    norm, inverse = normalized(base_ref[...].astype(F32) + dot(left_ref[...], w_ref[...]) + bias)
    value = norm * gain + shift
    norm_ref[...] = norm
    inverse_ref[...] = inverse
    if more:
        more[0][...] = value
        low_ref[...] = value.astype(BF16)
    else:
        low_ref[...] = (value * mask_ref[...]).astype(BF16)


def add_norm(left, weight, base, mask, vec, rows_of, keep):
    rows, depth = left.shape
    wide = pl.BlockSpec((BLOCK, D), lambda i: (i, 0))
    thin = pl.BlockSpec((BLOCK, 1), lambda i: (i, 0))
    shape = jax.ShapeDtypeStruct((rows, D), F32)
    return pl.pallas_call(
        functools.partial(add_norm_kernel, rows_of),
        grid=(rows // BLOCK,),
        in_specs=[
            pl.BlockSpec((BLOCK, depth), lambda i: (i, 0)),
            pl.BlockSpec((depth, D), lambda i: (0, 0)),
            wide,
            thin,
            pl.BlockSpec((8, D), lambda i: (0, 0)),
        ],
        out_specs=[wide, thin, wide] + [wide] * keep,
        out_shape=[
            shape,
            jax.ShapeDtypeStruct((rows, 1), F32),
            jax.ShapeDtypeStruct((rows, D), BF16),
        ]
        + [shape] * keep,
        compiler_params=pltpu.CompilerParams(vmem_limit_bytes=VMEM_LIMIT),
        cost_estimate=pl.CostEstimate(
            flops=2 * rows * D * depth,
            bytes_accessed=2 * (rows + D) * depth + 12 * rows * D,
            transcendentals=0,
        ),
        name="add_norm",
    )(left, weight, base, mask, vec)


def normalized(values):
    centred = values - jnp.mean(values, axis=-1, keepdims=True)
    spread = jnp.mean(centred * centred, axis=-1, keepdims=True)
    inverse = lax.rsqrt(spread + norm_eps)
    return centred * inverse, inverse


def norm_back(grad, gain, norm, inverse):
    scaled = grad * gain
    return inverse * (
        scaled
        - jnp.mean(scaled, axis=-1, keepdims=True)
        - norm * jnp.mean(scaled * norm, axis=-1, keepdims=True)
    )


def per_device(places, *args):
    (
        question_in,
        passage_in,
        question_len,
        passage_len,
        positive,
        question_cot,
        passage_cot,
        w_joined,
        w_output,
        w_expand,
        w_reduce,
        vectors,
        b_expand,
    ) = args
    pb, pa = lax.axis_index("pb"), lax.axis_index("pa")
    z, core = pa // 2, pa % 2
    tower = z // places.half
    is_q = tower == 0
    chip = pb * places.nz + z
    masks = [places.stack_masks(side) for side in range(2)]
    slots_of = [sorted(range(places.chips), key=side.__getitem__) for side in masks]

    def of_core(rows_of):
        both = jnp.array(rows_of, jnp.int32)
        return (
            lax.dynamic_index_in_dim(both, core, 0, keepdims=False),
            lax.dynamic_index_in_dim(both, 1 - core, 0, keepdims=False),
        )

    side = jnp.full((places.chips,), core, jnp.int32)
    table = jnp.stack([x ^ chip for x in of_core(masks)] + [side]).astype(jnp.int32)
    slots = [x ^ lax.dynamic_index_in_dim(x, chip, 0, keepdims=False) for x in of_core(slots_of)]
    slots = jnp.stack(slots + [side]).astype(jnp.int32)
    share = w_joined.shape[1]

    small = jnp.concatenate(
        [
            vectors.transpose(0, 2, 1),
            b_expand.reshape(2, share, 4),
            jnp.zeros((2, share, 116), BF16),
        ],
        axis=2,
    )
    first = jnp.concatenate([w_joined, w_output, small], axis=2)
    second, third = w_expand, w_reduce

    class Gather:
        def __init__(self, piece):
            self.stack = lax.dynamic_index_in_dim(piece, tower, 0, keepdims=True)
            self.send = lax.dynamic_index_in_dim(piece, 1 - tower, 0, keepdims=True)
            self.held = None

        def join(self, got):
            self.stack = jnp.concatenate([self.stack, got], axis=0)
            self.send = self.stack

        def move(self, first, last):
            for step in range(first, last):
                self.join(places.swap(self.send, step))

        def mid(self):
            self.move(0, 1)

        def along_z(self):
            self.move(1, z_steps)

        def pb_first(self):
            self.move(z_steps, places.steps - 1)

        def pb_last(self):
            self.held = places.swap(self.send, places.steps - 1)

        def core_stack(self):
            self.other = places.swap_core(self.stack)

        def core_held(self):
            self.parts = [self.stack, self.held, self.other, places.swap_core(self.held)]

        def whole(self, segments):
            if self.stack.shape[1] % 8 == 0:
                return assemble(self.parts, table, segments)
            return assemble_plain(self.parts, table, segments)

    z_steps = 1 + len(bits_of(places.half))

    rows_q = question_in.reshape(-1, D)
    rows_p = passage_in.reshape(-1, D)
    own_rows = rows_q.shape[0]

    def sides(q_side, p_side):
        return jnp.where(is_q, q_side, p_side), jnp.where(is_q, p_side, q_side)

    lq, lp = question_in.shape[1], passage_in.shape[1]
    rows = 2 * own_rows

    def chunked(values, sixteenths):
        out, row = [], 0
        for part in sixteenths:
            step = values.shape[0] * part // 16
            out.append(values[row : row + step])
            row += step
        return out

    def hand(values):
        return [places.swap_tower(x) for x in values]

    per_q = rows // lq
    every = lp // lq
    per_p = rows // lp
    nq, np_ = question_in.shape[0], passage_in.shape[0]
    shift = 2 * places.half
    low_pa = pa % shift
    g1, g2, g3 = Gather(first), Gather(second), Gather(third)
    my_tokens, send_tokens = sides(rows_q, rows_p)
    tokens_out = chunked(send_tokens, (5, 6, 5))
    g1.mid()
    g1.send, tokens_out, question_cot, passage_cot = tie(
        g1.send, tokens_out, question_cot, passage_cot
    )
    g1.along_z()
    tokens_in = hand(tokens_out[:1])
    my_cot, send_cot = sides(question_cot.reshape(-1, D), passage_cot.reshape(-1, D))
    g1.send, g2.send, tokens_in, my_cot, send_cot = tie(
        g1.send, g2.send, tokens_in, my_cot, send_cot
    )
    g1.pb_first()
    g2.mid()
    g1.stack, g2.send, tokens_out = tie(g1.stack, g2.send, tokens_out)
    g1.send = g1.stack
    g1.pb_last()
    g1.core_stack()
    g2.along_z()
    tokens_in = tokens_in + hand(tokens_out[1:2])
    g1.held, g2.send, tokens_in, tokens_out, question_len, passage_len, positive = tie(
        g1.held, g2.send, tokens_in, tokens_out, question_len, passage_len, positive
    )
    g1.core_held()
    g2.pb_first()
    tokens_in = tokens_in + hand(tokens_out[2:])
    full_j, full_o, full_small = g1.whole([(0, 3 * D), (3 * D, D), (4 * D, 128)])
    full_j, full_o, full_small, g2.stack, g3.send, tokens_in = tie(
        full_j, full_o, full_small, g2.stack, g3.send, tokens_in
    )
    g2.send = g2.stack
    g2.pb_last()
    g2.core_stack()
    g3.mid()
    wj = full_j.reshape(D, 3 * D)
    wo = full_o.reshape(D, D)
    small = full_small.reshape(D, 128).astype(F32)
    vec = small[:, :8].T
    bias_e = small[:, 8:12].reshape(1, FF)
    bias_j = jnp.concatenate([vec[0], jnp.zeros((D,), F32), vec[1]])
    tokens = join([my_tokens] + tokens_in)
    qkv = project(tokens, wj, bias_j[None])

    cot_out = chunked(send_cot, (4, 5, 4, 3))
    by_pa = positive.reshape(places.pa_n, nq)
    pair = [lax.dynamic_index_in_dim(by_pa, low_pa + k, 0, keepdims=False) for k in (0, shift)]
    pair = jnp.concatenate(pair)[None]
    wanted_rows = jnp.concatenate([pair // 16, pair % 16], axis=0).astype(BF16)
    wanted_rows = jnp.pad(wanted_rows, ((0, 0), (0, D - per_q)))
    valid_q = (jnp.arange(lq, dtype=jnp.int32)[None, :] < question_len[:, None]).astype(jnp.int32)
    valid_p = (jnp.arange(lp, dtype=jnp.int32)[None, :] < passage_len[:, None]).astype(jnp.int32)
    my_valid, send_valid = sides(valid_q.reshape(-1), valid_p.reshape(-1))
    valid = jnp.concatenate([my_valid, places.swap_tower(send_valid)])
    row_ids = jnp.arange(rows, dtype=jnp.int32)
    seq = jnp.where(is_q, row_ids // lq, row_ids // lp)
    qid = seq.reshape(rows, 1)
    kid = jnp.where(valid > 0, seq, -1).reshape(rows // BLOCK, 1, BLOCK)
    row_mask = valid.reshape(rows, 1).astype(F32)

    blocks = rows // BLOCK
    later = blocks // 2
    qkv, g3.send, cot_out = tie(qkv, g3.send, cot_out)
    g3.along_z()
    cot_in = hand(cot_out[:1])
    context, probs = attention(qkv, qid, kid)
    context, g2.held, g3.send, cot_in, cot_out = tie(context, g2.held, g3.send, cot_in, cot_out)
    g2.core_held()
    g3.pb_first()
    norm_one, inverse_one, mid_low, mid = add_norm(
        context, wo, tokens, row_mask, vec, (2, 3, 4), True
    )
    mid_low, g2.parts, g3.stack, cot_out = tie(mid_low, g2.parts, g3.stack, cot_out)
    g3.send = g3.stack
    g3.pb_last()
    g3.core_stack()
    cot_in = cot_in + hand(cot_out[1:2])
    (full_e,) = g2.whole([(0, FF)])
    we = full_e.reshape(D, FF)
    mid_low, we, cot_in, cot_out = tie(mid_low, we, cot_in, cot_out)
    cot_in = cot_in + hand(cot_out[2:3])
    gelu = expand(mid_low, we, bias_e, 0, 1)
    gelu, g3.held, g3.other, g3.stack, cot_in, cot_out = tie(
        gelu, g3.held, g3.other, g3.stack, cot_in, cot_out
    )
    g3.core_held()
    cot_in = cot_in + hand(cot_out[3:])
    active, slope = expand(mid_low, we, bias_e, 1, 1, tuple(gelu))
    active, g3.parts, cot_in = tie(active, g3.parts, cot_in)
    (full_r,) = g3.whole([(0, D)])
    wr = full_r.reshape(FF, D)
    norm_two, inverse_two, out = add_norm(active, wr, mid, row_mask, vec, (5, 6, 7), False)

    firsts = out.reshape(per_q, lq, D)[:, 0, :]
    others = places.swap_tower(firsts)
    cls_q = jnp.where(is_q, firsts, others)
    cls_p = jnp.where(is_q, others, firsts)[::every]
    pad = (-(per_q + per_p + 2)) % 8
    stack = jnp.concatenate([cls_q, cls_p, wanted_rows, jnp.zeros((pad, D), BF16)], axis=0)[None]
    pair_masks = [0]
    for bit in bits_of(places.half):
        got = lax.ppermute(stack, "pa", [(i, i ^ (2 * bit)) for i in range(places.pa_n)])
        stack = jnp.concatenate([stack, got], axis=0)
        pair_masks = pair_masks + [m ^ (2 * bit) for m in pair_masks]
    for bit in bits_of(places.pb_n):
        got = lax.ppermute(stack, "pb", [(i, i ^ bit) for i in range(places.pb_n)])
        stack = jnp.concatenate([stack, got], axis=0)
        pair_masks = pair_masks + [m ^ (bit * places.pa_n) for m in pair_masks]
    stack = jnp.concatenate([stack, places.swap_core(stack)], axis=0)
    pair_masks = pair_masks + [m ^ 1 for m in pair_masks]
    groups = len(pair_masks)
    me = pb * places.pa_n + low_pa
    place = jnp.array(pair_masks, jnp.int32) ^ me
    dev_p = jnp.stack([place + shift, place], axis=1)
    p_ids = (dev_p[:, :, None] * np_ + jnp.arange(np_, dtype=jnp.int32)).reshape(-1)
    digits = stack[:, per_q + per_p : per_q + per_p + 2, :per_q].astype(jnp.int32)
    wanted = (digits[:, 0] * 16 + digits[:, 1]).reshape(-1)

    all_q = stack[:, :per_q].reshape(groups * per_q, D)
    all_p = stack[:, per_q : per_q + per_p].reshape(groups * per_p, D)
    similarity = dot(all_q, all_p, ((1,), (1,))) * score_scale
    hot = (wanted[:, None] == p_ids[None, :]).astype(F32)
    top = jnp.max(similarity, axis=1, keepdims=True)
    grown = jnp.exp(similarity - top)
    total = jnp.sum(grown, axis=1, keepdims=True)
    own_sim = similarity[:per_q]
    loss = top[:per_q, 0] + jnp.log(total[:per_q, 0]) - jnp.sum(own_sim * hot[:per_q], axis=1)
    question_loss = lax.dynamic_slice_in_dim(loss, tower * nq, nq)
    d_sim = (loss_weight * (grown / total - hot)).astype(BF16)
    d_q = dot(d_sim[:per_q], all_p) * score_scale
    d_p = dot(d_sim[:, :per_p], all_q, ((0,), (0,))) * score_scale
    d_p = jnp.concatenate(
        [d_p.reshape(per_p, 1, D), jnp.zeros((per_p, every - 1, D), F32)], axis=1
    ).reshape(per_q, D)
    d_slot = jnp.where(is_q, d_q, d_p)

    d_second, d_reduced, sums_second = second_back(
        join([my_cot] + cot_in), d_slot, row_mask, norm_two, inverse_two, vec[6][None, :]
    )
    even = share % 8 == 0

    def gradient(left, right, **more):
        if left.shape[1] > D:
            return tall_grad(left, right, slots, places.nz)
        return weight_grad(left, right, slots, D, **more)

    def plain(left, right, extra=None):
        return grad_plain(left, right, table, extra)

    class Scatter:
        def __init__(self, mine, theirs):
            self.parts, self.theirs, self.send = [mine], theirs, None
            self.count = mine.shape[0]

        def cores(self):
            self.parts = self.parts + [places.swap_core(self.theirs)]

        def total(self, start, stop):
            out = self.parts[0][start:stop].astype(F32)
            for part in self.parts[1:]:
                out = out + part[start:stop].astype(F32)
            return out

        def prepare(self):
            self.send = self.total(self.count // 2, self.count).astype(BF16)

        def move(self, step):
            if self.send is None:
                self.prepare()
            self.parts = self.parts + [places.swap(self.send, step)]
            self.send = None
            self.count = self.count // 2

        def pb_first(self):
            self.move(places.steps - 1)

        def pb_rest(self):
            for step in range(places.steps - 2, z_steps - 1, -1):
                self.move(step)

        def along_z(self):
            for step in range(z_steps - 1, 0, -1):
                self.move(step)

        def mid(self):
            got = places.swap(self.total(1, 2).astype(BF16), 0).astype(F32)
            keep = self.total(0, 1)
            self.out = jnp.concatenate(
                [jnp.where(is_q, keep, got), jnp.where(is_q, got, keep)], axis=0
            )

    send_out = chunked(out[own_rows:], (4, 4, 4, 4))
    d_reduced, send_out = tie(d_reduced, send_out)
    got_out = hand(send_out[:1])
    sr = Scatter(*(gradient if even else plain)(active, d_reduced))
    sr.parts, sr.theirs, d_reduced, got_out, send_out = tie(
        sr.parts, sr.theirs, d_reduced, got_out, send_out
    )
    sr.cores()
    got_out = got_out + hand(send_out[1:2])
    d_expanded, g_bias_expand = hidden_grad(d_reduced, wr, slope)
    sr.parts, d_expanded, got_out, send_out = tie(sr.parts, d_expanded, got_out, send_out)
    sr.pb_first()
    got_out = got_out + hand(send_out[2:3])
    if even:
        partial = gradient(mid_low, d_expanded, room=D)
    else:
        partial = plain(mid_low, d_expanded)
    partial, d_expanded, got_out, send_out = tie(partial, d_expanded, got_out, send_out)
    got_out = got_out + hand(send_out[3:])
    d_first, d_attended, sums_first = first_back(
        d_expanded, we, d_second, norm_one, inverse_one, vec[3][None, :]
    )
    sr.parts, partial, d_attended, got_out = tie(sr.parts, partial, d_attended, got_out)
    sr.pb_rest()
    if even:
        partial = gradient(context, d_attended, into=tuple(partial))
    else:
        also = plain(context, d_attended)
        partial = [jnp.concatenate(x, axis=2) for x in zip(partial, also)]
    se = Scatter(*partial)
    se.parts, se.theirs, d_attended = tie(se.parts, se.theirs, d_attended)
    se.cores()
    d_context = dot(d_attended, wo, ((1,), (1,))).astype(BF16)
    d_joined, sums_one = attention_back(qkv, probs, d_context, later, blocks - later)
    sr.parts, se.parts, d_joined = tie(sr.parts, se.parts, d_joined)
    se.prepare()
    sr.prepare()
    sr.send, sr.parts, se.send, se.parts, d_joined = tie(
        sr.send, sr.parts, se.send, se.parts, d_joined
    )
    se.pb_first()
    sr.along_z()
    part = own_rows // 16
    send_grad = token_grad(d_joined, wj, d_first, own_rows, [5 * part] * 3 + [part], BF16)
    d_joined, send_grad = tie(d_joined, send_grad)
    got_grad = hand(send_grad[:1])
    d_joined, sums_two = attention_back(qkv, probs, d_context, 0, later, d_joined)
    sr.parts, se.parts, d_joined, sums_two, got_grad, send_grad = tie(
        sr.parts, se.parts, d_joined, sums_two, got_grad, send_grad
    )
    se.prepare()
    se.send, se.parts, d_joined, send_grad = tie(se.send, se.parts, d_joined, send_grad)
    se.pb_rest()
    sr.mid()
    got_grad = got_grad + hand(send_grad[1:2])
    g_joined_bias = (sums_one + sums_two)[0]
    g_vec = jnp.concatenate(
        [
            g_joined_bias[None, :D],
            g_joined_bias[None, 2 * D :],
            sums_first[2:3],
            sums_first[:2],
            sums_second[2:3],
            sums_second[:2],
        ]
    )
    g_small = jnp.concatenate(
        [g_vec.T, g_bias_expand.reshape(D, 4), jnp.zeros((D, 116), F32)], axis=1
    )
    sj = Scatter(*(gradient if even else plain)(tokens, d_joined, extra=g_small))
    se.parts, sj.parts, sj.theirs, d_joined, got_grad, send_grad = tie(
        se.parts, sj.parts, sj.theirs, d_joined, got_grad, send_grad
    )
    sj.cores()
    se.along_z()
    (own_grad,) = token_grad(d_joined, wj, d_first, 0, [own_rows], F32)
    sj.parts, own_grad, send_grad = tie(sj.parts, own_grad, send_grad)
    sj.pb_first()
    got_grad = got_grad + hand(send_grad[2:3])
    sj.parts, se.parts, got_grad, send_grad = tie(sj.parts, se.parts, got_grad, send_grad)
    sj.pb_rest()
    se.mid()
    sj.parts, se.out, sr.out, got_out, out, send_grad = tie(
        sj.parts, se.out, sr.out, got_out, out, send_grad
    )
    sj.along_z()
    got_grad = got_grad + hand(send_grad[3:])
    out_q, out_p = deal(tower.reshape(1), out, got_out)
    sj.parts, out_q, out_p, got_grad = tie(sj.parts, out_q, out_p, got_grad)
    grad_q, grad_p = deal(tower.reshape(1), own_grad, got_grad)
    sj.mid()
    grad_joined = sj.out[:, :, : 3 * D]
    grad_expand, grad_output, grad_reduce = se.out[:, :, :FF], se.out[:, :, FF:], sr.out
    extra = sj.out[:, :, 3 * D :]
    grad_vectors = extra[:, :, :8].transpose(0, 2, 1)
    grad_b_expand = extra[:, :, 8:12].reshape(2, 4 * share)

    return (
        out_q.reshape(question_in.shape),
        out_p.reshape(passage_in.shape),
        question_loss,
        grad_q.reshape(question_in.shape),
        grad_p.reshape(passage_in.shape),
        grad_joined,
        grad_output,
        grad_expand,
        grad_reduce,
        grad_vectors,
        grad_b_expand,
    )


def solution(mesh):
    in_specs = (
        P(("pb", "pa"), None, None),
        P(("pb", "pa"), None, None),
        P(("pb", "pa")),
        P(("pb", "pa")),
        P("pb"),
        P(("pb", "pa"), None, None),
        P(("pb", "pa"), None, None),
        P(None, ("pb", "pa"), None),
        P(None, ("pb", "pa"), None),
        P(None, ("pb", "pa"), None),
        P(None, ("pb", "pa"), None),
        P(None, None, ("pb", "pa")),
        P(None, ("pb", "pa")),
    )
    out_specs = (
        P(("pb", "pa"), None, None),
        P(("pb", "pa"), None, None),
        P(("pb", "pa")),
        P(("pb", "pa"), None, None),
        P(("pb", "pa"), None, None),
        P(None, ("pb", "pa"), None),
        P(None, ("pb", "pa"), None),
        P(None, ("pb", "pa"), None),
        P(None, ("pb", "pa"), None),
        P(None, None, ("pb", "pa")),
        P(None, ("pb", "pa")),
    )
    return jax.shard_map(
        functools.partial(per_device, Places(mesh)),
        mesh=mesh,
        in_specs=in_specs,
        out_specs=out_specs,
        check_vma=False,
    )
```

```python
import functools

import jax
import jax.numpy as jnp
from jax import lax
from jax.experimental import pallas as pl
from jax.experimental.pallas import tpu as pltpu
from jax.sharding import PartitionSpec as P

D = 768
HEADS = 12
HDIM = 64
FF = 3072
AXES = ("pb", "pa")
BLOCK = 256

norm_eps = 1e-06
masked_score = -1000000000.0
score_scale = 0.0625
loss_weight = 16.0
head_scale = HDIM ** (-0.5)
F32 = jnp.float32
BF16 = jnp.bfloat16
VMEM_LIMIT = 56 * 1024 * 1024


def bits_of(count):
    return [1 << shift for shift in range(count.bit_length() - 1)]


class Places:
    def __init__(self, mesh):
        self.pb_n = mesh.shape["pb"]
        self.pa_n = mesh.shape["pa"]
        self.nz = self.pa_n // 2
        self.half = self.nz // 2
        self.chips = self.pb_n * self.nz
        pb_bits = bits_of(self.pb_n)
        turn = len(pb_bits) // 2
        low_z = [("z", bit) for bit in bits_of(self.half)]
        first = [("pb", bit) for bit in pb_bits]
        second = first[turn:] + first[:turn]
        self.orders = ([("z", self.half)] + low_z + first, [("z", self.half)] + low_z + second)
        self.steps = len(self.orders[0])

    def chip_mask(self, move):
        axis, bit = move
        return bit * self.nz if axis == "pb" else bit

    def stack_masks(self, core):
        masks = [0]
        for move in self.orders[core]:
            masks = masks + [mask ^ self.chip_mask(move) for mask in masks]
        return masks

    def pairs(self, step):
        out = []
        for pb in range(self.pb_n):
            for pa in range(self.pa_n):
                axis, bit = self.orders[pa % 2][step]
                to_pb, to_pa = (pb ^ bit, pa) if axis == "pb" else (pb, pa ^ (2 * bit))
                out.append((pb * self.pa_n + pa, to_pb * self.pa_n + to_pa))
        return out

    def swap(self, values, step):
        return lax.ppermute(values, AXES, self.pairs(step))

    def swap_core(self, values):
        return lax.ppermute(values, "pa", [(i, i ^ 1) for i in range(self.pa_n)])

    def swap_tower(self, values):
        return lax.ppermute(values, "pa", [(i, i ^ (2 * self.half)) for i in range(self.pa_n)])


def dot(left, right, dims=((1,), (0,))):
    return lax.dot_general(left, right, (dims, ((), ())), preferred_element_type=F32)


def tie(*values):
    return lax.optimization_barrier(values)


def assemble_kernel(segments, idx_ref, *refs):
    count = len(segments)
    sources, outs = refs[:4], refs[4 : 4 + count]
    buffer, in_sem, out_sem = refs[4 + count :]
    core = idx_ref[2, 0]
    part = sources[0].shape[0]
    loads = [
        pltpu.make_async_copy(source, buffer.at[pl.ds(k * part, part)], in_sem.at[k])
        for k, source in enumerate(sources)
    ]
    for load in loads:
        load.start()
    stores = []
    for k in range(4):
        loads[k].wait()
        half = core if k < 2 else 1 - core
        for j in range(part):
            slot = k * part + j
            place = idx_ref[k // 2, (k % 2) * part + j]
            for s, (start, width) in enumerate(segments):
                store = pltpu.make_async_copy(
                    buffer.at[slot, :, pl.ds(start, width)],
                    outs[s].at[place, half],
                    out_sem.at[s, slot],
                )
                store.start()
                stores.append(store)
    for store in stores:
        store.wait()


def assemble(parts, table, segments):
    part, rows, width = parts[0].shape
    chips = 2 * part
    shapes = [jax.ShapeDtypeStruct((chips, 2, rows, w), BF16) for _, w in segments]
    return pl.pallas_call(
        functools.partial(assemble_kernel, segments),
        out_shape=shapes,
        in_specs=[pl.BlockSpec(memory_space=pltpu.SMEM)] + [pl.BlockSpec(memory_space=pl.ANY)] * 4,
        out_specs=[pl.BlockSpec(memory_space=pl.ANY)] * len(segments),
        scratch_shapes=[
            pltpu.VMEM((2 * chips, rows, width), BF16),
            pltpu.SemaphoreType.DMA((4,)),
            pltpu.SemaphoreType.DMA((len(segments), 2 * chips)),
        ],
        compiler_params=pltpu.CompilerParams(vmem_limit_bytes=VMEM_LIMIT),
        cost_estimate=pl.CostEstimate(
            flops=0, bytes_accessed=4 * 2 * chips * rows * width, transcendentals=0
        ),
        name="assemble",
    )(table, *parts)


def assemble_plain(parts, table, segments):
    own = jnp.take(jnp.concatenate(parts[:2], axis=0), jnp.argsort(table[0]), axis=0)
    other = jnp.take(jnp.concatenate(parts[2:], axis=0), jnp.argsort(table[1]), axis=0)
    first = table[2, 0] == 0
    both = jnp.stack([jnp.where(first, own, other), jnp.where(first, other, own)], axis=1)
    return [both[..., start : start + w] for start, w in segments]


def split_slabs(acc, core, chips, mine_ref, theirs_ref, cols, within):
    rows = acc.shape[0] // (2 * chips)
    for s in range(chips):
        low = acc[2 * s * rows : (2 * s + 1) * rows]
        high = acc[(2 * s + 1) * rows : (2 * s + 2) * rows]
        mine, theirs = within(s)
        mine_ref[mine, :, cols] = jnp.where(core == 0, low, high).astype(BF16)
        theirs_ref[theirs, :, cols] = jnp.where(core == 0, high, low).astype(BF16)


def weight_grad_kernel(chips, extra, table_ref, left_ref, right_ref, *refs):
    mine_ref, theirs_ref = refs[-2:]
    core = table_ref[2, 0]
    acc = dot(left_ref[...], right_ref[...], ((0,), (0,)))
    width = acc.shape[1]

    def within(s):
        return table_ref[0, s], table_ref[1, s]

    if extra == 0:
        split_slabs(acc, core, chips, mine_ref, theirs_ref, slice(None), within)
        return
    step = pl.program_id(0)
    cols = pl.ds(pl.multiple_of(step * width, 128), width)
    split_slabs(acc, core, chips, mine_ref, theirs_ref, cols, within)

    @pl.when(step == 0)
    def _():
        one, two, first, second, bias = (ref[...] for ref in refs[:extra])
        joined = one + two
        lines = [
            joined[:, :D],
            joined[:, 2 * D :],
            first[2:3],
            first[:2],
            second[2:3],
            second[:2],
            bias,
            jnp.zeros((116, D), F32),
        ]
        values = jnp.concatenate(lines, axis=0).T
        tail = pl.ds(mine_ref.shape[2] - 128, 128)
        split_slabs(values, core, chips, mine_ref, theirs_ref, tail, within)


def weight_grad(left, right, slots, tile, extra=None, room=0, into=()):
    rows, height = left.shape
    width = right.shape[1]
    chips = slots.shape[1]
    slab = height // (2 * chips)
    total = width + (room if extra is None else 128)
    first = 0
    if into:
        total = into[0].shape[2]
        first = (total - width) // tile
    block = (chips, slab, total if extra is not None else tile)
    place = (lambda j, t: (0, 0, 0)) if extra is not None else (lambda j, t: (0, 0, j + first))
    return pl.pallas_call(
        functools.partial(weight_grad_kernel, chips, len(extra or ())),
        grid_spec=pltpu.PrefetchScalarGridSpec(
            num_scalar_prefetch=1,
            grid=(width // tile,),
            in_specs=[
                pl.BlockSpec((rows, height), lambda j, t: (0, 0)),
                pl.BlockSpec((rows, tile), lambda j, t: (0, j)),
            ]
            + [pl.BlockSpec(x.shape, lambda j, t: (0, 0)) for x in extra or ()]
            + [pl.BlockSpec(memory_space=pl.ANY)] * len(into),
            out_specs=[pl.BlockSpec(block, place)] * 2,
        ),
        out_shape=[jax.ShapeDtypeStruct((chips, slab, total), BF16)] * 2,
        input_output_aliases={3: 0, 4: 1} if into else {},
        compiler_params=pltpu.CompilerParams(vmem_limit_bytes=VMEM_LIMIT),
        cost_estimate=pl.CostEstimate(
            flops=2 * rows * height * width,
            bytes_accessed=2 * (rows * (height + width) + height * width),
            transcendentals=0,
        ),
        name="weight_grad",
    )(slots, left, right, *(extra or ()), *into)


def tall_grad_kernel(chips, table_ref, left_ref, right_ref, mine_ref, theirs_ref):
    core = table_ref[2, 0]
    acc = dot(left_ref[...], right_ref[...], ((0,), (0,)))
    base = pl.program_id(0) * chips

    def within(s):
        return table_ref[0, base + s] % chips, table_ref[1, base + s] % chips

    split_slabs(acc, core, chips, mine_ref, theirs_ref, slice(None), within)


def tall_grad(left, right, slots, column):
    rows, height = left.shape
    width = right.shape[1]
    chips = slots.shape[1]
    slab = height // (2 * chips)
    tile = height // chips * column
    return pl.pallas_call(
        functools.partial(tall_grad_kernel, column),
        grid_spec=pltpu.PrefetchScalarGridSpec(
            num_scalar_prefetch=1,
            grid=(chips // column,),
            in_specs=[
                pl.BlockSpec((rows, tile), lambda i, t: (0, i)),
                pl.BlockSpec((rows, width), lambda i, t: (0, 0)),
            ],
            out_specs=[
                pl.BlockSpec((column, slab, width), lambda i, t: (t[0, i * column] // column, 0, 0)),
                pl.BlockSpec((column, slab, width), lambda i, t: (t[1, i * column] // column, 0, 0)),
            ],
        ),
        out_shape=[jax.ShapeDtypeStruct((chips, slab, width), BF16)] * 2,
        compiler_params=pltpu.CompilerParams(vmem_limit_bytes=VMEM_LIMIT),
        cost_estimate=pl.CostEstimate(
            flops=2 * rows * height * width,
            bytes_accessed=2 * (rows * (height + width) + height * width),
            transcendentals=0,
        ),
        name="tall_grad",
    )(slots, left, right)


def grad_plain(left, right, table, extra=None):
    full = dot(left, right, ((0,), (0,)))
    if extra is not None:
        full = jnp.concatenate([full, extra], axis=1)
    chips = table.shape[1]
    full = full.astype(BF16).reshape(chips, 2, full.shape[0] // (2 * chips), full.shape[1])
    core = table[2, 0]
    mine = lax.dynamic_index_in_dim(full, core, 1, keepdims=False)
    theirs = lax.dynamic_index_in_dim(full, 1 - core, 1, keepdims=False)
    return jnp.take(mine, table[0], axis=0), jnp.take(theirs, table[1], axis=0)


def hidden_grad_kernel(grad_ref, w_ref, slope_ref, out_ref, sum_ref):
    grad = dot(grad_ref[...], w_ref[...], ((1,), (1,))) * slope_ref[...].astype(F32)
    low = grad.astype(BF16)
    out_ref[...] = low
    sum_ref[...] = jnp.sum(low.astype(F32), axis=0, keepdims=True)


def hidden_grad(grad, w_reduce, slope):
    rows, tile = grad.shape[0], 512
    return pl.pallas_call(
        hidden_grad_kernel,
        grid=(FF // tile,),
        in_specs=[
            pl.BlockSpec((rows, D), lambda j: (0, 0)),
            pl.BlockSpec((tile, D), lambda j: (j, 0)),
            pl.BlockSpec((rows, tile), lambda j: (0, j)),
        ],
        out_specs=[
            pl.BlockSpec((rows, tile), lambda j: (0, j)),
            pl.BlockSpec((1, tile), lambda j: (0, j)),
        ],
        out_shape=[
            jax.ShapeDtypeStruct((rows, FF), BF16),
            jax.ShapeDtypeStruct((1, FF), F32),
        ],
        compiler_params=pltpu.CompilerParams(vmem_limit_bytes=VMEM_LIMIT),
        cost_estimate=pl.CostEstimate(
            flops=2 * rows * D * FF,
            bytes_accessed=2 * (rows * D + D * FF + 2 * rows * FF),
            transcendentals=0,
        ),
        name="hidden_grad",
    )(grad, w_reduce, slope)


def attention_kernel(qkv_ref, qid_ref, kid_ref, context_ref, probs_ref):
    allowed = qid_ref[...] == kid_ref[0]
    lane = lax.broadcasted_iota(jnp.int32, (BLOCK, 128), 1)
    zero = jnp.zeros((BLOCK, 128), BF16)
    for pair in range(HEADS // 2):
        queries = qkv_ref[:, pair * 128 : pair * 128 + 128]
        keys = qkv_ref[:, D + pair * 128 : D + pair * 128 + 128]
        values = qkv_ref[:, 2 * D + pair * 128 : 2 * D + pair * 128 + 128]
        outs = []
        for side in range(2):
            mine = (lane < HDIM) if side == 0 else (lane >= HDIM)
            scores = dot(queries, jnp.where(mine, keys, zero), ((1,), (1,))) * head_scale
            scores = jnp.where(allowed, scores, masked_score)
            top = jnp.max(scores, axis=1, keepdims=True)
            grown = jnp.exp(scores - top)
            total = jnp.sum(grown, axis=1, keepdims=True)
            probs = (grown * (1.0 / total)).astype(BF16)
            probs_ref[0, 2 * pair + side] = probs
            outs.append(dot(probs, values))
        context_ref[:, pair * 128 : pair * 128 + 128] = jnp.where(
            lane < HDIM, outs[0], outs[1]
        ).astype(BF16)


def attention(qkv, qid, kid):
    rows = qkv.shape[0]
    blocks = rows // BLOCK
    return pl.pallas_call(
        attention_kernel,
        grid=(blocks,),
        in_specs=[
            pl.BlockSpec((BLOCK, 3 * D), lambda i: (i, 0)),
            pl.BlockSpec((BLOCK, 1), lambda i: (i, 0)),
            pl.BlockSpec((1, 1, BLOCK), lambda i: (i, 0, 0)),
        ],
        out_specs=[
            pl.BlockSpec((BLOCK, D), lambda i: (i, 0)),
            pl.BlockSpec((1, HEADS, BLOCK, BLOCK), lambda i: (i, 0, 0, 0)),
        ],
        out_shape=[
            jax.ShapeDtypeStruct((rows, D), BF16),
            jax.ShapeDtypeStruct((blocks, HEADS, BLOCK, BLOCK), BF16),
        ],
        compiler_params=pltpu.CompilerParams(vmem_limit_bytes=VMEM_LIMIT),
        cost_estimate=pl.CostEstimate(
            flops=4 * rows * BLOCK * D * 2,
            bytes_accessed=rows * (4 * D + HEADS * BLOCK) * 2,
            transcendentals=rows * HEADS * BLOCK,
        ),
        name="attention",
    )(qkv, qid, kid)


def attention_back_kernel(qkv_ref, probs_ref, grad_ref, out_ref, sum_ref):
    lane = lax.broadcasted_iota(jnp.int32, (BLOCK, 128), 1)
    zero = jnp.zeros((BLOCK, 128), BF16)

    def at(pair, start=0):
        return pl.ds(pl.multiple_of(start + pair * 128, 128), 128)

    def some(step, carry):
        for k in range(2):
            pair = step * 2 + k
            cols = at(pair)
            queries = qkv_ref[:, at(pair)]
            keys = qkv_ref[:, at(pair, D)]
            values = qkv_ref[:, at(pair, 2 * D)]
            grad = grad_ref[:, cols]
            d_q, d_k, d_v = [], [], []
            for side in range(2):
                mine = (lane < HDIM) if side == 0 else (lane >= HDIM)
                low = probs_ref[0, 2 * pair + side]
                d_probs = dot(jnp.where(mine, grad, zero), values, ((1,), (1,)))
                d_v.append(dot(low, grad, ((0,), (0,))))
                probs = low.astype(F32)
                row_dot = jnp.sum(d_probs * probs, axis=1, keepdims=True)
                d_scores = (probs * (d_probs - row_dot)).astype(BF16)
                d_q.append(dot(d_scores, keys))
                d_k.append(dot(d_scores, queries, ((0,), (0,))))
            first = lane < HDIM
            out_ref[:, at(pair)] = (
                jnp.where(first, d_q[0], d_q[1]) * head_scale
            ).astype(BF16)
            out_ref[:, at(pair, D)] = (
                jnp.where(first, d_k[0], d_k[1]) * head_scale
            ).astype(BF16)
            out_ref[:, at(pair, 2 * D)] = jnp.where(
                first, d_v[0], d_v[1]
            ).astype(BF16)
        return carry

    lax.fori_loop(0, HEADS // 2 // 2, some, 0)
    sums = jnp.sum(out_ref[...].astype(F32), axis=0, keepdims=True)

    @pl.when(pl.program_id(0) == 0)
    def _():
        sum_ref[...] = sums

    @pl.when(pl.program_id(0) > 0)
    def _():
        sum_ref[...] += sums


def attention_back_more_kernel(qkv_ref, probs_ref, grad_ref, _, out_ref, sum_ref):
    attention_back_kernel(qkv_ref, probs_ref, grad_ref, out_ref, sum_ref)


def attention_back(qkv, probs, grad_context, start, count, into=None):
    rows = qkv.shape[0]
    more = into is not None
    return pl.pallas_call(
        attention_back_more_kernel if more else attention_back_kernel,
        grid=(count,),
        in_specs=[
            pl.BlockSpec((BLOCK, 3 * D), lambda i: (i + start, 0)),
            pl.BlockSpec((1, HEADS, BLOCK, BLOCK), lambda i: (i + start, 0, 0, 0)),
            pl.BlockSpec((BLOCK, D), lambda i: (i + start, 0)),
        ]
        + ([pl.BlockSpec(memory_space=pl.ANY)] if more else []),
        out_specs=[
            pl.BlockSpec((BLOCK, 3 * D), lambda i: (i + start, 0)),
            pl.BlockSpec((1, 3 * D), lambda i: (0, 0)),
        ],
        out_shape=[
            jax.ShapeDtypeStruct((rows, 3 * D), BF16),
            jax.ShapeDtypeStruct((1, 3 * D), F32),
        ],
        input_output_aliases={3: 0} if more else {},
        compiler_params=pltpu.CompilerParams(vmem_limit_bytes=VMEM_LIMIT),
        cost_estimate=pl.CostEstimate(
            flops=8 * count * BLOCK * BLOCK * D * 2,
            bytes_accessed=count * BLOCK * (7 * D + HEADS * BLOCK) * 2,
            transcendentals=0,
        ),
        name="attention_back",
    )(qkv, probs, grad_context, *([into] if more else []))


def join_kernel(*refs):
    row = 0
    for piece in refs[:-1]:
        rows = piece.shape[0]
        refs[-1][row : row + rows, :] = piece[...]
        row += rows


def join(pieces):
    rows, width = sum(x.shape[0] for x in pieces), pieces[0].shape[1]
    return pl.pallas_call(
        join_kernel,
        grid=(1,),
        in_specs=[pl.BlockSpec(x.shape, lambda i: (0, 0)) for x in pieces],
        out_specs=pl.BlockSpec((rows, width), lambda i: (0, 0)),
        out_shape=jax.ShapeDtypeStruct((rows, width), pieces[0].dtype),
        compiler_params=pltpu.CompilerParams(vmem_limit_bytes=VMEM_LIMIT),
        cost_estimate=pl.CostEstimate(
            flops=0, bytes_accessed=4 * rows * width, transcendentals=0
        ),
        name="join",
    )(*pieces)


def deal_kernel(tower_ref, own_ref, *refs):
    pieces, (q_ref, p_ref) = refs[:-2], refs[-2:]

    def give(own_out, other_out):
        own_out[...] = own_ref[...]
        row = 0
        for piece in pieces:
            rows = piece.shape[0]
            other_out[row : row + rows, :] = piece[...].astype(other_out.dtype)
            row += rows

    @pl.when(tower_ref[0] == 0)
    def _():
        give(q_ref, p_ref)

    @pl.when(tower_ref[0] != 0)
    def _():
        give(p_ref, q_ref)


def deal(tower, own, pieces):
    rows, width = sum(x.shape[0] for x in pieces), own.shape[1]
    shape = jax.ShapeDtypeStruct((rows, width), own.dtype)
    return pl.pallas_call(
        deal_kernel,
        grid=(1,),
        in_specs=[
            pl.BlockSpec(memory_space=pltpu.SMEM),
            pl.BlockSpec((rows, width), lambda i: (0, 0)),
        ]
        + [pl.BlockSpec(x.shape, lambda i: (0, 0)) for x in pieces],
        out_specs=[pl.BlockSpec((rows, width), lambda i: (0, 0))] * 2,
        out_shape=[shape] * 2,
        compiler_params=pltpu.CompilerParams(vmem_limit_bytes=VMEM_LIMIT),
        cost_estimate=pl.CostEstimate(
            flops=0, bytes_accessed=12 * rows * width, transcendentals=0
        ),
        name="deal",
    )(tower, own, *pieces)


def add_sums(sum_ref, values):
    total = jnp.concatenate(
        [jnp.sum(x, axis=0, keepdims=True) for x in values]
        + [jnp.zeros((8 - len(values), values[0].shape[1]), F32)],
        axis=0,
    )

    @pl.when(pl.program_id(0) == 0)
    def _():
        sum_ref[...] = total

    @pl.when(pl.program_id(0) > 0)
    def _():
        sum_ref[...] += total


def second_back_kernel(
    cot_ref, slot_ref, mask_ref, norm_ref, inverse_ref, gain_ref, grad_ref, low_ref, sum_ref
):
    group = slot_ref.shape[1]
    cot = cot_ref[...].astype(F32).reshape(group, BLOCK // group, D)
    first = lax.broadcasted_iota(jnp.int32, cot.shape, 1) == 0
    grad = cot + jnp.where(first, slot_ref[0][:, None, :], 0.0)
    grad = grad.reshape(BLOCK, D) * mask_ref[...]
    norm = norm_ref[...]
    second = norm_back(grad, gain_ref[...], norm, inverse_ref[...])
    low = second.astype(BF16)
    grad_ref[...] = second
    low_ref[...] = low
    add_sums(sum_ref, [grad * norm, grad, low.astype(F32)])


def second_back(cot, d_slot, mask, norm, inverse, gain):
    rows = cot.shape[0]
    blocks = rows // BLOCK
    wide = pl.BlockSpec((BLOCK, D), lambda i: (i, 0))
    thin = pl.BlockSpec((BLOCK, 1), lambda i: (i, 0))
    group = d_slot.shape[0] // blocks
    return pl.pallas_call(
        second_back_kernel,
        grid=(blocks,),
        in_specs=[
            wide,
            pl.BlockSpec((1, group, D), lambda i: (i, 0, 0)),
            thin,
            wide,
            thin,
            pl.BlockSpec((1, D), lambda i: (0, 0)),
        ],
        out_specs=[wide, wide, pl.BlockSpec((8, D), lambda i: (0, 0))],
        out_shape=[
            jax.ShapeDtypeStruct((rows, D), F32),
            jax.ShapeDtypeStruct((rows, D), BF16),
            jax.ShapeDtypeStruct((8, D), F32),
        ],
        compiler_params=pltpu.CompilerParams(vmem_limit_bytes=VMEM_LIMIT),
        cost_estimate=pl.CostEstimate(
            flops=20 * rows * D, bytes_accessed=12 * rows * D, transcendentals=0
        ),
        name="second_back",
    )(cot, d_slot.reshape(blocks, group, D), mask, norm, inverse, gain)


def first_back_kernel(
    hidden_ref, w_ref, second_ref, norm_ref, inverse_ref, gain_ref, grad_ref, low_ref, sum_ref
):
    grad = second_ref[...] + dot(hidden_ref[...], w_ref[...], ((1,), (1,)))
    norm = norm_ref[...]
    first = norm_back(grad, gain_ref[...], norm, inverse_ref[...])
    low = first.astype(BF16)
    grad_ref[...] = first
    low_ref[...] = low
    add_sums(sum_ref, [grad * norm, grad, low.astype(F32)])


def first_back(d_expanded, w_expand, d_second, norm, inverse, gain):
    rows = d_expanded.shape[0]
    wide = pl.BlockSpec((BLOCK, D), lambda i: (i, 0))
    return pl.pallas_call(
        first_back_kernel,
        grid=(rows // BLOCK,),
        in_specs=[
            pl.BlockSpec((BLOCK, FF), lambda i: (i, 0)),
            pl.BlockSpec((D, FF), lambda i: (0, 0)),
            wide,
            wide,
            pl.BlockSpec((BLOCK, 1), lambda i: (i, 0)),
            pl.BlockSpec((1, D), lambda i: (0, 0)),
        ],
        out_specs=[wide, wide, pl.BlockSpec((8, D), lambda i: (0, 0))],
        out_shape=[
            jax.ShapeDtypeStruct((rows, D), F32),
            jax.ShapeDtypeStruct((rows, D), BF16),
            jax.ShapeDtypeStruct((8, D), F32),
        ],
        compiler_params=pltpu.CompilerParams(vmem_limit_bytes=VMEM_LIMIT),
        cost_estimate=pl.CostEstimate(
            flops=2 * rows * D * FF,
            bytes_accessed=2 * (rows * FF + D * FF) + 14 * rows * D,
            transcendentals=0,
        ),
        name="first_back",
    )(d_expanded, w_expand, d_second, norm, inverse, gain)


def expand_kernel(mid_ref, w_ref, b_ref, active_ref, slope_ref):
    expanded = dot(mid_ref[...], w_ref[...]) + b_ref[...]
    phi = 0.5 + 0.5 * lax.erf(expanded * 0.7071067811865476)
    density = jnp.exp(expanded * expanded * -0.5) * 0.3989422804014327
    active_ref[...] = (expanded * phi).astype(BF16)
    slope_ref[...] = (phi + expanded * density).astype(BF16)


def expand_more_kernel(mid_ref, w_ref, b_ref, _, __, active_ref, slope_ref):
    expand_kernel(mid_ref, w_ref, b_ref, active_ref, slope_ref)


def expand(mid_low, w_expand, b_expand, start, count, into=()):
    rows = mid_low.shape[0]
    tile_r, tile_f = 256, FF // 2
    return pl.pallas_call(
        expand_more_kernel if into else expand_kernel,
        grid=(count, rows // tile_r),
        in_specs=[
            pl.BlockSpec((tile_r, D), lambda j, i: (i, 0)),
            pl.BlockSpec((D, tile_f), lambda j, i: (0, j + start)),
            pl.BlockSpec((1, tile_f), lambda j, i: (0, j + start)),
        ]
        + [pl.BlockSpec(memory_space=pl.ANY)] * len(into),
        out_specs=[
            pl.BlockSpec((tile_r, tile_f), lambda j, i: (i, j + start)),
            pl.BlockSpec((tile_r, tile_f), lambda j, i: (i, j + start)),
        ],
        out_shape=[jax.ShapeDtypeStruct((rows, FF), BF16)] * 2,
        input_output_aliases={3: 0, 4: 1} if into else {},
        compiler_params=pltpu.CompilerParams(vmem_limit_bytes=VMEM_LIMIT),
        cost_estimate=pl.CostEstimate(
            flops=2 * rows * D * count * tile_f,
            bytes_accessed=2 * (rows * D + D * count * tile_f + 2 * rows * count * tile_f),
            transcendentals=2 * rows * count * tile_f,
        ),
        name="expand",
    )(mid_low, w_expand, b_expand, *into)


def token_grad_kernel(grad_ref, w_ref, first_ref, *outs):
    block = first_ref[...] + dot(grad_ref[...], w_ref[...], ((1,), (1,)))
    block = block.astype(outs[0].dtype)
    step, start = pl.program_id(0), 0
    for out in outs:
        stop = start + out.shape[0]
        for k in range(start // BLOCK, (stop - 1) // BLOCK + 1):
            low, high = max(start, k * BLOCK), min(stop, (k + 1) * BLOCK)

            @pl.when(step == k)
            def _(out=out, k=k, low=low, high=high, start=start):
                out[low - start : high - start, :] = block[low - k * BLOCK : high - k * BLOCK]

        start = stop


def token_grad(d_joined, weight, d_first, start, pieces, dtype):
    width = weight.shape[1]
    first, count = start // BLOCK, sum(pieces) // BLOCK
    return pl.pallas_call(
        token_grad_kernel,
        grid=(count,),
        in_specs=[
            pl.BlockSpec((BLOCK, width), lambda i: (i + first, 0)),
            pl.BlockSpec((D, width), lambda i: (0, 0)),
            pl.BlockSpec((BLOCK, D), lambda i: (i + first, 0)),
        ],
        out_specs=[pl.BlockSpec((n, D), lambda i: (0, 0)) for n in pieces],
        out_shape=[jax.ShapeDtypeStruct((n, D), dtype) for n in pieces],
        compiler_params=pltpu.CompilerParams(vmem_limit_bytes=VMEM_LIMIT),
        cost_estimate=pl.CostEstimate(
            flops=2 * count * BLOCK * D * width,
            bytes_accessed=2 * D * width + count * BLOCK * (2 * width + 6 * D),
            transcendentals=0,
        ),
        name="token_grad",
    )(d_joined, weight, d_first)


def project_kernel(w_ref, b_ref, *refs):
    pieces, (tokens_ref, out_ref) = refs[:-2], refs[-2:]
    step = pl.program_id(0)

    @pl.when(step == 0)
    def _():
        join_kernel(*pieces, tokens_ref)

    tokens = tokens_ref[pl.ds(pl.multiple_of(step * BLOCK, BLOCK), BLOCK), :]
    out_ref[...] = (dot(tokens, w_ref[...]) + b_ref[...]).astype(BF16)


def project(pieces, weight, bias):
    rows, width = sum(x.shape[0] for x in pieces), weight.shape[1]
    return pl.pallas_call(
        project_kernel,
        grid=(rows // BLOCK,),
        in_specs=[
            pl.BlockSpec((D, width), lambda i: (0, 0)),
            pl.BlockSpec((1, width), lambda i: (0, 0)),
        ]
        + [pl.BlockSpec(x.shape, lambda i: (0, 0)) for x in pieces],
        out_specs=[
            pl.BlockSpec((rows, D), lambda i: (0, 0)),
            pl.BlockSpec((BLOCK, width), lambda i: (i, 0)),
        ],
        out_shape=[
            jax.ShapeDtypeStruct((rows, D), BF16),
            jax.ShapeDtypeStruct((rows, width), BF16),
        ],
        compiler_params=pltpu.CompilerParams(vmem_limit_bytes=VMEM_LIMIT),
        cost_estimate=pl.CostEstimate(
            flops=2 * rows * D * width,
            bytes_accessed=2 * (rows * (2 * D + width) + D * width),
            transcendentals=0,
        ),
        name="project",
    )(weight, bias, *pieces)


def add_norm_kernel(
    rows_of, left_ref, w_ref, base_ref, mask_ref, vec_ref, norm_ref, inverse_ref, low_ref, *more
):
    bias, gain, shift = (vec_ref[k : k + 1, :] for k in rows_of)
    norm, inverse = normalized(base_ref[...].astype(F32) + dot(left_ref[...], w_ref[...]) + bias)
    value = norm * gain + shift
    norm_ref[...] = norm
    inverse_ref[...] = inverse
    if more:
        more[0][...] = value
        low_ref[...] = value.astype(BF16)
    else:
        low_ref[...] = (value * mask_ref[...]).astype(BF16)


def add_norm(left, weight, base, mask, vec, rows_of, keep):
    rows, depth = left.shape
    wide = pl.BlockSpec((BLOCK, D), lambda i: (i, 0))
    thin = pl.BlockSpec((BLOCK, 1), lambda i: (i, 0))
    shape = jax.ShapeDtypeStruct((rows, D), F32)
    return pl.pallas_call(
        functools.partial(add_norm_kernel, rows_of),
        grid=(rows // BLOCK,),
        in_specs=[
            pl.BlockSpec((BLOCK, depth), lambda i: (i, 0)),
            pl.BlockSpec((depth, D), lambda i: (0, 0)),
            wide,
            thin,
            pl.BlockSpec((8, D), lambda i: (0, 0)),
        ],
        out_specs=[wide, thin, wide] + [wide] * keep,
        out_shape=[
            shape,
            jax.ShapeDtypeStruct((rows, 1), F32),
            jax.ShapeDtypeStruct((rows, D), BF16),
        ]
        + [shape] * keep,
        compiler_params=pltpu.CompilerParams(vmem_limit_bytes=VMEM_LIMIT),
        cost_estimate=pl.CostEstimate(
            flops=2 * rows * D * depth,
            bytes_accessed=2 * (rows + D) * depth + 12 * rows * D,
            transcendentals=0,
        ),
        name="add_norm",
    )(left, weight, base, mask, vec)


def normalized(values):
    centred = values - jnp.mean(values, axis=-1, keepdims=True)
    spread = jnp.mean(centred * centred, axis=-1, keepdims=True)
    inverse = lax.rsqrt(spread + norm_eps)
    return centred * inverse, inverse


def norm_back(grad, gain, norm, inverse):
    scaled = grad * gain
    return inverse * (
        scaled
        - jnp.mean(scaled, axis=-1, keepdims=True)
        - norm * jnp.mean(scaled * norm, axis=-1, keepdims=True)
    )


def per_device(places, *args):
    (
        question_in,
        passage_in,
        question_len,
        passage_len,
        positive,
        question_cot,
        passage_cot,
        w_joined,
        w_output,
        w_expand,
        w_reduce,
        vectors,
        b_expand,
    ) = args
    pb, pa = lax.axis_index("pb"), lax.axis_index("pa")
    z, core = pa // 2, pa % 2
    tower = z // places.half
    is_q = tower == 0
    chip = pb * places.nz + z
    masks = [places.stack_masks(side) for side in range(2)]
    slots_of = [sorted(range(places.chips), key=side.__getitem__) for side in masks]

    def of_core(rows_of):
        both = jnp.array(rows_of, jnp.int32)
        return (
            lax.dynamic_index_in_dim(both, core, 0, keepdims=False),
            lax.dynamic_index_in_dim(both, 1 - core, 0, keepdims=False),
        )

    side = jnp.full((places.chips,), core, jnp.int32)
    table = jnp.stack([x ^ chip for x in of_core(masks)] + [side]).astype(jnp.int32)
    slots = [x ^ lax.dynamic_index_in_dim(x, chip, 0, keepdims=False) for x in of_core(slots_of)]
    slots = jnp.stack(slots + [side]).astype(jnp.int32)
    share = w_joined.shape[1]

    small = jnp.concatenate(
        [
            vectors.transpose(0, 2, 1),
            b_expand.reshape(2, share, 4),
            jnp.zeros((2, share, 116), BF16),
        ],
        axis=2,
    )
    first = jnp.concatenate([w_joined, w_output, small], axis=2)
    second, third = w_expand, w_reduce

    class Gather:
        def __init__(self, piece):
            self.stack = lax.dynamic_index_in_dim(piece, tower, 0, keepdims=True)
            self.send = lax.dynamic_index_in_dim(piece, 1 - tower, 0, keepdims=True)
            self.held = None

        def join(self, got):
            self.stack = jnp.concatenate([self.stack, got], axis=0)
            self.send = self.stack

        def move(self, first, last):
            for step in range(first, last):
                self.join(places.swap(self.send, step))

        def mid(self):
            self.move(0, 1)

        def along_z(self):
            self.move(1, z_steps)

        def pb_first(self):
            self.move(z_steps, places.steps - 1)

        def pb_last(self):
            self.held = places.swap(self.send, places.steps - 1)

        def core_stack(self):
            self.other = places.swap_core(self.stack)

        def core_held(self):
            self.parts = [self.stack, self.held, self.other, places.swap_core(self.held)]

        def whole(self, segments):
            if self.stack.shape[1] % 8 == 0:
                return assemble(self.parts, table, segments)
            return assemble_plain(self.parts, table, segments)

    z_steps = 1 + len(bits_of(places.half))

    rows_q = question_in.reshape(-1, D)
    rows_p = passage_in.reshape(-1, D)
    own_rows = rows_q.shape[0]

    def sides(q_side, p_side):
        return jnp.where(is_q, q_side, p_side), jnp.where(is_q, p_side, q_side)

    lq, lp = question_in.shape[1], passage_in.shape[1]
    rows = 2 * own_rows

    def chunked(values, sixteenths):
        out, row = [], 0
        for part in sixteenths:
            step = values.shape[0] * part // 16
            out.append(values[row : row + step])
            row += step
        return out

    def hand(values):
        return [places.swap_tower(x) for x in values]

    per_q = rows // lq
    every = lp // lq
    per_p = rows // lp
    nq, np_ = question_in.shape[0], passage_in.shape[0]
    shift = 2 * places.half
    low_pa = pa % shift
    row_ids = jnp.arange(rows, dtype=jnp.int32)
    seq = jnp.where(is_q, row_ids // lq, row_ids // lp)
    qid = seq.reshape(rows, 1)
    g1, g2, g3 = Gather(first), Gather(second), Gather(third)
    my_tokens, send_tokens = sides(rows_q, rows_p)
    tokens_out = chunked(send_tokens, (5, 6, 5))
    g1.mid()
    g1.send, tokens_out, question_cot, passage_cot = tie(
        g1.send, tokens_out, question_cot, passage_cot
    )
    g1.along_z()
    tokens_in = hand(tokens_out[:1])
    my_cot, send_cot = sides(question_cot.reshape(-1, D), passage_cot.reshape(-1, D))
    g1.send, g2.send, tokens_in, my_cot, send_cot, table, slots, seq, qid = tie(
        g1.send, g2.send, tokens_in, my_cot, send_cot, table, slots, seq, qid
    )
    g3.send, g3.stack = tie(g3.send, g3.stack)
    g1.pb_first()
    g2.mid()
    g1.stack, g2.send, tokens_out = tie(g1.stack, g2.send, tokens_out)
    g1.send = g1.stack
    g1.pb_last()
    g1.core_stack()
    g2.along_z()
    tokens_in = tokens_in + hand(tokens_out[1:2])
    g1.held, g2.send, tokens_in, tokens_out, question_len, passage_len, positive = tie(
        g1.held, g2.send, tokens_in, tokens_out, question_len, passage_len, positive
    )
    g1.core_held()
    g2.pb_first()
    tokens_in = tokens_in + hand(tokens_out[2:])
    full_j, full_o, full_small = g1.whole([(0, 3 * D), (3 * D, D), (4 * D, 128)])
    full_j, full_o, full_small, g2.stack, g3.send, tokens_in = tie(
        full_j, full_o, full_small, g2.stack, g3.send, tokens_in
    )
    g2.send = g2.stack
    g2.pb_last()
    g2.core_stack()
    g3.mid()
    wj = full_j.reshape(D, 3 * D)
    wo = full_o.reshape(D, D)
    small = full_small.reshape(D, 128).astype(F32)
    vec = small[:, :8].T
    bias_e = small[:, 8:12].reshape(1, FF)
    bias_j = jnp.concatenate([vec[0], jnp.zeros((D,), F32), vec[1]])
    tokens, qkv = project([my_tokens] + tokens_in, wj, bias_j[None])

    cot_out = chunked(send_cot, (5, 3, 3, 2, 3))
    by_pa = positive.reshape(places.pa_n, nq)
    pair = [lax.dynamic_index_in_dim(by_pa, low_pa + k, 0, keepdims=False) for k in (0, shift)]
    pair = jnp.concatenate(pair)[None]
    wanted_rows = jnp.concatenate([pair // 16, pair % 16], axis=0).astype(BF16)
    wanted_rows = jnp.pad(wanted_rows, ((0, 0), (0, D - per_q)))
    valid_q = (jnp.arange(lq, dtype=jnp.int32)[None, :] < question_len[:, None]).astype(jnp.int32)
    valid_p = (jnp.arange(lp, dtype=jnp.int32)[None, :] < passage_len[:, None]).astype(jnp.int32)
    my_valid, send_valid = sides(valid_q.reshape(-1), valid_p.reshape(-1))
    valid = jnp.concatenate([my_valid, places.swap_tower(send_valid)])
    kid = jnp.where(valid > 0, seq, -1).reshape(rows // BLOCK, 1, BLOCK)
    row_mask = valid.reshape(rows, 1).astype(F32)

    blocks = rows // BLOCK
    later = blocks // 2
    qkv, g3.send, cot_out = tie(qkv, g3.send, cot_out)
    g3.along_z()
    cot_in = hand(cot_out[:1])
    context, probs = attention(qkv, qid, kid)
    context, g2.held, g3.send, cot_in, cot_out = tie(context, g2.held, g3.send, cot_in, cot_out)
    g2.core_held()
    g3.pb_first()
    cot_in = cot_in + hand(cot_out[1:2])
    norm_one, inverse_one, mid_low, mid = add_norm(
        context, wo, tokens, row_mask, vec, (2, 3, 4), True
    )
    mid_low, g2.parts, g3.stack, cot_in, cot_out = tie(mid_low, g2.parts, g3.stack, cot_in, cot_out)
    g3.send = g3.stack
    g3.pb_last()
    g3.core_stack()
    (full_e,) = g2.whole([(0, FF)])
    we = full_e.reshape(D, FF)
    mid_low, we, cot_out = tie(mid_low, we, cot_out)
    cot_in = cot_in + hand(cot_out[2:3])
    gelu = expand(mid_low, we, bias_e, 0, 1)
    gelu, g3.held, g3.other, g3.stack, cot_in, cot_out = tie(
        gelu, g3.held, g3.other, g3.stack, cot_in, cot_out
    )
    g3.core_held()
    cot_in = cot_in + hand(cot_out[3:4])
    active, slope = expand(mid_low, we, bias_e, 1, 1, tuple(gelu))
    active, g3.parts, cot_in, cot_out = tie(active, g3.parts, cot_in, cot_out)
    (full_r,) = g3.whole([(0, D)])
    wr = full_r.reshape(FF, D)
    wr, cot_out = tie(wr, cot_out)
    cot_in = cot_in + hand(cot_out[4:])
    norm_two, inverse_two, out = add_norm(active, wr, mid, row_mask, vec, (5, 6, 7), False)
    out, cot_in = tie(out, cot_in)

    firsts = out.reshape(per_q, lq, D)[:, 0, :]
    others = places.swap_tower(firsts)
    cls_q = jnp.where(is_q, firsts, others)
    cls_p = jnp.where(is_q, others, firsts)[::every]
    pad = (-(per_q + per_p + 2)) % 8
    stack = jnp.concatenate([cls_q, cls_p, wanted_rows, jnp.zeros((pad, D), BF16)], axis=0)[None]
    pair_masks = [0]
    for bit in bits_of(places.half):
        got = lax.ppermute(stack, "pa", [(i, i ^ (2 * bit)) for i in range(places.pa_n)])
        stack = jnp.concatenate([stack, got], axis=0)
        pair_masks = pair_masks + [m ^ (2 * bit) for m in pair_masks]
    for bit in bits_of(places.pb_n):
        got = lax.ppermute(stack, "pb", [(i, i ^ bit) for i in range(places.pb_n)])
        stack = jnp.concatenate([stack, got], axis=0)
        pair_masks = pair_masks + [m ^ (bit * places.pa_n) for m in pair_masks]
    stack = jnp.concatenate([stack, places.swap_core(stack)], axis=0)
    pair_masks = pair_masks + [m ^ 1 for m in pair_masks]
    groups = len(pair_masks)
    me = pb * places.pa_n + low_pa
    place = jnp.array(pair_masks, jnp.int32) ^ me
    dev_p = jnp.stack([place + shift, place], axis=1)
    p_ids = (dev_p[:, :, None] * np_ + jnp.arange(np_, dtype=jnp.int32)).reshape(-1)
    digits = stack[:, per_q + per_p : per_q + per_p + 2, :per_q].astype(jnp.int32)
    wanted = (digits[:, 0] * 16 + digits[:, 1]).reshape(-1)

    all_q = stack[:, :per_q].reshape(groups * per_q, D)
    all_p = stack[:, per_q : per_q + per_p].reshape(groups * per_p, D)
    similarity = dot(all_q, all_p, ((1,), (1,))) * score_scale
    hot = (wanted[:, None] == p_ids[None, :]).astype(F32)
    top = jnp.max(similarity, axis=1, keepdims=True)
    grown = jnp.exp(similarity - top)
    total = jnp.sum(grown, axis=1, keepdims=True)
    own_sim = similarity[:per_q]
    loss = top[:per_q, 0] + jnp.log(total[:per_q, 0]) - jnp.sum(own_sim * hot[:per_q], axis=1)
    question_loss = lax.dynamic_slice_in_dim(loss, tower * nq, nq)
    d_sim = (loss_weight * (grown / total - hot)).astype(BF16)
    d_q = dot(d_sim[:per_q], all_p) * score_scale
    d_p = dot(d_sim[:, :per_p], all_q, ((0,), (0,))) * score_scale
    d_p = jnp.concatenate(
        [d_p.reshape(per_p, 1, D), jnp.zeros((per_p, every - 1, D), F32)], axis=1
    ).reshape(per_q, D)
    d_slot = jnp.where(is_q, d_q, d_p)

    d_second, d_reduced, sums_second = second_back(
        join([my_cot] + cot_in), d_slot, row_mask, norm_two, inverse_two, vec[6][None, :]
    )
    even = share % 8 == 0

    def gradient(left, right, **more):
        if left.shape[1] > D:
            return tall_grad(left, right, slots, places.nz)
        return weight_grad(left, right, slots, D, **more)

    def plain(left, right, extra=None):
        if extra is not None:
            one, two, first, second, bias = extra
            joined = one + two
            lines = [joined[:, :D], joined[:, 2 * D :], first[2:3], first[:2]]
            lines = lines + [second[2:3], second[:2], bias, jnp.zeros((116, D), F32)]
            extra = jnp.concatenate(lines, axis=0).T
        return grad_plain(left, right, table, extra)

    class Scatter:
        def __init__(self, mine, theirs):
            self.parts, self.theirs, self.send = [mine], theirs, None
            self.count = mine.shape[0]

        def cores(self):
            self.parts = self.parts + [places.swap_core(self.theirs)]

        def total(self, start, stop):
            out = self.parts[0][start:stop].astype(F32)
            for part in self.parts[1:]:
                out = out + part[start:stop].astype(F32)
            return out

        def prepare(self):
            self.send = self.total(self.count // 2, self.count).astype(BF16)

        def move(self, step):
            if self.send is None:
                self.prepare()
            self.parts = self.parts + [places.swap(self.send, step)]
            self.send = None
            self.count = self.count // 2

        def pb_first(self):
            self.move(places.steps - 1)

        def pb_rest(self):
            for step in range(places.steps - 2, z_steps - 1, -1):
                self.move(step)

        def along_z(self):
            for step in range(z_steps - 1, 0, -1):
                self.move(step)

        def mid(self):
            got = places.swap(self.total(1, 2).astype(BF16), 0).astype(F32)
            keep = self.total(0, 1)
            self.out = jnp.concatenate(
                [jnp.where(is_q, keep, got), jnp.where(is_q, got, keep)], axis=0
            )

    send_out = chunked(out[own_rows:], (4, 4, 4, 4))
    d_reduced, send_out = tie(d_reduced, send_out)
    got_out = hand(send_out[:1])
    sr = Scatter(*(gradient if even else plain)(active, d_reduced))
    sr.parts, sr.theirs, d_reduced, got_out, send_out = tie(
        sr.parts, sr.theirs, d_reduced, got_out, send_out
    )
    sr.cores()
    got_out = got_out + hand(send_out[1:2])
    d_expanded, g_bias_expand = hidden_grad(d_reduced, wr, slope)
    sr.parts, d_expanded, got_out, send_out = tie(sr.parts, d_expanded, got_out, send_out)
    sr.pb_first()
    got_out = got_out + hand(send_out[2:3])
    if even:
        partial = gradient(mid_low, d_expanded, room=D)
    else:
        partial = plain(mid_low, d_expanded)
    partial, d_expanded, got_out, send_out = tie(partial, d_expanded, got_out, send_out)
    got_out = got_out + hand(send_out[3:])
    d_first, d_attended, sums_first = first_back(
        d_expanded, we, d_second, norm_one, inverse_one, vec[3][None, :]
    )
    sr.parts, partial, d_attended, got_out = tie(sr.parts, partial, d_attended, got_out)
    sr.pb_rest()
    if even:
        partial = gradient(context, d_attended, into=tuple(partial))
    else:
        also = plain(context, d_attended)
        partial = [jnp.concatenate(x, axis=2) for x in zip(partial, also)]
    se = Scatter(*partial)
    se.parts, se.theirs, d_attended = tie(se.parts, se.theirs, d_attended)
    se.cores()
    d_context = dot(d_attended, wo, ((1,), (1,))).astype(BF16)
    d_joined, sums_one = attention_back(qkv, probs, d_context, later, blocks - later)
    sr.parts, se.parts, d_joined = tie(sr.parts, se.parts, d_joined)
    se.prepare()
    sr.prepare()
    sr.send, sr.parts, se.send, se.parts, d_joined = tie(
        sr.send, sr.parts, se.send, se.parts, d_joined
    )
    se.pb_first()
    sr.along_z()
    part = own_rows // 16
    send_grad = token_grad(d_joined, wj, d_first, own_rows, [k * part for k in (5, 3, 3, 5)], BF16)
    d_joined, send_grad = tie(d_joined, send_grad)
    got_grad = hand(send_grad[:1])
    d_joined, sums_two = attention_back(qkv, probs, d_context, 0, later, d_joined)
    sr.parts, se.parts, d_joined, sums_two, got_grad, send_grad = tie(
        sr.parts, se.parts, d_joined, sums_two, got_grad, send_grad
    )
    se.prepare()
    se.send, se.parts, d_joined, send_grad = tie(se.send, se.parts, d_joined, send_grad)
    se.pb_rest()
    sr.mid()
    got_grad = got_grad + hand(send_grad[1:2])
    bias_sums = g_bias_expand.reshape(D, 4).T
    small_sums = (sums_one, sums_two, sums_first, sums_second, bias_sums)
    sj = Scatter(*(gradient if even else plain)(tokens, d_joined, extra=small_sums))
    se.parts, sr.out, sj.parts, sj.theirs, d_joined, got_grad, send_grad = tie(
        se.parts, sr.out, sj.parts, sj.theirs, d_joined, got_grad, send_grad
    )
    sj.cores()
    got_grad = got_grad + hand(send_grad[2:3])
    (own_grad,) = token_grad(d_joined, wj, d_first, 0, [own_rows], F32)
    sj.parts, own_grad, got_grad, send_grad = tie(sj.parts, own_grad, got_grad, send_grad)
    sj.pb_first()
    se.along_z()
    got_grad = got_grad + hand(send_grad[3:])
    sj.parts, se.parts, got_grad, send_grad = tie(sj.parts, se.parts, got_grad, send_grad)
    sj.pb_rest()
    se.mid()
    sj.parts, se.out, got_out, out = tie(sj.parts, se.out, got_out, out)
    sj.along_z()
    out_q, out_p = deal(tower.reshape(1), out, got_out)
    sj.parts, out_q, out_p, got_grad = tie(sj.parts, out_q, out_p, got_grad)
    grad_q, grad_p = deal(tower.reshape(1), own_grad, got_grad)
    sj.mid()
    grad_joined = sj.out[:, :, : 3 * D]
    grad_expand, grad_output, grad_reduce = se.out[:, :, :FF], se.out[:, :, FF:], sr.out
    extra = sj.out[:, :, 3 * D :]
    grad_vectors = extra[:, :, :8].transpose(0, 2, 1)
    grad_b_expand = extra[:, :, 8:12].reshape(2, 4 * share)

    return (
        out_q.reshape(question_in.shape),
        out_p.reshape(passage_in.shape),
        question_loss,
        grad_q.reshape(question_in.shape),
        grad_p.reshape(passage_in.shape),
        grad_joined,
        grad_output,
        grad_expand,
        grad_reduce,
        grad_vectors,
        grad_b_expand,
    )


def solution(mesh):
    in_specs = (
        P(("pb", "pa"), None, None),
        P(("pb", "pa"), None, None),
        P(("pb", "pa")),
        P(("pb", "pa")),
        P("pb"),
        P(("pb", "pa"), None, None),
        P(("pb", "pa"), None, None),
        P(None, ("pb", "pa"), None),
        P(None, ("pb", "pa"), None),
        P(None, ("pb", "pa"), None),
        P(None, ("pb", "pa"), None),
        P(None, None, ("pb", "pa")),
        P(None, ("pb", "pa")),
    )
    out_specs = (
        P(("pb", "pa"), None, None),
        P(("pb", "pa"), None, None),
        P(("pb", "pa")),
        P(("pb", "pa"), None, None),
        P(("pb", "pa"), None, None),
        P(None, ("pb", "pa"), None),
        P(None, ("pb", "pa"), None),
        P(None, ("pb", "pa"), None),
        P(None, ("pb", "pa"), None),
        P(None, None, ("pb", "pa")),
        P(None, ("pb", "pa")),
    )
    return jax.shard_map(
        functools.partial(per_device, Places(mesh)),
        mesh=mesh,
        in_specs=in_specs,
        out_specs=out_specs,
        check_vma=False,
    )
```

```python
import functools

import jax
import jax.numpy as jnp
from jax import lax
from jax.experimental import pallas as pl
from jax.experimental.pallas import tpu as pltpu
from jax.sharding import PartitionSpec as P

D = 768
HEADS = 12
HDIM = 64
FF = 3072
AXES = ("pb", "pa")
BLOCK = 256

norm_eps = 1e-06
masked_score = -1000000000.0
score_scale = 0.0625
loss_weight = 16.0
head_scale = HDIM ** (-0.5)
F32 = jnp.float32
BF16 = jnp.bfloat16
VMEM_LIMIT = 56 * 1024 * 1024


def bits_of(count):
    return [1 << shift for shift in range(count.bit_length() - 1)]


class Places:
    def __init__(self, mesh):
        self.pb_n = mesh.shape["pb"]
        self.pa_n = mesh.shape["pa"]
        self.nz = self.pa_n // 2
        self.half = self.nz // 2
        self.chips = self.pb_n * self.nz
        pb_bits = bits_of(self.pb_n)
        turn = len(pb_bits) // 2
        low_z = [("z", bit) for bit in bits_of(self.half)]
        first = [("pb", bit) for bit in pb_bits]
        second = first[turn:] + first[:turn]
        self.orders = ([("z", self.half)] + low_z + first, [("z", self.half)] + low_z + second)
        self.steps = len(self.orders[0])

    def chip_mask(self, move):
        axis, bit = move
        return bit * self.nz if axis == "pb" else bit

    def stack_masks(self, core):
        masks = [0]
        for move in self.orders[core]:
            masks = masks + [mask ^ self.chip_mask(move) for mask in masks]
        return masks

    def pairs(self, step):
        out = []
        for pb in range(self.pb_n):
            for pa in range(self.pa_n):
                axis, bit = self.orders[pa % 2][step]
                to_pb, to_pa = (pb ^ bit, pa) if axis == "pb" else (pb, pa ^ (2 * bit))
                out.append((pb * self.pa_n + pa, to_pb * self.pa_n + to_pa))
        return out

    def swap(self, values, step):
        return lax.ppermute(values, AXES, self.pairs(step))

    def swap_core(self, values):
        return lax.ppermute(values, "pa", [(i, i ^ 1) for i in range(self.pa_n)])

    def swap_tower(self, values):
        return lax.ppermute(values, "pa", [(i, i ^ (2 * self.half)) for i in range(self.pa_n)])


def dot(left, right, dims=((1,), (0,))):
    return lax.dot_general(left, right, (dims, ((), ())), preferred_element_type=F32)


def tie(*values):
    return lax.optimization_barrier(values)


def assemble_kernel(segments, idx_ref, *refs):
    count = len(segments)
    sources, outs = refs[:4], refs[4 : 4 + count]
    buffer, in_sem, out_sem = refs[4 + count :]
    core = idx_ref[2, 0]
    part = sources[0].shape[0]
    loads = [
        pltpu.make_async_copy(source, buffer.at[pl.ds(k * part, part)], in_sem.at[k])
        for k, source in enumerate(sources)
    ]
    for load in loads:
        load.start()
    stores = []
    for k in range(4):
        loads[k].wait()
        half = core if k < 2 else 1 - core
        for j in range(part):
            slot = k * part + j
            place = idx_ref[k // 2, (k % 2) * part + j]
            for s, (start, width) in enumerate(segments):
                store = pltpu.make_async_copy(
                    buffer.at[slot, :, pl.ds(start, width)],
                    outs[s].at[place, half],
                    out_sem.at[s, slot],
                )
                store.start()
                stores.append(store)
    for store in stores:
        store.wait()


def assemble(parts, table, segments):
    part, rows, width = parts[0].shape
    chips = 2 * part
    shapes = [jax.ShapeDtypeStruct((chips, 2, rows, w), BF16) for _, w in segments]
    return pl.pallas_call(
        functools.partial(assemble_kernel, segments),
        out_shape=shapes,
        in_specs=[pl.BlockSpec(memory_space=pltpu.SMEM)] + [pl.BlockSpec(memory_space=pl.ANY)] * 4,
        out_specs=[pl.BlockSpec(memory_space=pl.ANY)] * len(segments),
        scratch_shapes=[
            pltpu.VMEM((2 * chips, rows, width), BF16),
            pltpu.SemaphoreType.DMA((4,)),
            pltpu.SemaphoreType.DMA((len(segments), 2 * chips)),
        ],
        compiler_params=pltpu.CompilerParams(vmem_limit_bytes=VMEM_LIMIT),
        cost_estimate=pl.CostEstimate(
            flops=0, bytes_accessed=4 * 2 * chips * rows * width, transcendentals=0
        ),
        name="assemble",
    )(table, *parts)


def assemble_plain(parts, table, segments):
    own = jnp.take(jnp.concatenate(parts[:2], axis=0), jnp.argsort(table[0]), axis=0)
    other = jnp.take(jnp.concatenate(parts[2:], axis=0), jnp.argsort(table[1]), axis=0)
    first = table[2, 0] == 0
    both = jnp.stack([jnp.where(first, own, other), jnp.where(first, other, own)], axis=1)
    return [both[..., start : start + w] for start, w in segments]


def split_slabs(acc, core, chips, mine_ref, theirs_ref, cols, within):
    rows = acc.shape[0] // (2 * chips)
    for s in range(chips):
        low = acc[2 * s * rows : (2 * s + 1) * rows]
        high = acc[(2 * s + 1) * rows : (2 * s + 2) * rows]
        mine, theirs = within(s)
        mine_ref[mine, :, cols] = jnp.where(core == 0, low, high).astype(BF16)
        theirs_ref[theirs, :, cols] = jnp.where(core == 0, high, low).astype(BF16)


def weight_grad_kernel(chips, extra, table_ref, left_ref, right_ref, *refs):
    mine_ref, theirs_ref = refs[-2:]
    core = table_ref[2, 0]
    acc = dot(left_ref[...], right_ref[...], ((0,), (0,)))
    width = acc.shape[1]

    def within(s):
        return table_ref[0, s], table_ref[1, s]

    if extra == 0:
        split_slabs(acc, core, chips, mine_ref, theirs_ref, slice(None), within)
        return
    step = pl.program_id(0)
    cols = pl.ds(pl.multiple_of(step * width, 128), width)
    split_slabs(acc, core, chips, mine_ref, theirs_ref, cols, within)

    @pl.when(step == 0)
    def _():
        one, two, first, second, bias = (ref[...] for ref in refs[:extra])
        joined = one + two
        lines = [
            joined[:, :D],
            joined[:, 2 * D :],
            first[2:3],
            first[:2],
            second[2:3],
            second[:2],
            bias,
            jnp.zeros((116, D), F32),
        ]
        values = jnp.concatenate(lines, axis=0).T
        tail = pl.ds(mine_ref.shape[2] - 128, 128)
        split_slabs(values, core, chips, mine_ref, theirs_ref, tail, within)


def weight_grad(left, right, slots, tile, extra=None, room=0, into=()):
    rows, height = left.shape
    width = right.shape[1]
    chips = slots.shape[1]
    slab = height // (2 * chips)
    total = width + (room if extra is None else 128)
    first = 0
    if into:
        total = into[0].shape[2]
        first = (total - width) // tile
    block = (chips, slab, total if extra is not None else tile)
    place = (lambda j, t: (0, 0, 0)) if extra is not None else (lambda j, t: (0, 0, j + first))
    return pl.pallas_call(
        functools.partial(weight_grad_kernel, chips, len(extra or ())),
        grid_spec=pltpu.PrefetchScalarGridSpec(
            num_scalar_prefetch=1,
            grid=(width // tile,),
            in_specs=[
                pl.BlockSpec((rows, height), lambda j, t: (0, 0)),
                pl.BlockSpec((rows, tile), lambda j, t: (0, j)),
            ]
            + [pl.BlockSpec(x.shape, lambda j, t: (0, 0)) for x in extra or ()]
            + [pl.BlockSpec(memory_space=pl.ANY)] * len(into),
            out_specs=[pl.BlockSpec(block, place)] * 2,
        ),
        out_shape=[jax.ShapeDtypeStruct((chips, slab, total), BF16)] * 2,
        input_output_aliases={3: 0, 4: 1} if into else {},
        compiler_params=pltpu.CompilerParams(vmem_limit_bytes=VMEM_LIMIT),
        cost_estimate=pl.CostEstimate(
            flops=2 * rows * height * width,
            bytes_accessed=2 * (rows * (height + width) + height * width),
            transcendentals=0,
        ),
        name="weight_grad",
    )(slots, left, right, *(extra or ()), *into)


def tall_grad_kernel(chips, table_ref, left_ref, right_ref, mine_ref, theirs_ref):
    core = table_ref[2, 0]
    acc = dot(left_ref[...], right_ref[...], ((0,), (0,)))
    base = pl.program_id(0) * chips

    def within(s):
        return table_ref[0, base + s] % chips, table_ref[1, base + s] % chips

    split_slabs(acc, core, chips, mine_ref, theirs_ref, slice(None), within)


def tall_grad(left, right, slots, column):
    rows, height = left.shape
    width = right.shape[1]
    chips = slots.shape[1]
    slab = height // (2 * chips)
    tile = height // chips * column
    return pl.pallas_call(
        functools.partial(tall_grad_kernel, column),
        grid_spec=pltpu.PrefetchScalarGridSpec(
            num_scalar_prefetch=1,
            grid=(chips // column,),
            in_specs=[
                pl.BlockSpec((rows, tile), lambda i, t: (0, i)),
                pl.BlockSpec((rows, width), lambda i, t: (0, 0)),
            ],
            out_specs=[
                pl.BlockSpec((column, slab, width), lambda i, t: (t[0, i * column] // column, 0, 0)),
                pl.BlockSpec((column, slab, width), lambda i, t: (t[1, i * column] // column, 0, 0)),
            ],
        ),
        out_shape=[jax.ShapeDtypeStruct((chips, slab, width), BF16)] * 2,
        compiler_params=pltpu.CompilerParams(vmem_limit_bytes=VMEM_LIMIT),
        cost_estimate=pl.CostEstimate(
            flops=2 * rows * height * width,
            bytes_accessed=2 * (rows * (height + width) + height * width),
            transcendentals=0,
        ),
        name="tall_grad",
    )(slots, left, right)


def grad_plain(left, right, table, extra=None):
    full = dot(left, right, ((0,), (0,)))
    if extra is not None:
        full = jnp.concatenate([full, extra], axis=1)
    chips = table.shape[1]
    full = full.astype(BF16).reshape(chips, 2, full.shape[0] // (2 * chips), full.shape[1])
    core = table[2, 0]
    mine = lax.dynamic_index_in_dim(full, core, 1, keepdims=False)
    theirs = lax.dynamic_index_in_dim(full, 1 - core, 1, keepdims=False)
    return jnp.take(mine, table[0], axis=0), jnp.take(theirs, table[1], axis=0)


def hidden_grad_kernel(grad_ref, w_ref, slope_ref, out_ref, sum_ref):
    grad = dot(grad_ref[...], w_ref[...], ((1,), (1,))) * slope_ref[...].astype(F32)
    low = grad.astype(BF16)
    out_ref[...] = low
    sum_ref[...] = jnp.sum(low.astype(F32), axis=0, keepdims=True)


def hidden_grad(grad, w_reduce, slope):
    rows, tile = grad.shape[0], 512
    return pl.pallas_call(
        hidden_grad_kernel,
        grid=(FF // tile,),
        in_specs=[
            pl.BlockSpec((rows, D), lambda j: (0, 0)),
            pl.BlockSpec((tile, D), lambda j: (j, 0)),
            pl.BlockSpec((rows, tile), lambda j: (0, j)),
        ],
        out_specs=[
            pl.BlockSpec((rows, tile), lambda j: (0, j)),
            pl.BlockSpec((1, tile), lambda j: (0, j)),
        ],
        out_shape=[
            jax.ShapeDtypeStruct((rows, FF), BF16),
            jax.ShapeDtypeStruct((1, FF), F32),
        ],
        compiler_params=pltpu.CompilerParams(vmem_limit_bytes=VMEM_LIMIT),
        cost_estimate=pl.CostEstimate(
            flops=2 * rows * D * FF,
            bytes_accessed=2 * (rows * D + D * FF + 2 * rows * FF),
            transcendentals=0,
        ),
        name="hidden_grad",
    )(grad, w_reduce, slope)


def attention_kernel(qkv_ref, qid_ref, kid_ref, context_ref, probs_ref):
    allowed = qid_ref[...] == kid_ref[0]
    lane = lax.broadcasted_iota(jnp.int32, (BLOCK, 128), 1)
    zero = jnp.zeros((BLOCK, 128), BF16)
    for pair in range(HEADS // 2):
        queries = qkv_ref[:, pair * 128 : pair * 128 + 128]
        keys = qkv_ref[:, D + pair * 128 : D + pair * 128 + 128]
        values = qkv_ref[:, 2 * D + pair * 128 : 2 * D + pair * 128 + 128]
        outs = []
        for side in range(2):
            mine = (lane < HDIM) if side == 0 else (lane >= HDIM)
            scores = dot(queries, jnp.where(mine, keys, zero), ((1,), (1,))) * head_scale
            scores = jnp.where(allowed, scores, masked_score)
            top = jnp.max(scores, axis=1, keepdims=True)
            grown = jnp.exp(scores - top)
            total = jnp.sum(grown, axis=1, keepdims=True)
            probs = (grown * (1.0 / total)).astype(BF16)
            probs_ref[0, 2 * pair + side] = probs
            outs.append(dot(probs, values))
        context_ref[:, pair * 128 : pair * 128 + 128] = jnp.where(
            lane < HDIM, outs[0], outs[1]
        ).astype(BF16)


def attention(qkv, qid, kid):
    rows = qkv.shape[0]
    blocks = rows // BLOCK
    return pl.pallas_call(
        attention_kernel,
        grid=(blocks,),
        in_specs=[
            pl.BlockSpec((BLOCK, 3 * D), lambda i: (i, 0)),
            pl.BlockSpec((BLOCK, 1), lambda i: (i, 0)),
            pl.BlockSpec((1, 1, BLOCK), lambda i: (i, 0, 0)),
        ],
        out_specs=[
            pl.BlockSpec((BLOCK, D), lambda i: (i, 0)),
            pl.BlockSpec((1, HEADS, BLOCK, BLOCK), lambda i: (i, 0, 0, 0)),
        ],
        out_shape=[
            jax.ShapeDtypeStruct((rows, D), BF16),
            jax.ShapeDtypeStruct((blocks, HEADS, BLOCK, BLOCK), BF16),
        ],
        compiler_params=pltpu.CompilerParams(vmem_limit_bytes=VMEM_LIMIT),
        cost_estimate=pl.CostEstimate(
            flops=4 * rows * BLOCK * D * 2,
            bytes_accessed=rows * (4 * D + HEADS * BLOCK) * 2,
            transcendentals=rows * HEADS * BLOCK,
        ),
        name="attention",
    )(qkv, qid, kid)


def attention_back_kernel(qkv_ref, probs_ref, grad_ref, out_ref, sum_ref):
    lane = lax.broadcasted_iota(jnp.int32, (BLOCK, 128), 1)
    zero = jnp.zeros((BLOCK, 128), BF16)

    def at(pair, start=0):
        return pl.ds(pl.multiple_of(start + pair * 128, 128), 128)

    def some(step, carry):
        for k in range(2):
            pair = step * 2 + k
            cols = at(pair)
            queries = qkv_ref[:, at(pair)]
            keys = qkv_ref[:, at(pair, D)]
            values = qkv_ref[:, at(pair, 2 * D)]
            grad = grad_ref[:, cols]
            d_q, d_k, d_v = [], [], []
            for side in range(2):
                mine = (lane < HDIM) if side == 0 else (lane >= HDIM)
                low = probs_ref[0, 2 * pair + side]
                d_probs = dot(jnp.where(mine, grad, zero), values, ((1,), (1,)))
                d_v.append(dot(low, grad, ((0,), (0,))))
                probs = low.astype(F32)
                row_dot = jnp.sum(d_probs * probs, axis=1, keepdims=True)
                d_scores = (probs * (d_probs - row_dot)).astype(BF16)
                d_q.append(dot(d_scores, keys))
                d_k.append(dot(d_scores, queries, ((0,), (0,))))
            first = lane < HDIM
            out_ref[:, at(pair)] = (
                jnp.where(first, d_q[0], d_q[1]) * head_scale
            ).astype(BF16)
            out_ref[:, at(pair, D)] = (
                jnp.where(first, d_k[0], d_k[1]) * head_scale
            ).astype(BF16)
            out_ref[:, at(pair, 2 * D)] = jnp.where(
                first, d_v[0], d_v[1]
            ).astype(BF16)
        return carry

    lax.fori_loop(0, HEADS // 2 // 2, some, 0)
    sums = jnp.sum(out_ref[...].astype(F32), axis=0, keepdims=True)

    @pl.when(pl.program_id(0) == 0)
    def _():
        sum_ref[...] = sums

    @pl.when(pl.program_id(0) > 0)
    def _():
        sum_ref[...] += sums


def attention_back_more_kernel(qkv_ref, probs_ref, grad_ref, _, out_ref, sum_ref):
    attention_back_kernel(qkv_ref, probs_ref, grad_ref, out_ref, sum_ref)


def attention_back(qkv, probs, grad_context, start, count, into=None):
    rows = qkv.shape[0]
    more = into is not None
    return pl.pallas_call(
        attention_back_more_kernel if more else attention_back_kernel,
        grid=(count,),
        in_specs=[
            pl.BlockSpec((BLOCK, 3 * D), lambda i: (i + start, 0)),
            pl.BlockSpec((1, HEADS, BLOCK, BLOCK), lambda i: (i + start, 0, 0, 0)),
            pl.BlockSpec((BLOCK, D), lambda i: (i + start, 0)),
        ]
        + ([pl.BlockSpec(memory_space=pl.ANY)] if more else []),
        out_specs=[
            pl.BlockSpec((BLOCK, 3 * D), lambda i: (i + start, 0)),
            pl.BlockSpec((1, 3 * D), lambda i: (0, 0)),
        ],
        out_shape=[
            jax.ShapeDtypeStruct((rows, 3 * D), BF16),
            jax.ShapeDtypeStruct((1, 3 * D), F32),
        ],
        input_output_aliases={3: 0} if more else {},
        compiler_params=pltpu.CompilerParams(vmem_limit_bytes=VMEM_LIMIT),
        cost_estimate=pl.CostEstimate(
            flops=8 * count * BLOCK * BLOCK * D * 2,
            bytes_accessed=count * BLOCK * (7 * D + HEADS * BLOCK) * 2,
            transcendentals=0,
        ),
        name="attention_back",
    )(qkv, probs, grad_context, *([into] if more else []))


def join_kernel(*refs):
    row = 0
    for piece in refs[:-1]:
        rows = piece.shape[0]
        refs[-1][row : row + rows, :] = piece[...]
        row += rows


def join(pieces):
    rows, width = sum(x.shape[0] for x in pieces), pieces[0].shape[1]
    return pl.pallas_call(
        join_kernel,
        grid=(1,),
        in_specs=[pl.BlockSpec(x.shape, lambda i: (0, 0)) for x in pieces],
        out_specs=pl.BlockSpec((rows, width), lambda i: (0, 0)),
        out_shape=jax.ShapeDtypeStruct((rows, width), pieces[0].dtype),
        compiler_params=pltpu.CompilerParams(vmem_limit_bytes=VMEM_LIMIT),
        cost_estimate=pl.CostEstimate(
            flops=0, bytes_accessed=4 * rows * width, transcendentals=0
        ),
        name="join",
    )(*pieces)


def deal_kernel(tower_ref, own_ref, *refs):
    pieces, (q_ref, p_ref) = refs[:-2], refs[-2:]

    def give(own_out, other_out):
        own_out[...] = own_ref[...]
        row = 0
        for piece in pieces:
            rows = piece.shape[0]
            other_out[row : row + rows, :] = piece[...].astype(other_out.dtype)
            row += rows

    @pl.when(tower_ref[0] == 0)
    def _():
        give(q_ref, p_ref)

    @pl.when(tower_ref[0] != 0)
    def _():
        give(p_ref, q_ref)


def deal(tower, own, pieces):
    rows, width = sum(x.shape[0] for x in pieces), own.shape[1]
    shape = jax.ShapeDtypeStruct((rows, width), own.dtype)
    return pl.pallas_call(
        deal_kernel,
        grid=(1,),
        in_specs=[
            pl.BlockSpec(memory_space=pltpu.SMEM),
            pl.BlockSpec((rows, width), lambda i: (0, 0)),
        ]
        + [pl.BlockSpec(x.shape, lambda i: (0, 0)) for x in pieces],
        out_specs=[pl.BlockSpec((rows, width), lambda i: (0, 0))] * 2,
        out_shape=[shape] * 2,
        compiler_params=pltpu.CompilerParams(vmem_limit_bytes=VMEM_LIMIT),
        cost_estimate=pl.CostEstimate(
            flops=0, bytes_accessed=12 * rows * width, transcendentals=0
        ),
        name="deal",
    )(tower, own, *pieces)


def add_sums(sum_ref, values):
    total = jnp.concatenate(
        [jnp.sum(x, axis=0, keepdims=True) for x in values]
        + [jnp.zeros((8 - len(values), values[0].shape[1]), F32)],
        axis=0,
    )

    @pl.when(pl.program_id(0) == 0)
    def _():
        sum_ref[...] = total

    @pl.when(pl.program_id(0) > 0)
    def _():
        sum_ref[...] += total


def second_back_kernel(
    cot_ref, slot_ref, mask_ref, norm_ref, inverse_ref, gain_ref, grad_ref, low_ref, sum_ref
):
    group = slot_ref.shape[1]
    cot = cot_ref[...].astype(F32).reshape(group, BLOCK // group, D)
    first = lax.broadcasted_iota(jnp.int32, cot.shape, 1) == 0
    grad = cot + jnp.where(first, slot_ref[0][:, None, :], 0.0)
    grad = grad.reshape(BLOCK, D) * mask_ref[...]
    norm = norm_ref[...]
    second = norm_back(grad, gain_ref[...], norm, inverse_ref[...])
    low = second.astype(BF16)
    grad_ref[...] = second
    low_ref[...] = low
    add_sums(sum_ref, [grad * norm, grad, low.astype(F32)])


def second_back(cot, d_slot, mask, norm, inverse, gain):
    rows = cot.shape[0]
    blocks = rows // BLOCK
    wide = pl.BlockSpec((BLOCK, D), lambda i: (i, 0))
    thin = pl.BlockSpec((BLOCK, 1), lambda i: (i, 0))
    group = d_slot.shape[0] // blocks
    return pl.pallas_call(
        second_back_kernel,
        grid=(blocks,),
        in_specs=[
            wide,
            pl.BlockSpec((1, group, D), lambda i: (i, 0, 0)),
            thin,
            wide,
            thin,
            pl.BlockSpec((1, D), lambda i: (0, 0)),
        ],
        out_specs=[wide, wide, pl.BlockSpec((8, D), lambda i: (0, 0))],
        out_shape=[
            jax.ShapeDtypeStruct((rows, D), F32),
            jax.ShapeDtypeStruct((rows, D), BF16),
            jax.ShapeDtypeStruct((8, D), F32),
        ],
        compiler_params=pltpu.CompilerParams(vmem_limit_bytes=VMEM_LIMIT),
        cost_estimate=pl.CostEstimate(
            flops=20 * rows * D, bytes_accessed=12 * rows * D, transcendentals=0
        ),
        name="second_back",
    )(cot, d_slot.reshape(blocks, group, D), mask, norm, inverse, gain)


def first_back_kernel(
    hidden_ref, w_ref, second_ref, norm_ref, inverse_ref, gain_ref, grad_ref, low_ref, sum_ref
):
    grad = second_ref[...] + dot(hidden_ref[...], w_ref[...], ((1,), (1,)))
    norm = norm_ref[...]
    first = norm_back(grad, gain_ref[...], norm, inverse_ref[...])
    low = first.astype(BF16)
    grad_ref[...] = first
    low_ref[...] = low
    add_sums(sum_ref, [grad * norm, grad, low.astype(F32)])


def first_back(d_expanded, w_expand, d_second, norm, inverse, gain):
    rows = d_expanded.shape[0]
    wide = pl.BlockSpec((BLOCK, D), lambda i: (i, 0))
    return pl.pallas_call(
        first_back_kernel,
        grid=(rows // BLOCK,),
        in_specs=[
            pl.BlockSpec((BLOCK, FF), lambda i: (i, 0)),
            pl.BlockSpec((D, FF), lambda i: (0, 0)),
            wide,
            wide,
            pl.BlockSpec((BLOCK, 1), lambda i: (i, 0)),
            pl.BlockSpec((1, D), lambda i: (0, 0)),
        ],
        out_specs=[wide, wide, pl.BlockSpec((8, D), lambda i: (0, 0))],
        out_shape=[
            jax.ShapeDtypeStruct((rows, D), F32),
            jax.ShapeDtypeStruct((rows, D), BF16),
            jax.ShapeDtypeStruct((8, D), F32),
        ],
        compiler_params=pltpu.CompilerParams(vmem_limit_bytes=VMEM_LIMIT),
        cost_estimate=pl.CostEstimate(
            flops=2 * rows * D * FF,
            bytes_accessed=2 * (rows * FF + D * FF) + 14 * rows * D,
            transcendentals=0,
        ),
        name="first_back",
    )(d_expanded, w_expand, d_second, norm, inverse, gain)


def expand_kernel(mid_ref, w_ref, b_ref, active_ref, slope_ref):
    expanded = dot(mid_ref[...], w_ref[...]) + b_ref[...]
    phi = 0.5 + 0.5 * lax.erf(expanded * 0.7071067811865476)
    density = jnp.exp(expanded * expanded * -0.5) * 0.3989422804014327
    active_ref[...] = (expanded * phi).astype(BF16)
    slope_ref[...] = (phi + expanded * density).astype(BF16)


def expand_more_kernel(mid_ref, w_ref, b_ref, _, __, active_ref, slope_ref):
    expand_kernel(mid_ref, w_ref, b_ref, active_ref, slope_ref)


def expand(mid_low, w_expand, b_expand, start, count, into=()):
    rows = mid_low.shape[0]
    tile_r, tile_f = 256, FF // 2
    return pl.pallas_call(
        expand_more_kernel if into else expand_kernel,
        grid=(count, rows // tile_r),
        in_specs=[
            pl.BlockSpec((tile_r, D), lambda j, i: (i, 0)),
            pl.BlockSpec((D, tile_f), lambda j, i: (0, j + start)),
            pl.BlockSpec((1, tile_f), lambda j, i: (0, j + start)),
        ]
        + [pl.BlockSpec(memory_space=pl.ANY)] * len(into),
        out_specs=[
            pl.BlockSpec((tile_r, tile_f), lambda j, i: (i, j + start)),
            pl.BlockSpec((tile_r, tile_f), lambda j, i: (i, j + start)),
        ],
        out_shape=[jax.ShapeDtypeStruct((rows, FF), BF16)] * 2,
        input_output_aliases={3: 0, 4: 1} if into else {},
        compiler_params=pltpu.CompilerParams(vmem_limit_bytes=VMEM_LIMIT),
        cost_estimate=pl.CostEstimate(
            flops=2 * rows * D * count * tile_f,
            bytes_accessed=2 * (rows * D + D * count * tile_f + 2 * rows * count * tile_f),
            transcendentals=2 * rows * count * tile_f,
        ),
        name="expand",
    )(mid_low, w_expand, b_expand, *into)


def token_grad_kernel(grad_ref, w_ref, first_ref, *outs):
    block = first_ref[...] + dot(grad_ref[...], w_ref[...], ((1,), (1,)))
    block = block.astype(outs[0].dtype)
    step, start = pl.program_id(0), 0
    for out in outs:
        stop = start + out.shape[0]
        for k in range(start // BLOCK, (stop - 1) // BLOCK + 1):
            low, high = max(start, k * BLOCK), min(stop, (k + 1) * BLOCK)

            @pl.when(step == k)
            def _(out=out, k=k, low=low, high=high, start=start):
                out[low - start : high - start, :] = block[low - k * BLOCK : high - k * BLOCK]

        start = stop


def token_grad(d_joined, weight, d_first, start, pieces, dtype):
    width = weight.shape[1]
    first, count = start // BLOCK, sum(pieces) // BLOCK
    return pl.pallas_call(
        token_grad_kernel,
        grid=(count,),
        in_specs=[
            pl.BlockSpec((BLOCK, width), lambda i: (i + first, 0)),
            pl.BlockSpec((D, width), lambda i: (0, 0)),
            pl.BlockSpec((BLOCK, D), lambda i: (i + first, 0)),
        ],
        out_specs=[pl.BlockSpec((n, D), lambda i: (0, 0)) for n in pieces],
        out_shape=[jax.ShapeDtypeStruct((n, D), dtype) for n in pieces],
        compiler_params=pltpu.CompilerParams(vmem_limit_bytes=VMEM_LIMIT),
        cost_estimate=pl.CostEstimate(
            flops=2 * count * BLOCK * D * width,
            bytes_accessed=2 * D * width + count * BLOCK * (2 * width + 6 * D),
            transcendentals=0,
        ),
        name="token_grad",
    )(d_joined, weight, d_first)


def project_kernel(w_ref, b_ref, *refs):
    pieces, (tokens_ref, out_ref) = refs[:-2], refs[-2:]
    step = pl.program_id(0)

    @pl.when(step == 0)
    def _():
        join_kernel(*pieces, tokens_ref)

    tokens = tokens_ref[pl.ds(pl.multiple_of(step * BLOCK, BLOCK), BLOCK), :]
    out_ref[...] = (dot(tokens, w_ref[...]) + b_ref[...]).astype(BF16)


def project(pieces, weight, bias):
    rows, width = sum(x.shape[0] for x in pieces), weight.shape[1]
    return pl.pallas_call(
        project_kernel,
        grid=(rows // BLOCK,),
        in_specs=[
            pl.BlockSpec((D, width), lambda i: (0, 0)),
            pl.BlockSpec((1, width), lambda i: (0, 0)),
        ]
        + [pl.BlockSpec(x.shape, lambda i: (0, 0)) for x in pieces],
        out_specs=[
            pl.BlockSpec((rows, D), lambda i: (0, 0)),
            pl.BlockSpec((BLOCK, width), lambda i: (i, 0)),
        ],
        out_shape=[
            jax.ShapeDtypeStruct((rows, D), BF16),
            jax.ShapeDtypeStruct((rows, width), BF16),
        ],
        compiler_params=pltpu.CompilerParams(vmem_limit_bytes=VMEM_LIMIT),
        cost_estimate=pl.CostEstimate(
            flops=2 * rows * D * width,
            bytes_accessed=2 * (rows * (2 * D + width) + D * width),
            transcendentals=0,
        ),
        name="project",
    )(weight, bias, *pieces)


def add_norm_kernel(
    rows_of, left_ref, w_ref, base_ref, mask_ref, vec_ref, norm_ref, inverse_ref, low_ref, *more
):
    bias, gain, shift = (vec_ref[k : k + 1, :] for k in rows_of)
    norm, inverse = normalized(base_ref[...].astype(F32) + dot(left_ref[...], w_ref[...]) + bias)
    value = norm * gain + shift
    norm_ref[...] = norm
    inverse_ref[...] = inverse
    if more:
        more[0][...] = value
        low_ref[...] = value.astype(BF16)
    else:
        low_ref[...] = (value * mask_ref[...]).astype(BF16)


def add_norm(left, weight, base, mask, vec, rows_of, keep):
    rows, depth = left.shape
    wide = pl.BlockSpec((BLOCK, D), lambda i: (i, 0))
    thin = pl.BlockSpec((BLOCK, 1), lambda i: (i, 0))
    shape = jax.ShapeDtypeStruct((rows, D), F32)
    return pl.pallas_call(
        functools.partial(add_norm_kernel, rows_of),
        grid=(rows // BLOCK,),
        in_specs=[
            pl.BlockSpec((BLOCK, depth), lambda i: (i, 0)),
            pl.BlockSpec((depth, D), lambda i: (0, 0)),
            wide,
            thin,
            pl.BlockSpec((8, D), lambda i: (0, 0)),
        ],
        out_specs=[wide, thin, wide] + [wide] * keep,
        out_shape=[
            shape,
            jax.ShapeDtypeStruct((rows, 1), F32),
            jax.ShapeDtypeStruct((rows, D), BF16),
        ]
        + [shape] * keep,
        compiler_params=pltpu.CompilerParams(vmem_limit_bytes=VMEM_LIMIT),
        cost_estimate=pl.CostEstimate(
            flops=2 * rows * D * depth,
            bytes_accessed=2 * (rows + D) * depth + 12 * rows * D,
            transcendentals=0,
        ),
        name="add_norm",
    )(left, weight, base, mask, vec)


def normalized(values):
    centred = values - jnp.mean(values, axis=-1, keepdims=True)
    spread = jnp.mean(centred * centred, axis=-1, keepdims=True)
    inverse = lax.rsqrt(spread + norm_eps)
    return centred * inverse, inverse


def norm_back(grad, gain, norm, inverse):
    scaled = grad * gain
    return inverse * (
        scaled
        - jnp.mean(scaled, axis=-1, keepdims=True)
        - norm * jnp.mean(scaled * norm, axis=-1, keepdims=True)
    )


def per_device(places, *args):
    (
        question_in,
        passage_in,
        question_len,
        passage_len,
        positive,
        question_cot,
        passage_cot,
        w_joined,
        w_output,
        w_expand,
        w_reduce,
        vectors,
        b_expand,
    ) = args
    pb, pa = lax.axis_index("pb"), lax.axis_index("pa")
    z, core = pa // 2, pa % 2
    tower = z // places.half
    is_q = tower == 0
    chip = pb * places.nz + z
    masks = [places.stack_masks(side) for side in range(2)]
    slots_of = [sorted(range(places.chips), key=side.__getitem__) for side in masks]

    def of_core(rows_of):
        both = jnp.array(rows_of, jnp.int32)
        return (
            lax.dynamic_index_in_dim(both, core, 0, keepdims=False),
            lax.dynamic_index_in_dim(both, 1 - core, 0, keepdims=False),
        )

    side = jnp.full((places.chips,), core, jnp.int32)
    table = jnp.stack([x ^ chip for x in of_core(masks)] + [side]).astype(jnp.int32)
    slots = [x ^ lax.dynamic_index_in_dim(x, chip, 0, keepdims=False) for x in of_core(slots_of)]
    slots = jnp.stack(slots + [side]).astype(jnp.int32)
    share = w_joined.shape[1]

    small = jnp.concatenate(
        [
            vectors.transpose(0, 2, 1),
            b_expand.reshape(2, share, 4),
            jnp.zeros((2, share, 116), BF16),
        ],
        axis=2,
    )
    first = jnp.concatenate([w_joined, w_output, small], axis=2)
    second, third = w_expand, w_reduce

    class Gather:
        def __init__(self, piece):
            self.stack = lax.dynamic_index_in_dim(piece, tower, 0, keepdims=True)
            self.send = lax.dynamic_index_in_dim(piece, 1 - tower, 0, keepdims=True)
            self.held = None

        def join(self, got):
            self.stack = jnp.concatenate([self.stack, got], axis=0)
            self.send = self.stack

        def move(self, first, last):
            for step in range(first, last):
                self.join(places.swap(self.send, step))

        def mid(self):
            self.move(0, 1)

        def along_z(self):
            self.move(1, z_steps)

        def pb_first(self):
            self.move(z_steps, places.steps - 1)

        def pb_last(self):
            self.held = places.swap(self.send, places.steps - 1)

        def core_stack(self):
            self.other = places.swap_core(self.stack)

        def core_held(self):
            self.parts = [self.stack, self.held, self.other, places.swap_core(self.held)]

        def whole(self, segments):
            if self.stack.shape[1] % 8 == 0:
                return assemble(self.parts, table, segments)
            return assemble_plain(self.parts, table, segments)

    z_steps = 1 + len(bits_of(places.half))

    rows_q = question_in.reshape(-1, D)
    rows_p = passage_in.reshape(-1, D)
    own_rows = rows_q.shape[0]

    def sides(q_side, p_side):
        return jnp.where(is_q, q_side, p_side), jnp.where(is_q, p_side, q_side)

    lq, lp = question_in.shape[1], passage_in.shape[1]
    rows = 2 * own_rows

    def chunked(values, sixteenths):
        out, row = [], 0
        for part in sixteenths:
            step = values.shape[0] * part // 16
            out.append(values[row : row + step])
            row += step
        return out

    def hand(values):
        return [places.swap_tower(x) for x in values]

    per_q = rows // lq
    every = lp // lq
    per_p = rows // lp
    nq, np_ = question_in.shape[0], passage_in.shape[0]
    shift = 2 * places.half
    low_pa = pa % shift
    row_ids = jnp.arange(rows, dtype=jnp.int32)
    seq = jnp.where(is_q, row_ids // lq, row_ids // lp)
    qid = seq.reshape(rows, 1)
    g1, g2, g3 = Gather(first), Gather(second), Gather(third)
    my_tokens, send_tokens = sides(rows_q, rows_p)
    tokens_out = chunked(send_tokens, (5, 4, 7))
    g1.mid()
    g1.send, tokens_out, question_cot, passage_cot = tie(
        g1.send, tokens_out, question_cot, passage_cot
    )
    g1.along_z()
    tokens_in = hand(tokens_out[:1])
    my_cot, send_cot = sides(question_cot.reshape(-1, D), passage_cot.reshape(-1, D))
    g1.send, g2.send, tokens_in, my_cot, send_cot, table, slots, seq, qid = tie(
        g1.send, g2.send, tokens_in, my_cot, send_cot, table, slots, seq, qid
    )
    g3.send, g3.stack = tie(g3.send, g3.stack)
    g1.pb_first()
    g2.mid()
    g1.stack, g2.send, tokens_out = tie(g1.stack, g2.send, tokens_out)
    g1.send = g1.stack
    g1.pb_last()
    g1.core_stack()
    g2.along_z()
    tokens_in = tokens_in + hand(tokens_out[1:2])
    g1.held, g2.send, tokens_in, tokens_out, question_len, passage_len, positive = tie(
        g1.held, g2.send, tokens_in, tokens_out, question_len, passage_len, positive
    )
    g1.core_held()
    g2.pb_first()
    tokens_in = tokens_in + hand(tokens_out[2:])
    full_j, full_o, full_small = g1.whole([(0, 3 * D), (3 * D, D), (4 * D, 128)])
    full_j, full_o, full_small, g2.stack, g3.send, tokens_in = tie(
        full_j, full_o, full_small, g2.stack, g3.send, tokens_in
    )
    g2.send = g2.stack
    g2.pb_last()
    g2.core_stack()
    g3.mid()
    wj = full_j.reshape(D, 3 * D)
    wo = full_o.reshape(D, D)
    small = full_small.reshape(D, 128).astype(F32)
    vec = small[:, :8].T
    bias_e = small[:, 8:12].reshape(1, FF)
    bias_j = jnp.concatenate([vec[0], jnp.zeros((D,), F32), vec[1]])
    tokens, qkv = project([my_tokens] + tokens_in, wj, bias_j[None])

    cot_out = chunked(send_cot, (4, 3, 3, 2, 4))
    by_pa = positive.reshape(places.pa_n, nq)
    pair = [lax.dynamic_index_in_dim(by_pa, low_pa + k, 0, keepdims=False) for k in (0, shift)]
    pair = jnp.concatenate(pair)[None]
    wanted_rows = jnp.concatenate([pair // 16, pair % 16], axis=0).astype(BF16)
    wanted_rows = jnp.pad(wanted_rows, ((0, 0), (0, D - per_q)))
    valid_q = (jnp.arange(lq, dtype=jnp.int32)[None, :] < question_len[:, None]).astype(jnp.int32)
    valid_p = (jnp.arange(lp, dtype=jnp.int32)[None, :] < passage_len[:, None]).astype(jnp.int32)
    my_valid, send_valid = sides(valid_q.reshape(-1), valid_p.reshape(-1))
    valid = jnp.concatenate([my_valid, places.swap_tower(send_valid)])
    kid = jnp.where(valid > 0, seq, -1).reshape(rows // BLOCK, 1, BLOCK)
    row_mask = valid.reshape(rows, 1).astype(F32)

    blocks = rows // BLOCK
    later = blocks // 2
    qkv, g3.send, cot_out = tie(qkv, g3.send, cot_out)
    g3.along_z()
    cot_in = hand(cot_out[:1])
    context, probs = attention(qkv, qid, kid)
    context, g2.held, g3.send, cot_in, cot_out = tie(context, g2.held, g3.send, cot_in, cot_out)
    g2.core_held()
    g3.pb_first()
    cot_in = cot_in + hand(cot_out[1:2])
    norm_one, inverse_one, mid_low, mid = add_norm(
        context, wo, tokens, row_mask, vec, (2, 3, 4), True
    )
    mid_low, g2.parts, g3.stack, cot_in, cot_out = tie(mid_low, g2.parts, g3.stack, cot_in, cot_out)
    g3.send = g3.stack
    g3.pb_last()
    g3.core_stack()
    (full_e,) = g2.whole([(0, FF)])
    we = full_e.reshape(D, FF)
    mid_low, we, cot_out = tie(mid_low, we, cot_out)
    cot_in = cot_in + hand(cot_out[2:3])
    gelu = expand(mid_low, we, bias_e, 0, 1)
    gelu, g3.held, g3.other, g3.stack, cot_in, cot_out = tie(
        gelu, g3.held, g3.other, g3.stack, cot_in, cot_out
    )
    g3.core_held()
    cot_in = cot_in + hand(cot_out[3:4])
    active, slope = expand(mid_low, we, bias_e, 1, 1, tuple(gelu))
    active, g3.parts, cot_in, cot_out = tie(active, g3.parts, cot_in, cot_out)
    (full_r,) = g3.whole([(0, D)])
    wr = full_r.reshape(FF, D)
    wr, cot_out = tie(wr, cot_out)
    cot_in = cot_in + hand(cot_out[4:])
    norm_two, inverse_two, out = add_norm(active, wr, mid, row_mask, vec, (5, 6, 7), False)
    out, cot_in = tie(out, cot_in)

    firsts = out.reshape(per_q, lq, D)[:, 0, :]
    others = places.swap_tower(firsts)
    cls_q = jnp.where(is_q, firsts, others)
    cls_p = jnp.where(is_q, others, firsts)[::every]
    pad = (-(per_q + per_p + 2)) % 8
    stack = jnp.concatenate([cls_q, cls_p, wanted_rows, jnp.zeros((pad, D), BF16)], axis=0)[None]
    pair_masks = [0]
    for bit in bits_of(places.half):
        got = lax.ppermute(stack, "pa", [(i, i ^ (2 * bit)) for i in range(places.pa_n)])
        stack = jnp.concatenate([stack, got], axis=0)
        pair_masks = pair_masks + [m ^ (2 * bit) for m in pair_masks]
    for bit in bits_of(places.pb_n):
        got = lax.ppermute(stack, "pb", [(i, i ^ bit) for i in range(places.pb_n)])
        stack = jnp.concatenate([stack, got], axis=0)
        pair_masks = pair_masks + [m ^ (bit * places.pa_n) for m in pair_masks]
    stack = jnp.concatenate([stack, places.swap_core(stack)], axis=0)
    pair_masks = pair_masks + [m ^ 1 for m in pair_masks]
    groups = len(pair_masks)
    me = pb * places.pa_n + low_pa
    place = jnp.array(pair_masks, jnp.int32) ^ me
    dev_p = jnp.stack([place + shift, place], axis=1)
    p_ids = (dev_p[:, :, None] * np_ + jnp.arange(np_, dtype=jnp.int32)).reshape(-1)
    digits = stack[:, per_q + per_p : per_q + per_p + 2, :per_q].astype(jnp.int32)
    wanted = (digits[:, 0] * 16 + digits[:, 1]).reshape(-1)

    all_q = stack[:, :per_q].reshape(groups * per_q, D)
    all_p = stack[:, per_q : per_q + per_p].reshape(groups * per_p, D)
    similarity = dot(all_q, all_p, ((1,), (1,))) * score_scale
    hot = (wanted[:, None] == p_ids[None, :]).astype(F32)
    top = jnp.max(similarity, axis=1, keepdims=True)
    grown = jnp.exp(similarity - top)
    total = jnp.sum(grown, axis=1, keepdims=True)
    own_sim = similarity[:per_q]
    loss = top[:per_q, 0] + jnp.log(total[:per_q, 0]) - jnp.sum(own_sim * hot[:per_q], axis=1)
    question_loss = lax.dynamic_slice_in_dim(loss, tower * nq, nq)
    d_sim = (loss_weight * (grown / total - hot)).astype(BF16)
    d_q = dot(d_sim[:per_q], all_p) * score_scale
    d_p = dot(d_sim[:, :per_p], all_q, ((0,), (0,))) * score_scale
    d_p = jnp.concatenate(
        [d_p.reshape(per_p, 1, D), jnp.zeros((per_p, every - 1, D), F32)], axis=1
    ).reshape(per_q, D)
    d_slot = jnp.where(is_q, d_q, d_p)

    d_second, d_reduced, sums_second = second_back(
        join([my_cot] + cot_in), d_slot, row_mask, norm_two, inverse_two, vec[6][None, :]
    )
    even = share % 8 == 0

    def gradient(left, right, **more):
        if left.shape[1] > D:
            return tall_grad(left, right, slots, places.nz)
        return weight_grad(left, right, slots, D, **more)

    def plain(left, right, extra=None):
        if extra is not None:
            one, two, first, second, bias = extra
            joined = one + two
            lines = [joined[:, :D], joined[:, 2 * D :], first[2:3], first[:2]]
            lines = lines + [second[2:3], second[:2], bias, jnp.zeros((116, D), F32)]
            extra = jnp.concatenate(lines, axis=0).T
        return grad_plain(left, right, table, extra)

    class Scatter:
        def __init__(self, mine, theirs):
            self.parts, self.theirs, self.send = [mine], theirs, None
            self.count = mine.shape[0]

        def cores(self):
            self.parts = self.parts + [places.swap_core(self.theirs)]

        def total(self, start, stop):
            out = self.parts[0][start:stop].astype(F32)
            for part in self.parts[1:]:
                out = out + part[start:stop].astype(F32)
            return out

        def prepare(self):
            self.send = self.total(self.count // 2, self.count).astype(BF16)

        def move(self, step):
            if self.send is None:
                self.prepare()
            self.parts = self.parts + [places.swap(self.send, step)]
            self.send = None
            self.count = self.count // 2

        def pb_first(self):
            self.move(places.steps - 1)

        def pb_rest(self):
            for step in range(places.steps - 2, z_steps - 1, -1):
                self.move(step)

        def along_z(self):
            for step in range(z_steps - 1, 0, -1):
                self.move(step)

        def mid(self):
            if self.send is None:
                self.prepare()
            got = places.swap(self.send, 0).astype(F32)
            self.send = None
            keep = self.total(0, 1)
            self.out = jnp.concatenate(
                [jnp.where(is_q, keep, got), jnp.where(is_q, got, keep)], axis=0
            )

    send_out = chunked(out[own_rows:], (4, 4, 4, 4))
    d_reduced, send_out = tie(d_reduced, send_out)
    got_out = hand(send_out[:1])
    sr = Scatter(*(gradient if even else plain)(active, d_reduced))
    sr.parts, sr.theirs, d_reduced, got_out, send_out = tie(
        sr.parts, sr.theirs, d_reduced, got_out, send_out
    )
    sr.cores()
    got_out = got_out + hand(send_out[1:2])
    d_expanded, g_bias_expand = hidden_grad(d_reduced, wr, slope)
    sr.parts, d_expanded, got_out, send_out = tie(sr.parts, d_expanded, got_out, send_out)
    sr.pb_first()
    got_out = got_out + hand(send_out[2:3])
    if even:
        partial = gradient(mid_low, d_expanded, room=D)
    else:
        partial = plain(mid_low, d_expanded)
    sr.parts, partial, d_expanded, got_out, send_out = tie(
        sr.parts, partial, d_expanded, got_out, send_out
    )
    sr.pb_rest()
    got_out = got_out + hand(send_out[3:])
    d_first, d_attended, sums_first = first_back(
        d_expanded, we, d_second, norm_one, inverse_one, vec[3][None, :]
    )
    sr.parts, partial, d_attended, got_out = tie(sr.parts, partial, d_attended, got_out)
    if even:
        partial = gradient(context, d_attended, into=tuple(partial))
    else:
        also = plain(context, d_attended)
        partial = [jnp.concatenate(x, axis=2) for x in zip(partial, also)]
    se = Scatter(*partial)
    sr.prepare()
    se.parts, se.theirs, sr.send, sr.parts, d_attended = tie(
        se.parts, se.theirs, sr.send, sr.parts, d_attended
    )
    se.cores()
    sr.along_z()
    d_context = dot(d_attended, wo, ((1,), (1,))).astype(BF16)
    d_joined, sums_one = attention_back(qkv, probs, d_context, later, blocks - later)
    sr.parts, se.parts, d_joined = tie(sr.parts, se.parts, d_joined)
    se.prepare()
    sr.prepare()
    sr.send, sr.parts, se.send, se.parts, d_joined = tie(
        sr.send, sr.parts, se.send, se.parts, d_joined
    )
    se.pb_first()
    sr.mid()
    part = own_rows // 16
    send_grad = token_grad(d_joined, wj, d_first, own_rows, [k * part for k in (5, 5, 4, 2)], BF16)
    d_joined, send_grad, sr.out = tie(d_joined, send_grad, sr.out)
    got_grad = hand(send_grad[:1])
    d_joined, sums_two = attention_back(qkv, probs, d_context, 0, later, d_joined)
    se.parts, d_joined, sums_two, got_grad, send_grad = tie(
        se.parts, d_joined, sums_two, got_grad, send_grad
    )
    se.prepare()
    se.send, se.parts, d_joined, send_grad = tie(se.send, se.parts, d_joined, send_grad)
    se.pb_rest()
    got_grad = got_grad + hand(send_grad[1:2])
    bias_sums = g_bias_expand.reshape(D, 4).T
    small_sums = (sums_one, sums_two, sums_first, sums_second, bias_sums)
    sj = Scatter(*(gradient if even else plain)(tokens, d_joined, extra=small_sums))
    se.parts, sj.parts, sj.theirs, d_joined, got_grad, send_grad = tie(
        se.parts, sj.parts, sj.theirs, d_joined, got_grad, send_grad
    )
    sj.cores()
    se.along_z()
    (own_grad,) = token_grad(d_joined, wj, d_first, 0, [own_rows], F32)
    sj.parts, se.parts, own_grad, send_grad = tie(sj.parts, se.parts, own_grad, send_grad)
    sj.pb_first()
    got_grad = got_grad + hand(send_grad[2:3])
    sj.parts, se.parts, got_grad, send_grad = tie(sj.parts, se.parts, got_grad, send_grad)
    sj.pb_rest()
    se.mid()
    sj.parts, se.out, got_out, out, send_grad = tie(sj.parts, se.out, got_out, out, send_grad)
    sj.along_z()
    got_grad = got_grad + hand(send_grad[3:])
    out_q, out_p = deal(tower.reshape(1), out, got_out)
    sj.parts, out_q, out_p, got_grad = tie(sj.parts, out_q, out_p, got_grad)
    grad_q, grad_p = deal(tower.reshape(1), own_grad, got_grad)
    sj.mid()
    grad_joined = sj.out[:, :, : 3 * D]
    grad_expand, grad_output, grad_reduce = se.out[:, :, :FF], se.out[:, :, FF:], sr.out
    extra = sj.out[:, :, 3 * D :]
    grad_vectors = extra[:, :, :8].transpose(0, 2, 1)
    grad_b_expand = extra[:, :, 8:12].reshape(2, 4 * share)

    return (
        out_q.reshape(question_in.shape),
        out_p.reshape(passage_in.shape),
        question_loss,
        grad_q.reshape(question_in.shape),
        grad_p.reshape(passage_in.shape),
        grad_joined,
        grad_output,
        grad_expand,
        grad_reduce,
        grad_vectors,
        grad_b_expand,
    )


def solution(mesh):
    in_specs = (
        P(("pb", "pa"), None, None),
        P(("pb", "pa"), None, None),
        P(("pb", "pa")),
        P(("pb", "pa")),
        P("pb"),
        P(("pb", "pa"), None, None),
        P(("pb", "pa"), None, None),
        P(None, ("pb", "pa"), None),
        P(None, ("pb", "pa"), None),
        P(None, ("pb", "pa"), None),
        P(None, ("pb", "pa"), None),
        P(None, None, ("pb", "pa")),
        P(None, ("pb", "pa")),
    )
    out_specs = (
        P(("pb", "pa"), None, None),
        P(("pb", "pa"), None, None),
        P(("pb", "pa")),
        P(("pb", "pa"), None, None),
        P(("pb", "pa"), None, None),
        P(None, ("pb", "pa"), None),
        P(None, ("pb", "pa"), None),
        P(None, ("pb", "pa"), None),
        P(None, ("pb", "pa"), None),
        P(None, None, ("pb", "pa")),
        P(None, ("pb", "pa")),
    )
    return jax.shard_map(
        functools.partial(per_device, Places(mesh)),
        mesh=mesh,
        in_specs=in_specs,
        out_specs=out_specs,
        check_vma=False,
    )
```

```python
import functools

import jax
import jax.numpy as jnp
from jax import lax
from jax.experimental import pallas as pl
from jax.experimental.pallas import tpu as pltpu
from jax.sharding import PartitionSpec as P

D = 768
HEADS = 12
HDIM = 64
FF = 3072
AXES = ("pb", "pa")
BLOCK = 256

norm_eps = 1e-06
masked_score = -1000000000.0
score_scale = 0.0625
loss_weight = 16.0
head_scale = HDIM ** (-0.5)
F32 = jnp.float32
BF16 = jnp.bfloat16
VMEM_LIMIT = 56 * 1024 * 1024


def bits_of(count):
    return [1 << shift for shift in range(count.bit_length() - 1)]


class Places:
    def __init__(self, mesh):
        self.pb_n = mesh.shape["pb"]
        self.pa_n = mesh.shape["pa"]
        self.nz = self.pa_n // 2
        self.half = self.nz // 2
        self.chips = self.pb_n * self.nz
        pb_bits = bits_of(self.pb_n)
        turn = len(pb_bits) // 2
        low_z = [("z", bit) for bit in bits_of(self.half)]
        first = [("pb", bit) for bit in pb_bits]
        second = first[turn:] + first[:turn]
        self.orders = ([("z", self.half)] + low_z + first, [("z", self.half)] + low_z + second)
        self.steps = len(self.orders[0])

    def chip_mask(self, move):
        axis, bit = move
        return bit * self.nz if axis == "pb" else bit

    def stack_masks(self, core):
        masks = [0]
        for move in self.orders[core]:
            masks = masks + [mask ^ self.chip_mask(move) for mask in masks]
        return masks

    def pairs(self, step):
        out = []
        for pb in range(self.pb_n):
            for pa in range(self.pa_n):
                axis, bit = self.orders[pa % 2][step]
                to_pb, to_pa = (pb ^ bit, pa) if axis == "pb" else (pb, pa ^ (2 * bit))
                out.append((pb * self.pa_n + pa, to_pb * self.pa_n + to_pa))
        return out

    def swap(self, values, step):
        return lax.ppermute(values, AXES, self.pairs(step))

    def swap_core(self, values):
        return lax.ppermute(values, "pa", [(i, i ^ 1) for i in range(self.pa_n)])

    def swap_tower(self, values):
        return lax.ppermute(values, "pa", [(i, i ^ (2 * self.half)) for i in range(self.pa_n)])


def dot(left, right, dims=((1,), (0,))):
    return lax.dot_general(left, right, (dims, ((), ())), preferred_element_type=F32)


def tie(*values):
    return lax.optimization_barrier(values)


def assemble_kernel(segments, idx_ref, *refs):
    count = len(segments)
    sources, outs = refs[:4], refs[4 : 4 + count]
    buffer, in_sem, out_sem = refs[4 + count :]
    core = idx_ref[2, 0]
    part = sources[0].shape[0]
    loads = [
        pltpu.make_async_copy(source, buffer.at[pl.ds(k * part, part)], in_sem.at[k])
        for k, source in enumerate(sources)
    ]
    for load in loads:
        load.start()
    stores = []
    for k in range(4):
        loads[k].wait()
        half = core if k < 2 else 1 - core
        for j in range(part):
            slot = k * part + j
            place = idx_ref[k // 2, (k % 2) * part + j]
            for s, (start, width) in enumerate(segments):
                store = pltpu.make_async_copy(
                    buffer.at[slot, :, pl.ds(start, width)],
                    outs[s].at[place, half],
                    out_sem.at[s, slot],
                )
                store.start()
                stores.append(store)
    for store in stores:
        store.wait()


def assemble(parts, table, segments):
    part, rows, width = parts[0].shape
    chips = 2 * part
    shapes = [jax.ShapeDtypeStruct((chips, 2, rows, w), BF16) for _, w in segments]
    return pl.pallas_call(
        functools.partial(assemble_kernel, segments),
        out_shape=shapes,
        in_specs=[pl.BlockSpec(memory_space=pltpu.SMEM)] + [pl.BlockSpec(memory_space=pl.ANY)] * 4,
        out_specs=[pl.BlockSpec(memory_space=pl.ANY)] * len(segments),
        scratch_shapes=[
            pltpu.VMEM((2 * chips, rows, width), BF16),
            pltpu.SemaphoreType.DMA((4,)),
            pltpu.SemaphoreType.DMA((len(segments), 2 * chips)),
        ],
        compiler_params=pltpu.CompilerParams(vmem_limit_bytes=VMEM_LIMIT),
        cost_estimate=pl.CostEstimate(
            flops=0, bytes_accessed=4 * 2 * chips * rows * width, transcendentals=0
        ),
        name="assemble",
    )(table, *parts)


def assemble_plain(parts, table, segments):
    own = jnp.take(jnp.concatenate(parts[:2], axis=0), jnp.argsort(table[0]), axis=0)
    other = jnp.take(jnp.concatenate(parts[2:], axis=0), jnp.argsort(table[1]), axis=0)
    first = table[2, 0] == 0
    both = jnp.stack([jnp.where(first, own, other), jnp.where(first, other, own)], axis=1)
    return [both[..., start : start + w] for start, w in segments]


def split_slabs(acc, core, chips, mine_ref, theirs_ref, cols, within):
    rows = acc.shape[0] // (2 * chips)
    for s in range(chips):
        low = acc[2 * s * rows : (2 * s + 1) * rows]
        high = acc[(2 * s + 1) * rows : (2 * s + 2) * rows]
        mine, theirs = within(s)
        mine_ref[mine, :, cols] = jnp.where(core == 0, low, high).astype(BF16)
        theirs_ref[theirs, :, cols] = jnp.where(core == 0, high, low).astype(BF16)


def weight_grad_kernel(chips, extra, table_ref, left_ref, right_ref, *refs):
    mine_ref, theirs_ref = refs[-2:]
    core = table_ref[2, 0]
    acc = dot(left_ref[...], right_ref[...], ((0,), (0,)))
    width = acc.shape[1]

    def within(s):
        return table_ref[0, s], table_ref[1, s]

    if extra == 0:
        split_slabs(acc, core, chips, mine_ref, theirs_ref, slice(None), within)
        return
    step = pl.program_id(0)
    cols = pl.ds(pl.multiple_of(step * width, 128), width)
    split_slabs(acc, core, chips, mine_ref, theirs_ref, cols, within)

    @pl.when(step == 0)
    def _():
        one, two, first, second, bias = (ref[...] for ref in refs[:extra])
        joined = one + two
        lines = [
            joined[:, :D],
            joined[:, 2 * D :],
            first[2:3],
            first[:2],
            second[2:3],
            second[:2],
            bias,
            jnp.zeros((116, D), F32),
        ]
        values = jnp.concatenate(lines, axis=0).T
        tail = pl.ds(mine_ref.shape[2] - 128, 128)
        split_slabs(values, core, chips, mine_ref, theirs_ref, tail, within)


def weight_grad(left, right, slots, tile, extra=None, room=0, into=()):
    rows, height = left.shape
    width = right.shape[1]
    chips = slots.shape[1]
    slab = height // (2 * chips)
    total = width + (room if extra is None else 128)
    first = 0
    if into:
        total = into[0].shape[2]
        first = (total - width) // tile
    block = (chips, slab, total if extra is not None else tile)
    place = (lambda j, t: (0, 0, 0)) if extra is not None else (lambda j, t: (0, 0, j + first))
    return pl.pallas_call(
        functools.partial(weight_grad_kernel, chips, len(extra or ())),
        grid_spec=pltpu.PrefetchScalarGridSpec(
            num_scalar_prefetch=1,
            grid=(width // tile,),
            in_specs=[
                pl.BlockSpec((rows, height), lambda j, t: (0, 0)),
                pl.BlockSpec((rows, tile), lambda j, t: (0, j)),
            ]
            + [pl.BlockSpec(x.shape, lambda j, t: (0, 0)) for x in extra or ()]
            + [pl.BlockSpec(memory_space=pl.ANY)] * len(into),
            out_specs=[pl.BlockSpec(block, place)] * 2,
        ),
        out_shape=[jax.ShapeDtypeStruct((chips, slab, total), BF16)] * 2,
        input_output_aliases={3: 0, 4: 1} if into else {},
        compiler_params=pltpu.CompilerParams(vmem_limit_bytes=VMEM_LIMIT),
        cost_estimate=pl.CostEstimate(
            flops=2 * rows * height * width,
            bytes_accessed=2 * (rows * (height + width) + height * width),
            transcendentals=0,
        ),
        name="weight_grad",
    )(slots, left, right, *(extra or ()), *into)


def tall_grad_kernel(chips, table_ref, left_ref, right_ref, mine_ref, theirs_ref):
    core = table_ref[2, 0]
    acc = dot(left_ref[...], right_ref[...], ((0,), (0,)))
    base = pl.program_id(0) * chips

    def within(s):
        return table_ref[0, base + s] % chips, table_ref[1, base + s] % chips

    split_slabs(acc, core, chips, mine_ref, theirs_ref, slice(None), within)


def tall_grad(left, right, slots, column):
    rows, height = left.shape
    width = right.shape[1]
    chips = slots.shape[1]
    slab = height // (2 * chips)
    tile = height // chips * column
    return pl.pallas_call(
        functools.partial(tall_grad_kernel, column),
        grid_spec=pltpu.PrefetchScalarGridSpec(
            num_scalar_prefetch=1,
            grid=(chips // column,),
            in_specs=[
                pl.BlockSpec((rows, tile), lambda i, t: (0, i)),
                pl.BlockSpec((rows, width), lambda i, t: (0, 0)),
            ],
            out_specs=[
                pl.BlockSpec((column, slab, width), lambda i, t: (t[0, i * column] // column, 0, 0)),
                pl.BlockSpec((column, slab, width), lambda i, t: (t[1, i * column] // column, 0, 0)),
            ],
        ),
        out_shape=[jax.ShapeDtypeStruct((chips, slab, width), BF16)] * 2,
        compiler_params=pltpu.CompilerParams(vmem_limit_bytes=VMEM_LIMIT),
        cost_estimate=pl.CostEstimate(
            flops=2 * rows * height * width,
            bytes_accessed=2 * (rows * (height + width) + height * width),
            transcendentals=0,
        ),
        name="tall_grad",
    )(slots, left, right)


def grad_plain(left, right, table, extra=None):
    full = dot(left, right, ((0,), (0,)))
    if extra is not None:
        full = jnp.concatenate([full, extra], axis=1)
    chips = table.shape[1]
    full = full.astype(BF16).reshape(chips, 2, full.shape[0] // (2 * chips), full.shape[1])
    core = table[2, 0]
    mine = lax.dynamic_index_in_dim(full, core, 1, keepdims=False)
    theirs = lax.dynamic_index_in_dim(full, 1 - core, 1, keepdims=False)
    return jnp.take(mine, table[0], axis=0), jnp.take(theirs, table[1], axis=0)


def hidden_grad_kernel(grad_ref, w_ref, slope_ref, out_ref, sum_ref):
    grad = dot(grad_ref[...], w_ref[...], ((1,), (1,))) * slope_ref[...].astype(F32)
    low = grad.astype(BF16)
    out_ref[...] = low
    sum_ref[...] = jnp.sum(low.astype(F32), axis=0, keepdims=True)


def hidden_grad(grad, w_reduce, slope):
    rows, tile = grad.shape[0], 512
    return pl.pallas_call(
        hidden_grad_kernel,
        grid=(FF // tile,),
        in_specs=[
            pl.BlockSpec((rows, D), lambda j: (0, 0)),
            pl.BlockSpec((tile, D), lambda j: (j, 0)),
            pl.BlockSpec((rows, tile), lambda j: (0, j)),
        ],
        out_specs=[
            pl.BlockSpec((rows, tile), lambda j: (0, j)),
            pl.BlockSpec((1, tile), lambda j: (0, j)),
        ],
        out_shape=[
            jax.ShapeDtypeStruct((rows, FF), BF16),
            jax.ShapeDtypeStruct((1, FF), F32),
        ],
        compiler_params=pltpu.CompilerParams(vmem_limit_bytes=VMEM_LIMIT),
        cost_estimate=pl.CostEstimate(
            flops=2 * rows * D * FF,
            bytes_accessed=2 * (rows * D + D * FF + 2 * rows * FF),
            transcendentals=0,
        ),
        name="hidden_grad",
    )(grad, w_reduce, slope)


def attention_kernel(qkv_ref, qid_ref, kid_ref, context_ref, probs_ref):
    allowed = qid_ref[...] == kid_ref[0]
    lane = lax.broadcasted_iota(jnp.int32, (BLOCK, 128), 1)
    zero = jnp.zeros((BLOCK, 128), BF16)
    for pair in range(HEADS // 2):
        queries = qkv_ref[:, pair * 128 : pair * 128 + 128]
        keys = qkv_ref[:, D + pair * 128 : D + pair * 128 + 128]
        values = qkv_ref[:, 2 * D + pair * 128 : 2 * D + pair * 128 + 128]
        outs = []
        for side in range(2):
            mine = (lane < HDIM) if side == 0 else (lane >= HDIM)
            scores = dot(queries, jnp.where(mine, keys, zero), ((1,), (1,))) * head_scale
            scores = jnp.where(allowed, scores, masked_score)
            top = jnp.max(scores, axis=1, keepdims=True)
            grown = jnp.exp(scores - top)
            total = jnp.sum(grown, axis=1, keepdims=True)
            probs = (grown * (1.0 / total)).astype(BF16)
            probs_ref[0, 2 * pair + side] = probs
            outs.append(dot(probs, values))
        context_ref[:, pair * 128 : pair * 128 + 128] = jnp.where(
            lane < HDIM, outs[0], outs[1]
        ).astype(BF16)


def attention(qkv, qid, kid):
    rows = qkv.shape[0]
    blocks = rows // BLOCK
    return pl.pallas_call(
        attention_kernel,
        grid=(blocks,),
        in_specs=[
            pl.BlockSpec((BLOCK, 3 * D), lambda i: (i, 0)),
            pl.BlockSpec((BLOCK, 1), lambda i: (i, 0)),
            pl.BlockSpec((1, 1, BLOCK), lambda i: (i, 0, 0)),
        ],
        out_specs=[
            pl.BlockSpec((BLOCK, D), lambda i: (i, 0)),
            pl.BlockSpec((1, HEADS, BLOCK, BLOCK), lambda i: (i, 0, 0, 0)),
        ],
        out_shape=[
            jax.ShapeDtypeStruct((rows, D), BF16),
            jax.ShapeDtypeStruct((blocks, HEADS, BLOCK, BLOCK), BF16),
        ],
        compiler_params=pltpu.CompilerParams(vmem_limit_bytes=VMEM_LIMIT),
        cost_estimate=pl.CostEstimate(
            flops=4 * rows * BLOCK * D * 2,
            bytes_accessed=rows * (4 * D + HEADS * BLOCK) * 2,
            transcendentals=rows * HEADS * BLOCK,
        ),
        name="attention",
    )(qkv, qid, kid)


def attention_back_kernel(qkv_ref, probs_ref, grad_ref, out_ref, sum_ref):
    lane = lax.broadcasted_iota(jnp.int32, (BLOCK, 128), 1)
    zero = jnp.zeros((BLOCK, 128), BF16)

    def at(pair, start=0):
        return pl.ds(pl.multiple_of(start + pair * 128, 128), 128)

    def some(step, carry):
        for k in range(2):
            pair = step * 2 + k
            cols = at(pair)
            queries = qkv_ref[:, at(pair)]
            keys = qkv_ref[:, at(pair, D)]
            values = qkv_ref[:, at(pair, 2 * D)]
            grad = grad_ref[:, cols]
            d_q, d_k, d_v = [], [], []
            for side in range(2):
                mine = (lane < HDIM) if side == 0 else (lane >= HDIM)
                low = probs_ref[0, 2 * pair + side]
                d_probs = dot(jnp.where(mine, grad, zero), values, ((1,), (1,)))
                d_v.append(dot(low, grad, ((0,), (0,))))
                probs = low.astype(F32)
                row_dot = jnp.sum(d_probs * probs, axis=1, keepdims=True)
                d_scores = (probs * (d_probs - row_dot)).astype(BF16)
                d_q.append(dot(d_scores, keys))
                d_k.append(dot(d_scores, queries, ((0,), (0,))))
            first = lane < HDIM
            out_ref[:, at(pair)] = (
                jnp.where(first, d_q[0], d_q[1]) * head_scale
            ).astype(BF16)
            out_ref[:, at(pair, D)] = (
                jnp.where(first, d_k[0], d_k[1]) * head_scale
            ).astype(BF16)
            out_ref[:, at(pair, 2 * D)] = jnp.where(
                first, d_v[0], d_v[1]
            ).astype(BF16)
        return carry

    lax.fori_loop(0, HEADS // 2 // 2, some, 0)
    sums = jnp.sum(out_ref[...].astype(F32), axis=0, keepdims=True)

    @pl.when(pl.program_id(0) == 0)
    def _():
        sum_ref[...] = sums

    @pl.when(pl.program_id(0) > 0)
    def _():
        sum_ref[...] += sums


def attention_back_more_kernel(qkv_ref, probs_ref, grad_ref, _, out_ref, sum_ref):
    attention_back_kernel(qkv_ref, probs_ref, grad_ref, out_ref, sum_ref)


def attention_back(qkv, probs, grad_context, start, count, into=None):
    rows = qkv.shape[0]
    more = into is not None
    return pl.pallas_call(
        attention_back_more_kernel if more else attention_back_kernel,
        grid=(count,),
        in_specs=[
            pl.BlockSpec((BLOCK, 3 * D), lambda i: (i + start, 0)),
            pl.BlockSpec((1, HEADS, BLOCK, BLOCK), lambda i: (i + start, 0, 0, 0)),
            pl.BlockSpec((BLOCK, D), lambda i: (i + start, 0)),
        ]
        + ([pl.BlockSpec(memory_space=pl.ANY)] if more else []),
        out_specs=[
            pl.BlockSpec((BLOCK, 3 * D), lambda i: (i + start, 0)),
            pl.BlockSpec((1, 3 * D), lambda i: (0, 0)),
        ],
        out_shape=[
            jax.ShapeDtypeStruct((rows, 3 * D), BF16),
            jax.ShapeDtypeStruct((1, 3 * D), F32),
        ],
        input_output_aliases={3: 0} if more else {},
        compiler_params=pltpu.CompilerParams(vmem_limit_bytes=VMEM_LIMIT),
        cost_estimate=pl.CostEstimate(
            flops=8 * count * BLOCK * BLOCK * D * 2,
            bytes_accessed=count * BLOCK * (7 * D + HEADS * BLOCK) * 2,
            transcendentals=0,
        ),
        name="attention_back",
    )(qkv, probs, grad_context, *([into] if more else []))


def join_kernel(*refs):
    row = 0
    for piece in refs[:-1]:
        rows = piece.shape[0]
        refs[-1][row : row + rows, :] = piece[...]
        row += rows


def join(pieces):
    rows, width = sum(x.shape[0] for x in pieces), pieces[0].shape[1]
    return pl.pallas_call(
        join_kernel,
        grid=(1,),
        in_specs=[pl.BlockSpec(x.shape, lambda i: (0, 0)) for x in pieces],
        out_specs=pl.BlockSpec((rows, width), lambda i: (0, 0)),
        out_shape=jax.ShapeDtypeStruct((rows, width), pieces[0].dtype),
        compiler_params=pltpu.CompilerParams(vmem_limit_bytes=VMEM_LIMIT),
        cost_estimate=pl.CostEstimate(
            flops=0, bytes_accessed=4 * rows * width, transcendentals=0
        ),
        name="join",
    )(*pieces)


def deal_kernel(tower_ref, own_ref, *refs):
    pieces, (q_ref, p_ref) = refs[:-2], refs[-2:]

    def give(own_out, other_out):
        own_out[...] = own_ref[...]
        row = 0
        for piece in pieces:
            rows = piece.shape[0]
            other_out[row : row + rows, :] = piece[...].astype(other_out.dtype)
            row += rows

    @pl.when(tower_ref[0] == 0)
    def _():
        give(q_ref, p_ref)

    @pl.when(tower_ref[0] != 0)
    def _():
        give(p_ref, q_ref)


def deal(tower, own, pieces):
    rows, width = sum(x.shape[0] for x in pieces), own.shape[1]
    shape = jax.ShapeDtypeStruct((rows, width), own.dtype)
    return pl.pallas_call(
        deal_kernel,
        grid=(1,),
        in_specs=[
            pl.BlockSpec(memory_space=pltpu.SMEM),
            pl.BlockSpec((rows, width), lambda i: (0, 0)),
        ]
        + [pl.BlockSpec(x.shape, lambda i: (0, 0)) for x in pieces],
        out_specs=[pl.BlockSpec((rows, width), lambda i: (0, 0))] * 2,
        out_shape=[shape] * 2,
        compiler_params=pltpu.CompilerParams(vmem_limit_bytes=VMEM_LIMIT),
        cost_estimate=pl.CostEstimate(
            flops=0, bytes_accessed=12 * rows * width, transcendentals=0
        ),
        name="deal",
    )(tower, own, *pieces)


def add_sums(sum_ref, values):
    total = jnp.concatenate(
        [jnp.sum(x, axis=0, keepdims=True) for x in values]
        + [jnp.zeros((8 - len(values), values[0].shape[1]), F32)],
        axis=0,
    )

    @pl.when(pl.program_id(0) == 0)
    def _():
        sum_ref[...] = total

    @pl.when(pl.program_id(0) > 0)
    def _():
        sum_ref[...] += total


def second_back_kernel(
    cot_ref, slot_ref, mask_ref, norm_ref, inverse_ref, gain_ref, grad_ref, low_ref, sum_ref
):
    group = slot_ref.shape[1]
    cot = cot_ref[...].astype(F32).reshape(group, BLOCK // group, D)
    first = lax.broadcasted_iota(jnp.int32, cot.shape, 1) == 0
    grad = cot + jnp.where(first, slot_ref[0][:, None, :], 0.0)
    grad = grad.reshape(BLOCK, D) * mask_ref[...]
    norm = norm_ref[...]
    second = norm_back(grad, gain_ref[...], norm, inverse_ref[...])
    low = second.astype(BF16)
    grad_ref[...] = second
    low_ref[...] = low
    add_sums(sum_ref, [grad * norm, grad, low.astype(F32)])


def second_back(cot, d_slot, mask, norm, inverse, gain):
    rows = cot.shape[0]
    blocks = rows // BLOCK
    wide = pl.BlockSpec((BLOCK, D), lambda i: (i, 0))
    thin = pl.BlockSpec((BLOCK, 1), lambda i: (i, 0))
    group = d_slot.shape[0] // blocks
    return pl.pallas_call(
        second_back_kernel,
        grid=(blocks,),
        in_specs=[
            wide,
            pl.BlockSpec((1, group, D), lambda i: (i, 0, 0)),
            thin,
            wide,
            thin,
            pl.BlockSpec((1, D), lambda i: (0, 0)),
        ],
        out_specs=[wide, wide, pl.BlockSpec((8, D), lambda i: (0, 0))],
        out_shape=[
            jax.ShapeDtypeStruct((rows, D), F32),
            jax.ShapeDtypeStruct((rows, D), BF16),
            jax.ShapeDtypeStruct((8, D), F32),
        ],
        compiler_params=pltpu.CompilerParams(vmem_limit_bytes=VMEM_LIMIT),
        cost_estimate=pl.CostEstimate(
            flops=20 * rows * D, bytes_accessed=12 * rows * D, transcendentals=0
        ),
        name="second_back",
    )(cot, d_slot.reshape(blocks, group, D), mask, norm, inverse, gain)


def first_back_kernel(
    hidden_ref, w_ref, second_ref, norm_ref, inverse_ref, gain_ref, grad_ref, low_ref, sum_ref
):
    grad = second_ref[...] + dot(hidden_ref[...], w_ref[...], ((1,), (1,)))
    norm = norm_ref[...]
    first = norm_back(grad, gain_ref[...], norm, inverse_ref[...])
    low = first.astype(BF16)
    grad_ref[...] = first
    low_ref[...] = low
    add_sums(sum_ref, [grad * norm, grad, low.astype(F32)])


def first_back(d_expanded, w_expand, d_second, norm, inverse, gain):
    rows = d_expanded.shape[0]
    wide = pl.BlockSpec((BLOCK, D), lambda i: (i, 0))
    return pl.pallas_call(
        first_back_kernel,
        grid=(rows // BLOCK,),
        in_specs=[
            pl.BlockSpec((BLOCK, FF), lambda i: (i, 0)),
            pl.BlockSpec((D, FF), lambda i: (0, 0)),
            wide,
            wide,
            pl.BlockSpec((BLOCK, 1), lambda i: (i, 0)),
            pl.BlockSpec((1, D), lambda i: (0, 0)),
        ],
        out_specs=[wide, wide, pl.BlockSpec((8, D), lambda i: (0, 0))],
        out_shape=[
            jax.ShapeDtypeStruct((rows, D), F32),
            jax.ShapeDtypeStruct((rows, D), BF16),
            jax.ShapeDtypeStruct((8, D), F32),
        ],
        compiler_params=pltpu.CompilerParams(vmem_limit_bytes=VMEM_LIMIT),
        cost_estimate=pl.CostEstimate(
            flops=2 * rows * D * FF,
            bytes_accessed=2 * (rows * FF + D * FF) + 14 * rows * D,
            transcendentals=0,
        ),
        name="first_back",
    )(d_expanded, w_expand, d_second, norm, inverse, gain)


def expand_kernel(mid_ref, w_ref, b_ref, active_ref, slope_ref):
    expanded = dot(mid_ref[...], w_ref[...]) + b_ref[...]
    phi = 0.5 + 0.5 * lax.erf(expanded * 0.7071067811865476)
    density = jnp.exp(expanded * expanded * -0.5) * 0.3989422804014327
    active_ref[...] = (expanded * phi).astype(BF16)
    slope_ref[...] = (phi + expanded * density).astype(BF16)


def expand_more_kernel(mid_ref, w_ref, b_ref, _, __, active_ref, slope_ref):
    expand_kernel(mid_ref, w_ref, b_ref, active_ref, slope_ref)


def expand(mid_low, w_expand, b_expand, start, count, into=()):
    rows = mid_low.shape[0]
    tile_r, tile_f = 256, FF // 2
    return pl.pallas_call(
        expand_more_kernel if into else expand_kernel,
        grid=(count, rows // tile_r),
        in_specs=[
            pl.BlockSpec((tile_r, D), lambda j, i: (i, 0)),
            pl.BlockSpec((D, tile_f), lambda j, i: (0, j + start)),
            pl.BlockSpec((1, tile_f), lambda j, i: (0, j + start)),
        ]
        + [pl.BlockSpec(memory_space=pl.ANY)] * len(into),
        out_specs=[
            pl.BlockSpec((tile_r, tile_f), lambda j, i: (i, j + start)),
            pl.BlockSpec((tile_r, tile_f), lambda j, i: (i, j + start)),
        ],
        out_shape=[jax.ShapeDtypeStruct((rows, FF), BF16)] * 2,
        input_output_aliases={3: 0, 4: 1} if into else {},
        compiler_params=pltpu.CompilerParams(vmem_limit_bytes=VMEM_LIMIT),
        cost_estimate=pl.CostEstimate(
            flops=2 * rows * D * count * tile_f,
            bytes_accessed=2 * (rows * D + D * count * tile_f + 2 * rows * count * tile_f),
            transcendentals=2 * rows * count * tile_f,
        ),
        name="expand",
    )(mid_low, w_expand, b_expand, *into)


def token_grad_kernel(grad_ref, w_ref, first_ref, *outs):
    block = first_ref[...] + dot(grad_ref[...], w_ref[...], ((1,), (1,)))
    block = block.astype(outs[0].dtype)
    step, start = pl.program_id(0), 0
    for out in outs:
        stop = start + out.shape[0]
        for k in range(start // BLOCK, (stop - 1) // BLOCK + 1):
            low, high = max(start, k * BLOCK), min(stop, (k + 1) * BLOCK)

            @pl.when(step == k)
            def _(out=out, k=k, low=low, high=high, start=start):
                out[low - start : high - start, :] = block[low - k * BLOCK : high - k * BLOCK]

        start = stop


def token_grad(d_joined, weight, d_first, start, pieces, dtype):
    width = weight.shape[1]
    first, count = start // BLOCK, sum(pieces) // BLOCK
    return pl.pallas_call(
        token_grad_kernel,
        grid=(count,),
        in_specs=[
            pl.BlockSpec((BLOCK, width), lambda i: (i + first, 0)),
            pl.BlockSpec((D, width), lambda i: (0, 0)),
            pl.BlockSpec((BLOCK, D), lambda i: (i + first, 0)),
        ],
        out_specs=[pl.BlockSpec((n, D), lambda i: (0, 0)) for n in pieces],
        out_shape=[jax.ShapeDtypeStruct((n, D), dtype) for n in pieces],
        compiler_params=pltpu.CompilerParams(vmem_limit_bytes=VMEM_LIMIT),
        cost_estimate=pl.CostEstimate(
            flops=2 * count * BLOCK * D * width,
            bytes_accessed=2 * D * width + count * BLOCK * (2 * width + 6 * D),
            transcendentals=0,
        ),
        name="token_grad",
    )(d_joined, weight, d_first)


def project_kernel(w_ref, b_ref, *refs):
    pieces, (tokens_ref, out_ref) = refs[:-2], refs[-2:]
    step = pl.program_id(0)

    @pl.when(step == 0)
    def _():
        join_kernel(*pieces, tokens_ref)

    tokens = tokens_ref[pl.ds(pl.multiple_of(step * BLOCK, BLOCK), BLOCK), :]
    out_ref[...] = (dot(tokens, w_ref[...]) + b_ref[...]).astype(BF16)


def project(pieces, weight, bias):
    rows, width = sum(x.shape[0] for x in pieces), weight.shape[1]
    return pl.pallas_call(
        project_kernel,
        grid=(rows // BLOCK,),
        in_specs=[
            pl.BlockSpec((D, width), lambda i: (0, 0)),
            pl.BlockSpec((1, width), lambda i: (0, 0)),
        ]
        + [pl.BlockSpec(x.shape, lambda i: (0, 0)) for x in pieces],
        out_specs=[
            pl.BlockSpec((rows, D), lambda i: (0, 0)),
            pl.BlockSpec((BLOCK, width), lambda i: (i, 0)),
        ],
        out_shape=[
            jax.ShapeDtypeStruct((rows, D), BF16),
            jax.ShapeDtypeStruct((rows, width), BF16),
        ],
        compiler_params=pltpu.CompilerParams(vmem_limit_bytes=VMEM_LIMIT),
        cost_estimate=pl.CostEstimate(
            flops=2 * rows * D * width,
            bytes_accessed=2 * (rows * (2 * D + width) + D * width),
            transcendentals=0,
        ),
        name="project",
    )(weight, bias, *pieces)


def add_norm_kernel(
    rows_of, left_ref, w_ref, base_ref, mask_ref, vec_ref, norm_ref, inverse_ref, low_ref, *more
):
    bias, gain, shift = (vec_ref[k : k + 1, :] for k in rows_of)
    norm, inverse = normalized(base_ref[...].astype(F32) + dot(left_ref[...], w_ref[...]) + bias)
    value = norm * gain + shift
    norm_ref[...] = norm
    inverse_ref[...] = inverse
    if more:
        more[0][...] = value
        low_ref[...] = value.astype(BF16)
    else:
        low_ref[...] = (value * mask_ref[...]).astype(BF16)


def add_norm(left, weight, base, mask, vec, rows_of, keep):
    rows, depth = left.shape
    wide = pl.BlockSpec((BLOCK, D), lambda i: (i, 0))
    thin = pl.BlockSpec((BLOCK, 1), lambda i: (i, 0))
    shape = jax.ShapeDtypeStruct((rows, D), F32)
    return pl.pallas_call(
        functools.partial(add_norm_kernel, rows_of),
        grid=(rows // BLOCK,),
        in_specs=[
            pl.BlockSpec((BLOCK, depth), lambda i: (i, 0)),
            pl.BlockSpec((depth, D), lambda i: (0, 0)),
            wide,
            thin,
            pl.BlockSpec((8, D), lambda i: (0, 0)),
        ],
        out_specs=[wide, thin, wide] + [wide] * keep,
        out_shape=[
            shape,
            jax.ShapeDtypeStruct((rows, 1), F32),
            jax.ShapeDtypeStruct((rows, D), BF16),
        ]
        + [shape] * keep,
        compiler_params=pltpu.CompilerParams(vmem_limit_bytes=VMEM_LIMIT),
        cost_estimate=pl.CostEstimate(
            flops=2 * rows * D * depth,
            bytes_accessed=2 * (rows + D) * depth + 12 * rows * D,
            transcendentals=0,
        ),
        name="add_norm",
    )(left, weight, base, mask, vec)


def normalized(values):
    centred = values - jnp.mean(values, axis=-1, keepdims=True)
    spread = jnp.mean(centred * centred, axis=-1, keepdims=True)
    inverse = lax.rsqrt(spread + norm_eps)
    return centred * inverse, inverse


def norm_back(grad, gain, norm, inverse):
    scaled = grad * gain
    return inverse * (
        scaled
        - jnp.mean(scaled, axis=-1, keepdims=True)
        - norm * jnp.mean(scaled * norm, axis=-1, keepdims=True)
    )


def per_device(places, *args):
    (
        question_in,
        passage_in,
        question_len,
        passage_len,
        positive,
        question_cot,
        passage_cot,
        w_joined,
        w_output,
        w_expand,
        w_reduce,
        vectors,
        b_expand,
    ) = args
    pb, pa = lax.axis_index("pb"), lax.axis_index("pa")
    z, core = pa // 2, pa % 2
    tower = z // places.half
    is_q = tower == 0
    chip = pb * places.nz + z
    masks = [places.stack_masks(side) for side in range(2)]
    slots_of = [sorted(range(places.chips), key=side.__getitem__) for side in masks]

    def of_core(rows_of):
        both = jnp.array(rows_of, jnp.int32)
        return (
            lax.dynamic_index_in_dim(both, core, 0, keepdims=False),
            lax.dynamic_index_in_dim(both, 1 - core, 0, keepdims=False),
        )

    side = jnp.full((places.chips,), core, jnp.int32)
    table = jnp.stack([x ^ chip for x in of_core(masks)] + [side]).astype(jnp.int32)
    slots = [x ^ lax.dynamic_index_in_dim(x, chip, 0, keepdims=False) for x in of_core(slots_of)]
    slots = jnp.stack(slots + [side]).astype(jnp.int32)
    share = w_joined.shape[1]

    small = jnp.concatenate(
        [
            vectors.transpose(0, 2, 1),
            b_expand.reshape(2, share, 4),
            jnp.zeros((2, share, 116), BF16),
        ],
        axis=2,
    )
    first = jnp.concatenate([w_joined, w_output, small], axis=2)
    second, third = w_expand, w_reduce

    class Gather:
        def __init__(self, piece):
            self.stack = lax.dynamic_index_in_dim(piece, tower, 0, keepdims=True)
            self.send = lax.dynamic_index_in_dim(piece, 1 - tower, 0, keepdims=True)
            self.held = None

        def join(self, got):
            self.stack = jnp.concatenate([self.stack, got], axis=0)
            self.send = self.stack

        def move(self, first, last):
            for step in range(first, last):
                self.join(places.swap(self.send, step))

        def mid(self):
            self.move(0, 1)

        def along_z(self):
            self.move(1, z_steps)

        def pb_first(self):
            self.move(z_steps, places.steps - 1)

        def pb_last(self):
            self.held = places.swap(self.send, places.steps - 1)

        def core_stack(self):
            self.other = places.swap_core(self.stack)

        def core_held(self):
            self.parts = [self.stack, self.held, self.other, places.swap_core(self.held)]

        def whole(self, segments):
            if self.stack.shape[1] % 8 == 0:
                return assemble(self.parts, table, segments)
            return assemble_plain(self.parts, table, segments)

    z_steps = 1 + len(bits_of(places.half))

    rows_q = question_in.reshape(-1, D)
    rows_p = passage_in.reshape(-1, D)
    own_rows = rows_q.shape[0]

    def sides(q_side, p_side):
        return jnp.where(is_q, q_side, p_side), jnp.where(is_q, p_side, q_side)

    lq, lp = question_in.shape[1], passage_in.shape[1]
    rows = 2 * own_rows

    def chunked(values, sixteenths):
        out, row = [], 0
        for part in sixteenths:
            step = values.shape[0] * part // 16
            out.append(values[row : row + step])
            row += step
        return out

    def hand(values):
        return [places.swap_tower(x) for x in values]

    per_q = rows // lq
    every = lp // lq
    per_p = rows // lp
    nq, np_ = question_in.shape[0], passage_in.shape[0]
    shift = 2 * places.half
    low_pa = pa % shift
    row_ids = jnp.arange(rows, dtype=jnp.int32)
    seq = jnp.where(is_q, row_ids // lq, row_ids // lp)
    qid = seq.reshape(rows, 1)
    g1, g2, g3 = Gather(first), Gather(second), Gather(third)
    my_tokens, send_tokens = sides(rows_q, rows_p)
    tokens_out = chunked(send_tokens, (5, 4, 7))
    g1.mid()
    g1.send, tokens_out, question_cot, passage_cot = tie(
        g1.send, tokens_out, question_cot, passage_cot
    )
    g1.along_z()
    tokens_in = hand(tokens_out[:1])
    my_cot, send_cot = sides(question_cot.reshape(-1, D), passage_cot.reshape(-1, D))
    g1.send, g2.send, tokens_in, my_cot, send_cot, table, slots, seq, qid = tie(
        g1.send, g2.send, tokens_in, my_cot, send_cot, table, slots, seq, qid
    )
    g3.send, g3.stack = tie(g3.send, g3.stack)
    g1.pb_first()
    g2.mid()
    g1.stack, g2.send, tokens_out = tie(g1.stack, g2.send, tokens_out)
    g1.send = g1.stack
    g1.pb_last()
    g1.core_stack()
    g2.along_z()
    tokens_in = tokens_in + hand(tokens_out[1:2])
    g1.held, g2.send, tokens_in, tokens_out, question_len, passage_len, positive = tie(
        g1.held, g2.send, tokens_in, tokens_out, question_len, passage_len, positive
    )
    g1.core_held()
    g2.pb_first()
    tokens_in = tokens_in + hand(tokens_out[2:])
    full_j, full_o, full_small = g1.whole([(0, 3 * D), (3 * D, D), (4 * D, 128)])
    full_j, full_o, full_small, g2.stack, g3.send, tokens_in = tie(
        full_j, full_o, full_small, g2.stack, g3.send, tokens_in
    )
    g2.send = g2.stack
    g2.pb_last()
    g2.core_stack()
    g3.mid()
    wj = full_j.reshape(D, 3 * D)
    wo = full_o.reshape(D, D)
    small = full_small.reshape(D, 128).astype(F32)
    vec = small[:, :8].T
    bias_e = small[:, 8:12].reshape(1, FF)
    bias_j = jnp.concatenate([vec[0], jnp.zeros((D,), F32), vec[1]])
    tokens, qkv = project([my_tokens] + tokens_in, wj, bias_j[None])

    cot_out = chunked(send_cot, (4, 3, 3, 2, 4))
    by_pa = positive.reshape(places.pa_n, nq)
    pair = [lax.dynamic_index_in_dim(by_pa, low_pa + k, 0, keepdims=False) for k in (0, shift)]
    pair = jnp.concatenate(pair)[None]
    wanted_rows = jnp.concatenate([pair // 16, pair % 16], axis=0).astype(BF16)
    wanted_rows = jnp.pad(wanted_rows, ((0, 0), (0, D - per_q)))
    valid_q = (jnp.arange(lq, dtype=jnp.int32)[None, :] < question_len[:, None]).astype(jnp.int32)
    valid_p = (jnp.arange(lp, dtype=jnp.int32)[None, :] < passage_len[:, None]).astype(jnp.int32)
    my_valid, send_valid = sides(valid_q.reshape(-1), valid_p.reshape(-1))
    valid = jnp.concatenate([my_valid, places.swap_tower(send_valid)])
    kid = jnp.where(valid > 0, seq, -1).reshape(rows // BLOCK, 1, BLOCK)
    row_mask = valid.reshape(rows, 1).astype(F32)

    blocks = rows // BLOCK
    later = blocks // 2
    qkv, g3.send, cot_out = tie(qkv, g3.send, cot_out)
    g3.along_z()
    cot_in = hand(cot_out[:1])
    context, probs = attention(qkv, qid, kid)
    context, g2.held, g3.send, cot_in, cot_out = tie(context, g2.held, g3.send, cot_in, cot_out)
    g2.core_held()
    g3.pb_first()
    cot_in = cot_in + hand(cot_out[1:2])
    norm_one, inverse_one, mid_low, mid = add_norm(
        context, wo, tokens, row_mask, vec, (2, 3, 4), True
    )
    mid_low, g2.parts, g3.stack, cot_in, cot_out = tie(mid_low, g2.parts, g3.stack, cot_in, cot_out)
    g3.send = g3.stack
    g3.pb_last()
    g3.core_stack()
    (full_e,) = g2.whole([(0, FF)])
    we = full_e.reshape(D, FF)
    mid_low, we, cot_out = tie(mid_low, we, cot_out)
    cot_in = cot_in + hand(cot_out[2:3])
    gelu = expand(mid_low, we, bias_e, 0, 1)
    gelu, g3.held, g3.other, g3.stack, cot_in, cot_out = tie(
        gelu, g3.held, g3.other, g3.stack, cot_in, cot_out
    )
    g3.core_held()
    cot_in = cot_in + hand(cot_out[3:4])
    active, slope = expand(mid_low, we, bias_e, 1, 1, tuple(gelu))
    active, g3.parts, cot_in, cot_out = tie(active, g3.parts, cot_in, cot_out)
    (full_r,) = g3.whole([(0, D)])
    wr = full_r.reshape(FF, D)
    wr, cot_out = tie(wr, cot_out)
    cot_in = cot_in + hand(cot_out[4:])
    norm_two, inverse_two, out = add_norm(active, wr, mid, row_mask, vec, (5, 6, 7), False)
    out, cot_in = tie(out, cot_in)

    firsts = out.reshape(per_q, lq, D)[:, 0, :]
    others = places.swap_tower(firsts)
    cls_q = jnp.where(is_q, firsts, others)
    cls_p = jnp.where(is_q, others, firsts)[::every]
    pad = (-(per_q + per_p + 2)) % 8
    stack = jnp.concatenate([cls_q, cls_p, wanted_rows, jnp.zeros((pad, D), BF16)], axis=0)[None]
    pair_masks = [0]
    for bit in bits_of(places.half):
        got = lax.ppermute(stack, "pa", [(i, i ^ (2 * bit)) for i in range(places.pa_n)])
        stack = jnp.concatenate([stack, got], axis=0)
        pair_masks = pair_masks + [m ^ (2 * bit) for m in pair_masks]
    for bit in bits_of(places.pb_n):
        got = lax.ppermute(stack, "pb", [(i, i ^ bit) for i in range(places.pb_n)])
        stack = jnp.concatenate([stack, got], axis=0)
        pair_masks = pair_masks + [m ^ (bit * places.pa_n) for m in pair_masks]
    stack = jnp.concatenate([stack, places.swap_core(stack)], axis=0)
    pair_masks = pair_masks + [m ^ 1 for m in pair_masks]
    groups = len(pair_masks)
    me = pb * places.pa_n + low_pa
    place = jnp.array(pair_masks, jnp.int32) ^ me
    dev_p = jnp.stack([place + shift, place], axis=1)
    p_ids = (dev_p[:, :, None] * np_ + jnp.arange(np_, dtype=jnp.int32)).reshape(-1)
    digits = stack[:, per_q + per_p : per_q + per_p + 2, :per_q].astype(jnp.int32)
    wanted = (digits[:, 0] * 16 + digits[:, 1]).reshape(-1)

    all_q = stack[:, :per_q].reshape(groups * per_q, D)
    all_p = stack[:, per_q : per_q + per_p].reshape(groups * per_p, D)
    similarity = dot(all_q, all_p, ((1,), (1,))) * score_scale
    hot = (wanted[:, None] == p_ids[None, :]).astype(F32)
    top = jnp.max(similarity, axis=1, keepdims=True)
    grown = jnp.exp(similarity - top)
    total = jnp.sum(grown, axis=1, keepdims=True)
    own_sim = similarity[:per_q]
    loss = top[:per_q, 0] + jnp.log(total[:per_q, 0]) - jnp.sum(own_sim * hot[:per_q], axis=1)
    question_loss = lax.dynamic_slice_in_dim(loss, tower * nq, nq)
    d_sim = (loss_weight * (grown / total - hot)).astype(BF16)
    d_q = dot(d_sim[:per_q], all_p) * score_scale
    d_p = dot(d_sim[:, :per_p], all_q, ((0,), (0,))) * score_scale
    d_p = jnp.concatenate(
        [d_p.reshape(per_p, 1, D), jnp.zeros((per_p, every - 1, D), F32)], axis=1
    ).reshape(per_q, D)
    d_slot = jnp.where(is_q, d_q, d_p)

    d_second, d_reduced, sums_second = second_back(
        join([my_cot] + cot_in), d_slot, row_mask, norm_two, inverse_two, vec[6][None, :]
    )
    even = share % 8 == 0

    def gradient(left, right, **more):
        if left.shape[1] > D:
            return tall_grad(left, right, slots, places.nz)
        return weight_grad(left, right, slots, D, **more)

    def plain(left, right, extra=None):
        if extra is not None:
            one, two, first, second, bias = extra
            joined = one + two
            lines = [joined[:, :D], joined[:, 2 * D :], first[2:3], first[:2]]
            lines = lines + [second[2:3], second[:2], bias, jnp.zeros((116, D), F32)]
            extra = jnp.concatenate(lines, axis=0).T
        return grad_plain(left, right, table, extra)

    class Scatter:
        def __init__(self, mine, theirs):
            self.parts, self.theirs, self.send = [mine], theirs, None
            self.count = mine.shape[0]

        def cores(self):
            self.parts = self.parts + [places.swap_core(self.theirs)]

        def total(self, start, stop):
            out = self.parts[0][start:stop].astype(F32)
            for part in self.parts[1:]:
                out = out + part[start:stop].astype(F32)
            return out

        def prepare(self):
            self.send = self.total(self.count // 2, self.count).astype(BF16)

        def move(self, step):
            if self.send is None:
                self.prepare()
            self.parts = self.parts + [places.swap(self.send, step)]
            self.send = None
            self.count = self.count // 2

        def pb_first(self):
            self.move(places.steps - 1)

        def pb_rest(self):
            for step in range(places.steps - 2, z_steps - 1, -1):
                self.move(step)

        def along_z(self):
            for step in range(z_steps - 1, 0, -1):
                self.move(step)

        def mid(self):
            self.got = places.swap(self.total(1, 2).astype(BF16), 0)

        def finish(self):
            got, keep = self.got.astype(F32), self.total(0, 1)
            return jnp.concatenate(
                [jnp.where(is_q, keep, got), jnp.where(is_q, got, keep)], axis=0
            )

    send_out = chunked(out[own_rows:], (4, 4, 4, 4))
    d_reduced, send_out = tie(d_reduced, send_out)
    got_out = hand(send_out[:1])
    sr = Scatter(*(gradient if even else plain)(active, d_reduced))
    sr.parts, sr.theirs, d_reduced, got_out, send_out = tie(
        sr.parts, sr.theirs, d_reduced, got_out, send_out
    )
    sr.cores()
    got_out = got_out + hand(send_out[1:2])
    d_expanded, g_bias_expand = hidden_grad(d_reduced, wr, slope)
    sr.parts, d_expanded, got_out, send_out = tie(sr.parts, d_expanded, got_out, send_out)
    sr.pb_first()
    got_out = got_out + hand(send_out[2:3])
    if even:
        partial = gradient(mid_low, d_expanded, room=D)
    else:
        partial = plain(mid_low, d_expanded)
    partial, d_expanded, got_out, send_out = tie(partial, d_expanded, got_out, send_out)
    got_out = got_out + hand(send_out[3:])
    d_first, d_attended, sums_first = first_back(
        d_expanded, we, d_second, norm_one, inverse_one, vec[3][None, :]
    )
    sr.parts, partial, d_attended, got_out = tie(sr.parts, partial, d_attended, got_out)
    sr.pb_rest()
    if even:
        partial = gradient(context, d_attended, into=tuple(partial))
    else:
        also = plain(context, d_attended)
        partial = [jnp.concatenate(x, axis=2) for x in zip(partial, also)]
    se = Scatter(*partial)
    se.parts, se.theirs, d_attended = tie(se.parts, se.theirs, d_attended)
    se.cores()
    d_context = dot(d_attended, wo, ((1,), (1,))).astype(BF16)
    d_joined, sums_one = attention_back(qkv, probs, d_context, later, blocks - later)
    sr.parts, se.parts, d_joined = tie(sr.parts, se.parts, d_joined)
    se.prepare()
    sr.prepare()
    sr.send, sr.parts, se.send, se.parts, d_joined = tie(
        sr.send, sr.parts, se.send, se.parts, d_joined
    )
    se.pb_first()
    sr.along_z()
    part = own_rows // 16
    send_grad = token_grad(d_joined, wj, d_first, own_rows, [k * part for k in (5, 3, 3, 5)], BF16)
    d_joined, send_grad = tie(d_joined, send_grad)
    got_grad = hand(send_grad[:1])
    d_joined, sums_two = attention_back(qkv, probs, d_context, 0, later, d_joined)
    sr.parts, se.parts, d_joined, sums_two, got_grad, send_grad = tie(
        sr.parts, se.parts, d_joined, sums_two, got_grad, send_grad
    )
    se.prepare()
    se.send, se.parts, d_joined, send_grad = tie(se.send, se.parts, d_joined, send_grad)
    se.pb_rest()
    sr.mid()
    got_grad = got_grad + hand(send_grad[1:2])
    bias_sums = g_bias_expand.reshape(D, 4).T
    small_sums = (sums_one, sums_two, sums_first, sums_second, bias_sums)
    sj = Scatter(*(gradient if even else plain)(tokens, d_joined, extra=small_sums))
    se.parts, sr.got, sj.parts, sj.theirs, d_joined, got_grad, send_grad = tie(
        se.parts, sr.got, sj.parts, sj.theirs, d_joined, got_grad, send_grad
    )
    sj.cores()
    got_grad = got_grad + hand(send_grad[2:3])
    (own_grad,) = token_grad(d_joined, wj, d_first, 0, [own_rows], F32)
    sj.parts, own_grad, got_grad, send_grad = tie(sj.parts, own_grad, got_grad, send_grad)
    sj.pb_first()
    se.along_z()
    got_grad = got_grad + hand(send_grad[3:])
    sj.parts, se.parts, got_grad, send_grad = tie(sj.parts, se.parts, got_grad, send_grad)
    sj.pb_rest()
    se.mid()
    sj.parts, se.got, got_out, out = tie(sj.parts, se.got, got_out, out)
    sj.along_z()
    out_q, out_p = deal(tower.reshape(1), out, got_out)
    sj.parts, out_q, out_p, got_grad, sr.got, sr.parts, se.got, se.parts = tie(
        sj.parts, out_q, out_p, got_grad, sr.got, sr.parts, se.got, se.parts
    )
    grad_q, grad_p = deal(tower.reshape(1), own_grad, got_grad)
    sj.mid()
    grad_reduce, both, last = sr.finish(), se.finish(), sj.finish()
    grad_joined = last[:, :, : 3 * D]
    grad_expand, grad_output = both[:, :, :FF], both[:, :, FF:]
    extra = last[:, :, 3 * D :]
    grad_vectors = extra[:, :, :8].transpose(0, 2, 1)
    grad_b_expand = extra[:, :, 8:12].reshape(2, 4 * share)

    return (
        out_q.reshape(question_in.shape),
        out_p.reshape(passage_in.shape),
        question_loss,
        grad_q.reshape(question_in.shape),
        grad_p.reshape(passage_in.shape),
        grad_joined,
        grad_output,
        grad_expand,
        grad_reduce,
        grad_vectors,
        grad_b_expand,
    )


def solution(mesh):
    in_specs = (
        P(("pb", "pa"), None, None),
        P(("pb", "pa"), None, None),
        P(("pb", "pa")),
        P(("pb", "pa")),
        P("pb"),
        P(("pb", "pa"), None, None),
        P(("pb", "pa"), None, None),
        P(None, ("pb", "pa"), None),
        P(None, ("pb", "pa"), None),
        P(None, ("pb", "pa"), None),
        P(None, ("pb", "pa"), None),
        P(None, None, ("pb", "pa")),
        P(None, ("pb", "pa")),
    )
    out_specs = (
        P(("pb", "pa"), None, None),
        P(("pb", "pa"), None, None),
        P(("pb", "pa")),
        P(("pb", "pa"), None, None),
        P(("pb", "pa"), None, None),
        P(None, ("pb", "pa"), None),
        P(None, ("pb", "pa"), None),
        P(None, ("pb", "pa"), None),
        P(None, ("pb", "pa"), None),
        P(None, None, ("pb", "pa")),
        P(None, ("pb", "pa")),
    )
    return jax.shard_map(
        functools.partial(per_device, Places(mesh)),
        mesh=mesh,
        in_specs=in_specs,
        out_specs=out_specs,
        check_vma=False,
    )
```

```python
import functools

import jax
import jax.numpy as jnp
from jax import lax
from jax.experimental import pallas as pl
from jax.experimental.pallas import tpu as pltpu
from jax.sharding import PartitionSpec as P

D = 768
HEADS = 12
HDIM = 64
FF = 3072
AXES = ("pb", "pa")
BLOCK = 256

norm_eps = 1e-06
masked_score = -1000000000.0
score_scale = 0.0625
loss_weight = 16.0
head_scale = HDIM ** (-0.5)
F32 = jnp.float32
BF16 = jnp.bfloat16
VMEM_LIMIT = 56 * 1024 * 1024


def bits_of(count):
    return [1 << shift for shift in range(count.bit_length() - 1)]


class Places:
    def __init__(self, mesh):
        self.pb_n = mesh.shape["pb"]
        self.pa_n = mesh.shape["pa"]
        self.nz = self.pa_n // 2
        self.half = self.nz // 2
        self.chips = self.pb_n * self.nz
        pb_bits = bits_of(self.pb_n)
        turn = len(pb_bits) // 2
        low_z = [("z", bit) for bit in bits_of(self.half)]
        first = [("pb", bit) for bit in pb_bits]
        second = first[turn:] + first[:turn]
        self.orders = ([("z", self.half)] + low_z + first, [("z", self.half)] + low_z + second)
        self.steps = len(self.orders[0])

    def chip_mask(self, move):
        axis, bit = move
        return bit * self.nz if axis == "pb" else bit

    def stack_masks(self, core):
        masks = [0]
        for move in self.orders[core]:
            masks = masks + [mask ^ self.chip_mask(move) for mask in masks]
        return masks

    def pairs(self, step):
        out = []
        for pb in range(self.pb_n):
            for pa in range(self.pa_n):
                axis, bit = self.orders[pa % 2][step]
                to_pb, to_pa = (pb ^ bit, pa) if axis == "pb" else (pb, pa ^ (2 * bit))
                out.append((pb * self.pa_n + pa, to_pb * self.pa_n + to_pa))
        return out

    def swap(self, values, step):
        return lax.ppermute(values, AXES, self.pairs(step))

    def swap_core(self, values):
        return lax.ppermute(values, "pa", [(i, i ^ 1) for i in range(self.pa_n)])

    def swap_tower(self, values):
        return lax.ppermute(values, "pa", [(i, i ^ (2 * self.half)) for i in range(self.pa_n)])


def dot(left, right, dims=((1,), (0,))):
    return lax.dot_general(left, right, (dims, ((), ())), preferred_element_type=F32)


def tie(*values):
    return lax.optimization_barrier(values)


def assemble_kernel(segments, idx_ref, *refs):
    count = len(segments)
    sources, outs = refs[:4], refs[4 : 4 + count]
    buffer, in_sem, out_sem = refs[4 + count :]
    core = idx_ref[2, 0]
    part = sources[0].shape[0]
    loads = [
        pltpu.make_async_copy(source, buffer.at[pl.ds(k * part, part)], in_sem.at[k])
        for k, source in enumerate(sources)
    ]
    for load in loads:
        load.start()
    stores = []
    for k in range(4):
        loads[k].wait()
        half = core if k < 2 else 1 - core
        for j in range(part):
            slot = k * part + j
            place = idx_ref[k // 2, (k % 2) * part + j]
            for s, (start, width) in enumerate(segments):
                store = pltpu.make_async_copy(
                    buffer.at[slot, :, pl.ds(start, width)],
                    outs[s].at[place, half],
                    out_sem.at[s, slot],
                )
                store.start()
                stores.append(store)
    for store in stores:
        store.wait()


def assemble(parts, table, segments):
    part, rows, width = parts[0].shape
    chips = 2 * part
    shapes = [jax.ShapeDtypeStruct((chips, 2, rows, w), BF16) for _, w in segments]
    return pl.pallas_call(
        functools.partial(assemble_kernel, segments),
        out_shape=shapes,
        in_specs=[pl.BlockSpec(memory_space=pltpu.SMEM)] + [pl.BlockSpec(memory_space=pl.ANY)] * 4,
        out_specs=[pl.BlockSpec(memory_space=pl.ANY)] * len(segments),
        scratch_shapes=[
            pltpu.VMEM((2 * chips, rows, width), BF16),
            pltpu.SemaphoreType.DMA((4,)),
            pltpu.SemaphoreType.DMA((len(segments), 2 * chips)),
        ],
        compiler_params=pltpu.CompilerParams(vmem_limit_bytes=VMEM_LIMIT),
        cost_estimate=pl.CostEstimate(
            flops=0, bytes_accessed=4 * 2 * chips * rows * width, transcendentals=0
        ),
        name="assemble",
    )(table, *parts)


def assemble_plain(parts, table, segments):
    own = jnp.take(jnp.concatenate(parts[:2], axis=0), jnp.argsort(table[0]), axis=0)
    other = jnp.take(jnp.concatenate(parts[2:], axis=0), jnp.argsort(table[1]), axis=0)
    first = table[2, 0] == 0
    both = jnp.stack([jnp.where(first, own, other), jnp.where(first, other, own)], axis=1)
    return [both[..., start : start + w] for start, w in segments]


def split_slabs(acc, core, chips, mine_ref, theirs_ref, cols, within):
    rows = acc.shape[0] // (2 * chips)
    for s in range(chips):
        low = acc[2 * s * rows : (2 * s + 1) * rows]
        high = acc[(2 * s + 1) * rows : (2 * s + 2) * rows]
        mine, theirs = within(s)
        mine_ref[mine, :, cols] = jnp.where(core == 0, low, high).astype(BF16)
        theirs_ref[theirs, :, cols] = jnp.where(core == 0, high, low).astype(BF16)


def weight_grad_kernel(chips, extra, table_ref, left_ref, right_ref, *refs):
    mine_ref, theirs_ref = refs[-2:]
    core = table_ref[2, 0]
    acc = dot(left_ref[...], right_ref[...], ((0,), (0,)))
    width = acc.shape[1]

    def within(s):
        return table_ref[0, s], table_ref[1, s]

    if extra == 0:
        split_slabs(acc, core, chips, mine_ref, theirs_ref, slice(None), within)
        return
    step = pl.program_id(0)
    cols = pl.ds(pl.multiple_of(step * width, 128), width)
    split_slabs(acc, core, chips, mine_ref, theirs_ref, cols, within)

    @pl.when(step == 0)
    def _():
        one, two, first, second, bias = (ref[...] for ref in refs[:extra])
        joined = one + two
        lines = [
            joined[:, :D],
            joined[:, 2 * D :],
            first[2:3],
            first[:2],
            second[2:3],
            second[:2],
            bias,
            jnp.zeros((116, D), F32),
        ]
        values = jnp.concatenate(lines, axis=0).T
        tail = pl.ds(mine_ref.shape[2] - 128, 128)
        split_slabs(values, core, chips, mine_ref, theirs_ref, tail, within)


def weight_grad(left, right, slots, tile, extra=None, room=0, into=()):
    rows, height = left.shape
    width = right.shape[1]
    chips = slots.shape[1]
    slab = height // (2 * chips)
    total = width + (room if extra is None else 128)
    first = 0
    if into:
        total = into[0].shape[2]
        first = (total - width) // tile
    block = (chips, slab, total if extra is not None else tile)
    place = (lambda j, t: (0, 0, 0)) if extra is not None else (lambda j, t: (0, 0, j + first))
    return pl.pallas_call(
        functools.partial(weight_grad_kernel, chips, len(extra or ())),
        grid_spec=pltpu.PrefetchScalarGridSpec(
            num_scalar_prefetch=1,
            grid=(width // tile,),
            in_specs=[
                pl.BlockSpec((rows, height), lambda j, t: (0, 0)),
                pl.BlockSpec((rows, tile), lambda j, t: (0, j)),
            ]
            + [pl.BlockSpec(x.shape, lambda j, t: (0, 0)) for x in extra or ()]
            + [pl.BlockSpec(memory_space=pl.ANY)] * len(into),
            out_specs=[pl.BlockSpec(block, place)] * 2,
        ),
        out_shape=[jax.ShapeDtypeStruct((chips, slab, total), BF16)] * 2,
        input_output_aliases={3: 0, 4: 1} if into else {},
        compiler_params=pltpu.CompilerParams(vmem_limit_bytes=VMEM_LIMIT),
        cost_estimate=pl.CostEstimate(
            flops=2 * rows * height * width,
            bytes_accessed=2 * (rows * (height + width) + height * width),
            transcendentals=0,
        ),
        name="weight_grad",
    )(slots, left, right, *(extra or ()), *into)


def tall_grad_kernel(chips, table_ref, left_ref, right_ref, mine_ref, theirs_ref):
    core = table_ref[2, 0]
    acc = dot(left_ref[...], right_ref[...], ((0,), (0,)))
    base = pl.program_id(0) * chips

    def within(s):
        return table_ref[0, base + s] % chips, table_ref[1, base + s] % chips

    split_slabs(acc, core, chips, mine_ref, theirs_ref, slice(None), within)


def tall_grad(left, right, slots, column):
    rows, height = left.shape
    width = right.shape[1]
    chips = slots.shape[1]
    slab = height // (2 * chips)
    tile = height // chips * column
    return pl.pallas_call(
        functools.partial(tall_grad_kernel, column),
        grid_spec=pltpu.PrefetchScalarGridSpec(
            num_scalar_prefetch=1,
            grid=(chips // column,),
            in_specs=[
                pl.BlockSpec((rows, tile), lambda i, t: (0, i)),
                pl.BlockSpec((rows, width), lambda i, t: (0, 0)),
            ],
            out_specs=[
                pl.BlockSpec((column, slab, width), lambda i, t: (t[0, i * column] // column, 0, 0)),
                pl.BlockSpec((column, slab, width), lambda i, t: (t[1, i * column] // column, 0, 0)),
            ],
        ),
        out_shape=[jax.ShapeDtypeStruct((chips, slab, width), BF16)] * 2,
        compiler_params=pltpu.CompilerParams(vmem_limit_bytes=VMEM_LIMIT),
        cost_estimate=pl.CostEstimate(
            flops=2 * rows * height * width,
            bytes_accessed=2 * (rows * (height + width) + height * width),
            transcendentals=0,
        ),
        name="tall_grad",
    )(slots, left, right)


def grad_plain(left, right, table, extra=None):
    full = dot(left, right, ((0,), (0,)))
    if extra is not None:
        full = jnp.concatenate([full, extra], axis=1)
    chips = table.shape[1]
    full = full.astype(BF16).reshape(chips, 2, full.shape[0] // (2 * chips), full.shape[1])
    core = table[2, 0]
    mine = lax.dynamic_index_in_dim(full, core, 1, keepdims=False)
    theirs = lax.dynamic_index_in_dim(full, 1 - core, 1, keepdims=False)
    return jnp.take(mine, table[0], axis=0), jnp.take(theirs, table[1], axis=0)


def hidden_grad_kernel(grad_ref, w_ref, slope_ref, out_ref, sum_ref):
    grad = dot(grad_ref[...], w_ref[...], ((1,), (1,))) * slope_ref[...].astype(F32)
    low = grad.astype(BF16)
    out_ref[...] = low
    sum_ref[...] = jnp.sum(low.astype(F32), axis=0, keepdims=True)


def hidden_grad(grad, w_reduce, slope):
    rows, tile = grad.shape[0], 512
    return pl.pallas_call(
        hidden_grad_kernel,
        grid=(FF // tile,),
        in_specs=[
            pl.BlockSpec((rows, D), lambda j: (0, 0)),
            pl.BlockSpec((tile, D), lambda j: (j, 0)),
            pl.BlockSpec((rows, tile), lambda j: (0, j)),
        ],
        out_specs=[
            pl.BlockSpec((rows, tile), lambda j: (0, j)),
            pl.BlockSpec((1, tile), lambda j: (0, j)),
        ],
        out_shape=[
            jax.ShapeDtypeStruct((rows, FF), BF16),
            jax.ShapeDtypeStruct((1, FF), F32),
        ],
        compiler_params=pltpu.CompilerParams(vmem_limit_bytes=VMEM_LIMIT),
        cost_estimate=pl.CostEstimate(
            flops=2 * rows * D * FF,
            bytes_accessed=2 * (rows * D + D * FF + 2 * rows * FF),
            transcendentals=0,
        ),
        name="hidden_grad",
    )(grad, w_reduce, slope)


def attention_kernel(qkv_ref, qid_ref, kid_ref, context_ref, probs_ref):
    allowed = qid_ref[...] == kid_ref[0]
    lane = lax.broadcasted_iota(jnp.int32, (BLOCK, 128), 1)
    zero = jnp.zeros((BLOCK, 128), BF16)
    for pair in range(HEADS // 2):
        queries = qkv_ref[:, pair * 128 : pair * 128 + 128]
        keys = qkv_ref[:, D + pair * 128 : D + pair * 128 + 128]
        values = qkv_ref[:, 2 * D + pair * 128 : 2 * D + pair * 128 + 128]
        outs = []
        for side in range(2):
            mine = (lane < HDIM) if side == 0 else (lane >= HDIM)
            scores = dot(queries, jnp.where(mine, keys, zero), ((1,), (1,))) * head_scale
            scores = jnp.where(allowed, scores, masked_score)
            top = jnp.max(scores, axis=1, keepdims=True)
            grown = jnp.exp(scores - top)
            total = jnp.sum(grown, axis=1, keepdims=True)
            probs = (grown * (1.0 / total)).astype(BF16)
            probs_ref[0, 2 * pair + side] = probs
            outs.append(dot(probs, values))
        context_ref[:, pair * 128 : pair * 128 + 128] = jnp.where(
            lane < HDIM, outs[0], outs[1]
        ).astype(BF16)


def attention(qkv, qid, kid):
    rows = qkv.shape[0]
    blocks = rows // BLOCK
    return pl.pallas_call(
        attention_kernel,
        grid=(blocks,),
        in_specs=[
            pl.BlockSpec((BLOCK, 3 * D), lambda i: (i, 0)),
            pl.BlockSpec((BLOCK, 1), lambda i: (i, 0)),
            pl.BlockSpec((1, 1, BLOCK), lambda i: (i, 0, 0)),
        ],
        out_specs=[
            pl.BlockSpec((BLOCK, D), lambda i: (i, 0)),
            pl.BlockSpec((1, HEADS, BLOCK, BLOCK), lambda i: (i, 0, 0, 0)),
        ],
        out_shape=[
            jax.ShapeDtypeStruct((rows, D), BF16),
            jax.ShapeDtypeStruct((blocks, HEADS, BLOCK, BLOCK), BF16),
        ],
        compiler_params=pltpu.CompilerParams(vmem_limit_bytes=VMEM_LIMIT),
        cost_estimate=pl.CostEstimate(
            flops=4 * rows * BLOCK * D * 2,
            bytes_accessed=rows * (4 * D + HEADS * BLOCK) * 2,
            transcendentals=rows * HEADS * BLOCK,
        ),
        name="attention",
    )(qkv, qid, kid)


def attention_back_kernel(qkv_ref, probs_ref, grad_ref, out_ref, sum_ref):
    lane = lax.broadcasted_iota(jnp.int32, (BLOCK, 128), 1)
    zero = jnp.zeros((BLOCK, 128), BF16)

    def at(pair, start=0):
        return pl.ds(pl.multiple_of(start + pair * 128, 128), 128)

    def some(step, carry):
        for k in range(2):
            pair = step * 2 + k
            cols = at(pair)
            queries = qkv_ref[:, at(pair)]
            keys = qkv_ref[:, at(pair, D)]
            values = qkv_ref[:, at(pair, 2 * D)]
            grad = grad_ref[:, cols]
            d_q, d_k, d_v = [], [], []
            for side in range(2):
                mine = (lane < HDIM) if side == 0 else (lane >= HDIM)
                low = probs_ref[0, 2 * pair + side]
                d_probs = dot(jnp.where(mine, grad, zero), values, ((1,), (1,)))
                d_v.append(dot(low, grad, ((0,), (0,))))
                probs = low.astype(F32)
                row_dot = jnp.sum(d_probs * probs, axis=1, keepdims=True)
                d_scores = (probs * (d_probs - row_dot)).astype(BF16)
                d_q.append(dot(d_scores, keys))
                d_k.append(dot(d_scores, queries, ((0,), (0,))))
            first = lane < HDIM
            out_ref[:, at(pair)] = (
                jnp.where(first, d_q[0], d_q[1]) * head_scale
            ).astype(BF16)
            out_ref[:, at(pair, D)] = (
                jnp.where(first, d_k[0], d_k[1]) * head_scale
            ).astype(BF16)
            out_ref[:, at(pair, 2 * D)] = jnp.where(
                first, d_v[0], d_v[1]
            ).astype(BF16)
        return carry

    lax.fori_loop(0, HEADS // 2 // 2, some, 0)
    sums = jnp.sum(out_ref[...].astype(F32), axis=0, keepdims=True)

    @pl.when(pl.program_id(0) == 0)
    def _():
        sum_ref[...] = sums

    @pl.when(pl.program_id(0) > 0)
    def _():
        sum_ref[...] += sums


def attention_back_more_kernel(qkv_ref, probs_ref, grad_ref, _, out_ref, sum_ref):
    attention_back_kernel(qkv_ref, probs_ref, grad_ref, out_ref, sum_ref)


def attention_back(qkv, probs, grad_context, start, count, into=None):
    rows = qkv.shape[0]
    more = into is not None
    return pl.pallas_call(
        attention_back_more_kernel if more else attention_back_kernel,
        grid=(count,),
        in_specs=[
            pl.BlockSpec((BLOCK, 3 * D), lambda i: (i + start, 0)),
            pl.BlockSpec((1, HEADS, BLOCK, BLOCK), lambda i: (i + start, 0, 0, 0)),
            pl.BlockSpec((BLOCK, D), lambda i: (i + start, 0)),
        ]
        + ([pl.BlockSpec(memory_space=pl.ANY)] if more else []),
        out_specs=[
            pl.BlockSpec((BLOCK, 3 * D), lambda i: (i + start, 0)),
            pl.BlockSpec((1, 3 * D), lambda i: (0, 0)),
        ],
        out_shape=[
            jax.ShapeDtypeStruct((rows, 3 * D), BF16),
            jax.ShapeDtypeStruct((1, 3 * D), F32),
        ],
        input_output_aliases={3: 0} if more else {},
        compiler_params=pltpu.CompilerParams(vmem_limit_bytes=VMEM_LIMIT),
        cost_estimate=pl.CostEstimate(
            flops=8 * count * BLOCK * BLOCK * D * 2,
            bytes_accessed=count * BLOCK * (7 * D + HEADS * BLOCK) * 2,
            transcendentals=0,
        ),
        name="attention_back",
    )(qkv, probs, grad_context, *([into] if more else []))


def join_kernel(*refs):
    row = 0
    for piece in refs[:-1]:
        rows = piece.shape[0]
        refs[-1][row : row + rows, :] = piece[...]
        row += rows


def join(pieces):
    rows, width = sum(x.shape[0] for x in pieces), pieces[0].shape[1]
    return pl.pallas_call(
        join_kernel,
        grid=(1,),
        in_specs=[pl.BlockSpec(x.shape, lambda i: (0, 0)) for x in pieces],
        out_specs=pl.BlockSpec((rows, width), lambda i: (0, 0)),
        out_shape=jax.ShapeDtypeStruct((rows, width), pieces[0].dtype),
        compiler_params=pltpu.CompilerParams(vmem_limit_bytes=VMEM_LIMIT),
        cost_estimate=pl.CostEstimate(
            flops=0, bytes_accessed=4 * rows * width, transcendentals=0
        ),
        name="join",
    )(*pieces)


def deal_kernel(tower_ref, own_ref, *refs):
    pieces, (q_ref, p_ref) = refs[:-2], refs[-2:]

    def give(own_out, other_out):
        own_out[...] = own_ref[...]
        row = 0
        for piece in pieces:
            rows = piece.shape[0]
            other_out[row : row + rows, :] = piece[...].astype(other_out.dtype)
            row += rows

    @pl.when(tower_ref[0] == 0)
    def _():
        give(q_ref, p_ref)

    @pl.when(tower_ref[0] != 0)
    def _():
        give(p_ref, q_ref)


def deal(tower, own, pieces):
    rows, width = sum(x.shape[0] for x in pieces), own.shape[1]
    shape = jax.ShapeDtypeStruct((rows, width), own.dtype)
    return pl.pallas_call(
        deal_kernel,
        grid=(1,),
        in_specs=[
            pl.BlockSpec(memory_space=pltpu.SMEM),
            pl.BlockSpec((rows, width), lambda i: (0, 0)),
        ]
        + [pl.BlockSpec(x.shape, lambda i: (0, 0)) for x in pieces],
        out_specs=[pl.BlockSpec((rows, width), lambda i: (0, 0))] * 2,
        out_shape=[shape] * 2,
        compiler_params=pltpu.CompilerParams(vmem_limit_bytes=VMEM_LIMIT),
        cost_estimate=pl.CostEstimate(
            flops=0, bytes_accessed=12 * rows * width, transcendentals=0
        ),
        name="deal",
    )(tower, own, *pieces)


def add_sums(sum_ref, values):
    total = jnp.concatenate(
        [jnp.sum(x, axis=0, keepdims=True) for x in values]
        + [jnp.zeros((8 - len(values), values[0].shape[1]), F32)],
        axis=0,
    )

    @pl.when(pl.program_id(0) == 0)
    def _():
        sum_ref[...] = total

    @pl.when(pl.program_id(0) > 0)
    def _():
        sum_ref[...] += total


def second_back_kernel(
    cot_ref, slot_ref, mask_ref, norm_ref, inverse_ref, gain_ref, grad_ref, low_ref, sum_ref
):
    group = slot_ref.shape[1]
    cot = cot_ref[...].astype(F32).reshape(group, BLOCK // group, D)
    first = lax.broadcasted_iota(jnp.int32, cot.shape, 1) == 0
    grad = cot + jnp.where(first, slot_ref[0][:, None, :], 0.0)
    grad = grad.reshape(BLOCK, D) * mask_ref[...]
    norm = norm_ref[...]
    second = norm_back(grad, gain_ref[...], norm, inverse_ref[...])
    low = second.astype(BF16)
    grad_ref[...] = second
    low_ref[...] = low
    add_sums(sum_ref, [grad * norm, grad, low.astype(F32)])


def second_back(cot, d_slot, mask, norm, inverse, gain):
    rows = cot.shape[0]
    blocks = rows // BLOCK
    wide = pl.BlockSpec((BLOCK, D), lambda i: (i, 0))
    thin = pl.BlockSpec((BLOCK, 1), lambda i: (i, 0))
    group = d_slot.shape[0] // blocks
    return pl.pallas_call(
        second_back_kernel,
        grid=(blocks,),
        in_specs=[
            wide,
            pl.BlockSpec((1, group, D), lambda i: (i, 0, 0)),
            thin,
            wide,
            thin,
            pl.BlockSpec((1, D), lambda i: (0, 0)),
        ],
        out_specs=[wide, wide, pl.BlockSpec((8, D), lambda i: (0, 0))],
        out_shape=[
            jax.ShapeDtypeStruct((rows, D), F32),
            jax.ShapeDtypeStruct((rows, D), BF16),
            jax.ShapeDtypeStruct((8, D), F32),
        ],
        compiler_params=pltpu.CompilerParams(vmem_limit_bytes=VMEM_LIMIT),
        cost_estimate=pl.CostEstimate(
            flops=20 * rows * D, bytes_accessed=12 * rows * D, transcendentals=0
        ),
        name="second_back",
    )(cot, d_slot.reshape(blocks, group, D), mask, norm, inverse, gain)


def first_back_kernel(
    hidden_ref, w_ref, second_ref, norm_ref, inverse_ref, gain_ref, grad_ref, low_ref, sum_ref
):
    grad = second_ref[...] + dot(hidden_ref[...], w_ref[...], ((1,), (1,)))
    norm = norm_ref[...]
    first = norm_back(grad, gain_ref[...], norm, inverse_ref[...])
    low = first.astype(BF16)
    grad_ref[...] = first
    low_ref[...] = low
    add_sums(sum_ref, [grad * norm, grad, low.astype(F32)])


def first_back(d_expanded, w_expand, d_second, norm, inverse, gain):
    rows = d_expanded.shape[0]
    wide = pl.BlockSpec((BLOCK, D), lambda i: (i, 0))
    return pl.pallas_call(
        first_back_kernel,
        grid=(rows // BLOCK,),
        in_specs=[
            pl.BlockSpec((BLOCK, FF), lambda i: (i, 0)),
            pl.BlockSpec((D, FF), lambda i: (0, 0)),
            wide,
            wide,
            pl.BlockSpec((BLOCK, 1), lambda i: (i, 0)),
            pl.BlockSpec((1, D), lambda i: (0, 0)),
        ],
        out_specs=[wide, wide, pl.BlockSpec((8, D), lambda i: (0, 0))],
        out_shape=[
            jax.ShapeDtypeStruct((rows, D), F32),
            jax.ShapeDtypeStruct((rows, D), BF16),
            jax.ShapeDtypeStruct((8, D), F32),
        ],
        compiler_params=pltpu.CompilerParams(vmem_limit_bytes=VMEM_LIMIT),
        cost_estimate=pl.CostEstimate(
            flops=2 * rows * D * FF,
            bytes_accessed=2 * (rows * FF + D * FF) + 14 * rows * D,
            transcendentals=0,
        ),
        name="first_back",
    )(d_expanded, w_expand, d_second, norm, inverse, gain)


def expand_kernel(mid_ref, w_ref, b_ref, active_ref, slope_ref):
    expanded = dot(mid_ref[...], w_ref[...]) + b_ref[...]
    phi = 0.5 + 0.5 * lax.erf(expanded * 0.7071067811865476)
    density = jnp.exp(expanded * expanded * -0.5) * 0.3989422804014327
    active_ref[...] = (expanded * phi).astype(BF16)
    slope_ref[...] = (phi + expanded * density).astype(BF16)


def expand_more_kernel(mid_ref, w_ref, b_ref, _, __, active_ref, slope_ref):
    expand_kernel(mid_ref, w_ref, b_ref, active_ref, slope_ref)


def expand(mid_low, w_expand, b_expand, start, count, into=()):
    rows = mid_low.shape[0]
    tile_r, tile_f = 256, FF // 2
    return pl.pallas_call(
        expand_more_kernel if into else expand_kernel,
        grid=(count, rows // tile_r),
        in_specs=[
            pl.BlockSpec((tile_r, D), lambda j, i: (i, 0)),
            pl.BlockSpec((D, tile_f), lambda j, i: (0, j + start)),
            pl.BlockSpec((1, tile_f), lambda j, i: (0, j + start)),
        ]
        + [pl.BlockSpec(memory_space=pl.ANY)] * len(into),
        out_specs=[
            pl.BlockSpec((tile_r, tile_f), lambda j, i: (i, j + start)),
            pl.BlockSpec((tile_r, tile_f), lambda j, i: (i, j + start)),
        ],
        out_shape=[jax.ShapeDtypeStruct((rows, FF), BF16)] * 2,
        input_output_aliases={3: 0, 4: 1} if into else {},
        compiler_params=pltpu.CompilerParams(vmem_limit_bytes=VMEM_LIMIT),
        cost_estimate=pl.CostEstimate(
            flops=2 * rows * D * count * tile_f,
            bytes_accessed=2 * (rows * D + D * count * tile_f + 2 * rows * count * tile_f),
            transcendentals=2 * rows * count * tile_f,
        ),
        name="expand",
    )(mid_low, w_expand, b_expand, *into)


def token_grad_kernel(grad_ref, w_ref, first_ref, *outs):
    block = first_ref[...] + dot(grad_ref[...], w_ref[...], ((1,), (1,)))
    block = block.astype(outs[0].dtype)
    step, start = pl.program_id(0), 0
    for out in outs:
        stop = start + out.shape[0]
        for k in range(start // BLOCK, (stop - 1) // BLOCK + 1):
            low, high = max(start, k * BLOCK), min(stop, (k + 1) * BLOCK)

            @pl.when(step == k)
            def _(out=out, k=k, low=low, high=high, start=start):
                out[low - start : high - start, :] = block[low - k * BLOCK : high - k * BLOCK]

        start = stop


def token_grad(d_joined, weight, d_first, start, pieces, dtype):
    width = weight.shape[1]
    first, count = start // BLOCK, sum(pieces) // BLOCK
    return pl.pallas_call(
        token_grad_kernel,
        grid=(count,),
        in_specs=[
            pl.BlockSpec((BLOCK, width), lambda i: (i + first, 0)),
            pl.BlockSpec((D, width), lambda i: (0, 0)),
            pl.BlockSpec((BLOCK, D), lambda i: (i + first, 0)),
        ],
        out_specs=[pl.BlockSpec((n, D), lambda i: (0, 0)) for n in pieces],
        out_shape=[jax.ShapeDtypeStruct((n, D), dtype) for n in pieces],
        compiler_params=pltpu.CompilerParams(vmem_limit_bytes=VMEM_LIMIT),
        cost_estimate=pl.CostEstimate(
            flops=2 * count * BLOCK * D * width,
            bytes_accessed=2 * D * width + count * BLOCK * (2 * width + 6 * D),
            transcendentals=0,
        ),
        name="token_grad",
    )(d_joined, weight, d_first)


def project_kernel(w_ref, b_ref, *refs):
    pieces, (tokens_ref, out_ref) = refs[:-2], refs[-2:]
    step = pl.program_id(0)

    @pl.when(step == 0)
    def _():
        join_kernel(*pieces, tokens_ref)

    tokens = tokens_ref[pl.ds(pl.multiple_of(step * BLOCK, BLOCK), BLOCK), :]
    out_ref[...] = (dot(tokens, w_ref[...]) + b_ref[...]).astype(BF16)


def project(pieces, weight, bias):
    rows, width = sum(x.shape[0] for x in pieces), weight.shape[1]
    return pl.pallas_call(
        project_kernel,
        grid=(rows // BLOCK,),
        in_specs=[
            pl.BlockSpec((D, width), lambda i: (0, 0)),
            pl.BlockSpec((1, width), lambda i: (0, 0)),
        ]
        + [pl.BlockSpec(x.shape, lambda i: (0, 0)) for x in pieces],
        out_specs=[
            pl.BlockSpec((rows, D), lambda i: (0, 0)),
            pl.BlockSpec((BLOCK, width), lambda i: (i, 0)),
        ],
        out_shape=[
            jax.ShapeDtypeStruct((rows, D), BF16),
            jax.ShapeDtypeStruct((rows, width), BF16),
        ],
        compiler_params=pltpu.CompilerParams(vmem_limit_bytes=VMEM_LIMIT),
        cost_estimate=pl.CostEstimate(
            flops=2 * rows * D * width,
            bytes_accessed=2 * (rows * (2 * D + width) + D * width),
            transcendentals=0,
        ),
        name="project",
    )(weight, bias, *pieces)


def add_norm_kernel(
    rows_of, left_ref, w_ref, base_ref, mask_ref, vec_ref, norm_ref, inverse_ref, low_ref, *more
):
    bias, gain, shift = (vec_ref[k : k + 1, :] for k in rows_of)
    norm, inverse = normalized(base_ref[...].astype(F32) + dot(left_ref[...], w_ref[...]) + bias)
    value = norm * gain + shift
    norm_ref[...] = norm
    inverse_ref[...] = inverse
    if more:
        more[0][...] = value
        low_ref[...] = value.astype(BF16)
    else:
        low_ref[...] = (value * mask_ref[...]).astype(BF16)


def add_norm(left, weight, base, mask, vec, rows_of, keep):
    rows, depth = left.shape
    wide = pl.BlockSpec((BLOCK, D), lambda i: (i, 0))
    thin = pl.BlockSpec((BLOCK, 1), lambda i: (i, 0))
    shape = jax.ShapeDtypeStruct((rows, D), F32)
    return pl.pallas_call(
        functools.partial(add_norm_kernel, rows_of),
        grid=(rows // BLOCK,),
        in_specs=[
            pl.BlockSpec((BLOCK, depth), lambda i: (i, 0)),
            pl.BlockSpec((depth, D), lambda i: (0, 0)),
            wide,
            thin,
            pl.BlockSpec((8, D), lambda i: (0, 0)),
        ],
        out_specs=[wide, thin, wide] + [wide] * keep,
        out_shape=[
            shape,
            jax.ShapeDtypeStruct((rows, 1), F32),
            jax.ShapeDtypeStruct((rows, D), BF16),
        ]
        + [shape] * keep,
        compiler_params=pltpu.CompilerParams(vmem_limit_bytes=VMEM_LIMIT),
        cost_estimate=pl.CostEstimate(
            flops=2 * rows * D * depth,
            bytes_accessed=2 * (rows + D) * depth + 12 * rows * D,
            transcendentals=0,
        ),
        name="add_norm",
    )(left, weight, base, mask, vec)


def normalized(values):
    centred = values - jnp.mean(values, axis=-1, keepdims=True)
    spread = jnp.mean(centred * centred, axis=-1, keepdims=True)
    inverse = lax.rsqrt(spread + norm_eps)
    return centred * inverse, inverse


def norm_back(grad, gain, norm, inverse):
    scaled = grad * gain
    return inverse * (
        scaled
        - jnp.mean(scaled, axis=-1, keepdims=True)
        - norm * jnp.mean(scaled * norm, axis=-1, keepdims=True)
    )


def per_device(places, *args):
    (
        question_in,
        passage_in,
        question_len,
        passage_len,
        positive,
        question_cot,
        passage_cot,
        w_joined,
        w_output,
        w_expand,
        w_reduce,
        vectors,
        b_expand,
    ) = args
    pb, pa = lax.axis_index("pb"), lax.axis_index("pa")
    z, core = pa // 2, pa % 2
    tower = z // places.half
    is_q = tower == 0
    chip = pb * places.nz + z
    masks = [places.stack_masks(side) for side in range(2)]
    slots_of = [sorted(range(places.chips), key=side.__getitem__) for side in masks]

    def of_core(rows_of):
        both = jnp.array(rows_of, jnp.int32)
        return (
            lax.dynamic_index_in_dim(both, core, 0, keepdims=False),
            lax.dynamic_index_in_dim(both, 1 - core, 0, keepdims=False),
        )

    side = jnp.full((places.chips,), core, jnp.int32)
    table = jnp.stack([x ^ chip for x in of_core(masks)] + [side]).astype(jnp.int32)
    slots = [x ^ lax.dynamic_index_in_dim(x, chip, 0, keepdims=False) for x in of_core(slots_of)]
    slots = jnp.stack(slots + [side]).astype(jnp.int32)
    share = w_joined.shape[1]

    small = jnp.concatenate(
        [
            vectors.transpose(0, 2, 1),
            b_expand.reshape(2, share, 4),
            jnp.zeros((2, share, 116), BF16),
        ],
        axis=2,
    )
    first = jnp.concatenate([w_joined, w_output, small], axis=2)
    second, third = w_expand, w_reduce

    class Gather:
        def __init__(self, piece):
            self.stack = lax.dynamic_index_in_dim(piece, tower, 0, keepdims=True)
            self.send = lax.dynamic_index_in_dim(piece, 1 - tower, 0, keepdims=True)
            self.held = None

        def join(self, got):
            self.stack = jnp.concatenate([self.stack, got], axis=0)
            self.send = self.stack

        def move(self, first, last):
            for step in range(first, last):
                self.join(places.swap(self.send, step))

        def mid(self):
            self.move(0, 1)

        def along_z(self):
            self.move(1, z_steps)

        def pb_first(self):
            self.move(z_steps, places.steps - 1)

        def pb_last(self):
            self.held = places.swap(self.send, places.steps - 1)

        def core_stack(self):
            self.other = places.swap_core(self.stack)

        def core_held(self):
            self.parts = [self.stack, self.held, self.other, places.swap_core(self.held)]

        def whole(self, segments):
            if self.stack.shape[1] % 8 == 0:
                return assemble(self.parts, table, segments)
            return assemble_plain(self.parts, table, segments)

    z_steps = 1 + len(bits_of(places.half))

    rows_q = question_in.reshape(-1, D)
    rows_p = passage_in.reshape(-1, D)
    own_rows = rows_q.shape[0]

    def sides(q_side, p_side):
        return jnp.where(is_q, q_side, p_side), jnp.where(is_q, p_side, q_side)

    lq, lp = question_in.shape[1], passage_in.shape[1]
    rows = 2 * own_rows

    def chunked(values, sixteenths):
        out, row = [], 0
        for part in sixteenths:
            step = values.shape[0] * part // 16
            out.append(values[row : row + step])
            row += step
        return out

    def hand(values):
        return [places.swap_tower(x) for x in values]

    per_q = rows // lq
    every = lp // lq
    per_p = rows // lp
    nq, np_ = question_in.shape[0], passage_in.shape[0]
    shift = 2 * places.half
    low_pa = pa % shift
    row_ids = jnp.arange(rows, dtype=jnp.int32)
    seq = jnp.where(is_q, row_ids // lq, row_ids // lp)
    qid = seq.reshape(rows, 1)
    g1, g2, g3 = Gather(first), Gather(second), Gather(third)
    my_tokens, send_tokens = sides(rows_q, rows_p)
    tokens_out = chunked(send_tokens, (5, 4, 7))
    g1.mid()
    g1.send, tokens_out, question_cot, passage_cot = tie(
        g1.send, tokens_out, question_cot, passage_cot
    )
    g1.along_z()
    tokens_in = hand(tokens_out[:1])
    my_cot, send_cot = sides(question_cot.reshape(-1, D), passage_cot.reshape(-1, D))
    g1.send, g2.send, tokens_in, my_cot, send_cot, table, slots, seq, qid = tie(
        g1.send, g2.send, tokens_in, my_cot, send_cot, table, slots, seq, qid
    )
    g3.send, g3.stack = tie(g3.send, g3.stack)
    g1.pb_first()
    g2.mid()
    g1.stack, g2.send, tokens_out = tie(g1.stack, g2.send, tokens_out)
    g1.send = g1.stack
    g1.pb_last()
    g1.core_stack()
    g2.along_z()
    tokens_in = tokens_in + hand(tokens_out[1:2])
    g1.held, g2.send, tokens_in, tokens_out, question_len, passage_len, positive = tie(
        g1.held, g2.send, tokens_in, tokens_out, question_len, passage_len, positive
    )
    g1.core_held()
    g2.pb_first()
    tokens_in = tokens_in + hand(tokens_out[2:])
    full_j, full_o, full_small = g1.whole([(0, 3 * D), (3 * D, D), (4 * D, 128)])
    full_j, full_o, full_small, g2.stack, g3.send, tokens_in = tie(
        full_j, full_o, full_small, g2.stack, g3.send, tokens_in
    )
    g2.send = g2.stack
    g2.pb_last()
    g2.core_stack()
    g3.mid()
    wj = full_j.reshape(D, 3 * D)
    wo = full_o.reshape(D, D)
    small = full_small.reshape(D, 128).astype(F32)
    vec = small[:, :8].T
    bias_e = small[:, 8:12].reshape(1, FF)
    bias_j = jnp.concatenate([vec[0], jnp.zeros((D,), F32), vec[1]])
    tokens, qkv = project([my_tokens] + tokens_in, wj, bias_j[None])

    cot_out = chunked(send_cot, (4, 3, 3, 2, 4))
    by_pa = positive.reshape(places.pa_n, nq)
    pair = [lax.dynamic_index_in_dim(by_pa, low_pa + k, 0, keepdims=False) for k in (0, shift)]
    pair = jnp.concatenate(pair)[None]
    wanted_rows = jnp.concatenate([pair // 16, pair % 16], axis=0).astype(BF16)
    wanted_rows = jnp.pad(wanted_rows, ((0, 0), (0, D - per_q)))
    valid_q = (jnp.arange(lq, dtype=jnp.int32)[None, :] < question_len[:, None]).astype(jnp.int32)
    valid_p = (jnp.arange(lp, dtype=jnp.int32)[None, :] < passage_len[:, None]).astype(jnp.int32)
    my_valid, send_valid = sides(valid_q.reshape(-1), valid_p.reshape(-1))
    valid = jnp.concatenate([my_valid, places.swap_tower(send_valid)])
    kid = jnp.where(valid > 0, seq, -1).reshape(rows // BLOCK, 1, BLOCK)
    row_mask = valid.reshape(rows, 1).astype(F32)

    blocks = rows // BLOCK
    later = blocks // 2
    qkv, g3.send, cot_out = tie(qkv, g3.send, cot_out)
    g3.along_z()
    cot_in = hand(cot_out[:1])
    context, probs = attention(qkv, qid, kid)
    context, g2.held, g3.send, cot_in, cot_out = tie(context, g2.held, g3.send, cot_in, cot_out)
    g2.core_held()
    g3.pb_first()
    cot_in = cot_in + hand(cot_out[1:2])
    norm_one, inverse_one, mid_low, mid = add_norm(
        context, wo, tokens, row_mask, vec, (2, 3, 4), True
    )
    mid_low, g2.parts, g3.stack, cot_in, cot_out = tie(mid_low, g2.parts, g3.stack, cot_in, cot_out)
    g3.send = g3.stack
    g3.pb_last()
    g3.core_stack()
    (full_e,) = g2.whole([(0, FF)])
    we = full_e.reshape(D, FF)
    mid_low, we, cot_out = tie(mid_low, we, cot_out)
    cot_in = cot_in + hand(cot_out[2:3])
    gelu = expand(mid_low, we, bias_e, 0, 1)
    gelu, g3.held, g3.other, g3.stack, cot_in, cot_out = tie(
        gelu, g3.held, g3.other, g3.stack, cot_in, cot_out
    )
    g3.core_held()
    cot_in = cot_in + hand(cot_out[3:4])
    active, slope = expand(mid_low, we, bias_e, 1, 1, tuple(gelu))
    active, g3.parts, cot_in, cot_out = tie(active, g3.parts, cot_in, cot_out)
    (full_r,) = g3.whole([(0, D)])
    wr = full_r.reshape(FF, D)
    wr, cot_out = tie(wr, cot_out)
    cot_in = cot_in + hand(cot_out[4:])
    norm_two, inverse_two, out = add_norm(active, wr, mid, row_mask, vec, (5, 6, 7), False)
    out, cot_in = tie(out, cot_in)

    firsts = out.reshape(per_q, lq, D)[:, 0, :]
    others = places.swap_tower(firsts)
    cls_q = jnp.where(is_q, firsts, others)
    cls_p = jnp.where(is_q, others, firsts)[::every]
    pad = (-(per_q + per_p + 2)) % 8
    stack = jnp.concatenate([cls_q, cls_p, wanted_rows, jnp.zeros((pad, D), BF16)], axis=0)[None]
    pair_masks = [0]
    for bit in bits_of(places.half):
        got = lax.ppermute(stack, "pa", [(i, i ^ (2 * bit)) for i in range(places.pa_n)])
        stack = jnp.concatenate([stack, got], axis=0)
        pair_masks = pair_masks + [m ^ (2 * bit) for m in pair_masks]
    for bit in bits_of(places.pb_n):
        got = lax.ppermute(stack, "pb", [(i, i ^ bit) for i in range(places.pb_n)])
        stack = jnp.concatenate([stack, got], axis=0)
        pair_masks = pair_masks + [m ^ (bit * places.pa_n) for m in pair_masks]
    stack = jnp.concatenate([stack, places.swap_core(stack)], axis=0)
    pair_masks = pair_masks + [m ^ 1 for m in pair_masks]
    groups = len(pair_masks)
    me = pb * places.pa_n + low_pa
    place = jnp.array(pair_masks, jnp.int32) ^ me
    dev_p = jnp.stack([place + shift, place], axis=1)
    p_ids = (dev_p[:, :, None] * np_ + jnp.arange(np_, dtype=jnp.int32)).reshape(-1)
    digits = stack[:, per_q + per_p : per_q + per_p + 2, :per_q].astype(jnp.int32)
    wanted = (digits[:, 0] * 16 + digits[:, 1]).reshape(-1)

    all_q = stack[:, :per_q].reshape(groups * per_q, D)
    all_p = stack[:, per_q : per_q + per_p].reshape(groups * per_p, D)
    similarity = dot(all_q, all_p, ((1,), (1,))) * score_scale
    hot = (wanted[:, None] == p_ids[None, :]).astype(F32)
    top = jnp.max(similarity, axis=1, keepdims=True)
    grown = jnp.exp(similarity - top)
    total = jnp.sum(grown, axis=1, keepdims=True)
    own_sim = similarity[:per_q]
    loss = top[:per_q, 0] + jnp.log(total[:per_q, 0]) - jnp.sum(own_sim * hot[:per_q], axis=1)
    question_loss = lax.dynamic_slice_in_dim(loss, tower * nq, nq)
    d_sim = (loss_weight * (grown / total - hot)).astype(BF16)
    d_q = dot(d_sim[:per_q], all_p) * score_scale
    d_p = dot(d_sim[:, :per_p], all_q, ((0,), (0,))) * score_scale
    d_p = jnp.concatenate(
        [d_p.reshape(per_p, 1, D), jnp.zeros((per_p, every - 1, D), F32)], axis=1
    ).reshape(per_q, D)
    d_slot = jnp.where(is_q, d_q, d_p)

    d_second, d_reduced, sums_second = second_back(
        join([my_cot] + cot_in), d_slot, row_mask, norm_two, inverse_two, vec[6][None, :]
    )
    even = share % 8 == 0

    def gradient(left, right, **more):
        if left.shape[1] > D:
            return tall_grad(left, right, slots, places.nz)
        return weight_grad(left, right, slots, D, **more)

    def plain(left, right, extra=None):
        if extra is not None:
            one, two, first, second, bias = extra
            joined = one + two
            lines = [joined[:, :D], joined[:, 2 * D :], first[2:3], first[:2]]
            lines = lines + [second[2:3], second[:2], bias, jnp.zeros((116, D), F32)]
            extra = jnp.concatenate(lines, axis=0).T
        return grad_plain(left, right, table, extra)

    class Scatter:
        def __init__(self, mine, theirs):
            self.parts, self.theirs, self.send = [mine], theirs, None
            self.count = mine.shape[0]

        def cores(self):
            self.parts = self.parts + [places.swap_core(self.theirs)]

        def total(self, start, stop):
            out = self.parts[0][start:stop].astype(F32)
            for part in self.parts[1:]:
                out = out + part[start:stop].astype(F32)
            return out

        def prepare(self):
            self.send = self.total(self.count // 2, self.count).astype(BF16)

        def move(self, step):
            if self.send is None:
                self.prepare()
            self.parts = self.parts + [places.swap(self.send, step)]
            self.send = None
            self.count = self.count // 2

        def pb_first(self):
            self.move(places.steps - 1)

        def pb_rest(self):
            for step in range(places.steps - 2, z_steps - 1, -1):
                self.move(step)

        def along_z(self):
            for step in range(z_steps - 1, 0, -1):
                self.move(step)

        def mid(self):
            self.got = places.swap(self.total(1, 2).astype(BF16), 0)

        def finish(self):
            got, keep = self.got.astype(F32), self.total(0, 1)
            return jnp.concatenate(
                [jnp.where(is_q, keep, got), jnp.where(is_q, got, keep)], axis=0
            )

    send_out = chunked(out[own_rows:], (4, 4, 4, 4))
    d_reduced, send_out = tie(d_reduced, send_out)
    got_out = hand(send_out[:1])
    sr = Scatter(*(gradient if even else plain)(active, d_reduced))
    sr.parts, sr.theirs, d_reduced, got_out, send_out = tie(
        sr.parts, sr.theirs, d_reduced, got_out, send_out
    )
    sr.cores()
    got_out = got_out + hand(send_out[1:2])
    d_expanded, g_bias_expand = hidden_grad(d_reduced, wr, slope)
    sr.parts, d_expanded, got_out, send_out = tie(sr.parts, d_expanded, got_out, send_out)
    sr.pb_first()
    got_out = got_out + hand(send_out[2:3])
    if even:
        partial = gradient(mid_low, d_expanded, room=D)
    else:
        partial = plain(mid_low, d_expanded)
    partial, d_expanded, got_out, send_out = tie(partial, d_expanded, got_out, send_out)
    got_out = got_out + hand(send_out[3:])
    d_first, d_attended, sums_first = first_back(
        d_expanded, we, d_second, norm_one, inverse_one, vec[3][None, :]
    )
    sr.parts, partial, d_attended, got_out = tie(sr.parts, partial, d_attended, got_out)
    sr.pb_rest()
    if even:
        partial = gradient(context, d_attended, into=tuple(partial))
    else:
        also = plain(context, d_attended)
        partial = [jnp.concatenate(x, axis=2) for x in zip(partial, also)]
    se = Scatter(*partial)
    se.parts, se.theirs, d_attended = tie(se.parts, se.theirs, d_attended)
    se.cores()
    d_context = dot(d_attended, wo, ((1,), (1,))).astype(BF16)
    d_joined, sums_one = attention_back(qkv, probs, d_context, later, blocks - later)
    sr.parts, se.parts, d_joined = tie(sr.parts, se.parts, d_joined)
    se.prepare()
    sr.prepare()
    sr.send, sr.parts, se.send, se.parts, d_joined = tie(
        sr.send, sr.parts, se.send, se.parts, d_joined
    )
    se.pb_first()
    sr.along_z()
    part = own_rows // 16
    send_grad = token_grad(d_joined, wj, d_first, own_rows, [k * part for k in (5, 3, 3, 5)], BF16)
    d_joined, send_grad = tie(d_joined, send_grad)
    got_grad = hand(send_grad[:1])
    d_joined, sums_two = attention_back(qkv, probs, d_context, 0, later, d_joined)
    sr.parts, se.parts, d_joined, sums_two, got_grad, send_grad = tie(
        sr.parts, se.parts, d_joined, sums_two, got_grad, send_grad
    )
    se.prepare()
    se.send, se.parts, d_joined, send_grad = tie(se.send, se.parts, d_joined, send_grad)
    se.pb_rest()
    sr.mid()
    got_grad = got_grad + hand(send_grad[1:2])
    bias_sums = g_bias_expand.reshape(D, 4).T
    small_sums = (sums_one, sums_two, sums_first, sums_second, bias_sums)
    sj = Scatter(*(gradient if even else plain)(tokens, d_joined, extra=small_sums))
    se.parts, sr.got, sj.parts, sj.theirs, d_joined, got_grad, send_grad = tie(
        se.parts, sr.got, sj.parts, sj.theirs, d_joined, got_grad, send_grad
    )
    sj.cores()
    got_grad = got_grad + hand(send_grad[2:3])
    (own_grad,) = token_grad(d_joined, wj, d_first, 0, [own_rows], F32)
    sj.parts, own_grad, got_grad, send_grad = tie(sj.parts, own_grad, got_grad, send_grad)
    sj.pb_first()
    se.along_z()
    got_grad = got_grad + hand(send_grad[3:])
    out_q, out_p = deal(tower.reshape(1), out, got_out)
    grad_reduce = sr.finish()
    sj.parts, se.parts, got_grad, out_q, out_p, grad_reduce = tie(
        sj.parts, se.parts, got_grad, out_q, out_p, grad_reduce
    )
    sj.pb_rest()
    se.mid()
    grad_q, grad_p = deal(tower.reshape(1), own_grad, got_grad)
    sj.parts, se.got, se.parts, grad_q, grad_p = tie(sj.parts, se.got, se.parts, grad_q, grad_p)
    sj.along_z()
    both = se.finish()
    sj.parts, both = tie(sj.parts, both)
    sj.mid()
    last = sj.finish()
    grad_joined = last[:, :, : 3 * D]
    grad_expand, grad_output = both[:, :, :FF], both[:, :, FF:]
    extra = last[:, :, 3 * D :]
    grad_vectors = extra[:, :, :8].transpose(0, 2, 1)
    grad_b_expand = extra[:, :, 8:12].reshape(2, 4 * share)

    return (
        out_q.reshape(question_in.shape),
        out_p.reshape(passage_in.shape),
        question_loss,
        grad_q.reshape(question_in.shape),
        grad_p.reshape(passage_in.shape),
        grad_joined,
        grad_output,
        grad_expand,
        grad_reduce,
        grad_vectors,
        grad_b_expand,
    )


def solution(mesh):
    in_specs = (
        P(("pb", "pa"), None, None),
        P(("pb", "pa"), None, None),
        P(("pb", "pa")),
        P(("pb", "pa")),
        P("pb"),
        P(("pb", "pa"), None, None),
        P(("pb", "pa"), None, None),
        P(None, ("pb", "pa"), None),
        P(None, ("pb", "pa"), None),
        P(None, ("pb", "pa"), None),
        P(None, ("pb", "pa"), None),
        P(None, None, ("pb", "pa")),
        P(None, ("pb", "pa")),
    )
    out_specs = (
        P(("pb", "pa"), None, None),
        P(("pb", "pa"), None, None),
        P(("pb", "pa")),
        P(("pb", "pa"), None, None),
        P(("pb", "pa"), None, None),
        P(None, ("pb", "pa"), None),
        P(None, ("pb", "pa"), None),
        P(None, ("pb", "pa"), None),
        P(None, ("pb", "pa"), None),
        P(None, None, ("pb", "pa")),
        P(None, ("pb", "pa")),
    )
    return jax.shard_map(
        functools.partial(per_device, Places(mesh)),
        mesh=mesh,
        in_specs=in_specs,
        out_specs=out_specs,
        check_vma=False,
    )
```
